32 devices in a mesh: seq: 8 (over z, x), ch: 4 (over y, core).
Axes of the slice: x: 2, y: 2, z: 4, core: 2. Of those that a mesh axis runs over, the one named last changes fastest.
Arguments:
- x_in: bfloat16 [2048, 2048], P('seq'), may hold values from -6 to 6
- norm_gain: float32 [2048], replicated, may hold values from 0.25 to 1.75
- w_in: bfloat16 [3, 2048, 2, 4096], P(None, None, None, 'ch'), may hold values from -0.125 to 0.125
- conv_weight: float32 [4, 4096], P(None, 'ch'), may hold values from -3 to 3
- conv_bias: float32 [4096], P('ch'), may hold values from -1.5 to 1.5
- x_proj: bfloat16 [4096, 160], P('ch'), may hold values from -0.09375 to 0.09375
- dt_proj: bfloat16 [128, 4096], P(None, 'ch'), may hold values from -0.5 to 0.5
- dt_bias: float32 [4096], P('ch'), may hold values from -6 to -1
- a_log: float32 [16, 4096], P(None, 'ch'), may hold values from -4 to 2.8
- d_skip: float32 [4096], P('ch'), may hold values from 0.5 to 1.5
- w_out: bfloat16 [3, 2048, 4096], P(None, None, 'ch'), may hold values from -0.1875 to 0.1875
- modes: int32 [2048], replicated, may hold values from 0 to 2
- doc_lengths: int32 [4], replicated, may hold values from 1 to 1024, 2048 in all
- cotangent: bfloat16 [2048, 2048], P('seq', 'ch'), may hold values from -6 to 6
Outputs:
- block_out: bfloat16 [2048, 2048], P('seq', 'ch')
- d_x_in: float32 [2048, 2048], P('seq', 'ch')
- d_norm_gain: float32 [2048], P('ch')
- d_w_in: float32 [3, 2048, 2, 4096], P(None, 'seq', None, 'ch')
- d_conv_weight: float32 [4, 4096], P(None, 'ch')
- d_conv_bias: float32 [4096], P('ch')
- d_x_proj: float32 [4096, 160], P('ch')
- d_dt_proj: float32 [128, 4096], P(None, 'ch')
- d_dt_bias: float32 [4096], P('ch')
- d_a_log: float32 [16, 4096], P(None, 'ch')
- d_d_skip: float32 [4096], P('ch')
- d_w_out: float32 [3, 2048, 4096], P(None, 'seq', 'ch')
The draws below stay inside these ranges and needn't reach their ends.
Inputs may be any that keep to these rules, and one draw needn't show every extreme that they name: `doc_lengths`: the documents lie end to end in token order and their lengths sum to 2048. `modes`: 0 image, 1 text, 2 speech.
All inputs are finite; a program needn't handle non-finite values.
Results may differ from the reference program's by a relative error of at most 0.012.
Values may be sent and summed in bfloat16 or wider, within the bound.
A program may use at most 192 MiB of HBM per device.

```python
import math
import jax
import jax.numpy as jnp
import numpy as np
from jax import lax

D = 2048
INNER = 4096
STATE = 16
RANK = 128
CONV = 4
MODES = 3
TOKENS = 2048
DOC_MAX = 1024
DOCS = 4


def touch_ends(array, rng, smallest, top_value):
    longest = array.shape.index(max(array.shape))
    spots = []
    for shift in (0, 1):
        where = [jax.random.randint(jax.random.fold_in(rng, axis), (), 0, length) for axis, length in enumerate(array.shape)]
        where[longest] = (where[longest] + shift) % array.shape[longest]
        spots.append(tuple(where))
    return array.at[spots[0]].set(smallest).at[spots[1]].set(top_value)


def spiked(entries, stream_key, source, target, blocks, factor):
    owner, partner = [(jnp.arange(entries.shape[axis_at]) // (entries.shape[axis_at] // blocks)).reshape([-1 if axis == axis_at else 1 for axis in range(entries.ndim)]) for axis_at in (source, target)]
    chosen = jax.random.permutation(stream_key, blocks)[partner]
    strong = (owner == chosen) | (owner == (partner + blocks // 2) % blocks)
    return jnp.where(strong, factor * entries, entries)


def levels(key, shape, cuts, smallest, top_value):
    factor_of, own = 1.0, jax.random.fold_in(key, 6)
    for axis_at, shards_of in cuts:
        draws = jnp.exp(jax.random.uniform(jax.random.fold_in(own, axis_at), (shards_of,), jnp.float32, smallest / len(cuts), top_value / len(cuts)))
        factor_of = factor_of * jnp.repeat(draws, shape[axis_at] // shards_of).reshape([-1 if axis == axis_at else 1 for axis in range(len(shape))])
    return factor_of


def length_profile(number_of, total, reach, slope):
    portions = [(1 << 20) // math.isqrt(standing ** slope) + 1 for standing in range(2, number_of + 1)]
    spare, counts = total - reach - (number_of - 1), [1] * (number_of - 1)
    while spare > 0:
        free = [i for i in range(number_of - 1) if counts[i] < reach]
        mass, remaining = sum([portions[i] for i in free]), spare
        for i in free:
            addition = min(reach - counts[i], max(1, remaining * portions[i] // mass), spare)
            counts[i] = counts[i] + addition
            spare = spare - addition
    return np.array([reach] + counts)


def ragged_sizes(own_key, number_of, total, reach, skew):
    if number_of == 2:
        one = jax.random.randint(own_key, (), max(1, total - reach), min(reach, total - 1) + 1)
        return jnp.stack([one, total - one])
    lengths = jnp.asarray(length_profile(number_of, total, reach, skew), jnp.int32)
    couples = (number_of - 1) // 2
    giver, receiver = lengths[1:1 + 2 * couples:2], lengths[2:2 + 2 * couples:2]
    slack = jnp.minimum(giver - 1, reach - receiver)
    passed = jax.random.randint(jax.random.fold_in(own_key, 1), (couples,), 0, 1 << 20) % (slack + 1)
    lengths = lengths.at[1:1 + 2 * couples:2].set(giver - passed).at[2:2 + 2 * couples:2].set(receiver + passed)
    return lengths[jax.random.permutation(jax.random.fold_in(own_key, 2), number_of)]


def bell_draw(stream_key, dims, scale, limit, cuts=(), kind=jnp.bfloat16):
    values = jax.random.normal(stream_key, dims, jnp.float32) * scale
    if len(cuts) > 0:
        values = levels(stream_key, dims, cuts, -0.22, 0.18) * values
    return jnp.clip(values, min=-limit, max=limit).astype(kind)


def gaussian_with(own_key, extent, deviation, bound, cuts, heavy, kind=jnp.bfloat16):
    values = deviation * jax.random.normal(own_key, extent, jnp.float32)
    if cuts:
        values = values * levels(own_key, extent, cuts, -0.22, 0.18)
    return jnp.clip(spiked(values, jax.random.fold_in(own_key, 3), *heavy), -bound, bound).astype(kind)


def setup_inputs(seed: int = 0) -> dict:
    splits = jax.random.split(jax.random.key(seed), 15)
    x_in = bell_draw(splits[0], (TOKENS, D), 1.0, 6.0, ((0, 8),))
    norm_gain = jnp.clip(1.0 + 0.15 * jax.random.normal(splits[1], (D,), jnp.float32), 0.25, 1.75)
    w_in = bell_draw(splits[2], (MODES, D, 2, INNER), D ** -0.5, 0.125, ((3, 4),))
    conv_weight = bell_draw(splits[3], (CONV, INNER), CONV ** -0.5, 3.0, ((1, 4),), jnp.float32)
    conv_bias = bell_draw(splits[4], (INNER,), 0.3, 1.5, ((0, 4),), jnp.float32)
    x_proj = bell_draw(splits[5], (INNER, RANK + 2 * STATE), INNER ** -0.5, 0.09375, ((0, 4),))
    dt_proj = bell_draw(splits[6], (RANK, INNER), RANK ** -0.5, 0.5, ((1, 4),))
    dt_bias = jnp.clip(-6.0 + 5.0 * jax.random.uniform(splits[7], (INNER,), jnp.float32) ** levels(splits[7], (INNER,), ((0, 4),), -0.2, 0.2), -6.0, -1.0)
    a_log = jnp.clip(-4.0 + 6.8 * jax.random.uniform(splits[8], (STATE, INNER), jnp.float32) ** levels(splits[8], (STATE, INNER), ((1, 4),), -0.2, 0.2), -4.0, 2.8)
    d_skip = jnp.clip(0.5 + 1.0 * jax.random.uniform(splits[9], (INNER,), jnp.float32) ** levels(splits[9], (INNER,), ((0, 4),), -0.2, 0.2), 0.5, 1.5)
    w_out = bell_draw(splits[10], (MODES, D, INNER), (INNER // 4) ** -0.5, 0.1875, ((2, 4),))
    modes = touch_ends(jax.random.randint(splits[11], (TOKENS,), 0, MODES), jax.random.fold_in(splits[11], 1), 0, MODES - 1).astype(jnp.int32)
    doc_lengths = ragged_sizes(splits[12], DOCS, TOKENS, DOC_MAX, 2).astype(jnp.int32)
    cotangent = gaussian_with(splits[13], (TOKENS, D), 1.0, 6.0, ((0, 8), (1, 4)), (0, 1, 8, 2.0))
    return {"x_in": x_in, "norm_gain": norm_gain, "w_in": w_in, "conv_weight": conv_weight, "conv_bias": conv_bias, "x_proj": x_proj, "dt_proj": dt_proj, "dt_bias": dt_bias, "a_log": a_log, "d_skip": d_skip, "w_out": w_out, "modes": modes, "doc_lengths": doc_lengths, "cotangent": cotangent}


@jax.custom_vjp
def low(v):
    return lax.optimization_barrier(v.astype(jnp.bfloat16)).astype(jnp.float32)

@jax.custom_vjp
def low_back(v):
    return v

def low_keep(v):
    return (low(v), None)

def low_pass(kept, grad):
    return (grad,)

def back_keep(v):
    return (v, None)

def back_low(kept, grad):
    return (low(grad),)
low.defvjp(low_keep, low_pass)
low_back.defvjp(back_keep, back_low)
EPSILON = 1e-05
HIGHEST = lax.Precision.HIGHEST

def mix_pair(earlier, latter):
    return (earlier[0] * latter[0], latter[0] * earlier[1] + latter[1])

def doc_tables(doc_lengths, positions):
    doc_ends = jnp.cumsum(doc_lengths)
    doc_starts = doc_ends - doc_lengths
    doc_index = lax.optimization_barrier(jnp.sum((positions[:, None] >= doc_ends[None, :]).astype(jnp.int32), axis=1))
    begins = jnp.any(positions[:, None] == doc_starts[None, :], axis=1)
    return (doc_index, begins)

def block_forward(x_full, norm_gain, w_in, conv_weight, conv_bias, x_proj, dt_proj, dt_bias, a_log, d_skip, w_out, modes, doc_lengths):
    tok_count = x_full.shape[0]
    channels = conv_bias.shape[0]
    scale = lax.rsqrt(lax.optimization_barrier(jnp.mean(x_full * x_full, axis=1, keepdims=True)) + EPSILON)
    normed = low(x_full * scale * norm_gain[None])
    onehot = (modes[:, None] == jnp.arange(MODES, dtype=jnp.int32)[None]).astype(jnp.float32)
    expanded = (onehot[:, :, None] * normed[:, None, :]).reshape(tok_count, MODES * D)
    projected_xz = low_back(low(jnp.dot(expanded, w_in.reshape(MODES * D, 2 * channels), precision=HIGHEST)))
    projected_xz = projected_xz.reshape(tok_count, 2, channels)
    x_branch = projected_xz[:, 0]
    z_branch = projected_xz[:, 1]
    positions = jnp.arange(tok_count, dtype=jnp.int32)
    doc_index, begins = doc_tables(doc_lengths, positions)
    padded = jnp.pad(x_branch, ((CONV - 1, 0), (0, 0)))
    doc_padded = jnp.pad(doc_index, (CONV - 1, 0), constant_values=-1)
    conv_pre = jnp.zeros_like(x_branch) + conv_bias[None]
    for offset in range(CONV):
        same_doc = (doc_padded[offset:offset + tok_count] == doc_index).astype(jnp.float32)
        conv_pre = conv_pre + conv_weight[offset][None] * padded[offset:offset + tok_count] * same_doc[:, None]
    conv_out = low(jax.nn.silu(conv_pre))
    projected = low_back(jnp.dot(conv_out, x_proj, precision=HIGHEST))
    dt_low = low(projected[:, :RANK])
    b_in = projected[:, RANK:RANK + STATE]
    c_out = projected[:, RANK + STATE:]
    dt_raw = low_back(jnp.dot(dt_low, dt_proj, precision=HIGHEST))
    step_size = jax.nn.softplus(dt_raw + dt_bias[None])
    decay_rate = -jnp.exp(a_log)
    keep_mask = 1.0 - begins.astype(jnp.float32)
    block_len = math.gcd(256, tok_count)
    block_count = tok_count // block_len

    def scan_block(carried, pieces):
        step_piece, conv_piece, input_piece, output_piece, keep_piece = pieces
        decay = jnp.exp(step_piece[:, None, :] * decay_rate[None]) * keep_piece[:, None, None]
        drive = (step_piece * conv_piece)[:, None, :] * input_piece[:, :, None]
        decay_prod, local_sum = lax.associative_scan(mix_pair, (decay, drive), axis=0)
        states = local_sum + decay_prod * carried[None]
        return (states[-1], lax.optimization_barrier(jnp.sum(output_piece[:, :, None] * states, axis=1)))
    pieces = (step_size.reshape(block_count, block_len, channels), conv_out.reshape(block_count, block_len, channels), b_in.reshape(block_count, block_len, STATE), c_out.reshape(block_count, block_len, STATE), keep_mask.reshape(block_count, block_len))
    _, ssm_blocks = lax.scan(jax.checkpoint(scan_block), jnp.zeros((STATE, channels), jnp.float32), pieces)
    ssm = ssm_blocks.reshape(tok_count, channels) + d_skip[None] * conv_out
    gated = low(ssm * jax.nn.silu(z_branch))
    proj_all = jnp.einsum('te,mde->tmd', gated, w_out, precision=HIGHEST)
    mixer = lax.optimization_barrier(jnp.sum(onehot[:, :, None] * proj_all, axis=1))
    return x_full + mixer

def reference(x_in, norm_gain, w_in, conv_weight, conv_bias, x_proj, dt_proj, dt_bias, a_log, d_skip, w_out, modes, doc_lengths, cotangent):

    def run_block(x_full, gain_f, w_in_f, conv_w_f, conv_b_f, x_proj_f, dt_proj_f, dt_bias_f, a_log_f, d_skip_f, w_out_f):
        return block_forward(x_full, gain_f, w_in_f, conv_w_f, conv_b_f, x_proj_f, dt_proj_f, dt_bias_f, a_log_f, d_skip_f, w_out_f, modes, doc_lengths)
    result, pullback = jax.vjp(run_block, x_in.astype(jnp.float32), norm_gain, w_in.astype(jnp.float32), conv_weight, conv_bias, x_proj.astype(jnp.float32), dt_proj.astype(jnp.float32), dt_bias, a_log, d_skip, w_out.astype(jnp.float32))
    grads = pullback(cotangent.astype(jnp.float32))
    return (result.astype(jnp.bfloat16), grads[0], grads[1], grads[2], grads[3], grads[4], grads[5], grads[6], grads[7], grads[8], grads[9], grads[10])
```

```python
import functools
import math

import jax
import jax.numpy as jnp
from jax import lax
from jax.experimental import pallas as pl
from jax.experimental.pallas import tpu as pltpu
from jax.sharding import PartitionSpec as P

EPSILON = 1e-05


def from_behind(block, axis, distance):
    devices = range(lax.axis_size(axis))
    route = [(i - distance, i) for i in devices if i - distance in devices]
    return lax.ppermute(block, axis, route)


def doc_tables(doc_lengths, positions):
    count = doc_lengths.shape[0]
    order = jnp.arange(count, dtype=jnp.int32)
    doc_ends = jnp.sum(jnp.where(order[:, None] >= order[None, :], doc_lengths[None, :], 0), axis=1)
    doc_starts = doc_ends - doc_lengths
    doc_index = jnp.sum((positions[:, None] >= doc_ends[None, :]).astype(jnp.int32), axis=1)
    begins = jnp.any(positions[:, None] == doc_starts[None, :], axis=1)
    return (doc_index, begins)


def own_columns(values):
    rows, n = values.shape
    own = jnp.arange(16 * n)[None] // n == jnp.arange(rows)[:, None] % 16
    return jnp.where(own, jnp.tile(values, (1, 16)), 0).astype(jnp.bfloat16)


LB = 512
CH = 32
NS = 16

def tile_lanes(v, lanes):
    return jnp.concatenate([v] * (lanes // 128), axis=1)

def ends_kernel(lb, dtd_ref, u_ref, g_ref, b_ref, c_ref, rate_ref, out_ref):
    n = rate_ref.shape[0]
    rows, chans = dtd_ref.shape
    @pl.when(pl.program_id(0) == 0)
    def _():
        out_ref[0:n, :] = jnp.zeros((n, chans), jnp.float32)
        out_ref[n:2*n, :] = jnp.ones((n, chans), jnp.float32)
        out_ref[2*n:3*n, :] = jnp.zeros((n, chans), jnp.float32)
    for block in range(chans // lb):
        cut = slice(block * lb, (block + 1) * lb)
        rate = rate_ref[:, cut]
        h = out_ref[0:n, cut]
        reach = out_ref[n:2*n, cut]
        head = out_ref[2*n:3*n, cut]
        for t in range(rows):
            decay = jnp.exp2(dtd_ref[t:t+1, cut] * rate)
            h = decay * h + u_ref[t:t+1, cut] * tile_lanes(b_ref[t], lb)
            reach = reach * decay
            head = head + reach * (g_ref[t:t+1, cut] * tile_lanes(c_ref[t], lb))
        out_ref[0:n, cut] = h
        out_ref[n:2*n, cut] = reach
        out_ref[2*n:3*n, cut] = head

def scan_ends(dtd, u, g, b, c, rate, lb=LB, ch=CH):
    t, e = dtd.shape
    n = rate.shape[0]
    row = pl.BlockSpec((ch, e), lambda i: (i, 0))
    wide = pl.BlockSpec((ch, n, 128), lambda i: (i, 0, 0))
    return pl.pallas_call(
        functools.partial(ends_kernel, lb),
        grid=(t // ch,),
        in_specs=[row, row, row, wide, wide, pl.BlockSpec((n, e), lambda i: (0, 0))],
        out_specs=pl.BlockSpec((3 * n, e), lambda i: (0, 0)),
        out_shape=jax.ShapeDtypeStruct((3 * n, e), jnp.float32),
        compiler_params=pltpu.CompilerParams(vmem_limit_bytes=32 << 20),
        name="scan_ends",
    )(dtd, u, g, b, c, rate)

def forward_kernel(lb, dtd_ref, u_ref, b_ref, cblk_ref, rate_ref, h0_ref, y_ref, hist_ref, state_ref):
    n = rate_ref.shape[0]
    rows, chans = dtd_ref.shape
    @pl.when(pl.program_id(0) == 0)
    def _():
        state_ref[...] = h0_ref[...]
    for block in range(chans // lb):
        cut = slice(block * lb, (block + 1) * lb)
        rate = rate_ref[:, cut]
        h = state_ref[:, cut]
        for t in range(rows):
            decay = jnp.exp2(dtd_ref[t:t+1, cut] * rate)
            h = decay * h + u_ref[t:t+1, cut] * tile_lanes(b_ref[t], lb)
            hist_ref[t * n:(t + 1) * n, cut] = h.astype(jnp.bfloat16)
        state_ref[:, cut] = h
    for k in range(rows // 16):
        y_ref[k*16:(k+1)*16, :] = jnp.dot(cblk_ref[k*16:(k+1)*16, :], hist_ref[k*16*n:(k+1)*16*n, :], preferred_element_type=jnp.float32)

def scan_forward(dtd, u, b, cblk, rate, h0, lb=LB, ch=CH):
    t, e = dtd.shape
    n = rate.shape[0]
    row = pl.BlockSpec((ch, e), lambda i: (i, 0))
    wide = pl.BlockSpec((ch, n, 128), lambda i: (i, 0, 0))
    whole = pl.BlockSpec((n, e), lambda i: (0, 0))
    return pl.pallas_call(
        functools.partial(forward_kernel, lb),
        grid=(t // ch,),
        in_specs=[row, row, wide, pl.BlockSpec((ch, 16 * n), lambda i: (i, 0)), whole, whole],
        out_specs=(row, pl.BlockSpec((ch * n, e), lambda i: (i, 0))),
        out_shape=(jax.ShapeDtypeStruct((t, e), jnp.float32), jax.ShapeDtypeStruct((t * n, e), jnp.bfloat16)),
        scratch_shapes=[pltpu.VMEM((n, e), jnp.float32)],
        compiler_params=pltpu.CompilerParams(vmem_limit_bytes=32 << 20),
        name="scan_forward",
    )(dtd, u, b, cblk, rate, h0)

def backward_kernel(lb, dtd_ref, step_ref, conv_ref, g_ref, c_ref, bblk_ref, rate_ref, lam0_ref, h0_ref, hist_ref, prev_ref,
                    gstep_ref, gscan_ref, gb_ref, gc_ref, racc_ref, pend_ref, lam_ref, w_ref):
    n = rate_ref.shape[0]
    rows, chans = dtd_ref.shape
    last = pl.num_programs(0) - 1
    @pl.when(pl.program_id(0) == 0)
    def _():
        pend_ref[...] = lam0_ref[...]
        racc_ref[...] = jnp.zeros_like(racc_ref)
    first = pl.program_id(0) == last
    for block in range(chans // lb):
        cut = slice(block * lb, (block + 1) * lb)
        rate = rate_ref[:, cut]
        pend = pend_ref[:, cut]
        racc = racc_ref[:, cut]
        for t in reversed(range(rows)):
            decay = jnp.exp2(dtd_ref[t:t+1, cut] * rate)
            lam = g_ref[t:t+1, cut] * tile_lanes(c_ref[t], lb) + pend
            pend = decay * lam
            if t:
                before = hist_ref[(t - 1) * n:t * n, cut].astype(jnp.float32)
            else:
                before = jnp.where(first, h0_ref[:, cut], prev_ref[:, cut].astype(jnp.float32))
            w = pend * before
            racc = racc + w * step_ref[t:t+1, cut]
            lam_ref[t * n:(t + 1) * n, cut] = lam.astype(jnp.bfloat16)
            w_ref[t * n:(t + 1) * n, cut] = (w * rate).astype(jnp.bfloat16)
        pend_ref[:, cut] = pend
        racc_ref[:, cut] = racc
    for k in range(rows // 16):
        rc = slice(k * 16, (k + 1) * 16)
        hc = slice(k * 16 * n, (k + 1) * 16 * n)
        step = step_ref[rc, :]
        conv = conv_ref[rc, :]
        own = (lax.broadcasted_iota(jnp.int32, (16, 16 * n), 1) // n == lax.broadcasted_iota(jnp.int32, (16, 16 * n), 0))
        ones = own.astype(jnp.bfloat16)
        adj = jnp.dot(bblk_ref[rc, :], lam_ref[hc, :], preferred_element_type=jnp.float32)
        wsum = jnp.dot(ones, w_ref[hc, :], preferred_element_type=jnp.float32)
        gstep_ref[rc, :] = wsum * math.log(2.0) + adj * conv
        gscan_ref[rc, :] = adj * step
        nt = (((1,), (1,)), ((), ()))
        gb = lax.dot_general((step * conv).astype(jnp.bfloat16), lam_ref[hc, :], nt, preferred_element_type=jnp.float32)
        gc = lax.dot_general(g_ref[rc, :].astype(jnp.bfloat16), hist_ref[hc, :], nt, preferred_element_type=jnp.float32)
        gb_ref[k:k+1] = jnp.sum(jnp.where(own, gb, 0.0), axis=0, keepdims=True)[None]
        gc_ref[k:k+1] = jnp.sum(jnp.where(own, gc, 0.0), axis=0, keepdims=True)[None]

def scan_backward(dtd, step, conv, g, c, bblk, rate, lam0, h0, hist, lb=LB, ch=CH):
    t, e = dtd.shape
    n = rate.shape[0]
    k = t // ch
    row = pl.BlockSpec((ch, e), lambda i: (k - 1 - i, 0))
    wide = pl.BlockSpec((ch, n, 128), lambda i: (k - 1 - i, 0, 0))
    whole = pl.BlockSpec((n, e), lambda i: (0, 0))
    flat = pl.BlockSpec((ch // 16, 1, 16 * n), lambda i: (k - 1 - i, 0, 0))
    outs = pl.pallas_call(
        functools.partial(backward_kernel, lb),
        grid=(k,),
        in_specs=[row, row, row, row, wide, pl.BlockSpec((ch, 16 * n), lambda i: (k - 1 - i, 0)), whole, whole, whole,
                  pl.BlockSpec((ch * n, e), lambda i: (k - 1 - i, 0)),
                  pl.BlockSpec((n, e), lambda i: (jnp.maximum((k - 1 - i) * ch - 1, 0), 0))],
        out_specs=(row, row, flat, flat, whole),
        out_shape=(jax.ShapeDtypeStruct((t, e), jnp.float32), jax.ShapeDtypeStruct((t, e), jnp.float32),
                   jax.ShapeDtypeStruct((t // 16, 1, 16 * n), jnp.float32), jax.ShapeDtypeStruct((t // 16, 1, 16 * n), jnp.float32),
                   jax.ShapeDtypeStruct((n, e), jnp.float32)),
        scratch_shapes=[pltpu.VMEM((n, e), jnp.float32), pltpu.VMEM((ch * n, e), jnp.bfloat16), pltpu.VMEM((ch * n, e), jnp.bfloat16)],
        compiler_params=pltpu.CompilerParams(vmem_limit_bytes=48 << 20),
        name="scan_backward",
    )(dtd, step, conv, g, c, bblk, rate, lam0, h0, hist, hist)
    return outs[0], outs[1], outs[2].reshape(t, n), outs[3].reshape(t, n), outs[4]


def shards(
    x_in,
    norm_gain,
    w_in,
    conv_weight,
    conv_bias,
    x_proj,
    dt_proj,
    dt_bias,
    a_log,
    d_skip,
    w_out,
    modes,
    doc_lengths,
    cotangent,
):
    tok_rows, model_width = x_in.shape
    mode_count = w_in.shape[0]
    inner_local = conv_bias.shape[0]
    state_size = a_log.shape[0]
    rank_size = dt_proj.shape[0]
    conv_taps = conv_weight.shape[0]
    ch_count = lax.axis_size("ch")
    feat_part = model_width // ch_count
    seq_index = lax.axis_index("seq")
    ch_index = lax.axis_index("ch")
    first_pos = seq_index * tok_rows
    positions = first_pos + jnp.arange(tok_rows, dtype=jnp.int32)
    my_modes = lax.dynamic_slice_in_dim(modes, first_pos, tok_rows)
    onehot = (my_modes[:, None] == jnp.arange(mode_count, dtype=jnp.int32)[None]).astype(
        jnp.bfloat16
    )
    doc_index, begins = doc_tables(doc_lengths, positions)
    keep_mask = 1.0 - begins.astype(jnp.float32)
    x_full = x_in.astype(jnp.float32)
    scale = lax.rsqrt(jnp.mean(x_full * x_full, axis=1, keepdims=True) + EPSILON)
    normed = (x_full * scale * norm_gain[None]).astype(jnp.bfloat16)
    expanded = (onehot[:, :, None] * normed[:, None, :]).reshape(tok_rows, mode_count * model_width)
    w_in_flat = w_in.reshape(mode_count * model_width, 2 * inner_local)
    projected_xz = jnp.dot(expanded, w_in_flat, preferred_element_type=jnp.float32).astype(
        jnp.bfloat16
    )
    projected_xz = projected_xz.reshape(tok_rows, 2, inner_local)
    x_branch = projected_xz[:, 0]
    z_branch = projected_xz[:, 1].astype(jnp.float32)
    rim_rows = from_behind(x_branch[tok_rows - (conv_taps - 1) :], "seq", 1)
    extended = jnp.concatenate([rim_rows, x_branch], axis=0).astype(jnp.float32)
    ext_doc, _ = doc_tables(
        doc_lengths,
        first_pos - (conv_taps - 1) + jnp.arange(tok_rows + conv_taps - 1, dtype=jnp.int32),
    )
    conv_pre = jnp.zeros((tok_rows, inner_local), jnp.float32) + conv_bias[None]
    same_list = []
    for offset in range(conv_taps):
        same_doc = (ext_doc[offset : offset + tok_rows] == doc_index).astype(jnp.float32)[:, None]
        same_list.append(same_doc)
        conv_pre = (
            conv_pre + conv_weight[offset][None] * extended[offset : offset + tok_rows] * same_doc
        )
    conv_out = jax.nn.silu(conv_pre).astype(jnp.bfloat16)
    conv_float = conv_out.astype(jnp.float32)
    projected = lax.psum(jnp.dot(conv_out, x_proj, preferred_element_type=jnp.float32), "ch")
    dt_low = projected[:, :rank_size].astype(jnp.bfloat16)
    b_in = projected[:, rank_size : rank_size + state_size]
    c_out = projected[:, rank_size + state_size :]
    dt_raw = jnp.dot(dt_low, dt_proj, preferred_element_type=jnp.float32)
    step_size = jax.nn.softplus(dt_raw + dt_bias[None])
    decay_rate = -jnp.exp(a_log)
    seq_count = lax.axis_size("seq")
    rate_two = decay_rate * math.log2(math.e)
    masked_step = jnp.where(begins[:, None], 1e30, step_size)
    drive = step_size * conv_float
    wide = (tok_rows, state_size, 128)
    b_wide = jnp.broadcast_to(b_in[:, :, None], wide)
    c_wide = jnp.broadcast_to(c_out[:, :, None], wide)
    gate_act = jax.nn.silu(z_branch)
    cot_full = lax.all_gather(cotangent, "ch", axis=1, tiled=True)
    cot_expanded = onehot[:, :, None] * cot_full[:, None, :]
    d_gated = jnp.einsum("tmd,mde->te", cot_expanded, w_out, preferred_element_type=jnp.float32)
    d_ssm = d_gated * gate_act
    ends = lax.all_gather(
        scan_ends(masked_step, drive, d_ssm, b_wide, c_wide, rate_two), "seq", axis=0
    )
    incoming = jnp.zeros((state_size, inner_local), jnp.float32)
    pending = incoming
    for place in range(seq_count):
        part = ends[place]
        after = part[state_size : 2 * state_size] * incoming + part[:state_size]
        incoming = jnp.where(place < seq_index, after, incoming)
    for place in reversed(range(seq_count)):
        part = ends[place]
        after = part[state_size : 2 * state_size] * pending + part[2 * state_size :]
        pending = jnp.where(place > seq_index, after, pending)
    ssm, history = scan_forward(
        masked_step, drive, b_wide, own_columns(c_out), rate_two, incoming
    )
    ssm = ssm + d_skip[None] * conv_float
    gated = (ssm * gate_act).astype(jnp.bfloat16)
    proj_all = jnp.einsum("te,mde->tmd", gated, w_out, preferred_element_type=jnp.float32)
    mixer_part = jnp.sum(onehot.astype(jnp.float32)[:, :, None] * proj_all, axis=1)
    mixer = lax.psum_scatter(mixer_part, "ch", scatter_dimension=1, tiled=True)
    x_slice = lax.dynamic_slice_in_dim(x_full, ch_index * feat_part, feat_part, 1)
    block_out = (x_slice + mixer).astype(jnp.bfloat16)
    gate_sig = jax.nn.sigmoid(z_branch)
    d_z = d_gated * ssm * gate_sig * (1.0 + z_branch * (1.0 - gate_sig))
    d_z = d_z.astype(jnp.bfloat16)
    gated_all = lax.all_gather(gated, "seq", axis=0, tiled=True)
    d_z_all = lax.all_gather(d_z, "seq", axis=0, tiled=True)
    d_skip_local = jnp.sum(d_ssm * conv_float, axis=0)
    d_conv = d_ssm * d_skip[None]
    d_step, conv_grads, d_b, d_c, rate_grad = scan_backward(
        masked_step, step_size, conv_float, d_ssm, c_wide, own_columns(b_in), rate_two, pending, incoming, history
    )
    d_conv = d_conv + conv_grads
    d_a_log = rate_grad * decay_rate
    d_full = d_step * jax.nn.sigmoid(dt_raw + dt_bias[None])
    d_bias_local = jnp.sum(d_full, axis=0)
    d_raw = d_full.astype(jnp.bfloat16)
    d_dt_proj_local = jnp.einsum("tr,te->re", dt_low, d_raw, preferred_element_type=jnp.float32)
    d_low_part = jnp.einsum("te,re->tr", d_raw, dt_proj, preferred_element_type=jnp.float32)
    d_projected = lax.psum(jnp.concatenate([d_low_part, d_b, d_c], axis=1), "ch").astype(
        jnp.bfloat16
    )
    d_x_proj_local = jnp.einsum(
        "te,tk->ek", conv_out, d_projected, preferred_element_type=jnp.float32
    )
    d_conv = d_conv + jnp.einsum(
        "tk,ek->te", d_projected, x_proj, preferred_element_type=jnp.float32
    )
    conv_sig = jax.nn.sigmoid(conv_pre)
    d_pre = d_conv * conv_sig * (1.0 + conv_pre * (1.0 - conv_sig))
    d_conv_bias_local = jnp.sum(d_pre, axis=0)
    d_conv_weight_local = jnp.stack(
        [
            jnp.sum(d_pre * extended[offset : offset + tok_rows] * same_list[offset], axis=0)
            for offset in range(conv_taps)
        ],
        axis=0,
    )
    after_rows = from_behind(d_pre[: conv_taps - 1], "seq", -1)
    d_pre_ext = jnp.concatenate([d_pre, after_rows], axis=0)
    post_doc, _ = doc_tables(
        doc_lengths, first_pos + jnp.arange(tok_rows + conv_taps - 1, dtype=jnp.int32)
    )
    d_x_branch = jnp.zeros((tok_rows, inner_local), jnp.float32)
    for offset in range(conv_taps):
        lag = conv_taps - 1 - offset
        same_doc = (post_doc[lag : lag + tok_rows] == doc_index).astype(jnp.float32)[:, None]
        d_x_branch = (
            d_x_branch + d_pre_ext[lag : lag + tok_rows] * conv_weight[offset][None] * same_doc
        )
    d_x_branch = d_x_branch.astype(jnp.bfloat16)
    d_x_all = lax.all_gather(d_x_branch, "seq", axis=0, tiled=True)
    d_both = jnp.stack([d_x_branch, d_z], axis=1).reshape(tok_rows, 2 * inner_local)
    normed_terms = jnp.einsum(
        "tk,mdk->tmd",
        d_both,
        w_in.reshape(mode_count, model_width, 2 * inner_local),
        preferred_element_type=jnp.float32,
    )
    normed_part = jnp.sum(onehot.astype(jnp.float32)[:, :, None] * normed_terms, axis=1)
    gain_slice = lax.dynamic_slice_in_dim(norm_gain, ch_index * feat_part, feat_part, 0)
    d_normed = lax.psum(normed_part, "ch")
    weighted = d_normed * norm_gain[None]
    mean_term = jnp.mean(weighted * x_full, axis=1, keepdims=True)
    d_slice = lax.dynamic_slice_in_dim(d_normed, ch_index * feat_part, feat_part, 1)
    weighted_slice = d_slice * gain_slice[None]
    d_x_in = cotangent.astype(jnp.float32) + scale * weighted_slice - x_slice * scale**3 * mean_term
    d_gain_part = jnp.sum(d_slice * x_slice * scale, axis=0)
    pair = jnp.concatenate(
        [normed.reshape(tok_rows, seq_count, -1), cot_full.reshape(tok_rows, seq_count, -1)], axis=2
    ).reshape(tok_rows, -1)
    pair_cols = lax.all_to_all(pair, "seq", split_axis=1, concat_axis=0, tiled=True)
    slab = pair_cols.shape[1] // 2
    mode_mask = (modes[:, None] == jnp.arange(mode_count, dtype=jnp.int32)[None]).astype(
        jnp.bfloat16
    )
    x_spread = mode_mask[:, :, None] * pair_cols[:, None, :slab]
    c_spread = mode_mask[:, :, None] * pair_cols[:, None, slab:]
    d_w_out = jnp.einsum("tmd,te->mde", c_spread, gated_all, preferred_element_type=jnp.float32)
    d_w_z = jnp.einsum("tmd,te->mde", x_spread, d_z_all, preferred_element_type=jnp.float32)
    d_w_x = jnp.einsum("tmd,te->mde", x_spread, d_x_all, preferred_element_type=jnp.float32)
    d_w_in = jnp.stack([d_w_x, d_w_z], axis=2)
    small_sums = lax.psum(
        (
            d_gain_part,
            d_conv_weight_local,
            d_conv_bias_local,
            d_x_proj_local,
            d_dt_proj_local,
            d_bias_local,
            d_a_log,
            d_skip_local,
        ),
        "seq",
    )
    return (
        block_out,
        d_x_in,
        small_sums[0],
        d_w_in,
        small_sums[1],
        small_sums[2],
        small_sums[3],
        small_sums[4],
        small_sums[5],
        small_sums[6],
        small_sums[7],
        d_w_out,
    )


def solution(mesh):
    return jax.shard_map(
        shards,
        mesh=mesh,
        in_specs=(
            P("seq", None),
            P(),
            P(None, None, None, "ch"),
            P(None, "ch"),
            P("ch"),
            P("ch", None),
            P(None, "ch"),
            P("ch"),
            P(None, "ch"),
            P("ch"),
            P(None, None, "ch"),
            P(),
            P(),
            P("seq", "ch"),
        ),
        out_specs=(
            P("seq", "ch"),
            P("seq", "ch"),
            P("ch"),
            P(None, "seq", None, "ch"),
            P(None, "ch"),
            P("ch"),
            P("ch", None),
            P(None, "ch"),
            P("ch"),
            P(None, "ch"),
            P("ch"),
            P(None, "seq", "ch"),
        ),
        check_vma=False,
    )
```

```python
import functools
import math

import jax
import jax.numpy as jnp
from jax import lax
from jax.experimental import pallas as pl
from jax.experimental.pallas import tpu as pltpu
from jax.sharding import PartitionSpec as P

EPSILON = 1e-05


def from_behind(block, axis, distance):
    devices = range(lax.axis_size(axis))
    route = [(i - distance, i) for i in devices if i - distance in devices]
    return lax.ppermute(block, axis, route)


MESH = pl.DeviceIdType.MESH


def sum_over(part, axis):
    count = lax.axis_size(axis)
    sent = part.astype(jnp.bfloat16)
    total = part
    for distance in range(1, count):
        route = [(i, (i + distance) % count) for i in range(count)]
        total = total + lax.ppermute(sent, axis, route).astype(jnp.float32)
    return total


def sum_slices(part, axis):
    count = lax.axis_size(axis)
    place = lax.axis_index(axis)
    width = part.shape[1] // count
    total = lax.dynamic_slice_in_dim(part, place * width, width, 1)
    sent = part.astype(jnp.bfloat16)
    for distance in range(1, count):
        route = [(i, (i + distance) % count) for i in range(count)]
        piece = lax.dynamic_slice_in_dim(sent, (place + distance) % count * width, width, 1)
        total = total + lax.ppermute(piece, axis, route).astype(jnp.float32)
    return total


def cycle_of(count):
    across = count // 4
    walk = [(0, x) for x in range(across)]
    for turn, x in enumerate(reversed(range(across))):
        column = [(z, x) for z in range(1, 4)]
        walk += column[::-1] if turn % 2 else column
    return [z * across + x for z, x in walk]


def ring_gather(block, axis):
    count = lax.axis_size(axis)
    ring = cycle_of(count)
    onward = [(ring[i], ring[(i + 1) % count]) for i in range(count)]
    backward = [(b, a) for a, b in onward]
    half = block.shape[0] // 2
    ways = [[block[:half]], [block[half:]]]
    for _ in range(count - 1):
        ways[0].append(lax.ppermute(ways[0][-1], axis, onward))
        ways[1].append(lax.ppermute(ways[1][-1], axis, backward))
    return jnp.concatenate(ways[0] + ways[1], axis=0)


def ring_exchange(pieces, axis):
    count = lax.axis_size(axis)
    place = lax.axis_index(axis)
    ring = cycle_of(count)
    where = {s: i for i, s in enumerate(ring)}
    got = [lax.dynamic_index_in_dim(pieces, place, 1, False)]
    for distance in range(1, count):
        table = [ring[(where[s] + distance) % count] for s in range(count)]
        piece = lax.dynamic_index_in_dim(pieces, jnp.array(table, jnp.int32)[place], 1, False)
        got.append(lax.ppermute(piece, axis, list(enumerate(table))))
    half = pieces.shape[0] // 2
    first = [got[k][:half] for k in range(count)]
    second = [got[-k][half:] for k in range(count)]
    return jnp.concatenate(first + second, axis=0)


def ring_modes(modes, axis):
    count = lax.axis_size(axis)
    place = lax.axis_index(axis)
    ring = cycle_of(count)
    where = {s: i for i, s in enumerate(ring)}
    half = modes.shape[0] // (2 * count)
    parts = []
    for way in (0, 1):
        for k in range(count):
            step = k if way else -k
            table = [ring[(where[s] + step) % count] for s in range(count)]
            start = (2 * jnp.array(table, jnp.int32)[place] + way) * half
            parts.append(lax.dynamic_slice_in_dim(modes, start, half))
    return jnp.concatenate(parts)


def states_kernel(count, ends_ref, steps_ref, ends_out, steps_out, send, recv):
    me = lax.axis_index("seq")
    barrier = pltpu.get_barrier_semaphore()
    for distance in range(1, count):
        peer = {"seq": lax.rem(me + distance, count)}
        pl.semaphore_signal(barrier, inc=1, device_id=peer, device_id_type=MESH)
    pl.semaphore_wait(barrier, count - 1)
    copies = []
    for distance in range(1, count):
        peer = lax.rem(me + distance, count)
        side = jnp.where(peer > me, 0, 1)
        for kind, (source, target) in enumerate(
            ((ends_ref.at[side], ends_out), (steps_ref, steps_out))
        ):
            copies.append(
                pltpu.make_async_remote_copy(
                    src_ref=source,
                    dst_ref=target.at[distance - 1],
                    send_sem=send.at[kind, distance - 1],
                    recv_sem=recv.at[kind, distance - 1],
                    device_id={"seq": peer},
                    device_id_type=MESH,
                )
            )
    for copy in copies:
        copy.start()
    for copy in copies:
        copy.wait()


def exchange_states(ends, steps):
    others = lax.axis_size("seq") - 1
    vmem = pl.BlockSpec(memory_space=pltpu.VMEM)
    return pl.pallas_call(
        functools.partial(states_kernel, others + 1),
        in_specs=[vmem, vmem],
        out_specs=[vmem, vmem],
        out_shape=[
            jax.ShapeDtypeStruct((others,) + ends.shape[1:], ends.dtype),
            jax.ShapeDtypeStruct((others,) + steps.shape, steps.dtype),
        ],
        scratch_shapes=[
            pltpu.SemaphoreType.DMA((2, others)),
            pltpu.SemaphoreType.DMA((2, others)),
        ],
        compiler_params=pltpu.CompilerParams(
            collective_id=0, has_side_effects=True, vmem_limit_bytes=32 << 20
        ),
        name="exchange_states",
    )(ends, steps)


def doc_tables(doc_lengths, positions):
    count = doc_lengths.shape[0]
    order = jnp.arange(count, dtype=jnp.int32)
    doc_ends = jnp.sum(jnp.where(order[:, None] >= order[None, :], doc_lengths[None, :], 0), axis=1)
    doc_starts = doc_ends - doc_lengths
    doc_index = jnp.sum((positions[:, None] >= doc_ends[None, :]).astype(jnp.int32), axis=1)
    begins = jnp.any(positions[:, None] == doc_starts[None, :], axis=1)
    return (doc_index, begins)


def own_columns(values):
    rows, n = values.shape
    own = jnp.arange(16 * n)[None] // n == jnp.arange(rows)[:, None] % 16
    return jnp.where(own, jnp.tile(values, (1, 16)), 0).astype(jnp.bfloat16)


LB = 512
CH = 32
NS = 16

def tile_lanes(v, lanes):
    return jnp.concatenate([v] * (lanes // 128), axis=1)

def ends_kernel(lb, dtd_ref, u_ref, g_ref, b_ref, c_ref, rate_ref, out_ref, acc_ref):
    n = rate_ref.shape[0]
    rows, chans = dtd_ref.shape
    @pl.when(pl.program_id(0) == 0)
    def _():
        acc_ref[0:n, :] = jnp.zeros((n, chans), jnp.float32)
        acc_ref[n:2*n, :] = jnp.ones((n, chans), jnp.float32)
        acc_ref[2*n:3*n, :] = jnp.zeros((n, chans), jnp.float32)
    for block in range(chans // lb):
        cut = slice(block * lb, (block + 1) * lb)
        rate = rate_ref[:, cut]
        h = acc_ref[0:n, cut]
        reach = acc_ref[n:2*n, cut]
        head = acc_ref[2*n:3*n, cut]
        for t in range(rows):
            decay = jnp.exp2(dtd_ref[t:t+1, cut] * rate)
            h = decay * h + u_ref[t:t+1, cut] * tile_lanes(b_ref[t], lb)
            reach = reach * decay
            head = head + reach * (g_ref[t:t+1, cut] * tile_lanes(c_ref[t], lb))
        acc_ref[0:n, cut] = h
        acc_ref[n:2*n, cut] = reach
        acc_ref[2*n:3*n, cut] = head
    @pl.when(pl.program_id(0) == pl.num_programs(0) - 1)
    def _():
        out_ref[0] = acc_ref[0:n, :].astype(jnp.bfloat16)
        out_ref[1] = acc_ref[2*n:3*n, :].astype(jnp.bfloat16)

def scan_ends(dtd, u, g, b, c, rate, lb=LB, ch=CH):
    t, e = dtd.shape
    n = rate.shape[0]
    row = pl.BlockSpec((ch, e), lambda i: (i, 0))
    wide = pl.BlockSpec((ch, n, 128), lambda i: (i, 0, 0))
    return pl.pallas_call(
        functools.partial(ends_kernel, lb),
        grid=(t // ch,),
        in_specs=[row, row, row, wide, wide, pl.BlockSpec((n, e), lambda i: (0, 0))],
        out_specs=pl.BlockSpec((2, n, e), lambda i: (0, 0, 0)),
        out_shape=jax.ShapeDtypeStruct((2, n, e), jnp.bfloat16),
        scratch_shapes=[pltpu.VMEM((3 * n, e), jnp.float32)],
        compiler_params=pltpu.CompilerParams(vmem_limit_bytes=32 << 20),
        name="scan_ends",
    )(dtd, u, g, b, c, rate)

def forward_kernel(lb, dtd_ref, u_ref, b_ref, cblk_ref, rate_ref, h0_ref, y_ref, hist_ref, state_ref):
    n = rate_ref.shape[0]
    rows, chans = dtd_ref.shape
    @pl.when(pl.program_id(0) == 0)
    def _():
        state_ref[...] = h0_ref[...]
    for block in range(chans // lb):
        cut = slice(block * lb, (block + 1) * lb)
        rate = rate_ref[:, cut]
        h = state_ref[:, cut]
        for t in range(rows):
            decay = jnp.exp2(dtd_ref[t:t+1, cut] * rate)
            h = decay * h + u_ref[t:t+1, cut] * tile_lanes(b_ref[t], lb)
            hist_ref[t * n:(t + 1) * n, cut] = h.astype(jnp.bfloat16)
        state_ref[:, cut] = h
    for k in range(rows // 16):
        y_ref[k*16:(k+1)*16, :] = jnp.dot(cblk_ref[k*16:(k+1)*16, :], hist_ref[k*16*n:(k+1)*16*n, :], preferred_element_type=jnp.float32)

def scan_forward(dtd, u, b, cblk, rate, h0, lb=LB, ch=CH):
    t, e = dtd.shape
    n = rate.shape[0]
    row = pl.BlockSpec((ch, e), lambda i: (i, 0))
    wide = pl.BlockSpec((ch, n, 128), lambda i: (i, 0, 0))
    whole = pl.BlockSpec((n, e), lambda i: (0, 0))
    return pl.pallas_call(
        functools.partial(forward_kernel, lb),
        grid=(t // ch,),
        in_specs=[row, row, wide, pl.BlockSpec((ch, 16 * n), lambda i: (i, 0)), whole, whole],
        out_specs=(row, pl.BlockSpec((ch * n, e), lambda i: (i, 0))),
        out_shape=(jax.ShapeDtypeStruct((t, e), jnp.float32), jax.ShapeDtypeStruct((t * n, e), jnp.bfloat16)),
        scratch_shapes=[pltpu.VMEM((n, e), jnp.float32)],
        compiler_params=pltpu.CompilerParams(vmem_limit_bytes=32 << 20),
        name="scan_forward",
    )(dtd, u, b, cblk, rate, h0)

def backward_kernel(lb, dtd_ref, step_ref, conv_ref, g_ref, c_ref, bblk_ref, rate_ref, lam0_ref, h0_ref, hist_ref, prev_ref,
                    gstep_ref, gscan_ref, gb_ref, gc_ref, racc_ref, pend_ref, lam_ref, w_ref):
    n = rate_ref.shape[0]
    rows, chans = dtd_ref.shape
    last = pl.num_programs(0) - 1
    @pl.when(pl.program_id(0) == 0)
    def _():
        pend_ref[...] = lam0_ref[...]
        racc_ref[...] = jnp.zeros_like(racc_ref)
    first = pl.program_id(0) == last
    for block in range(chans // lb):
        cut = slice(block * lb, (block + 1) * lb)
        rate = rate_ref[:, cut]
        pend = pend_ref[:, cut]
        racc = racc_ref[:, cut]
        for t in reversed(range(rows)):
            decay = jnp.exp2(dtd_ref[t:t+1, cut] * rate)
            lam = g_ref[t:t+1, cut] * tile_lanes(c_ref[t], lb) + pend
            pend = decay * lam
            if t:
                before = hist_ref[(t - 1) * n:t * n, cut].astype(jnp.float32)
            else:
                before = jnp.where(first, h0_ref[:, cut], prev_ref[:, cut].astype(jnp.float32))
            w = pend * before
            racc = racc + w * step_ref[t:t+1, cut]
            lam_ref[t * n:(t + 1) * n, cut] = lam.astype(jnp.bfloat16)
            w_ref[t * n:(t + 1) * n, cut] = (w * rate).astype(jnp.bfloat16)
        pend_ref[:, cut] = pend
        racc_ref[:, cut] = racc
    for k in range(rows // 16):
        rc = slice(k * 16, (k + 1) * 16)
        hc = slice(k * 16 * n, (k + 1) * 16 * n)
        step = step_ref[rc, :]
        conv = conv_ref[rc, :]
        own = (lax.broadcasted_iota(jnp.int32, (16, 16 * n), 1) // n == lax.broadcasted_iota(jnp.int32, (16, 16 * n), 0))
        ones = own.astype(jnp.bfloat16)
        adj = jnp.dot(bblk_ref[rc, :], lam_ref[hc, :], preferred_element_type=jnp.float32)
        wsum = jnp.dot(ones, w_ref[hc, :], preferred_element_type=jnp.float32)
        gstep_ref[rc, :] = wsum * math.log(2.0) + adj * conv
        gscan_ref[rc, :] = adj * step
        nt = (((1,), (1,)), ((), ()))
        gb = lax.dot_general((step * conv).astype(jnp.bfloat16), lam_ref[hc, :], nt, preferred_element_type=jnp.float32)
        gc = lax.dot_general(g_ref[rc, :].astype(jnp.bfloat16), hist_ref[hc, :], nt, preferred_element_type=jnp.float32)
        gb_ref[k:k+1] = jnp.sum(jnp.where(own, gb, 0.0), axis=0, keepdims=True)[None]
        gc_ref[k:k+1] = jnp.sum(jnp.where(own, gc, 0.0), axis=0, keepdims=True)[None]

def scan_backward(dtd, step, conv, g, c, bblk, rate, lam0, h0, hist, lb=LB, ch=CH):
    t, e = dtd.shape
    n = rate.shape[0]
    k = t // ch
    row = pl.BlockSpec((ch, e), lambda i: (k - 1 - i, 0))
    wide = pl.BlockSpec((ch, n, 128), lambda i: (k - 1 - i, 0, 0))
    whole = pl.BlockSpec((n, e), lambda i: (0, 0))
    flat = pl.BlockSpec((ch // 16, 1, 16 * n), lambda i: (k - 1 - i, 0, 0))
    outs = pl.pallas_call(
        functools.partial(backward_kernel, lb),
        grid=(k,),
        in_specs=[row, row, row, row, wide, pl.BlockSpec((ch, 16 * n), lambda i: (k - 1 - i, 0)), whole, whole, whole,
                  pl.BlockSpec((ch * n, e), lambda i: (k - 1 - i, 0)),
                  pl.BlockSpec((n, e), lambda i: (jnp.maximum((k - 1 - i) * ch - 1, 0), 0))],
        out_specs=(row, row, flat, flat, whole),
        out_shape=(jax.ShapeDtypeStruct((t, e), jnp.float32), jax.ShapeDtypeStruct((t, e), jnp.float32),
                   jax.ShapeDtypeStruct((t // 16, 1, 16 * n), jnp.float32), jax.ShapeDtypeStruct((t // 16, 1, 16 * n), jnp.float32),
                   jax.ShapeDtypeStruct((n, e), jnp.float32)),
        scratch_shapes=[pltpu.VMEM((n, e), jnp.float32), pltpu.VMEM((ch * n, e), jnp.bfloat16), pltpu.VMEM((ch * n, e), jnp.bfloat16)],
        compiler_params=pltpu.CompilerParams(vmem_limit_bytes=48 << 20),
        name="scan_backward",
    )(dtd, step, conv, g, c, bblk, rate, lam0, h0, hist, hist)
    return outs[0], outs[1], outs[2].reshape(t, n), outs[3].reshape(t, n), outs[4]


def shards(
    x_in,
    norm_gain,
    w_in,
    conv_weight,
    conv_bias,
    x_proj,
    dt_proj,
    dt_bias,
    a_log,
    d_skip,
    w_out,
    modes,
    doc_lengths,
    cotangent,
):
    tok_rows, model_width = x_in.shape
    mode_count = w_in.shape[0]
    inner_local = conv_bias.shape[0]
    state_size = a_log.shape[0]
    rank_size = dt_proj.shape[0]
    conv_taps = conv_weight.shape[0]
    ch_count = lax.axis_size("ch")
    feat_part = model_width // ch_count
    seq_index = lax.axis_index("seq")
    ch_index = lax.axis_index("ch")
    first_pos = seq_index * tok_rows
    positions = first_pos + jnp.arange(tok_rows, dtype=jnp.int32)
    my_modes = lax.dynamic_slice_in_dim(modes, first_pos, tok_rows)
    onehot = (my_modes[:, None] == jnp.arange(mode_count, dtype=jnp.int32)[None]).astype(
        jnp.bfloat16
    )
    doc_index, begins = doc_tables(doc_lengths, positions)
    keep_mask = 1.0 - begins.astype(jnp.float32)
    x_full = x_in.astype(jnp.float32)
    scale = lax.rsqrt(jnp.mean(x_full * x_full, axis=1, keepdims=True) + EPSILON)
    normed = (x_full * scale * norm_gain[None]).astype(jnp.bfloat16)
    expanded = (onehot[:, :, None] * normed[:, None, :]).reshape(tok_rows, mode_count * model_width)
    w_in_flat = w_in.reshape(mode_count * model_width, 2 * inner_local)
    projected_xz = jnp.dot(expanded, w_in_flat, preferred_element_type=jnp.float32).astype(
        jnp.bfloat16
    )
    projected_xz = projected_xz.reshape(tok_rows, 2, inner_local)
    x_branch = projected_xz[:, 0]
    z_branch = projected_xz[:, 1].astype(jnp.float32)
    rim_rows = from_behind(x_branch[tok_rows - (conv_taps - 1) :], "seq", 1)
    extended = jnp.concatenate([rim_rows, x_branch], axis=0).astype(jnp.float32)
    ext_doc, _ = doc_tables(
        doc_lengths,
        first_pos - (conv_taps - 1) + jnp.arange(tok_rows + conv_taps - 1, dtype=jnp.int32),
    )
    conv_pre = jnp.zeros((tok_rows, inner_local), jnp.float32) + conv_bias[None]
    same_list = []
    for offset in range(conv_taps):
        same_doc = (ext_doc[offset : offset + tok_rows] == doc_index).astype(jnp.float32)[:, None]
        same_list.append(same_doc)
        conv_pre = (
            conv_pre + conv_weight[offset][None] * extended[offset : offset + tok_rows] * same_doc
        )
    conv_out = jax.nn.silu(conv_pre).astype(jnp.bfloat16)
    conv_float = conv_out.astype(jnp.float32)
    projected = sum_over(jnp.dot(conv_out, x_proj, preferred_element_type=jnp.float32), "ch")
    dt_low = projected[:, :rank_size].astype(jnp.bfloat16)
    b_in = projected[:, rank_size : rank_size + state_size]
    c_out = projected[:, rank_size + state_size :]
    dt_raw = jnp.dot(dt_low, dt_proj, preferred_element_type=jnp.float32)
    step_size = jax.nn.softplus(dt_raw + dt_bias[None])
    decay_rate = -jnp.exp(a_log)
    seq_count = lax.axis_size("seq")
    rate_two = decay_rate * math.log2(math.e)
    masked_step = jnp.where(begins[:, None], 1e30, step_size)
    drive = step_size * conv_float
    wide = (tok_rows, state_size, 128)
    b_wide = jnp.broadcast_to(b_in[:, :, None], wide)
    c_wide = jnp.broadcast_to(c_out[:, :, None], wide)
    gate_act = jax.nn.silu(z_branch)
    cot_full = lax.all_gather(cotangent, "ch", axis=1, tiled=True)
    cot_expanded = onehot[:, :, None] * cot_full[:, None, :]
    d_gated = jnp.einsum("tmd,mde->te", cot_expanded, w_out, preferred_element_type=jnp.float32)
    d_ssm = d_gated * gate_act
    pair = jnp.concatenate(
        [normed.reshape(tok_rows, seq_count, -1), cot_full.reshape(tok_rows, seq_count, -1)], axis=2
    )
    pair_cols = ring_exchange(pair, "seq")
    masked_step, pair_cols = lax.optimization_barrier((masked_step, pair_cols))
    ends = scan_ends(masked_step, drive, d_ssm, b_wide, c_wide, rate_two)
    steps = jnp.sum(masked_step, axis=0)
    ends_in, steps_in = exchange_states(ends, steps.reshape(8, -1))
    steps_in = steps_in.reshape(seq_count - 1, inner_local)
    incoming = jnp.zeros((state_size, inner_local), jnp.float32)
    pending = incoming
    gap = jnp.zeros((inner_local,), jnp.float32)
    for distance in range(1, seq_count):
        part = ends_in[distance - 1].astype(jnp.float32) * jnp.exp2(rate_two * gap[None])
        incoming = incoming + jnp.where(distance <= seq_index, part, 0.0)
        gap = gap + steps_in[distance - 1]
    gap = jnp.zeros((inner_local,), jnp.float32)
    for distance in range(1, seq_count):
        slot = seq_count - 1 - distance
        part = ends_in[slot].astype(jnp.float32) * jnp.exp2(rate_two * gap[None])
        pending = pending + jnp.where(distance + seq_index < seq_count, part, 0.0)
        gap = gap + steps_in[slot]
    ssm, history = scan_forward(
        masked_step, drive, b_wide, own_columns(c_out), rate_two, incoming
    )
    ssm = ssm + d_skip[None] * conv_float
    gated = (ssm * gate_act).astype(jnp.bfloat16)
    proj_all = jnp.einsum("te,mde->tmd", gated, w_out, preferred_element_type=jnp.float32)
    mixer_part = jnp.sum(onehot.astype(jnp.float32)[:, :, None] * proj_all, axis=1)
    mixer = sum_slices(mixer_part, "ch")
    x_slice = lax.dynamic_slice_in_dim(x_full, ch_index * feat_part, feat_part, 1)
    block_out = (x_slice + mixer).astype(jnp.bfloat16)
    gate_sig = jax.nn.sigmoid(z_branch)
    d_z = d_gated * ssm * gate_sig * (1.0 + z_branch * (1.0 - gate_sig))
    d_z = d_z.astype(jnp.bfloat16)
    gated_all = ring_gather(gated, "seq")
    d_z_all = ring_gather(d_z, "seq")
    d_skip_local = jnp.sum(d_ssm * conv_float, axis=0)
    d_conv = d_ssm * d_skip[None]
    d_step, conv_grads, d_b, d_c, rate_grad = scan_backward(
        masked_step, step_size, conv_float, d_ssm, c_wide, own_columns(b_in), rate_two, pending, incoming, history
    )
    d_conv = d_conv + conv_grads
    d_a_log = rate_grad * decay_rate
    d_full = d_step * jax.nn.sigmoid(dt_raw + dt_bias[None])
    d_bias_local = jnp.sum(d_full, axis=0)
    d_raw = d_full.astype(jnp.bfloat16)
    d_dt_proj_local = jnp.einsum("tr,te->re", dt_low, d_raw, preferred_element_type=jnp.float32)
    d_low_part = jnp.einsum("te,re->tr", d_raw, dt_proj, preferred_element_type=jnp.float32)
    d_projected = sum_over(jnp.concatenate([d_low_part, d_b, d_c], axis=1), "ch").astype(
        jnp.bfloat16
    )
    d_x_proj_local = jnp.einsum(
        "te,tk->ek", conv_out, d_projected, preferred_element_type=jnp.float32
    )
    d_conv = d_conv + jnp.einsum(
        "tk,ek->te", d_projected, x_proj, preferred_element_type=jnp.float32
    )
    conv_sig = jax.nn.sigmoid(conv_pre)
    d_pre = d_conv * conv_sig * (1.0 + conv_pre * (1.0 - conv_sig))
    d_conv_bias_local = jnp.sum(d_pre, axis=0)
    d_conv_weight_local = jnp.stack(
        [
            jnp.sum(d_pre * extended[offset : offset + tok_rows] * same_list[offset], axis=0)
            for offset in range(conv_taps)
        ],
        axis=0,
    )
    after_rows = from_behind(d_pre[: conv_taps - 1], "seq", -1)
    d_pre_ext = jnp.concatenate([d_pre, after_rows], axis=0)
    post_doc, _ = doc_tables(
        doc_lengths, first_pos + jnp.arange(tok_rows + conv_taps - 1, dtype=jnp.int32)
    )
    d_x_branch = jnp.zeros((tok_rows, inner_local), jnp.float32)
    for offset in range(conv_taps):
        lag = conv_taps - 1 - offset
        same_doc = (post_doc[lag : lag + tok_rows] == doc_index).astype(jnp.float32)[:, None]
        d_x_branch = (
            d_x_branch + d_pre_ext[lag : lag + tok_rows] * conv_weight[offset][None] * same_doc
        )
    d_x_branch = d_x_branch.astype(jnp.bfloat16)
    d_x_all = ring_gather(d_x_branch, "seq")
    d_both = jnp.stack([d_x_branch, d_z], axis=1).reshape(tok_rows, 2 * inner_local)
    normed_terms = jnp.einsum(
        "tk,mdk->tmd",
        d_both,
        w_in.reshape(mode_count, model_width, 2 * inner_local),
        preferred_element_type=jnp.float32,
    )
    normed_part = jnp.sum(onehot.astype(jnp.float32)[:, :, None] * normed_terms, axis=1)
    gain_slice = lax.dynamic_slice_in_dim(norm_gain, ch_index * feat_part, feat_part, 0)
    d_slice = sum_slices(normed_part, "ch")
    own_dots = jnp.sum(normed_part * norm_gain[None] * x_full, axis=1)
    dots = own_dots
    for distance in range(1, ch_count):
        route = [(i, (i + distance) % ch_count) for i in range(ch_count)]
        dots = dots + lax.ppermute(own_dots, "ch", route)
    mean_term = (dots / model_width)[:, None]
    weighted_slice = d_slice * gain_slice[None]
    d_x_in = cotangent.astype(jnp.float32) + scale * weighted_slice - x_slice * scale**3 * mean_term
    d_gain_part = jnp.sum(d_slice * x_slice * scale, axis=0)
    all_modes = ring_modes(modes, "seq")
    slab = pair_cols.shape[1] // 2
    mode_mask = (all_modes[:, None] == jnp.arange(mode_count, dtype=jnp.int32)[None]).astype(
        jnp.bfloat16
    )
    x_spread = mode_mask[:, :, None] * pair_cols[:, None, :slab]
    c_spread = mode_mask[:, :, None] * pair_cols[:, None, slab:]
    d_w_out = jnp.einsum("tmd,te->mde", c_spread, gated_all, preferred_element_type=jnp.float32)
    d_w_z = jnp.einsum("tmd,te->mde", x_spread, d_z_all, preferred_element_type=jnp.float32)
    d_w_x = jnp.einsum("tmd,te->mde", x_spread, d_x_all, preferred_element_type=jnp.float32)
    d_w_in = jnp.stack([d_w_x, d_w_z], axis=2)
    small_sums = lax.psum(
        (
            d_gain_part,
            d_conv_weight_local,
            d_conv_bias_local,
            d_x_proj_local,
            d_dt_proj_local,
            d_bias_local,
            d_a_log,
            d_skip_local,
        ),
        "seq",
    )
    return (
        block_out,
        d_x_in,
        small_sums[0],
        d_w_in,
        small_sums[1],
        small_sums[2],
        small_sums[3],
        small_sums[4],
        small_sums[5],
        small_sums[6],
        small_sums[7],
        d_w_out,
    )


def solution(mesh):
    return jax.shard_map(
        shards,
        mesh=mesh,
        in_specs=(
            P("seq", None),
            P(),
            P(None, None, None, "ch"),
            P(None, "ch"),
            P("ch"),
            P("ch", None),
            P(None, "ch"),
            P("ch"),
            P(None, "ch"),
            P("ch"),
            P(None, None, "ch"),
            P(),
            P(),
            P("seq", "ch"),
        ),
        out_specs=(
            P("seq", "ch"),
            P("seq", "ch"),
            P("ch"),
            P(None, "seq", None, "ch"),
            P(None, "ch"),
            P("ch"),
            P("ch", None),
            P(None, "ch"),
            P("ch"),
            P(None, "ch"),
            P("ch"),
            P(None, "seq", "ch"),
        ),
        check_vma=False,
    )
```

```python
import functools
import math

import jax
import jax.numpy as jnp
from jax import lax
from jax.experimental import pallas as pl
from jax.experimental.pallas import tpu as pltpu
from jax.sharding import PartitionSpec as P

EPSILON = 1e-05


def from_behind(block, axis, distance):
    devices = range(lax.axis_size(axis))
    route = [(i - distance, i) for i in devices if i - distance in devices]
    return lax.ppermute(block, axis, route)


MESH = pl.DeviceIdType.MESH


def sum_over(part, axis):
    count = lax.axis_size(axis)
    sent = part.astype(jnp.bfloat16)
    total = part
    for distance in range(1, count):
        route = [(i, (i + distance) % count) for i in range(count)]
        total = total + lax.ppermute(sent, axis, route).astype(jnp.float32)
    return total


def sum_slices(part, axis):
    count = lax.axis_size(axis)
    place = lax.axis_index(axis)
    width = part.shape[1] // count
    total = lax.dynamic_slice_in_dim(part, place * width, width, 1)
    sent = part.astype(jnp.bfloat16)
    for distance in range(1, count):
        route = [(i, (i + distance) % count) for i in range(count)]
        piece = lax.dynamic_slice_in_dim(sent, (place + distance) % count * width, width, 1)
        total = total + lax.ppermute(piece, axis, route).astype(jnp.float32)
    return total


def cycle_of(count):
    across = count // 4
    walk = [(0, x) for x in range(across)]
    for turn, x in enumerate(reversed(range(across))):
        column = [(z, x) for z in range(1, 4)]
        walk += column[::-1] if turn % 2 else column
    return [z * across + x for z, x in walk]


def ring_gather(block, axis):
    count = lax.axis_size(axis)
    ring = cycle_of(count)
    onward = [(ring[i], ring[(i + 1) % count]) for i in range(count)]
    backward = [(b, a) for a, b in onward]
    half = block.shape[0] // 2
    ways = [[block[:half]], [block[half:]]]
    for _ in range(count - 1):
        ways[0].append(lax.ppermute(ways[0][-1], axis, onward))
        ways[1].append(lax.ppermute(ways[1][-1], axis, backward))
    return jnp.concatenate(ways[0] + ways[1], axis=0)


def ring_modes(modes, axis):
    count = lax.axis_size(axis)
    place = lax.axis_index(axis)
    ring = cycle_of(count)
    where = {s: i for i, s in enumerate(ring)}
    half = modes.shape[0] // (2 * count)
    parts = []
    for way in (0, 1):
        for k in range(count):
            step = k if way else -k
            table = [ring[(where[s] + step) % count] for s in range(count)]
            start = (2 * jnp.array(table, jnp.int32)[place] + way) * half
            parts.append(lax.dynamic_slice_in_dim(modes, start, half))
    return jnp.concatenate(parts)


def states_kernel(count, ends_ref, steps_ref, ends_out, steps_out, send, recv):
    me = lax.axis_index("seq")
    barrier = pltpu.get_barrier_semaphore()
    for distance in range(1, count):
        peer = {"seq": lax.rem(me + distance, count)}
        pl.semaphore_signal(barrier, inc=1, device_id=peer, device_id_type=MESH)
    pl.semaphore_wait(barrier, count - 1)
    copies = []
    for distance in range(1, count):
        peer = lax.rem(me + distance, count)
        side = jnp.where(peer > me, 0, 1)
        for kind, (source, target) in enumerate(
            ((ends_ref.at[side], ends_out), (steps_ref, steps_out))
        ):
            copies.append(
                pltpu.make_async_remote_copy(
                    src_ref=source,
                    dst_ref=target.at[distance - 1],
                    send_sem=send.at[kind, distance - 1],
                    recv_sem=recv.at[kind, distance - 1],
                    device_id={"seq": peer},
                    device_id_type=MESH,
                )
            )
    for copy in copies:
        copy.start()
    for copy in copies:
        copy.wait()


def exchange_states(ends, steps):
    others = lax.axis_size("seq") - 1
    vmem = pl.BlockSpec(memory_space=pltpu.VMEM)
    return pl.pallas_call(
        functools.partial(states_kernel, others + 1),
        in_specs=[vmem, vmem],
        out_specs=[vmem, vmem],
        out_shape=[
            jax.ShapeDtypeStruct((others,) + ends.shape[1:], ends.dtype),
            jax.ShapeDtypeStruct((others,) + steps.shape, steps.dtype),
        ],
        scratch_shapes=[
            pltpu.SemaphoreType.DMA((2, others)),
            pltpu.SemaphoreType.DMA((2, others)),
        ],
        compiler_params=pltpu.CompilerParams(
            collective_id=0, has_side_effects=True, vmem_limit_bytes=32 << 20
        ),
        name="exchange_states",
    )(ends, steps)


def table_of(index, values):
    picked = jnp.int32(values[0])
    for i in range(1, len(values)):
        picked = jnp.where(index == i, jnp.int32(values[i]), picked)
    return picked


def front_kernel(
    sizes, x2_ref, normed_ref, mask_ref, cot_ref, w_in_ref, w_out_ref,
    x_ref, z_ref, gated_ref, cols_ref,
    cotg_ref, in_buf, out_buf, in_sem, out_sem, cot_send, cot_recv, seq_send, seq_recv, twin_send, twin_recv, own_sem,
):
    count, twins = sizes
    rows, width = normed_ref.shape
    modes = mask_ref.shape[0]
    half = rows // 2
    slab = width // count
    part = cot_ref.shape[1]
    inner = x_ref.shape[1]
    ring = cycle_of(count)
    me = lax.axis_index("seq")
    mine = lax.axis_index("ch")
    side = lax.rem(mine, 2)
    twin = mine + 1 - 2 * side
    where = {s: i for i, s in enumerate(ring)}
    place = table_of(me, [where[s] for s in range(count)])

    barrier = pltpu.get_barrier_semaphore()
    for k in range(1, count):
        peer = {"seq": lax.rem(me + k, count)}
        pl.semaphore_signal(barrier, inc=1, device_id=peer, device_id_type=MESH)
    for k in range(1, twins):
        peer = {"ch": lax.rem(mine + k, twins)}
        pl.semaphore_signal(barrier, inc=1, device_id=peer, device_id_type=MESH)

    pairs = inner // 256
    steps = pairs * modes

    def in_copy(step, b):
        slot = lax.rem(step, 2)
        return pltpu.make_async_copy(
            w_in_ref.at[lax.rem(step, modes), :, step // modes * 2 + b], in_buf.at[slot, b], in_sem.at[slot, b]
        )

    wide = out_buf.shape[2]
    out_steps = inner // wide * modes

    def out_copy(step):
        slot = lax.rem(step, 2)
        columns = pl.ds(pl.multiple_of(step // modes * wide, wide), wide)
        return pltpu.make_async_copy(
            w_out_ref.at[lax.rem(step, modes), :, columns], out_buf.at[slot], out_sem.at[slot]
        )

    for b in (0, 1):
        in_copy(0, b).start()
    out_copy(0).start()
    pl.semaphore_wait(barrier, count - 1 + twins - 1)

    cot_copies = [
        pltpu.make_async_remote_copy(
            src_ref=cot_ref, dst_ref=cotg_ref.at[mine], send_sem=cot_send.at[k - 1], recv_sem=cot_recv.at[k - 1],
            device_id={"ch": lax.rem(mine + k, twins)}, device_id_type=MESH,
        )
        for k in range(1, twins)
    ]
    for copy in cot_copies:
        copy.start()
    side_rows = pl.ds(pl.multiple_of(side * half, half), half)

    def seq_copies(kind):
        copies = []
        for k in range(1, count):
            step = jnp.where(side == 0, k, count - k)
            peer = table_of(lax.rem(place + step, count), ring)
            if kind == 0:
                source = normed_ref.at[side_rows, pl.ds(pl.multiple_of(peer * slab, slab), slab)]
            else:
                start = lax.rem(peer * slab, part)
                source = cotg_ref.at[peer * slab // part, side_rows, pl.ds(pl.multiple_of(start, slab), slab)]
            copies.append(
                pltpu.make_async_remote_copy(
                    src_ref=source, dst_ref=cols_ref.at[kind, side, k], send_sem=seq_send.at[kind, k - 1],
                    recv_sem=seq_recv.at[kind, k - 1], device_id={"seq": peer}, device_id_type=MESH,
                )
            )
        return copies

    def twin_copy(kind):
        return pltpu.make_async_remote_copy(
            src_ref=cols_ref.at[kind, side, pl.ds(1, count - 1)], dst_ref=cols_ref.at[kind, side, pl.ds(1, count - 1)],
            send_sem=twin_send.at[kind], recv_sem=twin_recv.at[kind],
            device_id={"ch": twin}, device_id_type=MESH,
        )

    normed_copies = seq_copies(0)
    for copy in normed_copies:
        copy.start()
    own_copy = pltpu.make_async_copy(cot_ref, cotg_ref.at[mine], own_sem.at[0])
    own_copy.start()
    own_start = pl.multiple_of(me * slab, slab)
    for way in (0, 1):
        cols_ref[0, way, 0] = normed_ref[way * half : (way + 1) * half, pl.ds(own_start, slab)]

    def in_step(step, carry):
        slot = lax.rem(step, 2)
        mode = lax.rem(step, modes)

        @pl.when(step + 1 < steps)
        def _():
            for b in (0, 1):
                in_copy(step + 1, b).start()

        for b in (0, 1):
            in_copy(step, b).wait()
        weights = jnp.concatenate([in_buf.at[slot, b].reshape(2 * width, 128)[...] for b in (0, 1)], axis=1)
        mask = jnp.concatenate([mask_ref[mode]] * 2, axis=1) > 0
        columns = pl.ds(pl.multiple_of(step // modes * 256, 256), 256)
        for j, target in enumerate((x_ref, z_ref)):
            found = jnp.dot(x2_ref[j], weights, preferred_element_type=jnp.float32).astype(jnp.bfloat16)
            target[:, columns] = jnp.where(mask, found, target[:, columns])
        return carry

    x_ref[...] = jnp.zeros_like(x_ref)
    z_ref[...] = jnp.zeros_like(z_ref)
    first = steps // 2
    lax.fori_loop(0, first, in_step, 0)
    own_copy.wait()
    for copy in cot_copies:
        copy.wait_recv()
    tail_copies = seq_copies(1)
    for copy in tail_copies:
        copy.start()
    own_slab = cotg_ref.at[me * slab // part]
    for way in (0, 1):
        cols_ref[1, way, 0] = own_slab[way * half : (way + 1) * half, pl.ds(pl.multiple_of(lax.rem(me * slab, part), slab), slab)]
    for copy in normed_copies:
        copy.wait_recv()
    twin_copy(0).start()
    lax.fori_loop(first, steps, in_step, 0)

    def out_step(step, carry):
        slot = lax.rem(step, 2)
        mode = lax.rem(step, modes)

        @pl.when(step + 1 < out_steps)
        def _():
            out_copy(step + 1).start()

        out_copy(step).wait()
        mask = jnp.concatenate([mask_ref[mode]] * (wide // 128), axis=1) > 0
        columns = pl.ds(pl.multiple_of(step // modes * wide, wide), wide)
        found = jnp.zeros((rows, wide), jnp.float32)
        for c in range(twins):
            found = found + jnp.dot(
                cotg_ref[c], out_buf[slot, c * part : (c + 1) * part], preferred_element_type=jnp.float32
            )
        gated_ref[:, columns] = jnp.where(mask, found, gated_ref[:, columns])
        return carry

    gated_ref[...] = jnp.zeros_like(gated_ref)
    lax.fori_loop(0, out_steps, out_step, 0)
    for copy in tail_copies:
        copy.wait_recv()
    twin_copy(1).start()
    for kind in (0, 1):
        twin_copy(kind).wait_recv()
        twin_copy(kind).wait_send()
    for copy in cot_copies + normed_copies + tail_copies:
        copy.wait_send()


def front(x2, normed, masks, cot, w_in, w_out):
    count, twins = lax.axis_size("seq"), lax.axis_size("ch")
    rows, width = normed.shape
    inner = w_out.shape[2]
    modes = w_out.shape[0]
    blocks = w_in.reshape(modes, width, 2, inner // 128, 128).transpose(0, 1, 3, 2, 4)
    vmem = pl.BlockSpec(memory_space=pltpu.VMEM)
    hbm = pl.BlockSpec(memory_space=pl.ANY)
    wide = min(512, inner)
    return pl.pallas_call(
        functools.partial(front_kernel, (count, twins)),
        in_specs=[vmem, vmem, vmem, vmem, hbm, hbm],
        out_specs=[vmem, vmem, vmem, vmem],
        out_shape=[
            jax.ShapeDtypeStruct((rows, inner), jnp.bfloat16),
            jax.ShapeDtypeStruct((rows, inner), jnp.bfloat16),
            jax.ShapeDtypeStruct((rows, inner), jnp.float32),
            jax.ShapeDtypeStruct((2, 2, count, rows // 2, width // count), jnp.bfloat16),
        ],
        scratch_shapes=[
            pltpu.VMEM((twins,) + cot.shape, jnp.bfloat16),
            pltpu.VMEM((2, 2, width, 2, 128), jnp.bfloat16),
            pltpu.VMEM((2, width, wide), jnp.bfloat16),
            pltpu.SemaphoreType.DMA((2, 2)),
            pltpu.SemaphoreType.DMA((2,)),
            pltpu.SemaphoreType.DMA((twins - 1,)),
            pltpu.SemaphoreType.DMA((twins - 1,)),
            pltpu.SemaphoreType.DMA((2, count - 1)),
            pltpu.SemaphoreType.DMA((2, count - 1)),
            pltpu.SemaphoreType.DMA((2,)),
            pltpu.SemaphoreType.DMA((2,)),
            pltpu.SemaphoreType.DMA((1,)),
        ],
        compiler_params=pltpu.CompilerParams(collective_id=1, has_side_effects=True, vmem_limit_bytes=56 << 20),
        name="front",
    )(x2, normed, masks, cot, blocks, w_out)


def doc_tables(doc_lengths, positions):
    count = doc_lengths.shape[0]
    order = jnp.arange(count, dtype=jnp.int32)
    doc_ends = jnp.sum(jnp.where(order[:, None] >= order[None, :], doc_lengths[None, :], 0), axis=1)
    doc_starts = doc_ends - doc_lengths
    doc_index = jnp.sum((positions[:, None] >= doc_ends[None, :]).astype(jnp.int32), axis=1)
    begins = jnp.any(positions[:, None] == doc_starts[None, :], axis=1)
    return (doc_index, begins)


def own_columns(values):
    rows, n = values.shape
    own = jnp.arange(16 * n)[None] // n == jnp.arange(rows)[:, None] % 16
    return jnp.where(own, jnp.tile(values, (1, 16)), 0).astype(jnp.bfloat16)


LB = 512
CH = 32
NS = 16

def tile_lanes(v, lanes):
    return jnp.concatenate([v] * (lanes // 128), axis=1)

def ends_kernel(lb, dtd_ref, u_ref, g_ref, b_ref, c_ref, rate_ref, out_ref, acc_ref):
    n = rate_ref.shape[0]
    rows, chans = dtd_ref.shape
    @pl.when(pl.program_id(0) == 0)
    def _():
        acc_ref[0:n, :] = jnp.zeros((n, chans), jnp.float32)
        acc_ref[n:2*n, :] = jnp.ones((n, chans), jnp.float32)
        acc_ref[2*n:3*n, :] = jnp.zeros((n, chans), jnp.float32)
    for block in range(chans // lb):
        cut = slice(block * lb, (block + 1) * lb)
        rate = rate_ref[:, cut]
        h = acc_ref[0:n, cut]
        reach = acc_ref[n:2*n, cut]
        head = acc_ref[2*n:3*n, cut]
        for t in range(rows):
            decay = jnp.exp2(dtd_ref[t:t+1, cut] * rate)
            h = decay * h + u_ref[t:t+1, cut] * tile_lanes(b_ref[t], lb)
            reach = reach * decay
            head = head + reach * (g_ref[t:t+1, cut] * tile_lanes(c_ref[t], lb))
        acc_ref[0:n, cut] = h
        acc_ref[n:2*n, cut] = reach
        acc_ref[2*n:3*n, cut] = head
    @pl.when(pl.program_id(0) == pl.num_programs(0) - 1)
    def _():
        out_ref[0] = acc_ref[0:n, :].astype(jnp.bfloat16)
        out_ref[1] = acc_ref[2*n:3*n, :].astype(jnp.bfloat16)

def scan_ends(dtd, u, g, b, c, rate, lb=LB, ch=CH):
    t, e = dtd.shape
    n = rate.shape[0]
    row = pl.BlockSpec((ch, e), lambda i: (i, 0))
    wide = pl.BlockSpec((ch, n, 128), lambda i: (i, 0, 0))
    return pl.pallas_call(
        functools.partial(ends_kernel, lb),
        grid=(t // ch,),
        in_specs=[row, row, row, wide, wide, pl.BlockSpec((n, e), lambda i: (0, 0))],
        out_specs=pl.BlockSpec((2, n, e), lambda i: (0, 0, 0)),
        out_shape=jax.ShapeDtypeStruct((2, n, e), jnp.bfloat16),
        scratch_shapes=[pltpu.VMEM((3 * n, e), jnp.float32)],
        compiler_params=pltpu.CompilerParams(vmem_limit_bytes=32 << 20),
        name="scan_ends",
    )(dtd, u, g, b, c, rate)

def forward_kernel(lb, dtd_ref, u_ref, b_ref, cblk_ref, rate_ref, h0_ref, y_ref, hist_ref, state_ref):
    n = rate_ref.shape[0]
    rows, chans = dtd_ref.shape
    @pl.when(pl.program_id(0) == 0)
    def _():
        state_ref[...] = h0_ref[...]
    for block in range(chans // lb):
        cut = slice(block * lb, (block + 1) * lb)
        rate = rate_ref[:, cut]
        h = state_ref[:, cut]
        for t in range(rows):
            decay = jnp.exp2(dtd_ref[t:t+1, cut] * rate)
            h = decay * h + u_ref[t:t+1, cut] * tile_lanes(b_ref[t], lb)
            hist_ref[t * n:(t + 1) * n, cut] = h.astype(jnp.bfloat16)
        state_ref[:, cut] = h
    for k in range(rows // 16):
        y_ref[k*16:(k+1)*16, :] = jnp.dot(cblk_ref[k*16:(k+1)*16, :], hist_ref[k*16*n:(k+1)*16*n, :], preferred_element_type=jnp.float32)

def scan_forward(dtd, u, b, cblk, rate, h0, lb=LB, ch=CH):
    t, e = dtd.shape
    n = rate.shape[0]
    row = pl.BlockSpec((ch, e), lambda i: (i, 0))
    wide = pl.BlockSpec((ch, n, 128), lambda i: (i, 0, 0))
    whole = pl.BlockSpec((n, e), lambda i: (0, 0))
    return pl.pallas_call(
        functools.partial(forward_kernel, lb),
        grid=(t // ch,),
        in_specs=[row, row, wide, pl.BlockSpec((ch, 16 * n), lambda i: (i, 0)), whole, whole],
        out_specs=(row, pl.BlockSpec((ch * n, e), lambda i: (i, 0))),
        out_shape=(jax.ShapeDtypeStruct((t, e), jnp.float32), jax.ShapeDtypeStruct((t * n, e), jnp.bfloat16)),
        scratch_shapes=[pltpu.VMEM((n, e), jnp.float32)],
        compiler_params=pltpu.CompilerParams(vmem_limit_bytes=32 << 20),
        name="scan_forward",
    )(dtd, u, b, cblk, rate, h0)

def backward_kernel(lb, dtd_ref, step_ref, conv_ref, g_ref, c_ref, bblk_ref, rate_ref, lam0_ref, h0_ref, hist_ref, prev_ref,
                    gstep_ref, gscan_ref, gb_ref, gc_ref, racc_ref, pend_ref, lam_ref, w_ref):
    n = rate_ref.shape[0]
    rows, chans = dtd_ref.shape
    last = pl.num_programs(0) - 1
    @pl.when(pl.program_id(0) == 0)
    def _():
        pend_ref[...] = lam0_ref[...]
        racc_ref[...] = jnp.zeros_like(racc_ref)
    first = pl.program_id(0) == last
    for block in range(chans // lb):
        cut = slice(block * lb, (block + 1) * lb)
        rate = rate_ref[:, cut]
        pend = pend_ref[:, cut]
        racc = racc_ref[:, cut]
        for t in reversed(range(rows)):
            decay = jnp.exp2(dtd_ref[t:t+1, cut] * rate)
            lam = g_ref[t:t+1, cut] * tile_lanes(c_ref[t], lb) + pend
            pend = decay * lam
            if t:
                before = hist_ref[(t - 1) * n:t * n, cut].astype(jnp.float32)
            else:
                before = jnp.where(first, h0_ref[:, cut], prev_ref[:, cut].astype(jnp.float32))
            w = pend * before
            racc = racc + w * step_ref[t:t+1, cut]
            lam_ref[t * n:(t + 1) * n, cut] = lam.astype(jnp.bfloat16)
            w_ref[t * n:(t + 1) * n, cut] = (w * rate).astype(jnp.bfloat16)
        pend_ref[:, cut] = pend
        racc_ref[:, cut] = racc
    for k in range(rows // 16):
        rc = slice(k * 16, (k + 1) * 16)
        hc = slice(k * 16 * n, (k + 1) * 16 * n)
        step = step_ref[rc, :]
        conv = conv_ref[rc, :]
        own = (lax.broadcasted_iota(jnp.int32, (16, 16 * n), 1) // n == lax.broadcasted_iota(jnp.int32, (16, 16 * n), 0))
        ones = own.astype(jnp.bfloat16)
        adj = jnp.dot(bblk_ref[rc, :], lam_ref[hc, :], preferred_element_type=jnp.float32)
        wsum = jnp.dot(ones, w_ref[hc, :], preferred_element_type=jnp.float32)
        gstep_ref[rc, :] = wsum * math.log(2.0) + adj * conv
        gscan_ref[rc, :] = adj * step
        nt = (((1,), (1,)), ((), ()))
        gb = lax.dot_general((step * conv).astype(jnp.bfloat16), lam_ref[hc, :], nt, preferred_element_type=jnp.float32)
        gc = lax.dot_general(g_ref[rc, :].astype(jnp.bfloat16), hist_ref[hc, :], nt, preferred_element_type=jnp.float32)
        gb_ref[k:k+1] = jnp.sum(jnp.where(own, gb, 0.0), axis=0, keepdims=True)[None]
        gc_ref[k:k+1] = jnp.sum(jnp.where(own, gc, 0.0), axis=0, keepdims=True)[None]

def scan_backward(dtd, step, conv, g, c, bblk, rate, lam0, h0, hist, lb=LB, ch=CH):
    t, e = dtd.shape
    n = rate.shape[0]
    k = t // ch
    row = pl.BlockSpec((ch, e), lambda i: (k - 1 - i, 0))
    wide = pl.BlockSpec((ch, n, 128), lambda i: (k - 1 - i, 0, 0))
    whole = pl.BlockSpec((n, e), lambda i: (0, 0))
    flat = pl.BlockSpec((ch // 16, 1, 16 * n), lambda i: (k - 1 - i, 0, 0))
    outs = pl.pallas_call(
        functools.partial(backward_kernel, lb),
        grid=(k,),
        in_specs=[row, row, row, row, wide, pl.BlockSpec((ch, 16 * n), lambda i: (k - 1 - i, 0)), whole, whole, whole,
                  pl.BlockSpec((ch * n, e), lambda i: (k - 1 - i, 0)),
                  pl.BlockSpec((n, e), lambda i: (jnp.maximum((k - 1 - i) * ch - 1, 0), 0))],
        out_specs=(row, row, flat, flat, whole),
        out_shape=(jax.ShapeDtypeStruct((t, e), jnp.float32), jax.ShapeDtypeStruct((t, e), jnp.float32),
                   jax.ShapeDtypeStruct((t // 16, 1, 16 * n), jnp.float32), jax.ShapeDtypeStruct((t // 16, 1, 16 * n), jnp.float32),
                   jax.ShapeDtypeStruct((n, e), jnp.float32)),
        scratch_shapes=[pltpu.VMEM((n, e), jnp.float32), pltpu.VMEM((ch * n, e), jnp.bfloat16), pltpu.VMEM((ch * n, e), jnp.bfloat16)],
        compiler_params=pltpu.CompilerParams(vmem_limit_bytes=48 << 20),
        name="scan_backward",
    )(dtd, step, conv, g, c, bblk, rate, lam0, h0, hist, hist)
    return outs[0], outs[1], outs[2].reshape(t, n), outs[3].reshape(t, n), outs[4]


def shards(
    x_in,
    norm_gain,
    w_in,
    conv_weight,
    conv_bias,
    x_proj,
    dt_proj,
    dt_bias,
    a_log,
    d_skip,
    w_out,
    modes,
    doc_lengths,
    cotangent,
):
    tok_rows, model_width = x_in.shape
    mode_count = w_in.shape[0]
    inner_local = conv_bias.shape[0]
    state_size = a_log.shape[0]
    rank_size = dt_proj.shape[0]
    conv_taps = conv_weight.shape[0]
    ch_count = lax.axis_size("ch")
    feat_part = model_width // ch_count
    seq_index = lax.axis_index("seq")
    ch_index = lax.axis_index("ch")
    first_pos = seq_index * tok_rows
    positions = first_pos + jnp.arange(tok_rows, dtype=jnp.int32)
    my_modes = lax.dynamic_slice_in_dim(modes, first_pos, tok_rows)
    onehot = (my_modes[:, None] == jnp.arange(mode_count, dtype=jnp.int32)[None]).astype(
        jnp.bfloat16
    )
    doc_index, begins = doc_tables(doc_lengths, positions)
    keep_mask = 1.0 - begins.astype(jnp.float32)
    x_full = x_in.astype(jnp.float32)
    scale = lax.rsqrt(jnp.mean(x_full * x_full, axis=1, keepdims=True) + EPSILON)
    normed = (x_full * scale * norm_gain[None]).astype(jnp.bfloat16)
    spread = jnp.eye(256, dtype=jnp.bfloat16)
    spread = jnp.stack([spread, jnp.zeros_like(spread)], axis=2)
    spread = jnp.stack([spread, spread[:, :, ::-1]], axis=0).reshape(2, 256, 512)
    doubled = jnp.einsum("tbd,jdk->jtbk", normed.reshape(tok_rows, -1, 256), spread)
    doubled = doubled.reshape(2, tok_rows, 2 * model_width)
    masks = jnp.broadcast_to(onehot.T[:, :, None], (mode_count, tok_rows, 128))
    x_branch, z_branch, d_gated, cols = front(doubled, normed, masks, cotangent, w_in, w_out)
    z_branch = z_branch.astype(jnp.float32)
    rim_rows = from_behind(x_branch[tok_rows - (conv_taps - 1) :], "seq", 1)
    extended = jnp.concatenate([rim_rows, x_branch], axis=0).astype(jnp.float32)
    ext_doc, _ = doc_tables(
        doc_lengths,
        first_pos - (conv_taps - 1) + jnp.arange(tok_rows + conv_taps - 1, dtype=jnp.int32),
    )
    conv_pre = jnp.zeros((tok_rows, inner_local), jnp.float32) + conv_bias[None]
    same_list = []
    for offset in range(conv_taps):
        same_doc = (ext_doc[offset : offset + tok_rows] == doc_index).astype(jnp.float32)[:, None]
        same_list.append(same_doc)
        conv_pre = (
            conv_pre + conv_weight[offset][None] * extended[offset : offset + tok_rows] * same_doc
        )
    conv_out = jax.nn.silu(conv_pre).astype(jnp.bfloat16)
    conv_float = conv_out.astype(jnp.float32)
    projected = sum_over(jnp.dot(conv_out, x_proj, preferred_element_type=jnp.float32), "ch")
    dt_low = projected[:, :rank_size].astype(jnp.bfloat16)
    b_in = projected[:, rank_size : rank_size + state_size]
    c_out = projected[:, rank_size + state_size :]
    dt_raw = jnp.dot(dt_low, dt_proj, preferred_element_type=jnp.float32)
    step_size = jax.nn.softplus(dt_raw + dt_bias[None])
    decay_rate = -jnp.exp(a_log)
    seq_count = lax.axis_size("seq")
    rate_two = decay_rate * math.log2(math.e)
    masked_step = jnp.where(begins[:, None], 1e30, step_size)
    drive = step_size * conv_float
    wide = (tok_rows, state_size, 128)
    b_wide = jnp.broadcast_to(b_in[:, :, None], wide)
    c_wide = jnp.broadcast_to(c_out[:, :, None], wide)
    gate_act = jax.nn.silu(z_branch)
    d_ssm = d_gated * gate_act
    ends = scan_ends(masked_step, drive, d_ssm, b_wide, c_wide, rate_two)
    steps = jnp.sum(masked_step, axis=0)
    ends_in, steps_in = exchange_states(ends, steps.reshape(8, -1))
    steps_in = steps_in.reshape(seq_count - 1, inner_local)
    incoming = jnp.zeros((state_size, inner_local), jnp.float32)
    pending = incoming
    gap = jnp.zeros((inner_local,), jnp.float32)
    for distance in range(1, seq_count):
        part = ends_in[distance - 1].astype(jnp.float32) * jnp.exp2(rate_two * gap[None])
        incoming = incoming + jnp.where(distance <= seq_index, part, 0.0)
        gap = gap + steps_in[distance - 1]
    gap = jnp.zeros((inner_local,), jnp.float32)
    for distance in range(1, seq_count):
        slot = seq_count - 1 - distance
        part = ends_in[slot].astype(jnp.float32) * jnp.exp2(rate_two * gap[None])
        pending = pending + jnp.where(distance + seq_index < seq_count, part, 0.0)
        gap = gap + steps_in[slot]
    ssm, history = scan_forward(
        masked_step, drive, b_wide, own_columns(c_out), rate_two, incoming
    )
    ssm = ssm + d_skip[None] * conv_float
    gated = (ssm * gate_act).astype(jnp.bfloat16)
    proj_all = jnp.einsum("te,mde->tmd", gated, w_out, preferred_element_type=jnp.float32)
    mixer_part = jnp.sum(onehot.astype(jnp.float32)[:, :, None] * proj_all, axis=1)
    mixer = sum_slices(mixer_part, "ch")
    x_slice = lax.dynamic_slice_in_dim(x_full, ch_index * feat_part, feat_part, 1)
    block_out = (x_slice + mixer).astype(jnp.bfloat16)
    gate_sig = jax.nn.sigmoid(z_branch)
    d_z = d_gated * ssm * gate_sig * (1.0 + z_branch * (1.0 - gate_sig))
    d_z = d_z.astype(jnp.bfloat16)
    gated_all = ring_gather(gated, "seq")
    d_z_all = ring_gather(d_z, "seq")
    d_skip_local = jnp.sum(d_ssm * conv_float, axis=0)
    d_conv = d_ssm * d_skip[None]
    d_step, conv_grads, d_b, d_c, rate_grad = scan_backward(
        masked_step, step_size, conv_float, d_ssm, c_wide, own_columns(b_in), rate_two, pending, incoming, history
    )
    d_conv = d_conv + conv_grads
    d_a_log = rate_grad * decay_rate
    d_full = d_step * jax.nn.sigmoid(dt_raw + dt_bias[None])
    d_bias_local = jnp.sum(d_full, axis=0)
    d_raw = d_full.astype(jnp.bfloat16)
    d_dt_proj_local = jnp.einsum("tr,te->re", dt_low, d_raw, preferred_element_type=jnp.float32)
    d_low_part = jnp.einsum("te,re->tr", d_raw, dt_proj, preferred_element_type=jnp.float32)
    d_projected = sum_over(jnp.concatenate([d_low_part, d_b, d_c], axis=1), "ch").astype(
        jnp.bfloat16
    )
    d_x_proj_local = jnp.einsum(
        "te,tk->ek", conv_out, d_projected, preferred_element_type=jnp.float32
    )
    d_conv = d_conv + jnp.einsum(
        "tk,ek->te", d_projected, x_proj, preferred_element_type=jnp.float32
    )
    conv_sig = jax.nn.sigmoid(conv_pre)
    d_pre = d_conv * conv_sig * (1.0 + conv_pre * (1.0 - conv_sig))
    d_conv_bias_local = jnp.sum(d_pre, axis=0)
    d_conv_weight_local = jnp.stack(
        [
            jnp.sum(d_pre * extended[offset : offset + tok_rows] * same_list[offset], axis=0)
            for offset in range(conv_taps)
        ],
        axis=0,
    )
    after_rows = from_behind(d_pre[: conv_taps - 1], "seq", -1)
    d_pre_ext = jnp.concatenate([d_pre, after_rows], axis=0)
    post_doc, _ = doc_tables(
        doc_lengths, first_pos + jnp.arange(tok_rows + conv_taps - 1, dtype=jnp.int32)
    )
    d_x_branch = jnp.zeros((tok_rows, inner_local), jnp.float32)
    for offset in range(conv_taps):
        lag = conv_taps - 1 - offset
        same_doc = (post_doc[lag : lag + tok_rows] == doc_index).astype(jnp.float32)[:, None]
        d_x_branch = (
            d_x_branch + d_pre_ext[lag : lag + tok_rows] * conv_weight[offset][None] * same_doc
        )
    d_x_branch = d_x_branch.astype(jnp.bfloat16)
    d_x_all = ring_gather(d_x_branch, "seq")
    d_both = jnp.stack([d_x_branch, d_z], axis=1).reshape(tok_rows, 2 * inner_local)
    normed_terms = jnp.einsum(
        "tk,mdk->tmd",
        d_both,
        w_in.reshape(mode_count, model_width, 2 * inner_local),
        preferred_element_type=jnp.float32,
    )
    normed_part = jnp.sum(onehot.astype(jnp.float32)[:, :, None] * normed_terms, axis=1)
    gain_slice = lax.dynamic_slice_in_dim(norm_gain, ch_index * feat_part, feat_part, 0)
    d_slice = sum_slices(normed_part, "ch")
    own_dots = jnp.sum(normed_part * norm_gain[None] * x_full, axis=1)
    dots = own_dots
    for distance in range(1, ch_count):
        route = [(i, (i + distance) % ch_count) for i in range(ch_count)]
        dots = dots + lax.ppermute(own_dots, "ch", route)
    mean_term = (dots / model_width)[:, None]
    weighted_slice = d_slice * gain_slice[None]
    d_x_in = cotangent.astype(jnp.float32) + scale * weighted_slice - x_slice * scale**3 * mean_term
    d_gain_part = jnp.sum(d_slice * x_slice * scale, axis=0)
    all_modes = ring_modes(modes, "seq")
    cols = cols.reshape(2, seq_count * tok_rows, -1)
    mode_mask = (all_modes[:, None] == jnp.arange(mode_count, dtype=jnp.int32)[None]).astype(
        jnp.bfloat16
    )
    x_spread = mode_mask[:, :, None] * cols[0][:, None, :]
    c_spread = mode_mask[:, :, None] * cols[1][:, None, :]
    d_w_out = jnp.einsum("tmd,te->mde", c_spread, gated_all, preferred_element_type=jnp.float32)
    d_w_z = jnp.einsum("tmd,te->mde", x_spread, d_z_all, preferred_element_type=jnp.float32)
    d_w_x = jnp.einsum("tmd,te->mde", x_spread, d_x_all, preferred_element_type=jnp.float32)
    d_w_in = jnp.stack([d_w_x, d_w_z], axis=2)
    small_sums = lax.psum(
        (
            d_gain_part,
            d_conv_weight_local,
            d_conv_bias_local,
            d_x_proj_local,
            d_dt_proj_local,
            d_bias_local,
            d_a_log,
            d_skip_local,
        ),
        "seq",
    )
    return (
        block_out,
        d_x_in,
        small_sums[0],
        d_w_in,
        small_sums[1],
        small_sums[2],
        small_sums[3],
        small_sums[4],
        small_sums[5],
        small_sums[6],
        small_sums[7],
        d_w_out,
    )


def solution(mesh):
    return jax.shard_map(
        shards,
        mesh=mesh,
        in_specs=(
            P("seq", None),
            P(),
            P(None, None, None, "ch"),
            P(None, "ch"),
            P("ch"),
            P("ch", None),
            P(None, "ch"),
            P("ch"),
            P(None, "ch"),
            P("ch"),
            P(None, None, "ch"),
            P(),
            P(),
            P("seq", "ch"),
        ),
        out_specs=(
            P("seq", "ch"),
            P("seq", "ch"),
            P("ch"),
            P(None, "seq", None, "ch"),
            P(None, "ch"),
            P("ch"),
            P("ch", None),
            P(None, "ch"),
            P("ch"),
            P(None, "ch"),
            P("ch"),
            P(None, "seq", "ch"),
        ),
        check_vma=False,
    )
```

```python
import functools
import math

import jax
import jax.numpy as jnp
from jax import lax
from jax.experimental import pallas as pl
from jax.experimental.pallas import tpu as pltpu
from jax.sharding import PartitionSpec as P

EPSILON = 1e-05


def from_behind(block, axis, distance):
    devices = range(lax.axis_size(axis))
    route = [(i - distance, i) for i in devices if i - distance in devices]
    return lax.ppermute(block, axis, route)


MESH = pl.DeviceIdType.MESH


def sum_over(part, axis):
    count = lax.axis_size(axis)
    sent = part.astype(jnp.bfloat16)
    total = part
    for distance in range(1, count):
        route = [(i, (i + distance) % count) for i in range(count)]
        total = total + lax.ppermute(sent, axis, route).astype(jnp.float32)
    return total


def cycle_of(count):
    across = count // 4
    walk = [(0, x) for x in range(across)]
    for turn, x in enumerate(reversed(range(across))):
        column = [(z, x) for z in range(1, 4)]
        walk += column[::-1] if turn % 2 else column
    return [z * across + x for z, x in walk]


def states_kernel(count, ends_ref, steps_ref, ends_out, steps_out, send, recv):
    me = lax.axis_index("seq")
    barrier = pltpu.get_barrier_semaphore()
    for distance in range(1, count):
        peer = {"seq": lax.rem(me + distance, count)}
        pl.semaphore_signal(barrier, inc=1, device_id=peer, device_id_type=MESH)
    pl.semaphore_wait(barrier, count - 1)
    copies = []
    for distance in range(1, count):
        peer = lax.rem(me + distance, count)
        side = jnp.where(peer > me, 0, 1)
        for kind, (source, target) in enumerate(
            ((ends_ref.at[side], ends_out), (steps_ref, steps_out))
        ):
            copies.append(
                pltpu.make_async_remote_copy(
                    src_ref=source,
                    dst_ref=target.at[distance - 1],
                    send_sem=send.at[kind, distance - 1],
                    recv_sem=recv.at[kind, distance - 1],
                    device_id={"seq": peer},
                    device_id_type=MESH,
                )
            )
    for copy in copies:
        copy.start()
    for copy in copies:
        copy.wait()


def exchange_states(ends, steps):
    others = lax.axis_size("seq") - 1
    vmem = pl.BlockSpec(memory_space=pltpu.VMEM)
    return pl.pallas_call(
        functools.partial(states_kernel, others + 1),
        in_specs=[vmem, vmem],
        out_specs=[vmem, vmem],
        out_shape=[
            jax.ShapeDtypeStruct((others,) + ends.shape[1:], ends.dtype),
            jax.ShapeDtypeStruct((others,) + steps.shape, steps.dtype),
        ],
        scratch_shapes=[
            pltpu.SemaphoreType.DMA((2, others)),
            pltpu.SemaphoreType.DMA((2, others)),
        ],
        compiler_params=pltpu.CompilerParams(
            collective_id=0, has_side_effects=True, vmem_limit_bytes=32 << 20
        ),
        name="exchange_states",
    )(ends, steps)


def table_of(index, values):
    picked = jnp.int32(values[0])
    for i in range(1, len(values)):
        picked = jnp.where(index == i, jnp.int32(values[i]), picked)
    return picked


def front_kernel(
    sizes, x2_ref, normed_ref, mask_ref, cot_ref, w_in_ref, w_out_ref,
    x_ref, z_ref, gated_ref, cols_ref,
    cotg_ref, in_buf, out_buf, in_sem, out_sem, cot_send, cot_recv, seq_send, seq_recv, twin_send, twin_recv, own_sem,
):
    count, twins = sizes
    rows, width = normed_ref.shape
    modes = mask_ref.shape[0]
    half = rows // 2
    slab = width // count
    part = cot_ref.shape[1]
    inner = x_ref.shape[1]
    ring = cycle_of(count)
    me = lax.axis_index("seq")
    mine = lax.axis_index("ch")
    side = lax.rem(mine, 2)
    twin = mine + 1 - 2 * side
    where = {s: i for i, s in enumerate(ring)}
    place = table_of(me, [where[s] for s in range(count)])

    barrier = pltpu.get_barrier_semaphore()
    for k in range(1, count):
        peer = {"seq": lax.rem(me + k, count)}
        pl.semaphore_signal(barrier, inc=1, device_id=peer, device_id_type=MESH)
    for k in range(1, twins):
        peer = {"ch": lax.rem(mine + k, twins)}
        pl.semaphore_signal(barrier, inc=1, device_id=peer, device_id_type=MESH)

    pairs = inner // 256
    steps = pairs * modes

    def in_copy(step, b):
        slot = lax.rem(step, 2)
        return pltpu.make_async_copy(
            w_in_ref.at[lax.rem(step, modes), :, step // modes * 2 + b], in_buf.at[slot, b], in_sem.at[slot, b]
        )

    wide = out_buf.shape[2]
    out_steps = inner // wide * modes

    def out_copy(step):
        slot = lax.rem(step, 2)
        columns = pl.ds(pl.multiple_of(step // modes * wide, wide), wide)
        return pltpu.make_async_copy(
            w_out_ref.at[lax.rem(step, modes), :, columns], out_buf.at[slot], out_sem.at[slot]
        )

    for b in (0, 1):
        in_copy(0, b).start()
    out_copy(0).start()
    pl.semaphore_wait(barrier, count - 1 + twins - 1)

    cot_copies = [
        pltpu.make_async_remote_copy(
            src_ref=cot_ref, dst_ref=cotg_ref.at[mine], send_sem=cot_send.at[k - 1], recv_sem=cot_recv.at[k - 1],
            device_id={"ch": lax.rem(mine + k, twins)}, device_id_type=MESH,
        )
        for k in range(1, twins)
    ]
    for copy in cot_copies:
        copy.start()
    side_rows = pl.ds(pl.multiple_of(side * half, half), half)

    def seq_copies(kind):
        copies = []
        for k in range(1, count):
            step = jnp.where(side == 0, k, count - k)
            peer = table_of(lax.rem(place + step, count), ring)
            if kind == 0:
                source = normed_ref.at[side_rows, pl.ds(pl.multiple_of(peer * slab, slab), slab)]
            else:
                start = lax.rem(peer * slab, part)
                source = cotg_ref.at[peer * slab // part, side_rows, pl.ds(pl.multiple_of(start, slab), slab)]
            copies.append(
                pltpu.make_async_remote_copy(
                    src_ref=source, dst_ref=cols_ref.at[kind, side, k], send_sem=seq_send.at[kind, k - 1],
                    recv_sem=seq_recv.at[kind, k - 1], device_id={"seq": peer}, device_id_type=MESH,
                )
            )
        return copies

    def twin_copy(kind):
        return pltpu.make_async_remote_copy(
            src_ref=cols_ref.at[kind, side, pl.ds(1, count - 1)], dst_ref=cols_ref.at[kind, side, pl.ds(1, count - 1)],
            send_sem=twin_send.at[kind], recv_sem=twin_recv.at[kind],
            device_id={"ch": twin}, device_id_type=MESH,
        )

    normed_copies = seq_copies(0)
    for copy in normed_copies:
        copy.start()
    own_copy = pltpu.make_async_copy(cot_ref, cotg_ref.at[mine], own_sem.at[0])
    own_copy.start()
    own_start = pl.multiple_of(me * slab, slab)
    for way in (0, 1):
        cols_ref[0, way, 0] = normed_ref[way * half : (way + 1) * half, pl.ds(own_start, slab)]

    def in_step(step, carry):
        slot = lax.rem(step, 2)
        mode = lax.rem(step, modes)

        @pl.when(step + 1 < steps)
        def _():
            for b in (0, 1):
                in_copy(step + 1, b).start()

        for b in (0, 1):
            in_copy(step, b).wait()
        weights = jnp.concatenate([in_buf.at[slot, b].reshape(2 * width, 128)[...] for b in (0, 1)], axis=1)
        mask = jnp.concatenate([mask_ref[mode]] * 2, axis=1) > 0
        columns = pl.ds(pl.multiple_of(step // modes * 256, 256), 256)
        for j, target in enumerate((x_ref, z_ref)):
            found = jnp.dot(x2_ref[j], weights, preferred_element_type=jnp.float32).astype(jnp.bfloat16)
            target[:, columns] = jnp.where(mask, found, target[:, columns])
        return carry

    x_ref[...] = jnp.zeros_like(x_ref)
    z_ref[...] = jnp.zeros_like(z_ref)
    first = steps // 2
    lax.fori_loop(0, first, in_step, 0)
    own_copy.wait()
    for copy in cot_copies:
        copy.wait_recv()
    tail_copies = seq_copies(1)
    for copy in tail_copies:
        copy.start()
    own_slab = cotg_ref.at[me * slab // part]
    for way in (0, 1):
        cols_ref[1, way, 0] = own_slab[way * half : (way + 1) * half, pl.ds(pl.multiple_of(lax.rem(me * slab, part), slab), slab)]
    for copy in normed_copies:
        copy.wait_recv()
    twin_copy(0).start()
    lax.fori_loop(first, steps, in_step, 0)

    def out_step(step, carry):
        slot = lax.rem(step, 2)
        mode = lax.rem(step, modes)

        @pl.when(step + 1 < out_steps)
        def _():
            out_copy(step + 1).start()

        out_copy(step).wait()
        mask = jnp.concatenate([mask_ref[mode]] * (wide // 128), axis=1) > 0
        columns = pl.ds(pl.multiple_of(step // modes * wide, wide), wide)
        found = jnp.zeros((rows, wide), jnp.float32)
        for c in range(twins):
            found = found + jnp.dot(
                cotg_ref[c], out_buf[slot, c * part : (c + 1) * part], preferred_element_type=jnp.float32
            )
        gated_ref[:, columns] = jnp.where(mask, found, gated_ref[:, columns])
        return carry

    gated_ref[...] = jnp.zeros_like(gated_ref)
    lax.fori_loop(0, out_steps, out_step, 0)
    for copy in tail_copies:
        copy.wait_recv()
    twin_copy(1).start()
    for kind in (0, 1):
        twin_copy(kind).wait_recv()
        twin_copy(kind).wait_send()
    for copy in cot_copies + normed_copies + tail_copies:
        copy.wait_send()


def front(x2, normed, masks, cot, w_in, w_out):
    count, twins = lax.axis_size("seq"), lax.axis_size("ch")
    rows, width = normed.shape
    inner = w_out.shape[2]
    modes = w_out.shape[0]
    blocks = w_in.reshape(modes, width, 2, inner // 128, 128).transpose(0, 1, 3, 2, 4)
    vmem = pl.BlockSpec(memory_space=pltpu.VMEM)
    hbm = pl.BlockSpec(memory_space=pl.ANY)
    wide = min(512, inner)
    return pl.pallas_call(
        functools.partial(front_kernel, (count, twins)),
        in_specs=[vmem, vmem, vmem, vmem, hbm, hbm],
        out_specs=[vmem, vmem, vmem, vmem],
        out_shape=[
            jax.ShapeDtypeStruct((rows, inner), jnp.bfloat16),
            jax.ShapeDtypeStruct((rows, inner), jnp.bfloat16),
            jax.ShapeDtypeStruct((rows, inner), jnp.float32),
            jax.ShapeDtypeStruct((2, 2, count, rows // 2, width // count), jnp.bfloat16),
        ],
        scratch_shapes=[
            pltpu.VMEM((twins,) + cot.shape, jnp.bfloat16),
            pltpu.VMEM((2, 2, width, 2, 128), jnp.bfloat16),
            pltpu.VMEM((2, width, wide), jnp.bfloat16),
            pltpu.SemaphoreType.DMA((2, 2)),
            pltpu.SemaphoreType.DMA((2,)),
            pltpu.SemaphoreType.DMA((twins - 1,)),
            pltpu.SemaphoreType.DMA((twins - 1,)),
            pltpu.SemaphoreType.DMA((2, count - 1)),
            pltpu.SemaphoreType.DMA((2, count - 1)),
            pltpu.SemaphoreType.DMA((2,)),
            pltpu.SemaphoreType.DMA((2,)),
            pltpu.SemaphoreType.DMA((1,)),
        ],
        compiler_params=pltpu.CompilerParams(collective_id=1, has_side_effects=True, vmem_limit_bytes=56 << 20),
        name="front",
    )(x2, normed, masks, cot, blocks, w_out)


def doc_tables(doc_lengths, positions):
    count = doc_lengths.shape[0]
    order = jnp.arange(count, dtype=jnp.int32)
    doc_ends = jnp.sum(jnp.where(order[:, None] >= order[None, :], doc_lengths[None, :], 0), axis=1)
    doc_starts = doc_ends - doc_lengths
    doc_index = jnp.sum((positions[:, None] >= doc_ends[None, :]).astype(jnp.int32), axis=1)
    begins = jnp.any(positions[:, None] == doc_starts[None, :], axis=1)
    return (doc_index, begins)


def own_columns(values):
    rows, n = values.shape
    own = jnp.arange(16 * n)[None] // n == jnp.arange(rows)[:, None] % 16
    return jnp.where(own, jnp.tile(values, (1, 16)), 0).astype(jnp.bfloat16)


LB = 512
CH = 32
NS = 16

def tile_lanes(v, lanes):
    return jnp.concatenate([v] * (lanes // 128), axis=1)

def ends_kernel(lb, dtd_ref, u_ref, g_ref, b_ref, c_ref, rate_ref, out_ref, acc_ref):
    n = rate_ref.shape[0]
    rows, chans = dtd_ref.shape
    @pl.when(pl.program_id(0) == 0)
    def _():
        acc_ref[0:n, :] = jnp.zeros((n, chans), jnp.float32)
        acc_ref[n:2*n, :] = jnp.ones((n, chans), jnp.float32)
        acc_ref[2*n:3*n, :] = jnp.zeros((n, chans), jnp.float32)
    for block in range(chans // lb):
        cut = slice(block * lb, (block + 1) * lb)
        rate = rate_ref[:, cut]
        h = acc_ref[0:n, cut]
        reach = acc_ref[n:2*n, cut]
        head = acc_ref[2*n:3*n, cut]
        for t in range(rows):
            decay = jnp.exp2(dtd_ref[t:t+1, cut] * rate)
            h = decay * h + u_ref[t:t+1, cut] * tile_lanes(b_ref[t], lb)
            reach = reach * decay
            head = head + reach * (g_ref[t:t+1, cut] * tile_lanes(c_ref[t], lb))
        acc_ref[0:n, cut] = h
        acc_ref[n:2*n, cut] = reach
        acc_ref[2*n:3*n, cut] = head
    @pl.when(pl.program_id(0) == pl.num_programs(0) - 1)
    def _():
        out_ref[0] = acc_ref[0:n, :].astype(jnp.bfloat16)
        out_ref[1] = acc_ref[2*n:3*n, :].astype(jnp.bfloat16)

def scan_ends(dtd, u, g, b, c, rate, lb=LB, ch=CH):
    t, e = dtd.shape
    n = rate.shape[0]
    row = pl.BlockSpec((ch, e), lambda i: (i, 0))
    wide = pl.BlockSpec((ch, n, 128), lambda i: (i, 0, 0))
    return pl.pallas_call(
        functools.partial(ends_kernel, lb),
        grid=(t // ch,),
        in_specs=[row, row, row, wide, wide, pl.BlockSpec((n, e), lambda i: (0, 0))],
        out_specs=pl.BlockSpec((2, n, e), lambda i: (0, 0, 0)),
        out_shape=jax.ShapeDtypeStruct((2, n, e), jnp.bfloat16),
        scratch_shapes=[pltpu.VMEM((3 * n, e), jnp.float32)],
        compiler_params=pltpu.CompilerParams(vmem_limit_bytes=32 << 20),
        name="scan_ends",
    )(dtd, u, g, b, c, rate)

def forward_kernel(lb, dtd_ref, u_ref, b_ref, cblk_ref, rate_ref, h0_ref, y_ref, hist_ref, state_ref):
    n = rate_ref.shape[0]
    rows, chans = dtd_ref.shape
    @pl.when(pl.program_id(0) == 0)
    def _():
        state_ref[...] = h0_ref[...]
    for block in range(chans // lb):
        cut = slice(block * lb, (block + 1) * lb)
        rate = rate_ref[:, cut]
        h = state_ref[:, cut]
        for t in range(rows):
            decay = jnp.exp2(dtd_ref[t:t+1, cut] * rate)
            h = decay * h + u_ref[t:t+1, cut] * tile_lanes(b_ref[t], lb)
            hist_ref[t * n:(t + 1) * n, cut] = h.astype(jnp.bfloat16)
        state_ref[:, cut] = h
    for k in range(rows // 16):
        y_ref[k*16:(k+1)*16, :] = jnp.dot(cblk_ref[k*16:(k+1)*16, :], hist_ref[k*16*n:(k+1)*16*n, :], preferred_element_type=jnp.float32)

def scan_forward(dtd, u, b, cblk, rate, h0, lb=LB, ch=CH):
    t, e = dtd.shape
    n = rate.shape[0]
    row = pl.BlockSpec((ch, e), lambda i: (i, 0))
    wide = pl.BlockSpec((ch, n, 128), lambda i: (i, 0, 0))
    whole = pl.BlockSpec((n, e), lambda i: (0, 0))
    return pl.pallas_call(
        functools.partial(forward_kernel, lb),
        grid=(t // ch,),
        in_specs=[row, row, wide, pl.BlockSpec((ch, 16 * n), lambda i: (i, 0)), whole, whole],
        out_specs=(row, pl.BlockSpec((ch * n, e), lambda i: (i, 0))),
        out_shape=(jax.ShapeDtypeStruct((t, e), jnp.float32), jax.ShapeDtypeStruct((t * n, e), jnp.bfloat16)),
        scratch_shapes=[pltpu.VMEM((n, e), jnp.float32)],
        compiler_params=pltpu.CompilerParams(vmem_limit_bytes=32 << 20),
        name="scan_forward",
    )(dtd, u, b, cblk, rate, h0)

def ring_places(count):
    ring = cycle_of(count)
    where = {s: i for i, s in enumerate(ring)}
    me = lax.axis_index("seq")
    onward = table_of(me, [ring[(where[s] + 1) % count] for s in range(count)])
    backward = table_of(me, [ring[(where[s] - 1) % count] for s in range(count)])
    place = table_of(me, [where[s] for s in range(count)])
    return ring, place, onward, backward


def add_products(acc_ref, kind, k, cols_ref, blocks, modes_ref, ring, place, count):
    parts = []
    for way in (0, 1):
        step = k if way else count - k
        source = table_of(lax.rem(place + step, count), ring)
        parts.append((cols_ref[kind, way, k], modes_ref[pl.ds(2 * source + way, 1), :]))
    right = jnp.concatenate(blocks, axis=0)
    for m in range(acc_ref.shape[0]):
        left = jnp.concatenate(
            [part * jnp.where(row == m, 1.0, 0.0).astype(jnp.bfloat16) for part, row in parts], axis=1
        )
        acc_ref[m] += jnp.dot(left, right, preferred_element_type=jnp.float32)


def back_kernel(
    sizes, gz_ref, dtd_ref, step_ref, conv_ref, g_ref, c_ref, bblk_ref, rate_ref, lam0_ref, h0_ref, hist_hbm,
    sig_ref, pre_ref, ext_ref, same_ref, low_t_ref, dt_proj_ref, x_proj_ref, skip_ref, taps_ref, cols_ref, modes_ref,
    dwo_ref, dwz_ref, gx_ref, racc_ref, bias_ref, dtp_ref, xpt_ref, cbias_ref, cw_ref,
    ring_ref, hist_ref, lam_ref, w_ref, pend_ref, gstep_ref, gscan_ref, part_ref, sent_ref, got_ref, gpre_ref, edge_ref,
    hist_sem, ring_send, ring_recv, ch_send, ch_recv, edge_send, edge_recv,
):
    count, twins = sizes
    chunks, _, chans = dtd_ref.shape
    rows = chunks * 16
    n = rate_ref.shape[0]
    half = rows // 2
    ring, place, onward, backward = ring_places(count)
    me = lax.axis_index("seq")
    mine = lax.axis_index("ch")
    before = lax.rem(me + count - 1, count)
    after = lax.rem(me + 1, count)

    span = 32
    spans = rows // span

    def hist_copy(i):
        part = pl.ds(i * (span // 16), span // 16)
        return pltpu.make_async_copy(hist_hbm.at[part], hist_ref.at[part], hist_sem.at[i])

    barrier = pltpu.get_barrier_semaphore()
    for peer in (onward, backward, before, after):
        pl.semaphore_signal(barrier, inc=1, device_id={"seq": peer}, device_id_type=MESH)
    for k in range(1, twins):
        peer = {"ch": lax.rem(mine + k, twins)}
        pl.semaphore_signal(barrier, inc=1, device_id=peer, device_id_type=MESH)
    for i in reversed(range(spans)):
        hist_copy(i).start()
    pl.semaphore_wait(barrier, 4 + twins - 1)

    def ring_copy(kind, way, k):
        if k == 0:
            source = gz_ref.at[kind, pl.ds(way * half, half)]
        else:
            source = ring_ref.at[kind, way, k - 1]
        return pltpu.make_async_remote_copy(
            src_ref=source, dst_ref=ring_ref.at[kind, way, k], send_sem=ring_send.at[kind, way, k],
            recv_sem=ring_recv.at[kind, way, k], device_id={"seq": backward if way else onward}, device_id_type=MESH,
        )

    def relay(kind, k):
        for way in (0, 1):
            ring_copy(kind, way, k - 1).wait_recv()
            if k < count - 1:
                ring_copy(kind, way, k).start()

    for kind in (0, 1):
        for way in (0, 1):
            ring_copy(kind, way, 0).start()
    turns = [(kind, k) for k in range(1, count) for kind in (0, 1)]
    early = turns[:2]
    late = turns[2:]

    pend_ref[...] = lam0_ref[...]
    racc_ref[...] = jnp.zeros_like(racc_ref)
    lb = min(512, chans)
    own = (
        lax.broadcasted_iota(jnp.int32, (16, 16 * n), 1) // n == lax.broadcasted_iota(jnp.int32, (16, 16 * n), 0)
    )
    ones = own.astype(jnp.bfloat16)
    pick_row = lax.broadcasted_iota(jnp.int32, (16 * n, 128), 0)
    pick_col = lax.broadcasted_iota(jnp.int32, (16 * n, 128), 1)
    pick_b = (pick_row % n == pick_col).astype(jnp.bfloat16)
    pick_c = (pick_row % n + n == pick_col).astype(jnp.bfloat16)
    nt = (((1,), (1,)), ((), ()))

    def span_body(i, carry):
        at = spans - 1 - i

        @pl.when(at > 0)
        def _():
            hist_copy(at - 1).wait()

        for sub in reversed(range(span // 16)):
            chunk = at * (span // 16) + sub
            for block in range(chans // lb):
                cut = slice(block * lb, (block + 1) * lb)
                rate = rate_ref[:, cut]
                pend = pend_ref[:, cut]
                racc = racc_ref[:, cut]
                for t in reversed(range(16)):
                    decay = jnp.exp2(dtd_ref[chunk, t : t + 1, cut] * rate)
                    lam = g_ref[chunk, t : t + 1, cut] * tile_lanes(c_ref[chunk * 16 + t], lb) + pend
                    pend = decay * lam
                    if t:
                        prior = hist_ref[chunk, (t - 1) * n : t * n, cut].astype(jnp.float32)
                    else:
                        prior = hist_ref[jnp.maximum(chunk - 1, 0), 15 * n : 16 * n, cut].astype(jnp.float32)
                        prior = jnp.where(chunk == 0, h0_ref[:, cut], prior)
                    w = pend * prior
                    racc = racc + w * step_ref[chunk, t : t + 1, cut]
                    lam_ref[t * n : (t + 1) * n, cut] = lam.astype(jnp.bfloat16)
                    w_ref[t * n : (t + 1) * n, cut] = (w * rate).astype(jnp.bfloat16)
                pend_ref[:, cut] = pend
                racc_ref[:, cut] = racc
            step = step_ref[chunk]
            conv = conv_ref[chunk].astype(jnp.float32)
            adj = jnp.dot(bblk_ref[chunk], lam_ref[...], preferred_element_type=jnp.float32)
            wsum = jnp.dot(ones, w_ref[...], preferred_element_type=jnp.float32)
            gstep_ref[chunk] = wsum * math.log(2.0) + adj * conv
            gscan_ref[chunk] = adj * step
            gb = lax.dot_general((step * conv).astype(jnp.bfloat16), lam_ref[...], nt, preferred_element_type=jnp.float32)
            gc = lax.dot_general(
                g_ref[chunk].astype(jnp.bfloat16), hist_ref[chunk], nt, preferred_element_type=jnp.float32
            )
            gb = jnp.where(own, gb, 0.0).astype(jnp.bfloat16)
            gc = jnp.where(own, gc, 0.0).astype(jnp.bfloat16)
            part_ref[pl.ds(pl.multiple_of(chunk * 16, 16), 16), 128:256] = jnp.dot(
                gb, pick_b, preferred_element_type=jnp.float32
            ) + jnp.dot(gc, pick_c, preferred_element_type=jnp.float32)
        return carry

    hist_copy(spans - 1).wait()
    lax.fori_loop(0, spans // 2, span_body, 0)
    relay(*early[0])
    lax.fori_loop(spans // 2, spans, span_body, 0)
    relay(*early[1])

    bias_ref[...] = jnp.zeros_like(bias_ref)

    def raw_body(i, carry):
        full = gstep_ref[i] * sig_ref[i]
        bias_ref[...] += jnp.sum(full, axis=0, keepdims=True)
        gx_ref[pl.ds(pl.multiple_of(i * 16, 16), 16), :] = full.astype(jnp.bfloat16)
        return carry

    lax.fori_loop(0, chunks, raw_body, 0)
    part_ref[:, 0:128] = lax.dot_general(gx_ref[...], dt_proj_ref[...], nt, preferred_element_type=jnp.float32)
    sent_ref[...] = part_ref[...].astype(jnp.bfloat16)
    ch_copies = [
        pltpu.make_async_remote_copy(
            src_ref=sent_ref, dst_ref=got_ref.at[k - 1], send_sem=ch_send.at[k - 1], recv_sem=ch_recv.at[k - 1],
            device_id={"ch": lax.rem(mine + k, twins)}, device_id_type=MESH,
        )
        for k in range(1, twins)
    ]
    for copy in ch_copies:
        copy.start()
    relay(*late[0])
    dtp_ref[...] = jnp.dot(low_t_ref[...], gx_ref[...], preferred_element_type=jnp.float32)
    for copy in ch_copies:
        copy.wait_recv()
    total = part_ref[...]
    for k in range(twins - 1):
        total = total + got_ref[k].astype(jnp.float32)
    part_ref[...] = total
    relay(*late[1])

    skip = skip_ref[...]
    cbias_ref[...] = jnp.zeros_like(cbias_ref)
    cw_ref[...] = jnp.zeros_like(cw_ref)

    def pre_body(i, carry):
        rc = pl.ds(pl.multiple_of(i * 16, 16), 16)
        g_conv = jnp.dot(part_ref[rc, :].astype(jnp.bfloat16), x_proj_ref[...], preferred_element_type=jnp.float32)
        g_conv = g_conv + skip * g_ref[i] + gscan_ref[i]
        pre = pre_ref[i]
        sig = 1.0 / (1.0 + jnp.exp(-pre))
        gpre = g_conv * sig * (1.0 + pre * (1.0 - sig))
        gpre_ref[rc, :] = gpre
        return carry

    pre_body(0, 0)
    edge_ref[...] = gpre_ref[0:8, :]
    edge_copy = pltpu.make_async_remote_copy(
        src_ref=edge_ref, dst_ref=gpre_ref.at[pl.ds(rows, 8)], send_sem=edge_send.at[0], recv_sem=edge_recv.at[0],
        device_id={"seq": before}, device_id_type=MESH,
    )
    edge_copy.start()
    lax.fori_loop(1, chunks, pre_body, 0)
    flipped = jnp.transpose(part_ref[...]).astype(jnp.bfloat16)
    xpt_ref[...] = jnp.dot(flipped, conv_ref[...].reshape(rows, chans), preferred_element_type=jnp.float32)
    relay(*late[2])
    edge_copy.wait_recv()

    def taps_body(block, carry):
        cut = pl.ds(pl.multiple_of(block * 128, 128), 128)
        gpre = gpre_ref[0:rows, cut]
        cbias_ref[:, cut] = jnp.sum(gpre, axis=0, keepdims=True)
        total = jnp.zeros((rows, 128), jnp.float32)
        for k in range(4):
            lag = 3 - k
            total = total + gpre_ref[lag : lag + rows, cut] * taps_ref[k : k + 1, cut] * same_ref[4 + lag].astype(jnp.float32)
            cw_ref[k : k + 1, cut] = jnp.sum(
                gpre * ext_ref[5 + k : 5 + k + rows, cut] * same_ref[k].astype(jnp.float32), axis=0, keepdims=True
            )
        gx_ref[:, cut] = total.astype(jnp.bfloat16)
        return carry

    lax.fori_loop(0, chans // 128, taps_body, 0)
    dwo_ref[...] = jnp.zeros_like(dwo_ref)
    dwz_ref[...] = jnp.zeros_like(dwz_ref)

    def products(kind, k):
        if k == 0:
            blocks = [gz_ref[kind, way * half : (way + 1) * half] for way in (0, 1)]
        else:
            blocks = [ring_ref[kind, way, k - 1] for way in (0, 1)]
        add_products(dwz_ref if kind else dwo_ref, 1 - kind, k, cols_ref, blocks, modes_ref, ring, place, count)

    ready = [(kind, 0) for kind in (0, 1)] + early + late[:3]
    for turn in late[3:]:
        relay(*turn)
        ready.append(turn)
        products(*ready.pop(0))
        if len(ready) > 1:
            products(*ready.pop(0))
    for turn in ready:
        products(*turn)

    for kind in (0, 1):
        for way in (0, 1):
            for k in range(count - 1):
                ring_copy(kind, way, k).wait_send()
    for copy in ch_copies:
        copy.wait_send()
    edge_copy.wait_send()


def back(gz, dtd, step, conv, g, c_wide, b_own, rate, lam0, h0, hist, sig, pre, ext, same, low_t, dt_proj, x_proj_t, skip, taps, cols, modes):
    count, twins = lax.axis_size("seq"), lax.axis_size("ch")
    rows, chans = dtd.shape
    n = rate.shape[0]
    chunks = rows // 16
    slab = cols.shape[3]
    vmem = pl.BlockSpec(memory_space=pltpu.VMEM)
    hbm = pl.BlockSpec(memory_space=pl.ANY)
    cube = lambda a: a.reshape((chunks, a.shape[0] // chunks) + a.shape[1:])
    f32, b16 = jnp.float32, jnp.bfloat16
    shape = jax.ShapeDtypeStruct
    operands = [gz, cube(dtd), cube(step), cube(conv), cube(g), c_wide, cube(b_own), rate, lam0, h0, cube(hist),
                cube(sig), cube(pre), ext, same, low_t, dt_proj, x_proj_t, skip, taps, cols, modes]
    return pl.pallas_call(
        functools.partial(back_kernel, (count, twins)),
        in_specs=[hbm if i == 10 else vmem for i in range(len(operands))],
        out_specs=[vmem] * 9,
        out_shape=[
            shape((3, slab, chans), f32), shape((3, slab, chans), f32), shape((rows, chans), b16), shape((n, chans), f32),
            shape((1, chans), f32), shape((128, chans), f32), shape((256, chans), f32), shape((1, chans), f32),
            shape((4, chans), f32),
        ],
        scratch_shapes=[
            pltpu.VMEM((2, 2, count - 1, rows // 2, chans), b16),
            pltpu.VMEM((chunks, 16 * n, chans), b16),
            pltpu.VMEM((16 * n, chans), b16),
            pltpu.VMEM((16 * n, chans), b16),
            pltpu.VMEM((n, chans), f32),
            pltpu.VMEM((chunks, 16, chans), f32),
            pltpu.VMEM((chunks, 16, chans), f32),
            pltpu.VMEM((rows, 256), f32),
            pltpu.VMEM((rows, 256), b16),
            pltpu.VMEM((twins - 1, rows, 256), b16),
            pltpu.VMEM((rows + 8, chans), f32),
            pltpu.VMEM((8, chans), f32),
            pltpu.SemaphoreType.DMA((rows // 32,)),
            pltpu.SemaphoreType.DMA((2, 2, count - 1)),
            pltpu.SemaphoreType.DMA((2, 2, count - 1)),
            pltpu.SemaphoreType.DMA((twins - 1,)),
            pltpu.SemaphoreType.DMA((twins - 1,)),
            pltpu.SemaphoreType.DMA((1,)),
            pltpu.SemaphoreType.DMA((1,)),
        ],
        compiler_params=pltpu.CompilerParams(collective_id=2, has_side_effects=True, vmem_limit_bytes=60 << 20),
        name="back",
    )(*operands)


def tail_kernel(
    sizes, gx_ref, gz_ref, x_ref, gain_ref, mask_ref, cols_ref, modes_ref, dwz_ref, pick_ref, w_in_ref, w_out_ref,
    dw_ref, slice_ref, dots_ref, mix_ref,
    ring_ref, acc_ref, in_buf, out_buf, norm_sent, norm_got, mix_sent, mix_got, dots_sent, dots_got, weave_ref,
    in_sem, out_sem, ring_send, ring_recv, norm_send, norm_recv, mix_send, mix_recv, dots_send, dots_recv, weave_sem,
):
    count, twins = sizes
    rows, chans = gx_ref.shape
    modes = mask_ref.shape[0]
    half = rows // 2
    quarter = half // 2
    width = x_ref.shape[1]
    part = width // twins
    eighths = chans // 128
    ring, place, onward, backward = ring_places(count)
    mine = lax.axis_index("ch")

    barrier = pltpu.get_barrier_semaphore()
    for peer in (onward, backward):
        pl.semaphore_signal(barrier, inc=1, device_id={"seq": peer}, device_id_type=MESH)
    for k in range(1, twins):
        pl.semaphore_signal(barrier, inc=1, device_id={"ch": lax.rem(mine + k, twins)}, device_id_type=MESH)

    steps = twins * modes

    def chunk_of(step):
        return lax.rem(mine + 1 + step // modes, twins)

    def in_copy(step, b):
        slot = lax.rem(step, 2)
        features = pl.ds(pl.multiple_of(chunk_of(step) * part, part), part)
        return pltpu.make_async_copy(
            w_in_ref.at[lax.rem(step, modes), features, b], in_buf.at[slot, b], in_sem.at[slot, b]
        )

    def out_copy(step):
        slot = lax.rem(step, 2)
        features = pl.ds(pl.multiple_of(chunk_of(step) * part, part), part)
        return pltpu.make_async_copy(w_out_ref.at[lax.rem(step, modes), features], out_buf.at[slot], out_sem.at[slot])

    for b in range(eighths):
        in_copy(0, b).start()
    out_copy(0).start()
    pl.semaphore_wait(barrier, 2 + twins - 1)

    def ring_copy(way, piece, k):
        if k == 0:
            source = gx_ref.at[pl.ds(way * half + piece * quarter, quarter)]
        else:
            source = ring_ref.at[way, k - 1, pl.ds(piece * quarter, quarter)]
        return pltpu.make_async_remote_copy(
            src_ref=source, dst_ref=ring_ref.at[way, k, pl.ds(piece * quarter, quarter)],
            send_sem=ring_send.at[way, piece, k], recv_sem=ring_recv.at[way, piece, k],
            device_id={"seq": backward if way else onward}, device_id_type=MESH,
        )

    def relay(k):
        for piece in (0, 1):
            for way in (0, 1):
                ring_copy(way, piece, k - 1).wait_recv()
                if k < count - 1:
                    ring_copy(way, piece, k).start()

    for piece in (0, 1):
        for way in (0, 1):
            ring_copy(way, piece, 0).start()

    def peer_copy(kind, j):
        sent, got, send, recv = (
            (norm_sent, norm_got, norm_send, norm_recv) if kind == 0 else (mix_sent, mix_got, mix_send, mix_recv)
        )
        return pltpu.make_async_remote_copy(
            src_ref=sent.at[j], dst_ref=got.at[j], send_sem=send.at[j], recv_sem=recv.at[j],
            device_id={"ch": lax.rem(mine + 1 + j, twins)}, device_id_type=MESH,
        )

    nt = (((1,), (1,)), ((), ()))
    pick = pick_ref[...]
    dots_ref[...] = jnp.zeros_like(dots_ref)
    for j in range(twins):
        lanes = pl.ds(pl.multiple_of(lax.rem(mine + 1 + j, twins) * part, part), part)
        for m in range(modes):
            step = j * modes + m
            slot = step % 2
            if step + 1 < steps:
                for b in range(eighths):
                    in_copy(step + 1, b).start()
            for b in range(eighths):
                in_copy(step, b).wait()
            mask = mask_ref[m] > 0
            for q in range(2 * part // 256):
                weights = jnp.concatenate(
                    [in_buf.at[slot, b].reshape(2 * part, 128)[q * 256 : (q + 1) * 256] for b in range(eighths)], axis=1
                )
                both = []
                for i, source in enumerate((gx_ref[...], gz_ref[1])):
                    found = lax.dot_general(source, weights, nt, preferred_element_type=jnp.float32)
                    both.append(jnp.dot(found.astype(jnp.bfloat16), pick[i], preferred_element_type=jnp.float32))
                found = both[0] + both[1]
                target = pl.ds(q * 128, 128)
                slice_ref[:, target] = jnp.where(mask, found, slice_ref[:, target]) if m else found
        for q in range(part // 128):
            cut = pl.ds(pl.multiple_of(lax.rem(mine + 1 + j, twins) * part + q * 128, 128), 128)
            dots_ref[...] += slice_ref[:, q * 128 : (q + 1) * 128] * x_ref[:, cut].astype(jnp.float32) * gain_ref[:, cut]
        if j < twins - 1:
            norm_sent[j] = slice_ref[...].astype(jnp.bfloat16)
            peer_copy(0, j).start()
        for m in range(modes):
            step = j * modes + m
            slot = step % 2
            if step + 1 < steps:
                out_copy(step + 1).start()
            out_copy(step).wait()
            mask = jnp.concatenate([mask_ref[m]] * (part // 128), axis=1) > 0
            found = lax.dot_general(gz_ref[0], out_buf[slot], nt, preferred_element_type=jnp.float32)
            mix_ref[...] = jnp.where(mask, found, mix_ref[...]) if m else found
        if j < twins - 1:
            mix_sent[j] = mix_ref[...].astype(jnp.bfloat16)
            peer_copy(1, j).start()
        if j < 3:
            relay(j + 1)
    dots_sent[...] = dots_ref[...].astype(jnp.bfloat16)
    dots_copies = [
        pltpu.make_async_remote_copy(
            src_ref=dots_sent, dst_ref=dots_got.at[k - 1], send_sem=dots_send.at[k - 1], recv_sem=dots_recv.at[k - 1],
            device_id={"ch": lax.rem(mine + k, twins)}, device_id_type=MESH,
        )
        for k in range(1, twins)
    ]
    for copy in dots_copies:
        copy.start()

    acc_ref[...] = jnp.zeros_like(acc_ref)

    def products(k):
        if k == 0:
            blocks = [gx_ref[way * half : (way + 1) * half] for way in (0, 1)]
        else:
            blocks = [ring_ref[way, k - 1] for way in (0, 1)]
        add_products(acc_ref, 0, k, cols_ref, blocks, modes_ref, ring, place, count)

    for k in range(min(3, twins) + 1):
        products(k)
    for j in range(twins - 1):
        for kind, target, got in ((0, slice_ref, norm_got), (1, mix_ref, mix_got)):
            peer_copy(kind, j).wait_recv()
            target[...] += got[j].astype(jnp.float32)
    for k, copy in enumerate(dots_copies):
        copy.wait_recv()
        dots_ref[...] += dots_got[k].astype(jnp.float32)
    for k in range(min(3, twins) + 1, count):
        relay(k)
        products(k)

    slab = acc_ref.shape[1]

    def weave_copy(m, b):
        slot = (m * eighths + b) % 4
        return pltpu.make_async_copy(weave_ref.at[slot], dw_ref.at[m, :, b], weave_sem.at[slot])

    for m in range(modes):
        for b in range(eighths):
            slot = (m * eighths + b) % 4
            if m * eighths + b >= 4:
                weave_copy(m, b).wait()
            flat = weave_ref.at[slot].reshape(2 * slab, 128)
            flat[pl.ds(0, slab, stride=2), :] = acc_ref[m, :, b * 128 : (b + 1) * 128]
            flat[pl.ds(1, slab, stride=2), :] = dwz_ref[m, :, b * 128 : (b + 1) * 128]
            weave_copy(m, b).start()
    for i in range(4):
        weave_copy(modes - 1, eighths - 4 + i).wait()
    for way in (0, 1):
        for piece in (0, 1):
            for k in range(count - 1):
                ring_copy(way, piece, k).wait_send()
    for j in range(twins - 1):
        for kind in (0, 1):
            peer_copy(kind, j).wait_send()
    for copy in dots_copies:
        copy.wait_send()


def tail(gx, gz, x_in, gain, masks, cols, modes, dwz, w_in, w_out):
    count, twins = lax.axis_size("seq"), lax.axis_size("ch")
    rows, chans = gx.shape
    width = x_in.shape[1]
    part = width // twins
    slab = dwz.shape[1]
    kinds = w_in.shape[0]
    blocks = w_in.reshape(kinds, width, 2, chans // 128, 128).transpose(0, 1, 3, 2, 4)
    order = jnp.arange(256)
    pick = jnp.stack([order[:, None] == 2 * jnp.arange(128)[None] + j for j in (0, 1)]).astype(jnp.bfloat16)
    vmem = pl.BlockSpec(memory_space=pltpu.VMEM)
    hbm = pl.BlockSpec(memory_space=pl.ANY)
    f32, b16 = jnp.float32, jnp.bfloat16
    shape = jax.ShapeDtypeStruct
    dma = pltpu.SemaphoreType.DMA
    dw, total, dots, mix = pl.pallas_call(
        functools.partial(tail_kernel, (count, twins)),
        in_specs=[vmem] * 9 + [hbm] * 2,
        out_specs=[hbm, vmem, vmem, vmem],
        out_shape=[
            shape((kinds, slab, chans // 128, 2, 128), f32), shape((rows, part), f32), shape((rows, 128), f32),
            shape((rows, part), f32),
        ],
        scratch_shapes=[
            pltpu.VMEM((2, count - 1, rows // 2, chans), b16),
            pltpu.VMEM((kinds, slab, chans), f32),
            pltpu.VMEM((2, chans // 128, part, 2, 128), b16),
            pltpu.VMEM((2, part, chans), b16),
            pltpu.VMEM((twins - 1, rows, part), b16),
            pltpu.VMEM((twins - 1, rows, part), b16),
            pltpu.VMEM((twins - 1, rows, part), b16),
            pltpu.VMEM((twins - 1, rows, part), b16),
            pltpu.VMEM((rows, 128), b16),
            pltpu.VMEM((twins - 1, rows, 128), b16),
            pltpu.VMEM((4, slab, 2, 128), f32),
            dma((2, chans // 128)), dma((2,)), dma((2, 2, count - 1)), dma((2, 2, count - 1)),
            dma((twins - 1,)), dma((twins - 1,)), dma((twins - 1,)), dma((twins - 1,)),
            dma((twins - 1,)), dma((twins - 1,)), dma((4,)),
        ],
        compiler_params=pltpu.CompilerParams(collective_id=3, has_side_effects=True, vmem_limit_bytes=60 << 20),
        name="tail",
    )(gx, gz, x_in, gain.reshape(1, -1), masks, cols, modes, dwz, pick, blocks, w_out)
    dw = dw.transpose(0, 1, 3, 2, 4).reshape(kinds, slab, 2, chans)
    return dw, total, dots, mix


def shards(
    x_in,
    norm_gain,
    w_in,
    conv_weight,
    conv_bias,
    x_proj,
    dt_proj,
    dt_bias,
    a_log,
    d_skip,
    w_out,
    modes,
    doc_lengths,
    cotangent,
):
    tok_rows, model_width = x_in.shape
    mode_count = w_in.shape[0]
    inner_local = conv_bias.shape[0]
    state_size = a_log.shape[0]
    rank_size = dt_proj.shape[0]
    conv_taps = conv_weight.shape[0]
    ch_count = lax.axis_size("ch")
    feat_part = model_width // ch_count
    seq_index = lax.axis_index("seq")
    ch_index = lax.axis_index("ch")
    first_pos = seq_index * tok_rows
    positions = first_pos + jnp.arange(tok_rows, dtype=jnp.int32)
    my_modes = lax.dynamic_slice_in_dim(modes, first_pos, tok_rows)
    onehot = (my_modes[:, None] == jnp.arange(mode_count, dtype=jnp.int32)[None]).astype(
        jnp.bfloat16
    )
    doc_index, begins = doc_tables(doc_lengths, positions)
    keep_mask = 1.0 - begins.astype(jnp.float32)
    x_full = x_in.astype(jnp.float32)
    scale = lax.rsqrt(jnp.mean(x_full * x_full, axis=1, keepdims=True) + EPSILON)
    normed = (x_full * scale * norm_gain[None]).astype(jnp.bfloat16)
    spread = jnp.eye(256, dtype=jnp.bfloat16)
    spread = jnp.stack([spread, jnp.zeros_like(spread)], axis=2)
    spread = jnp.stack([spread, spread[:, :, ::-1]], axis=0).reshape(2, 256, 512)
    doubled = jnp.einsum("tbd,jdk->jtbk", normed.reshape(tok_rows, -1, 256), spread)
    doubled = doubled.reshape(2, tok_rows, 2 * model_width)
    masks = jnp.broadcast_to(onehot.T[:, :, None], (mode_count, tok_rows, 128))
    x_branch, z_branch, d_gated, cols = front(doubled, normed, masks, cotangent, w_in, w_out)
    z_branch = z_branch.astype(jnp.float32)
    rim_rows = from_behind(x_branch[tok_rows - (conv_taps - 1) :], "seq", 1)
    extended = jnp.concatenate([rim_rows, x_branch], axis=0).astype(jnp.float32)
    ext_doc, _ = doc_tables(
        doc_lengths,
        first_pos - (conv_taps - 1) + jnp.arange(tok_rows + conv_taps - 1, dtype=jnp.int32),
    )
    conv_pre = jnp.zeros((tok_rows, inner_local), jnp.float32) + conv_bias[None]
    same_list = []
    for offset in range(conv_taps):
        same_doc = (ext_doc[offset : offset + tok_rows] == doc_index).astype(jnp.float32)[:, None]
        same_list.append(same_doc)
        conv_pre = (
            conv_pre + conv_weight[offset][None] * extended[offset : offset + tok_rows] * same_doc
        )
    conv_out = jax.nn.silu(conv_pre).astype(jnp.bfloat16)
    conv_float = conv_out.astype(jnp.float32)
    projected = sum_over(jnp.dot(conv_out, x_proj, preferred_element_type=jnp.float32), "ch")
    dt_low = projected[:, :rank_size].astype(jnp.bfloat16)
    b_in = projected[:, rank_size : rank_size + state_size]
    c_out = projected[:, rank_size + state_size :]
    dt_raw = jnp.dot(dt_low, dt_proj, preferred_element_type=jnp.float32)
    step_size = jax.nn.softplus(dt_raw + dt_bias[None])
    decay_rate = -jnp.exp(a_log)
    seq_count = lax.axis_size("seq")
    rate_two = decay_rate * math.log2(math.e)
    masked_step = jnp.where(begins[:, None], 1e30, step_size)
    drive = step_size * conv_float
    wide = (tok_rows, state_size, 128)
    b_wide = jnp.broadcast_to(b_in[:, :, None], wide)
    c_wide = jnp.broadcast_to(c_out[:, :, None], wide)
    gate_act = jax.nn.silu(z_branch)
    d_ssm = d_gated * gate_act
    ends = scan_ends(masked_step, drive, d_ssm, b_wide, c_wide, rate_two)
    steps = jnp.sum(masked_step, axis=0)
    ends_in, steps_in = exchange_states(ends, steps.reshape(8, -1))
    steps_in = steps_in.reshape(seq_count - 1, inner_local)
    incoming = jnp.zeros((state_size, inner_local), jnp.float32)
    pending = incoming
    gap = jnp.zeros((inner_local,), jnp.float32)
    for distance in range(1, seq_count):
        part = ends_in[distance - 1].astype(jnp.float32) * jnp.exp2(rate_two * gap[None])
        incoming = incoming + jnp.where(distance <= seq_index, part, 0.0)
        gap = gap + steps_in[distance - 1]
    gap = jnp.zeros((inner_local,), jnp.float32)
    for distance in range(1, seq_count):
        slot = seq_count - 1 - distance
        part = ends_in[slot].astype(jnp.float32) * jnp.exp2(rate_two * gap[None])
        pending = pending + jnp.where(distance + seq_index < seq_count, part, 0.0)
        gap = gap + steps_in[slot]
    ssm, history = scan_forward(
        masked_step, drive, b_wide, own_columns(c_out), rate_two, incoming
    )
    ssm = ssm + d_skip[None] * conv_float
    gated = (ssm * gate_act).astype(jnp.bfloat16)
    gate_sig = jax.nn.sigmoid(z_branch)
    d_z = d_gated * ssm * gate_sig * (1.0 + z_branch * (1.0 - gate_sig))
    both = jnp.stack([gated, d_z.astype(jnp.bfloat16)])
    d_skip_local = jnp.sum(d_ssm * conv_float, axis=0)
    wide = lambda a: jnp.broadcast_to(a, (tok_rows, 128)).astype(jnp.bfloat16)
    post_doc, _ = doc_tables(
        doc_lengths, first_pos + jnp.arange(tok_rows + conv_taps - 1, dtype=jnp.int32)
    )
    later = [
        (post_doc[lag : lag + tok_rows] == doc_index).astype(jnp.float32)[:, None]
        for lag in range(conv_taps)
    ]
    same = jnp.stack([wide(a) for a in same_list + later])
    columns = jnp.swapaxes(cols, 3, 4)
    mode_rows = modes.reshape(2 * seq_count, tok_rows // 2)
    (
        d_w_out, d_w_z, d_x_branch, rate_grad, d_bias_local, d_dt_proj_local, d_x_proj_t, d_conv_bias_local,
        d_conv_weight_local,
    ) = back(
        both, masked_step, step_size, conv_out, d_ssm, c_wide, own_columns(b_in), rate_two, pending, incoming, history,
        jax.nn.sigmoid(dt_raw + dt_bias[None]), conv_pre, jnp.pad(extended, ((5, 0), (0, 0))), same, dt_low.T, dt_proj,
        jnp.pad(x_proj.T, ((0, 256 - x_proj.shape[1]), (0, 0))), d_skip[None], conv_weight, columns, mode_rows,
    )
    d_a_log = rate_grad * decay_rate
    d_x_proj_local = d_x_proj_t[: x_proj.shape[1]]
    d_w_in, d_slice, dots, mixer = tail(
        d_x_branch, both, x_in, norm_gain, masks, columns, mode_rows, d_w_z, w_in, w_out
    )
    x_slice = lax.dynamic_slice_in_dim(x_full, ch_index * feat_part, feat_part, 1)
    block_out = (x_slice + mixer).astype(jnp.bfloat16)
    gain_slice = lax.dynamic_slice_in_dim(norm_gain, ch_index * feat_part, feat_part, 0)
    mean_term = (jnp.sum(dots, axis=1) / model_width)[:, None]
    weighted_slice = d_slice * gain_slice[None]
    d_x_in = cotangent.astype(jnp.float32) + scale * weighted_slice - x_slice * scale**3 * mean_term
    d_gain = lax.psum(jnp.sum(d_slice * x_slice * scale, axis=0), "seq")
    small_sums = lax.psum(
        (
            d_conv_weight_local,
            d_conv_bias_local[0],
            d_x_proj_local,
            d_dt_proj_local,
            d_bias_local[0],
            d_a_log,
            d_skip_local,
        ),
        "seq",
    )
    return (
        block_out,
        d_x_in,
        d_gain,
        d_w_in,
        small_sums[0],
        small_sums[1],
        small_sums[2].T,
        small_sums[3],
        small_sums[4],
        small_sums[5],
        small_sums[6],
        d_w_out,
    )


def solution(mesh):
    return jax.shard_map(
        shards,
        mesh=mesh,
        in_specs=(
            P("seq", None),
            P(),
            P(None, None, None, "ch"),
            P(None, "ch"),
            P("ch"),
            P("ch", None),
            P(None, "ch"),
            P("ch"),
            P(None, "ch"),
            P("ch"),
            P(None, None, "ch"),
            P(),
            P(),
            P("seq", "ch"),
        ),
        out_specs=(
            P("seq", "ch"),
            P("seq", "ch"),
            P("ch"),
            P(None, "seq", None, "ch"),
            P(None, "ch"),
            P("ch"),
            P("ch", None),
            P(None, "ch"),
            P("ch"),
            P(None, "ch"),
            P("ch"),
            P(None, "seq", "ch"),
        ),
        check_vma=False,
    )
```

```python
import functools
import math

import jax
import jax.numpy as jnp
from jax import lax
from jax.experimental import pallas as pl
from jax.experimental.pallas import tpu as pltpu
from jax.sharding import PartitionSpec as P

EPSILON = 1e-05


def from_behind(block, axis, distance):
    devices = range(lax.axis_size(axis))
    route = [(i - distance, i) for i in devices if i - distance in devices]
    return lax.ppermute(block, axis, route)


MESH = pl.DeviceIdType.MESH


def sum_over(part, axis):
    count = lax.axis_size(axis)
    sent = part.astype(jnp.bfloat16)
    total = part
    for distance in range(1, count):
        route = [(i, (i + distance) % count) for i in range(count)]
        total = total + lax.ppermute(sent, axis, route).astype(jnp.float32)
    return total


def cycle_of(count):
    across = count // 4
    walk = [(0, x) for x in range(across)]
    for turn, x in enumerate(reversed(range(across))):
        column = [(z, x) for z in range(1, 4)]
        walk += column[::-1] if turn % 2 else column
    return [z * across + x for z, x in walk]


def states_kernel(count, ends_ref, steps_ref, ends_out, steps_out, send, recv):
    me = lax.axis_index("seq")
    barrier = pltpu.get_barrier_semaphore()
    for distance in range(1, count):
        peer = {"seq": lax.rem(me + distance, count)}
        pl.semaphore_signal(barrier, inc=1, device_id=peer, device_id_type=MESH)
    pl.semaphore_wait(barrier, count - 1)
    copies = []
    for distance in range(1, count):
        peer = lax.rem(me + distance, count)
        side = jnp.where(peer > me, 0, 1)
        for kind, (source, target) in enumerate(
            ((ends_ref.at[side], ends_out), (steps_ref, steps_out))
        ):
            copies.append(
                pltpu.make_async_remote_copy(
                    src_ref=source,
                    dst_ref=target.at[distance - 1],
                    send_sem=send.at[kind, distance - 1],
                    recv_sem=recv.at[kind, distance - 1],
                    device_id={"seq": peer},
                    device_id_type=MESH,
                )
            )
    for copy in copies:
        copy.start()
    for copy in copies:
        copy.wait()


def exchange_states(ends, steps):
    others = lax.axis_size("seq") - 1
    vmem = pl.BlockSpec(memory_space=pltpu.VMEM)
    return pl.pallas_call(
        functools.partial(states_kernel, others + 1),
        in_specs=[vmem, vmem],
        out_specs=[vmem, vmem],
        out_shape=[
            jax.ShapeDtypeStruct((others,) + ends.shape[1:], ends.dtype),
            jax.ShapeDtypeStruct((others,) + steps.shape, steps.dtype),
        ],
        scratch_shapes=[
            pltpu.SemaphoreType.DMA((2, others)),
            pltpu.SemaphoreType.DMA((2, others)),
        ],
        compiler_params=pltpu.CompilerParams(
            collective_id=0, has_side_effects=True, vmem_limit_bytes=32 << 20
        ),
        name="exchange_states",
    )(ends, steps)


def table_of(index, values):
    picked = jnp.int32(values[0])
    for i in range(1, len(values)):
        picked = jnp.where(index == i, jnp.int32(values[i]), picked)
    return picked


def front_kernel(
    sizes, x2_ref, normed_ref, mask_ref, cot_ref, w_in_ref, w_out_ref,
    x_ref, z_ref, gated_ref, cols_ref,
    cotg_ref, in_buf, out_buf, in_sem, out_sem, cot_send, cot_recv, seq_send, seq_recv, twin_send, twin_recv, own_sem,
):
    count, twins = sizes
    rows, width = normed_ref.shape
    modes = mask_ref.shape[0]
    half = rows // 2
    slab = width // count
    part = cot_ref.shape[1]
    inner = x_ref.shape[1]
    ring = cycle_of(count)
    me = lax.axis_index("seq")
    mine = lax.axis_index("ch")
    side = lax.rem(mine, 2)
    twin = mine + 1 - 2 * side
    where = {s: i for i, s in enumerate(ring)}
    place = table_of(me, [where[s] for s in range(count)])

    barrier = pltpu.get_barrier_semaphore()
    for k in range(1, count):
        peer = {"seq": lax.rem(me + k, count)}
        pl.semaphore_signal(barrier, inc=1, device_id=peer, device_id_type=MESH)
    for k in range(1, twins):
        peer = {"ch": lax.rem(mine + k, twins)}
        pl.semaphore_signal(barrier, inc=1, device_id=peer, device_id_type=MESH)

    pairs = inner // 256
    steps = pairs * modes

    def in_copy(step, b):
        slot = lax.rem(step, 2)
        return pltpu.make_async_copy(
            w_in_ref.at[lax.rem(step, modes), :, step // modes * 2 + b], in_buf.at[slot, b], in_sem.at[slot, b]
        )

    wide = out_buf.shape[2]
    out_steps = inner // wide * modes

    def out_copy(step):
        slot = lax.rem(step, 2)
        columns = pl.ds(pl.multiple_of(step // modes * wide, wide), wide)
        return pltpu.make_async_copy(
            w_out_ref.at[lax.rem(step, modes), :, columns], out_buf.at[slot], out_sem.at[slot]
        )

    for b in (0, 1):
        in_copy(0, b).start()
    out_copy(0).start()
    pl.semaphore_wait(barrier, count - 1 + twins - 1)

    cot_copies = [
        pltpu.make_async_remote_copy(
            src_ref=cot_ref, dst_ref=cotg_ref.at[mine], send_sem=cot_send.at[k - 1], recv_sem=cot_recv.at[k - 1],
            device_id={"ch": lax.rem(mine + k, twins)}, device_id_type=MESH,
        )
        for k in range(1, twins)
    ]
    for copy in cot_copies:
        copy.start()
    side_rows = pl.ds(pl.multiple_of(side * half, half), half)

    def seq_copies(kind):
        copies = []
        for k in range(1, count):
            step = jnp.where(side == 0, k, count - k)
            peer = table_of(lax.rem(place + step, count), ring)
            if kind == 0:
                source = normed_ref.at[side_rows, pl.ds(pl.multiple_of(peer * slab, slab), slab)]
            else:
                start = lax.rem(peer * slab, part)
                source = cotg_ref.at[peer * slab // part, side_rows, pl.ds(pl.multiple_of(start, slab), slab)]
            copies.append(
                pltpu.make_async_remote_copy(
                    src_ref=source, dst_ref=cols_ref.at[kind, side, k], send_sem=seq_send.at[kind, k - 1],
                    recv_sem=seq_recv.at[kind, k - 1], device_id={"seq": peer}, device_id_type=MESH,
                )
            )
        return copies

    def twin_copy(kind):
        return pltpu.make_async_remote_copy(
            src_ref=cols_ref.at[kind, side, pl.ds(1, count - 1)], dst_ref=cols_ref.at[kind, side, pl.ds(1, count - 1)],
            send_sem=twin_send.at[kind], recv_sem=twin_recv.at[kind],
            device_id={"ch": twin}, device_id_type=MESH,
        )

    normed_copies = seq_copies(0)
    for copy in normed_copies:
        copy.start()
    own_copy = pltpu.make_async_copy(cot_ref, cotg_ref.at[mine], own_sem.at[0])
    own_copy.start()
    own_start = pl.multiple_of(me * slab, slab)
    for way in (0, 1):
        cols_ref[0, way, 0] = normed_ref[way * half : (way + 1) * half, pl.ds(own_start, slab)]

    def in_step(step, carry):
        slot = lax.rem(step, 2)
        mode = lax.rem(step, modes)

        @pl.when(step + 1 < steps)
        def _():
            for b in (0, 1):
                in_copy(step + 1, b).start()

        for b in (0, 1):
            in_copy(step, b).wait()
        weights = jnp.concatenate([in_buf.at[slot, b].reshape(2 * width, 128)[...] for b in (0, 1)], axis=1)
        mask = jnp.concatenate([mask_ref[mode]] * 2, axis=1) > 0
        columns = pl.ds(pl.multiple_of(step // modes * 256, 256), 256)
        for j, target in enumerate((x_ref, z_ref)):
            found = jnp.dot(x2_ref[j], weights, preferred_element_type=jnp.float32).astype(jnp.bfloat16)
            target[:, columns] = jnp.where(mask, found, target[:, columns])
        return carry

    x_ref[...] = jnp.zeros_like(x_ref)
    z_ref[...] = jnp.zeros_like(z_ref)
    first = steps // 2
    lax.fori_loop(0, first, in_step, 0)
    own_copy.wait()
    for copy in cot_copies:
        copy.wait_recv()
    tail_copies = seq_copies(1)
    for copy in tail_copies:
        copy.start()
    own_slab = cotg_ref.at[me * slab // part]
    for way in (0, 1):
        cols_ref[1, way, 0] = own_slab[way * half : (way + 1) * half, pl.ds(pl.multiple_of(lax.rem(me * slab, part), slab), slab)]
    for copy in normed_copies:
        copy.wait_recv()
    twin_copy(0).start()
    lax.fori_loop(first, steps, in_step, 0)

    def out_step(step, carry):
        slot = lax.rem(step, 2)
        mode = lax.rem(step, modes)

        @pl.when(step + 1 < out_steps)
        def _():
            out_copy(step + 1).start()

        out_copy(step).wait()
        mask = jnp.concatenate([mask_ref[mode]] * (wide // 128), axis=1) > 0
        columns = pl.ds(pl.multiple_of(step // modes * wide, wide), wide)
        found = jnp.zeros((rows, wide), jnp.float32)
        for c in range(twins):
            found = found + jnp.dot(
                cotg_ref[c], out_buf[slot, c * part : (c + 1) * part], preferred_element_type=jnp.float32
            )
        gated_ref[:, columns] = jnp.where(mask, found, gated_ref[:, columns])
        return carry

    gated_ref[...] = jnp.zeros_like(gated_ref)
    lax.fori_loop(0, out_steps, out_step, 0)
    for copy in tail_copies:
        copy.wait_recv()
    twin_copy(1).start()
    for kind in (0, 1):
        twin_copy(kind).wait_recv()
        twin_copy(kind).wait_send()
    for copy in cot_copies + normed_copies + tail_copies:
        copy.wait_send()


def front(x2, normed, masks, cot, w_in, w_out):
    count, twins = lax.axis_size("seq"), lax.axis_size("ch")
    rows, width = normed.shape
    inner = w_out.shape[2]
    modes = w_out.shape[0]
    blocks = w_in.reshape(modes, width, 2, inner // 128, 128).transpose(0, 1, 3, 2, 4)
    vmem = pl.BlockSpec(memory_space=pltpu.VMEM)
    hbm = pl.BlockSpec(memory_space=pl.ANY)
    wide = min(512, inner)
    return pl.pallas_call(
        functools.partial(front_kernel, (count, twins)),
        in_specs=[vmem, vmem, vmem, vmem, hbm, hbm],
        out_specs=[vmem, vmem, vmem, vmem],
        out_shape=[
            jax.ShapeDtypeStruct((rows, inner), jnp.bfloat16),
            jax.ShapeDtypeStruct((rows, inner), jnp.bfloat16),
            jax.ShapeDtypeStruct((rows, inner), jnp.float32),
            jax.ShapeDtypeStruct((2, 2, count, rows // 2, width // count), jnp.bfloat16),
        ],
        scratch_shapes=[
            pltpu.VMEM((twins,) + cot.shape, jnp.bfloat16),
            pltpu.VMEM((2, 2, width, 2, 128), jnp.bfloat16),
            pltpu.VMEM((2, width, wide), jnp.bfloat16),
            pltpu.SemaphoreType.DMA((2, 2)),
            pltpu.SemaphoreType.DMA((2,)),
            pltpu.SemaphoreType.DMA((twins - 1,)),
            pltpu.SemaphoreType.DMA((twins - 1,)),
            pltpu.SemaphoreType.DMA((2, count - 1)),
            pltpu.SemaphoreType.DMA((2, count - 1)),
            pltpu.SemaphoreType.DMA((2,)),
            pltpu.SemaphoreType.DMA((2,)),
            pltpu.SemaphoreType.DMA((1,)),
        ],
        compiler_params=pltpu.CompilerParams(collective_id=1, has_side_effects=True, vmem_limit_bytes=56 << 20),
        name="front",
    )(x2, normed, masks, cot, blocks, w_out)


def doc_tables(doc_lengths, positions):
    count = doc_lengths.shape[0]
    order = jnp.arange(count, dtype=jnp.int32)
    doc_ends = jnp.sum(jnp.where(order[:, None] >= order[None, :], doc_lengths[None, :], 0), axis=1)
    doc_starts = doc_ends - doc_lengths
    doc_index = jnp.sum((positions[:, None] >= doc_ends[None, :]).astype(jnp.int32), axis=1)
    begins = jnp.any(positions[:, None] == doc_starts[None, :], axis=1)
    return (doc_index, begins)


def own_columns(values):
    rows, n = values.shape
    own = jnp.arange(16 * n)[None] // n == jnp.arange(rows)[:, None] % 16
    return jnp.where(own, jnp.tile(values, (1, 16)), 0).astype(jnp.bfloat16)


LB = 512
CH = 32
NS = 16

def tile_lanes(v, lanes):
    return jnp.concatenate([v] * (lanes // 128), axis=1)

def ends_kernel(lb, dtd_ref, u_ref, g_ref, b_ref, c_ref, rate_ref, out_ref, acc_ref):
    n = rate_ref.shape[0]
    rows, chans = dtd_ref.shape
    @pl.when(pl.program_id(0) == 0)
    def _():
        acc_ref[0:n, :] = jnp.zeros((n, chans), jnp.float32)
        acc_ref[n:2*n, :] = jnp.ones((n, chans), jnp.float32)
        acc_ref[2*n:3*n, :] = jnp.zeros((n, chans), jnp.float32)
    for block in range(chans // lb):
        cut = slice(block * lb, (block + 1) * lb)
        rate = rate_ref[:, cut]
        h = acc_ref[0:n, cut]
        reach = acc_ref[n:2*n, cut]
        head = acc_ref[2*n:3*n, cut]
        for t in range(rows):
            decay = jnp.exp2(dtd_ref[t:t+1, cut] * rate)
            h = decay * h + u_ref[t:t+1, cut] * tile_lanes(b_ref[t], lb)
            reach = reach * decay
            head = head + reach * (g_ref[t:t+1, cut] * tile_lanes(c_ref[t], lb))
        acc_ref[0:n, cut] = h
        acc_ref[n:2*n, cut] = reach
        acc_ref[2*n:3*n, cut] = head
    @pl.when(pl.program_id(0) == pl.num_programs(0) - 1)
    def _():
        out_ref[0] = acc_ref[0:n, :].astype(jnp.bfloat16)
        out_ref[1] = acc_ref[2*n:3*n, :].astype(jnp.bfloat16)

def scan_ends(dtd, u, g, b, c, rate, lb=LB, ch=CH):
    t, e = dtd.shape
    n = rate.shape[0]
    row = pl.BlockSpec((ch, e), lambda i: (i, 0))
    wide = pl.BlockSpec((ch, n, 128), lambda i: (i, 0, 0))
    return pl.pallas_call(
        functools.partial(ends_kernel, lb),
        grid=(t // ch,),
        in_specs=[row, row, row, wide, wide, pl.BlockSpec((n, e), lambda i: (0, 0))],
        out_specs=pl.BlockSpec((2, n, e), lambda i: (0, 0, 0)),
        out_shape=jax.ShapeDtypeStruct((2, n, e), jnp.bfloat16),
        scratch_shapes=[pltpu.VMEM((3 * n, e), jnp.float32)],
        compiler_params=pltpu.CompilerParams(vmem_limit_bytes=32 << 20),
        name="scan_ends",
    )(dtd, u, g, b, c, rate)

def forward_kernel(lb, dtd_ref, u_ref, b_ref, cblk_ref, rate_ref, h0_ref, y_ref, hist_ref, state_ref):
    n = rate_ref.shape[0]
    rows, chans = dtd_ref.shape
    @pl.when(pl.program_id(0) == 0)
    def _():
        state_ref[...] = h0_ref[...]
    for block in range(chans // lb):
        cut = slice(block * lb, (block + 1) * lb)
        rate = rate_ref[:, cut]
        h = state_ref[:, cut]
        for t in range(rows):
            decay = jnp.exp2(dtd_ref[t:t+1, cut] * rate)
            h = decay * h + u_ref[t:t+1, cut] * tile_lanes(b_ref[t], lb)
            hist_ref[t * n:(t + 1) * n, cut] = h.astype(jnp.bfloat16)
        state_ref[:, cut] = h
    for k in range(rows // 16):
        y_ref[k*16:(k+1)*16, :] = jnp.dot(cblk_ref[k*16:(k+1)*16, :], hist_ref[k*16*n:(k+1)*16*n, :], preferred_element_type=jnp.float32)

def scan_forward(dtd, u, b, cblk, rate, h0, lb=LB, ch=CH):
    t, e = dtd.shape
    n = rate.shape[0]
    row = pl.BlockSpec((ch, e), lambda i: (i, 0))
    wide = pl.BlockSpec((ch, n, 128), lambda i: (i, 0, 0))
    whole = pl.BlockSpec((n, e), lambda i: (0, 0))
    return pl.pallas_call(
        functools.partial(forward_kernel, lb),
        grid=(t // ch,),
        in_specs=[row, row, wide, pl.BlockSpec((ch, 16 * n), lambda i: (i, 0)), whole, whole],
        out_specs=(row, pl.BlockSpec((ch * n, e), lambda i: (i, 0))),
        out_shape=(jax.ShapeDtypeStruct((t, e), jnp.float32), jax.ShapeDtypeStruct((t * n, e), jnp.bfloat16)),
        scratch_shapes=[pltpu.VMEM((n, e), jnp.float32)],
        compiler_params=pltpu.CompilerParams(vmem_limit_bytes=32 << 20),
        name="scan_forward",
    )(dtd, u, b, cblk, rate, h0)

def ring_places(count):
    ring = cycle_of(count)
    where = {s: i for i, s in enumerate(ring)}
    me = lax.axis_index("seq")
    onward = table_of(me, [ring[(where[s] + 1) % count] for s in range(count)])
    backward = table_of(me, [ring[(where[s] - 1) % count] for s in range(count)])
    place = table_of(me, [where[s] for s in range(count)])
    return ring, place, onward, backward


def add_products(acc_ref, kind, k, cols_ref, blocks, modes_ref, ring, place, count):
    parts = []
    for way in (0, 1):
        step = k if way else count - k
        source = table_of(lax.rem(place + step, count), ring)
        parts.append((cols_ref[kind, way, k], modes_ref[pl.ds(2 * source + way, 1), :]))
    right = jnp.concatenate(blocks, axis=0)
    for m in range(acc_ref.shape[0]):
        left = jnp.concatenate(
            [part * jnp.where(row == m, 1.0, 0.0).astype(jnp.bfloat16) for part, row in parts], axis=1
        )
        acc_ref[m] += jnp.dot(left, right, preferred_element_type=jnp.float32)


def back_kernel(
    sizes, w_in_ref, w_out_ref, gz_ref, dtd_ref, step_ref, conv_ref, g_ref, c_ref, bblk_ref, rate_ref, lam0_ref, h0_ref, hist_hbm,
    sig_ref, pre_ref, ext_ref, same_ref, low_t_ref, dt_proj_ref, x_proj_ref, skip_ref, taps_ref, cols_ref, modes_ref, mask_ref, pick_ref,
    dwo_ref, dwz_ref, gx_ref, zpart_ref, mix_ref, small_ref,
    racc_ref, rows_ref, sum_ref, half_ref, half_got, four_ref, four_b16, four_got, in_buf, out_buf, mix_sent, mix_got,
    ring_ref, hist_ref, lam_ref, w_ref, pend_ref, gstep_ref, gscan_ref, part_ref, sent_ref, got_ref, gpre_ref, edge_ref,
    in_sem, out_sem, mix_send, mix_recv, half_send, half_recv, four_send, four_recv, last_send, last_recv, all_send, all_recv,
    hist_sem, ring_send, ring_recv, ch_send, ch_recv, edge_send, edge_recv,
):
    count, twins = sizes
    chunks, _, chans = dtd_ref.shape
    rows = chunks * 16
    n = rate_ref.shape[0]
    half = rows // 2
    ring, place, onward, backward = ring_places(count)
    me = lax.axis_index("seq")
    mine = lax.axis_index("ch")
    before = lax.rem(me + count - 1, count)
    after = lax.rem(me + 1, count)

    span = 32
    spans = rows // span

    def hist_copy(i):
        part = pl.ds(i * (span // 16), span // 16)
        return pltpu.make_async_copy(hist_hbm.at[part], hist_ref.at[part], hist_sem.at[i])

    modes = mask_ref.shape[0]
    width = w_out_ref.shape[1]
    part = width // twins
    eighths = chans // 128
    across = half_ref.shape[1]
    tall = half_ref.shape[0]
    depth = half_ref.shape[2]
    z_at = me // across
    x_at = lax.rem(me, across)

    def chunk_of(step):
        return pl.ds(pl.multiple_of(lax.rem(mine + 1 + step // modes, twins) * part, part), part)

    def in_copy(step, b):
        slot = step % 2
        return pltpu.make_async_copy(w_in_ref.at[step % modes, chunk_of(step), b], in_buf.at[slot, b], in_sem.at[slot, b])

    def in_copies(step, wait):
        for b in range(eighths):
            if wait:
                in_copy(step, b).wait()
            else:
                in_copy(step, b).start()

    def out_copy(step):
        slot = step % 2
        return pltpu.make_async_copy(w_out_ref.at[step % modes, chunk_of(step)], out_buf.at[slot], out_sem.at[slot])

    barrier = pltpu.get_barrier_semaphore()
    for k in range(1, count):
        pl.semaphore_signal(barrier, inc=1, device_id={"seq": lax.rem(me + k, count)}, device_id_type=MESH)
    for k in range(1, twins):
        peer = {"ch": lax.rem(mine + k, twins)}
        pl.semaphore_signal(barrier, inc=1, device_id=peer, device_id_type=MESH)
    for i in reversed(range(spans)):
        hist_copy(i).start()
    in_copies(0, 0)
    out_copy(0).start()
    pl.semaphore_wait(barrier, count - 1 + twins - 1)

    def ring_copy(kind, way, k):
        if k == 0:
            source = gz_ref.at[kind, pl.ds(way * half, half)]
        else:
            source = ring_ref.at[kind, way, k - 1]
        return pltpu.make_async_remote_copy(
            src_ref=source, dst_ref=ring_ref.at[kind, way, k], send_sem=ring_send.at[kind, way, k],
            recv_sem=ring_recv.at[kind, way, k], device_id={"seq": backward if way else onward}, device_id_type=MESH,
        )

    def relay(kind, k):
        for way in (0, 1):
            ring_copy(kind, way, k - 1).wait_recv()
            if k < count - 1:
                ring_copy(kind, way, k).start()

    for kind in (0, 1):
        for way in (0, 1):
            ring_copy(kind, way, 0).start()
    turns = [(kind, k) for k in range(1, count) for kind in (0, 1)]
    early = turns[:2]
    late = turns[2:]

    pend_ref[...] = lam0_ref[...]
    racc_ref[...] = jnp.zeros_like(racc_ref)
    lb = min(512, chans)
    own = (
        lax.broadcasted_iota(jnp.int32, (16, 16 * n), 1) // n == lax.broadcasted_iota(jnp.int32, (16, 16 * n), 0)
    )
    ones = own.astype(jnp.bfloat16)
    pick_row = lax.broadcasted_iota(jnp.int32, (16 * n, 128), 0)
    pick_col = lax.broadcasted_iota(jnp.int32, (16 * n, 128), 1)
    pick_b = (pick_row % n == pick_col).astype(jnp.bfloat16)
    pick_c = (pick_row % n + n == pick_col).astype(jnp.bfloat16)
    nt = (((1,), (1,)), ((), ()))

    def span_body(i, carry):
        at = spans - 1 - i

        @pl.when(at > 0)
        def _():
            hist_copy(at - 1).wait()

        for sub in reversed(range(span // 16)):
            chunk = at * (span // 16) + sub
            for block in range(chans // lb):
                cut = slice(block * lb, (block + 1) * lb)
                rate = rate_ref[:, cut]
                pend = pend_ref[:, cut]
                racc = racc_ref[:, cut]
                for t in reversed(range(16)):
                    decay = jnp.exp2(dtd_ref[chunk, t : t + 1, cut] * rate)
                    lam = g_ref[chunk, t : t + 1, cut] * tile_lanes(c_ref[chunk * 16 + t], lb) + pend
                    pend = decay * lam
                    if t:
                        prior = hist_ref[chunk, (t - 1) * n : t * n, cut].astype(jnp.float32)
                    else:
                        prior = hist_ref[jnp.maximum(chunk - 1, 0), 15 * n : 16 * n, cut].astype(jnp.float32)
                        prior = jnp.where(chunk == 0, h0_ref[:, cut], prior)
                    w = pend * prior
                    racc = racc + w * step_ref[chunk, t : t + 1, cut]
                    lam_ref[t * n : (t + 1) * n, cut] = lam.astype(jnp.bfloat16)
                    w_ref[t * n : (t + 1) * n, cut] = (w * rate).astype(jnp.bfloat16)
                pend_ref[:, cut] = pend
                racc_ref[:, cut] = racc
            step = step_ref[chunk]
            conv = conv_ref[chunk].astype(jnp.float32)
            adj = jnp.dot(bblk_ref[chunk], lam_ref[...], preferred_element_type=jnp.float32)
            wsum = jnp.dot(ones, w_ref[...], preferred_element_type=jnp.float32)
            gstep_ref[chunk] = wsum * math.log(2.0) + adj * conv
            gscan_ref[chunk] = adj * step
            gb = lax.dot_general((step * conv).astype(jnp.bfloat16), lam_ref[...], nt, preferred_element_type=jnp.float32)
            gc = lax.dot_general(
                g_ref[chunk].astype(jnp.bfloat16), hist_ref[chunk], nt, preferred_element_type=jnp.float32
            )
            gb = jnp.where(own, gb, 0.0).astype(jnp.bfloat16)
            gc = jnp.where(own, gc, 0.0).astype(jnp.bfloat16)
            part_ref[pl.ds(pl.multiple_of(chunk * 16, 16), 16), 128:256] = jnp.dot(
                gb, pick_b, preferred_element_type=jnp.float32
            ) + jnp.dot(gc, pick_c, preferred_element_type=jnp.float32)
        return carry

    hist_copy(spans - 1).wait()
    lax.fori_loop(0, spans // 2, span_body, 0)
    relay(*early[0])
    lax.fori_loop(spans // 2, spans, span_body, 0)
    relay(*early[1])

    rows_ref[...] = jnp.zeros_like(rows_ref)

    def raw_body(i, carry):
        full = gstep_ref[i] * sig_ref[i]
        rows_ref[5:6] += jnp.sum(full, axis=0, keepdims=True)
        rows_ref[6:7] += jnp.sum(g_ref[i] * conv_ref[i].astype(jnp.float32), axis=0, keepdims=True)
        gx_ref[pl.ds(pl.multiple_of(i * 16, 16), 16), :] = full.astype(jnp.bfloat16)
        return carry

    lax.fori_loop(0, chunks, raw_body, 0)
    part_ref[:, 0:128] = lax.dot_general(gx_ref[...], dt_proj_ref[...], nt, preferred_element_type=jnp.float32)
    sent_ref[...] = part_ref[...].astype(jnp.bfloat16)
    ch_copies = [
        pltpu.make_async_remote_copy(
            src_ref=sent_ref, dst_ref=got_ref.at[k - 1], send_sem=ch_send.at[k - 1], recv_sem=ch_recv.at[k - 1],
            device_id={"ch": lax.rem(mine + k, twins)}, device_id_type=MESH,
        )
        for k in range(1, twins)
    ]
    for copy in ch_copies:
        copy.start()
    relay(*late[0])
    sum_ref[160:288] = jnp.dot(low_t_ref[...], gx_ref[...], preferred_element_type=jnp.float32)
    for copy in ch_copies:
        copy.wait_recv()
    total = part_ref[...]
    for k in range(twins - 1):
        total = total + got_ref[k].astype(jnp.float32)
    part_ref[...] = total
    relay(*late[1])

    skip = skip_ref[...]
    def pre_body(i, carry):
        rc = pl.ds(pl.multiple_of(i * 16, 16), 16)
        g_conv = jnp.dot(part_ref[rc, :].astype(jnp.bfloat16), x_proj_ref[...], preferred_element_type=jnp.float32)
        g_conv = g_conv + skip * g_ref[i] + gscan_ref[i]
        pre = pre_ref[i]
        sig = 1.0 / (1.0 + jnp.exp(-pre))
        gpre = g_conv * sig * (1.0 + pre * (1.0 - sig))
        gpre_ref[rc, :] = gpre
        return carry

    pre_body(0, 0)
    edge_ref[...] = gpre_ref[0:8, :]
    edge_copy = pltpu.make_async_remote_copy(
        src_ref=edge_ref, dst_ref=gpre_ref.at[pl.ds(rows, 8)], send_sem=edge_send.at[0], recv_sem=edge_recv.at[0],
        device_id={"seq": before}, device_id_type=MESH,
    )
    edge_copy.start()
    lax.fori_loop(1, chunks, pre_body, 0)
    flipped = jnp.transpose(part_ref[...]).astype(jnp.bfloat16)
    sum_ref[0:160] = jnp.dot(flipped[0:160], conv_ref[...].reshape(rows, chans), preferred_element_type=jnp.float32)
    relay(*late[2])
    edge_copy.wait_recv()

    def taps_body(block, carry):
        cut = pl.ds(pl.multiple_of(block * 128, 128), 128)
        gpre = gpre_ref[0:rows, cut]
        rows_ref[4:5, cut] = jnp.sum(gpre, axis=0, keepdims=True)
        total = jnp.zeros((rows, 128), jnp.float32)
        for k in range(4):
            lag = 3 - k
            total = total + gpre_ref[lag : lag + rows, cut] * taps_ref[k : k + 1, cut] * same_ref[4 + lag].astype(jnp.float32)
            rows_ref[k : k + 1, cut] = jnp.sum(
                gpre * ext_ref[5 + k : 5 + k + rows, cut] * same_ref[k].astype(jnp.float32), axis=0, keepdims=True
            )
        gx_ref[:, cut] = total.astype(jnp.bfloat16)
        return carry

    lax.fori_loop(0, chans // 128, taps_body, 0)
    sum_ref[288:304] = racc_ref[...] * rate_ref[...] * math.log(2.0)
    sum_ref[304:312] = rows_ref[...]
    if tall * across * depth > 312:
        sum_ref[312:] = jnp.zeros((tall * across * depth - 312, chans), jnp.float32)
    for z in range(tall):
        for x in range(across):
            first = (z * across + x) * depth
            half_ref[z, x] = sum_ref[first : first + depth].astype(jnp.bfloat16)

    def to(device):
        return dict(device_id={"seq": device}, device_id_type=MESH)

    half_copies = [
        pltpu.make_async_remote_copy(
            src_ref=half_ref.at[:, lax.rem(x_at + k, across)], dst_ref=half_got.at[k - 1], send_sem=half_send.at[k - 1],
            recv_sem=half_recv.at[k - 1], **to(z_at * across + lax.rem(x_at + k, across)),
        )
        for k in range(1, across)
    ]
    four_copies = [
        pltpu.make_async_remote_copy(
            src_ref=four_b16.at[lax.rem(z_at + k, tall)], dst_ref=four_got.at[k - 1], send_sem=four_send.at[k - 1],
            recv_sem=four_recv.at[k - 1], **to(lax.rem(z_at + k, tall) * across + x_at),
        )
        for k in range(1, tall)
    ]
    last_copies = [
        pltpu.make_async_remote_copy(
            src_ref=small_ref.at[z_at, x_at], dst_ref=small_ref.at[z_at, x_at], send_sem=last_send.at[k - 1],
            recv_sem=last_recv.at[k - 1], **to(lax.rem(z_at + k, tall) * across + x_at),
        )
        for k in range(1, tall)
    ]
    all_copies = [
        pltpu.make_async_remote_copy(
            src_ref=small_ref.at[:, x_at], dst_ref=small_ref.at[:, x_at], send_sem=all_send.at[k - 1],
            recv_sem=all_recv.at[k - 1], **to(z_at * across + lax.rem(x_at + k, across)),
        )
        for k in range(1, across)
    ]

    def small_phase(phase):
        if phase == 0:
            for copy in half_copies:
                copy.start()
        elif phase == 1:
            for copy in half_copies:
                copy.wait_recv()
            for z in range(tall):
                first = pl.multiple_of((z * across + x_at) * depth, depth)
                total = sum_ref[pl.ds(first, depth)]
                for k in range(across - 1):
                    total = total + half_got[k, z].astype(jnp.float32)
                four_ref[z] = total
                four_b16[z] = total.astype(jnp.bfloat16)
            for copy in four_copies:
                copy.start()
        elif phase == 2:
            for copy in four_copies:
                copy.wait_recv()
            total = four_ref[z_at]
            for k in range(tall - 1):
                total = total + four_got[k].astype(jnp.float32)
            small_ref[z_at, x_at] = total.astype(jnp.bfloat16)
            for copy in last_copies:
                copy.start()
        elif phase == 3:
            for copy in last_copies:
                copy.wait_recv()
            for copy in all_copies:
                copy.start()
        else:
            for copy in all_copies:
                copy.wait_recv()
            for copy in half_copies + four_copies + last_copies + all_copies:
                copy.wait_send()

    small_phase(0)
    dwo_ref[...] = jnp.zeros_like(dwo_ref)
    dwz_ref[...] = jnp.zeros_like(dwz_ref)

    def products(kind, k):
        if k == 0:
            blocks = [gz_ref[kind, way * half : (way + 1) * half] for way in (0, 1)]
        else:
            blocks = [ring_ref[kind, way, k - 1] for way in (0, 1)]
        add_products(dwz_ref if kind else dwo_ref, 1 - kind, k, cols_ref, blocks, modes_ref, ring, place, count)

    def mix_copy(j):
        return pltpu.make_async_remote_copy(
            src_ref=mix_sent.at[j], dst_ref=mix_got.at[j], send_sem=mix_send.at[j], recv_sem=mix_recv.at[j],
            device_id={"ch": lax.rem(mine + 1 + j, twins)}, device_id_type=MESH,
        )

    steps = twins * modes

    def normed_unit(j):
        for m in range(modes):
            step = j * modes + m
            if step + 1 < steps:
                in_copies(step + 1, 0)
            in_copies(step, 1)
            spread_products(in_buf.at[step % 2], gz_ref.at[1], mask_ref.at[m], pick_ref[1], gpre_ref, m, part)
        zpart_ref[j] = gpre_ref[0:rows, 0:part].astype(jnp.bfloat16)

    def mix_unit(j):
        for m in range(modes):
            step = j * modes + m
            if step + 1 < steps:
                out_copy(step + 1).start()
            out_copy(step).wait()
            mask = jnp.concatenate([mask_ref[m]] * (part // 128), axis=1) > 0
            found = lax.dot_general(gz_ref[0], out_buf[step % 2], nt, preferred_element_type=jnp.float32)
            mix_ref[...] = jnp.where(mask, found, mix_ref[...]) if m else found
        if j < twins - 1:
            mix_sent[j] = mix_ref[...].astype(jnp.bfloat16)
            mix_copy(j).start()

    edge_copy.wait_send()
    work = [lambda: small_phase(1)]
    for j in range(twins):
        work.append(functools.partial(normed_unit, j))
        work.append(functools.partial(mix_unit, j))
        if j < 3:
            work.append(functools.partial(small_phase, j + 2))
    ready = [(kind, 0) for kind in (0, 1)] + early + late[:3]
    per_turn = max(1, -(-len(work) // max(1, min(4, len(late) - 3))))
    for turn in late[3:]:
        for _ in range(per_turn):
            if work:
                work.pop(0)()
        relay(*turn)
        ready.append(turn)
        products(*ready.pop(0))
        if not work and len(ready) > 2:
            products(*ready.pop(0))
    for unit in work:
        unit()
    for turn in ready:
        products(*turn)
    for j in range(twins - 1):
        mix_copy(j).wait_recv()
        mix_ref[...] += mix_got[j].astype(jnp.float32)
    for j in range(twins - 1):
        mix_copy(j).wait_send()

    for kind in (0, 1):
        for way in (0, 1):
            for k in range(count - 1):
                ring_copy(kind, way, k).wait_send()
    for copy in ch_copies:
        copy.wait_send()


def spread_products(buf, source, mask, pick, target, m, part):
    nt = (((1,), (1,)), ((), ()))
    rows = source.shape[0]
    chosen = mask[...] > 0
    for q in range(2 * part // 256):
        weights = jnp.concatenate(
            [buf.at[b].reshape(2 * part, 128)[q * 256 : (q + 1) * 256] for b in range(buf.shape[0])], axis=1
        )
        found = lax.dot_general(source[...], weights, nt, preferred_element_type=jnp.float32)
        found = jnp.dot(found.astype(jnp.bfloat16), pick, preferred_element_type=jnp.float32)
        cut = pl.ds(q * 128, 128)
        target[0:rows, cut] = jnp.where(chosen, found, target[0:rows, cut]) if m else found


def back(w_in, w_out, gz, dtd, step, conv, g, c_wide, b_own, rate, lam0, h0, hist, sig, pre, ext, same, low_t, dt_proj, x_proj_t, skip, taps, cols, modes, masks, pick):
    count, twins = lax.axis_size("seq"), lax.axis_size("ch")
    rows, chans = dtd.shape
    n = rate.shape[0]
    chunks = rows // 16
    slab = cols.shape[3]
    vmem = pl.BlockSpec(memory_space=pltpu.VMEM)
    hbm = pl.BlockSpec(memory_space=pl.ANY)
    cube = lambda a: a.reshape((chunks, a.shape[0] // chunks) + a.shape[1:])
    f32, b16 = jnp.float32, jnp.bfloat16
    shape = jax.ShapeDtypeStruct
    width = w_out.shape[1]
    part = width // twins
    tall, across = 4, count // 4
    depth = -(-312 // (16 * count)) * 16
    dma = pltpu.SemaphoreType.DMA
    operands = [w_in, w_out, gz, cube(dtd), cube(step), cube(conv), cube(g), c_wide, cube(b_own), rate, lam0, h0, cube(hist),
                cube(sig), cube(pre), ext, same, low_t, dt_proj, x_proj_t, skip, taps, cols, modes, masks, pick]
    return pl.pallas_call(
        functools.partial(back_kernel, (count, twins)),
        in_specs=[hbm if i in (0, 1, 12) else vmem for i in range(len(operands))],
        out_specs=[vmem] * 6,
        out_shape=[
            shape((3, slab, chans), f32), shape((3, slab, chans), f32), shape((rows, chans), b16),
            shape((twins, rows, part), b16), shape((rows, part), f32), shape((tall, across, depth, chans), b16),
        ],
        scratch_shapes=[
            pltpu.VMEM((n, chans), f32),
            pltpu.VMEM((8, chans), f32),
            pltpu.VMEM((tall * across * depth, chans), f32),
            pltpu.VMEM((tall, across, depth, chans), b16),
            pltpu.VMEM((max(1, across - 1), tall, depth, chans), b16),
            pltpu.VMEM((tall, depth, chans), f32),
            pltpu.VMEM((tall, depth, chans), b16),
            pltpu.VMEM((tall - 1, depth, chans), b16),
            pltpu.VMEM((2, chans // 128, part, 2, 128), b16),
            pltpu.VMEM((2, part, chans), b16),
            pltpu.VMEM((twins - 1, rows, part), b16),
            pltpu.VMEM((twins - 1, rows, part), b16),
            pltpu.VMEM((2, 2, count - 1, rows // 2, chans), b16),
            pltpu.VMEM((chunks, 16 * n, chans), b16),
            pltpu.VMEM((16 * n, chans), b16),
            pltpu.VMEM((16 * n, chans), b16),
            pltpu.VMEM((n, chans), f32),
            pltpu.VMEM((chunks, 16, chans), f32),
            pltpu.VMEM((chunks, 16, chans), f32),
            pltpu.VMEM((rows, 256), f32),
            pltpu.VMEM((rows, 256), b16),
            pltpu.VMEM((twins - 1, rows, 256), b16),
            pltpu.VMEM((rows + 8, chans), f32),
            pltpu.VMEM((8, chans), f32),
            dma((2, chans // 128)), dma((2,)), dma((twins - 1,)), dma((twins - 1,)), dma((across - 1,)), dma((across - 1,)),
            dma((tall - 1,)), dma((tall - 1,)), dma((tall - 1,)), dma((tall - 1,)), dma((across - 1,)), dma((across - 1,)),
            pltpu.SemaphoreType.DMA((rows // 32,)),
            pltpu.SemaphoreType.DMA((2, 2, count - 1)),
            pltpu.SemaphoreType.DMA((2, 2, count - 1)),
            pltpu.SemaphoreType.DMA((twins - 1,)),
            pltpu.SemaphoreType.DMA((twins - 1,)),
            pltpu.SemaphoreType.DMA((1,)),
            pltpu.SemaphoreType.DMA((1,)),
        ],
        compiler_params=pltpu.CompilerParams(collective_id=2, has_side_effects=True, vmem_limit_bytes=60 << 20),
        name="back",
    )(*operands)


def tail_kernel(
    sizes, gx_ref, zpart_ref, x_ref, gain_ref, scaled_ref, mask_ref, cols_ref, modes_ref, pick_ref, w_in_ref,
    acc_ref, slice_ref, dots_ref, dgain_ref,
    ring_ref, in_buf, norm_sent, norm_got, dots_sent, dots_got, gain_sent, gain_got,
    in_sem, ring_send, ring_recv, norm_send, norm_recv, dots_send, dots_recv, gain_send, gain_recv,
):
    count, twins = sizes
    rows, chans = gx_ref.shape
    modes = mask_ref.shape[0]
    half = rows // 2
    quarter = half // 2
    width = x_ref.shape[1]
    part = width // twins
    eighths = chans // 128
    ring, place, onward, backward = ring_places(count)
    mine = lax.axis_index("ch")

    barrier = pltpu.get_barrier_semaphore()
    me = lax.axis_index("seq")
    for k in range(1, count):
        pl.semaphore_signal(barrier, inc=1, device_id={"seq": lax.rem(me + k, count)}, device_id_type=MESH)
    for k in range(1, twins):
        pl.semaphore_signal(barrier, inc=1, device_id={"ch": lax.rem(mine + k, twins)}, device_id_type=MESH)

    steps = twins * modes

    def chunk_of(step):
        return lax.rem(mine + 1 + step // modes, twins)

    def in_copy(step, b):
        slot = lax.rem(step, 2)
        features = pl.ds(pl.multiple_of(chunk_of(step) * part, part), part)
        return pltpu.make_async_copy(
            w_in_ref.at[lax.rem(step, modes), features, b], in_buf.at[slot, b], in_sem.at[slot, b]
        )

    for b in range(eighths):
        in_copy(0, b).start()
    pl.semaphore_wait(barrier, count - 1 + twins - 1)

    def ring_copy(way, piece, k):
        if k == 0:
            source = gx_ref.at[pl.ds(way * half + piece * quarter, quarter)]
        else:
            source = ring_ref.at[way, k - 1, pl.ds(piece * quarter, quarter)]
        return pltpu.make_async_remote_copy(
            src_ref=source, dst_ref=ring_ref.at[way, k, pl.ds(piece * quarter, quarter)],
            send_sem=ring_send.at[way, piece, k], recv_sem=ring_recv.at[way, piece, k],
            device_id={"seq": backward if way else onward}, device_id_type=MESH,
        )

    def relay(k):
        for piece in (0, 1):
            for way in (0, 1):
                ring_copy(way, piece, k - 1).wait_recv()
                if k < count - 1:
                    ring_copy(way, piece, k).start()

    for piece in (0, 1):
        for way in (0, 1):
            ring_copy(way, piece, 0).start()

    def peer_copy(j):
        return pltpu.make_async_remote_copy(
            src_ref=norm_sent.at[j], dst_ref=norm_got.at[j], send_sem=norm_send.at[j], recv_sem=norm_recv.at[j],
            device_id={"ch": lax.rem(mine + 1 + j, twins)}, device_id_type=MESH,
        )

    dots_ref[...] = jnp.zeros_like(dots_ref)
    for j in range(twins):
        for m in range(modes):
            step = j * modes + m
            if step + 1 < steps:
                for b in range(eighths):
                    in_copy(step + 1, b).start()
            for b in range(eighths):
                in_copy(step, b).wait()
            spread_products(in_buf.at[step % 2], gx_ref, mask_ref.at[m], pick_ref[0], slice_ref, m, part)
        for q in range(part // 128):
            lanes = slice(q * 128, (q + 1) * 128)
            cut = pl.ds(pl.multiple_of(lax.rem(mine + 1 + j, twins) * part + q * 128, 128), 128)
            found = slice_ref[:, lanes] + zpart_ref[j, :, lanes].astype(jnp.float32)
            slice_ref[:, lanes] = found
            dots_ref[...] += found * x_ref[:, cut].astype(jnp.float32) * gain_ref[:, cut]
        if j < twins - 1:
            norm_sent[j] = slice_ref[...].astype(jnp.bfloat16)
            peer_copy(j).start()
        if j < 3:
            relay(j + 1)
    dots_sent[...] = dots_ref[...].astype(jnp.bfloat16)
    dots_copies = [
        pltpu.make_async_remote_copy(
            src_ref=dots_sent, dst_ref=dots_got.at[k - 1], send_sem=dots_send.at[k - 1], recv_sem=dots_recv.at[k - 1],
            device_id={"ch": lax.rem(mine + k, twins)}, device_id_type=MESH,
        )
        for k in range(1, twins)
    ]
    for copy in dots_copies:
        copy.start()

    acc_ref[...] = jnp.zeros_like(acc_ref)

    def products(k):
        if k == 0:
            blocks = [gx_ref[way * half : (way + 1) * half] for way in (0, 1)]
        else:
            blocks = [ring_ref[way, k - 1] for way in (0, 1)]
        add_products(acc_ref, 0, k, cols_ref, blocks, modes_ref, ring, place, count)

    for k in range(min(3, twins) + 1):
        products(k)
    for j in range(twins - 1):
        peer_copy(j).wait_recv()
        slice_ref[...] += norm_got[j].astype(jnp.float32)
    dgain_ref[...] = jnp.zeros_like(dgain_ref) + jnp.sum(slice_ref[...] * scaled_ref[...], axis=0, keepdims=True)
    gain_sent[...] = dgain_ref[...]
    gain_copies = [
        pltpu.make_async_remote_copy(
            src_ref=gain_sent, dst_ref=gain_got.at[k - 1], send_sem=gain_send.at[k - 1], recv_sem=gain_recv.at[k - 1],
            device_id={"seq": lax.rem(me + k, count)}, device_id_type=MESH,
        )
        for k in range(1, count)
    ]
    for copy in gain_copies:
        copy.start()
    for k, copy in enumerate(dots_copies):
        copy.wait_recv()
        dots_ref[...] += dots_got[k].astype(jnp.float32)
    for k in range(min(3, twins) + 1, count):
        relay(k)
        products(k)

    for k, copy in enumerate(gain_copies):
        copy.wait_recv()
        dgain_ref[...] += gain_got[k]
    for way in (0, 1):
        for piece in (0, 1):
            for k in range(count - 1):
                ring_copy(way, piece, k).wait_send()
    for j in range(twins - 1):
        peer_copy(j).wait_send()
    for copy in dots_copies + gain_copies:
        copy.wait_send()


def picks():
    order = jnp.arange(256)
    return jnp.stack([order[:, None] == 2 * jnp.arange(128)[None] + j for j in (0, 1)]).astype(jnp.bfloat16)


def lane_blocks(w_in):
    kinds, width, _, chans = w_in.shape
    return w_in.reshape(kinds, width, 2, chans // 128, 128).transpose(0, 1, 3, 2, 4)


def tail(gx, zpart, x_in, gain, scaled, masks, cols, modes, pick, w_in):
    count, twins = lax.axis_size("seq"), lax.axis_size("ch")
    rows, chans = gx.shape
    width = x_in.shape[1]
    part = width // twins
    slab = cols.shape[3]
    kinds = w_in.shape[0]
    vmem = pl.BlockSpec(memory_space=pltpu.VMEM)
    hbm = pl.BlockSpec(memory_space=pl.ANY)
    f32, b16 = jnp.float32, jnp.bfloat16
    shape = jax.ShapeDtypeStruct
    dma = pltpu.SemaphoreType.DMA
    return pl.pallas_call(
        functools.partial(tail_kernel, (count, twins)),
        in_specs=[vmem] * 9 + [hbm],
        out_specs=[vmem] * 4,
        out_shape=[
            shape((kinds, slab, chans), f32), shape((rows, part), f32), shape((rows, 128), f32), shape((8, part), f32),
        ],
        scratch_shapes=[
            pltpu.VMEM((2, count - 1, rows // 2, chans), b16),
            pltpu.VMEM((2, chans // 128, part, 2, 128), b16),
            pltpu.VMEM((twins - 1, rows, part), b16),
            pltpu.VMEM((twins - 1, rows, part), b16),
            pltpu.VMEM((rows, 128), b16),
            pltpu.VMEM((twins - 1, rows, 128), b16),
            pltpu.VMEM((8, part), f32),
            pltpu.VMEM((count - 1, 8, part), f32),
            dma((2, chans // 128)), dma((2, 2, count - 1)), dma((2, 2, count - 1)), dma((twins - 1,)), dma((twins - 1,)),
            dma((twins - 1,)), dma((twins - 1,)), dma((count - 1,)), dma((count - 1,)),
        ],
        compiler_params=pltpu.CompilerParams(collective_id=3, has_side_effects=True, vmem_limit_bytes=60 << 20),
        name="tail",
    )(gx, zpart, x_in, gain.reshape(1, -1), scaled, masks, cols, modes, pick, w_in)


def weave_kernel(x_ref, z_ref, out_ref, sems):
    kinds, _, chans = x_ref.shape
    copies = []
    for m in range(kinds):
        for b in range(chans // 128):
            for j, source in enumerate((x_ref, z_ref)):
                copies.append(
                    pltpu.make_async_copy(
                        source.at[m, :, pl.ds(b * 128, 128)], out_ref.at[m, :, b, j], sems.at[len(copies)]
                    )
                )
    for copy in copies:
        copy.start()
    for copy in copies:
        copy.wait()


def weave(x_part, z_part):
    kinds, slab, chans = x_part.shape
    out = pl.pallas_call(
        weave_kernel,
        in_specs=[pl.BlockSpec(memory_space=pltpu.VMEM)] * 2,
        out_specs=pl.BlockSpec(memory_space=pl.ANY),
        out_shape=jax.ShapeDtypeStruct((kinds, slab, chans // 128, 2, 128), jnp.float32),
        scratch_shapes=[pltpu.SemaphoreType.DMA((kinds * chans // 64,))],
        compiler_params=pltpu.CompilerParams(vmem_limit_bytes=32 << 20),
        name="weave",
    )(x_part, z_part)
    return out.transpose(0, 1, 3, 2, 4).reshape(kinds, slab, 2, chans)


def shards(
    x_in,
    norm_gain,
    w_in,
    conv_weight,
    conv_bias,
    x_proj,
    dt_proj,
    dt_bias,
    a_log,
    d_skip,
    w_out,
    modes,
    doc_lengths,
    cotangent,
):
    tok_rows, model_width = x_in.shape
    mode_count = w_in.shape[0]
    inner_local = conv_bias.shape[0]
    state_size = a_log.shape[0]
    rank_size = dt_proj.shape[0]
    conv_taps = conv_weight.shape[0]
    ch_count = lax.axis_size("ch")
    feat_part = model_width // ch_count
    seq_index = lax.axis_index("seq")
    ch_index = lax.axis_index("ch")
    first_pos = seq_index * tok_rows
    positions = first_pos + jnp.arange(tok_rows, dtype=jnp.int32)
    my_modes = lax.dynamic_slice_in_dim(modes, first_pos, tok_rows)
    onehot = (my_modes[:, None] == jnp.arange(mode_count, dtype=jnp.int32)[None]).astype(
        jnp.bfloat16
    )
    doc_index, begins = doc_tables(doc_lengths, positions)
    keep_mask = 1.0 - begins.astype(jnp.float32)
    x_full = x_in.astype(jnp.float32)
    scale = lax.rsqrt(jnp.mean(x_full * x_full, axis=1, keepdims=True) + EPSILON)
    normed = (x_full * scale * norm_gain[None]).astype(jnp.bfloat16)
    spread = jnp.eye(256, dtype=jnp.bfloat16)
    spread = jnp.stack([spread, jnp.zeros_like(spread)], axis=2)
    spread = jnp.stack([spread, spread[:, :, ::-1]], axis=0).reshape(2, 256, 512)
    doubled = jnp.einsum("tbd,jdk->jtbk", normed.reshape(tok_rows, -1, 256), spread)
    doubled = doubled.reshape(2, tok_rows, 2 * model_width)
    masks = jnp.broadcast_to(onehot.T[:, :, None], (mode_count, tok_rows, 128))
    x_branch, z_branch, d_gated, cols = front(doubled, normed, masks, cotangent, w_in, w_out)
    z_branch = z_branch.astype(jnp.float32)
    rim_rows = from_behind(x_branch[tok_rows - (conv_taps - 1) :], "seq", 1)
    extended = jnp.concatenate([rim_rows, x_branch], axis=0).astype(jnp.float32)
    ext_doc, _ = doc_tables(
        doc_lengths,
        first_pos - (conv_taps - 1) + jnp.arange(tok_rows + conv_taps - 1, dtype=jnp.int32),
    )
    conv_pre = jnp.zeros((tok_rows, inner_local), jnp.float32) + conv_bias[None]
    same_list = []
    for offset in range(conv_taps):
        same_doc = (ext_doc[offset : offset + tok_rows] == doc_index).astype(jnp.float32)[:, None]
        same_list.append(same_doc)
        conv_pre = (
            conv_pre + conv_weight[offset][None] * extended[offset : offset + tok_rows] * same_doc
        )
    conv_out = jax.nn.silu(conv_pre).astype(jnp.bfloat16)
    conv_float = conv_out.astype(jnp.float32)
    projected = sum_over(jnp.dot(conv_out, x_proj, preferred_element_type=jnp.float32), "ch")
    dt_low = projected[:, :rank_size].astype(jnp.bfloat16)
    b_in = projected[:, rank_size : rank_size + state_size]
    c_out = projected[:, rank_size + state_size :]
    dt_raw = jnp.dot(dt_low, dt_proj, preferred_element_type=jnp.float32)
    step_size = jax.nn.softplus(dt_raw + dt_bias[None])
    decay_rate = -jnp.exp(a_log)
    seq_count = lax.axis_size("seq")
    rate_two = decay_rate * math.log2(math.e)
    masked_step = jnp.where(begins[:, None], 1e30, step_size)
    drive = step_size * conv_float
    wide = (tok_rows, state_size, 128)
    b_wide = jnp.broadcast_to(b_in[:, :, None], wide)
    c_wide = jnp.broadcast_to(c_out[:, :, None], wide)
    gate_act = jax.nn.silu(z_branch)
    d_ssm = d_gated * gate_act
    ends = scan_ends(masked_step, drive, d_ssm, b_wide, c_wide, rate_two)
    steps = jnp.sum(masked_step, axis=0)
    ends_in, steps_in = exchange_states(ends, steps.reshape(8, -1))
    steps_in = steps_in.reshape(seq_count - 1, inner_local)
    incoming = jnp.zeros((state_size, inner_local), jnp.float32)
    pending = incoming
    gap = jnp.zeros((inner_local,), jnp.float32)
    for distance in range(1, seq_count):
        part = ends_in[distance - 1].astype(jnp.float32) * jnp.exp2(rate_two * gap[None])
        incoming = incoming + jnp.where(distance <= seq_index, part, 0.0)
        gap = gap + steps_in[distance - 1]
    gap = jnp.zeros((inner_local,), jnp.float32)
    for distance in range(1, seq_count):
        slot = seq_count - 1 - distance
        part = ends_in[slot].astype(jnp.float32) * jnp.exp2(rate_two * gap[None])
        pending = pending + jnp.where(distance + seq_index < seq_count, part, 0.0)
        gap = gap + steps_in[slot]
    ssm, history = scan_forward(
        masked_step, drive, b_wide, own_columns(c_out), rate_two, incoming
    )
    ssm = ssm + d_skip[None] * conv_float
    gated = (ssm * gate_act).astype(jnp.bfloat16)
    gate_sig = jax.nn.sigmoid(z_branch)
    d_z = d_gated * ssm * gate_sig * (1.0 + z_branch * (1.0 - gate_sig))
    both = jnp.stack([gated, d_z.astype(jnp.bfloat16)])
    wide = lambda a: jnp.broadcast_to(a, (tok_rows, 128)).astype(jnp.bfloat16)
    post_doc, _ = doc_tables(
        doc_lengths, first_pos + jnp.arange(tok_rows + conv_taps - 1, dtype=jnp.int32)
    )
    later = [
        (post_doc[lag : lag + tok_rows] == doc_index).astype(jnp.float32)[:, None]
        for lag in range(conv_taps)
    ]
    same = jnp.stack([wide(a) for a in same_list + later])
    columns = jnp.swapaxes(cols, 3, 4)
    mode_rows = modes.reshape(2 * seq_count, tok_rows // 2)
    blocks = lane_blocks(w_in)
    pick = picks()
    d_w_out, d_w_z, d_x_branch, zpart, mixer, smalls = back(
        blocks, w_out, both, masked_step, step_size, conv_out, d_ssm, c_wide, own_columns(b_in), rate_two, pending,
        incoming, history, jax.nn.sigmoid(dt_raw + dt_bias[None]), conv_pre, jnp.pad(extended, ((5, 0), (0, 0))), same,
        dt_low.T, dt_proj, jnp.pad(x_proj.T, ((0, 256 - x_proj.shape[1]), (0, 0))), d_skip[None], conv_weight, columns,
        mode_rows, masks, pick,
    )
    x_slice = lax.dynamic_slice_in_dim(x_full, ch_index * feat_part, feat_part, 1)
    gain_slice = lax.dynamic_slice_in_dim(norm_gain, ch_index * feat_part, feat_part, 0)
    d_w_x, d_slice, dots, d_gain = tail(
        d_x_branch, zpart, x_in, norm_gain, x_slice * scale, masks, columns, mode_rows, pick, blocks
    )
    d_w_in = weave(d_w_x, d_w_z)
    block_out = (x_slice + mixer).astype(jnp.bfloat16)
    mean_term = (jnp.sum(dots, axis=1) / model_width)[:, None]
    weighted_slice = d_slice * gain_slice[None]
    d_x_in = cotangent.astype(jnp.float32) + scale * weighted_slice - x_slice * scale**3 * mean_term
    smalls = smalls.reshape(-1, inner_local).astype(jnp.float32)
    return (
        block_out,
        d_x_in,
        d_gain[0],
        d_w_in,
        smalls[304:308],
        smalls[308],
        smalls[:160].T,
        smalls[160:288],
        smalls[309],
        smalls[288:304],
        smalls[310],
        d_w_out,
    )


def solution(mesh):
    return jax.shard_map(
        shards,
        mesh=mesh,
        in_specs=(
            P("seq", None),
            P(),
            P(None, None, None, "ch"),
            P(None, "ch"),
            P("ch"),
            P("ch", None),
            P(None, "ch"),
            P("ch"),
            P(None, "ch"),
            P("ch"),
            P(None, None, "ch"),
            P(),
            P(),
            P("seq", "ch"),
        ),
        out_specs=(
            P("seq", "ch"),
            P("seq", "ch"),
            P("ch"),
            P(None, "seq", None, "ch"),
            P(None, "ch"),
            P("ch"),
            P("ch", None),
            P(None, "ch"),
            P("ch"),
            P(None, "ch"),
            P("ch"),
            P(None, "seq", "ch"),
        ),
        check_vma=False,
    )
```

```python
import functools
import math

import jax
import jax.numpy as jnp
from jax import lax
from jax.experimental import pallas as pl
from jax.experimental.pallas import tpu as pltpu
from jax.sharding import PartitionSpec as P

EPSILON = 1e-05


MESH = pl.DeviceIdType.MESH


def cycle_of(count):
    across = count // 4
    walk = [(0, x) for x in range(across)]
    for turn, x in enumerate(reversed(range(across))):
        column = [(z, x) for z in range(1, 4)]
        walk += column[::-1] if turn % 2 else column
    return [z * across + x for z, x in walk]


def table_of(index, values):
    picked = jnp.int32(values[0])
    for i in range(1, len(values)):
        picked = jnp.where(index == i, jnp.int32(values[i]), picked)
    return picked


def front_kernel(
    sizes, normed_ref, mask_ref, cot_ref, w_in_ref, w_out_ref,
    x_ref, z_ref, gated_ref, cols_ref, halo_ref,
    x2_ref, halo_send, halo_recv, cotg_ref, in_buf, out_buf, in_sem, out_sem, cot_send, cot_recv, seq_send, seq_recv, twin_send, twin_recv, own_sem,
):
    count, twins = sizes
    rows, width = normed_ref.shape
    modes = mask_ref.shape[0]
    half = rows // 2
    slab = width // count
    part = cot_ref.shape[1]
    inner = x_ref.shape[1]
    ring = cycle_of(count)
    me = lax.axis_index("seq")
    mine = lax.axis_index("ch")
    side = lax.rem(mine, 2)
    twin = mine + 1 - 2 * side
    where = {s: i for i, s in enumerate(ring)}
    place = table_of(me, [where[s] for s in range(count)])

    barrier = pltpu.get_barrier_semaphore()
    for k in range(1, count):
        peer = {"seq": lax.rem(me + k, count)}
        pl.semaphore_signal(barrier, inc=1, device_id=peer, device_id_type=MESH)
    for k in range(1, twins):
        peer = {"ch": lax.rem(mine + k, twins)}
        pl.semaphore_signal(barrier, inc=1, device_id=peer, device_id_type=MESH)

    pairs = inner // 256
    steps = pairs * modes

    def in_copy(step, b):
        slot = lax.rem(step, 2)
        return pltpu.make_async_copy(
            w_in_ref.at[lax.rem(step, modes), :, step // modes * 2 + b], in_buf.at[slot, b], in_sem.at[slot, b]
        )

    wide = out_buf.shape[2]
    out_steps = inner // wide * modes

    def out_copy(step):
        slot = lax.rem(step, 2)
        columns = pl.ds(pl.multiple_of(step // modes * wide, wide), wide)
        return pltpu.make_async_copy(
            w_out_ref.at[lax.rem(step, modes), :, columns], out_buf.at[slot], out_sem.at[slot]
        )

    for b in (0, 1):
        in_copy(0, b).start()
    out_copy(0).start()
    pl.semaphore_wait(barrier, count - 1 + twins - 1)

    cot_copies = [
        pltpu.make_async_remote_copy(
            src_ref=cot_ref, dst_ref=cotg_ref.at[mine], send_sem=cot_send.at[k - 1], recv_sem=cot_recv.at[k - 1],
            device_id={"ch": lax.rem(mine + k, twins)}, device_id_type=MESH,
        )
        for k in range(1, twins)
    ]
    for copy in cot_copies:
        copy.start()
    side_rows = pl.ds(pl.multiple_of(side * half, half), half)

    def seq_copies(kind):
        copies = []
        for k in range(1, count):
            step = jnp.where(side == 0, k, count - k)
            peer = table_of(lax.rem(place + step, count), ring)
            if kind == 0:
                source = normed_ref.at[side_rows, pl.ds(pl.multiple_of(peer * slab, slab), slab)]
            else:
                start = lax.rem(peer * slab, part)
                source = cotg_ref.at[peer * slab // part, side_rows, pl.ds(pl.multiple_of(start, slab), slab)]
            copies.append(
                pltpu.make_async_remote_copy(
                    src_ref=source, dst_ref=cols_ref.at[kind, side, k], send_sem=seq_send.at[kind, k - 1],
                    recv_sem=seq_recv.at[kind, k - 1], device_id={"seq": peer}, device_id_type=MESH,
                )
            )
        return copies

    def twin_copy(kind):
        return pltpu.make_async_remote_copy(
            src_ref=cols_ref.at[kind, side, pl.ds(1, count - 1)], dst_ref=cols_ref.at[kind, side, pl.ds(1, count - 1)],
            send_sem=twin_send.at[kind], recv_sem=twin_recv.at[kind],
            device_id={"ch": twin}, device_id_type=MESH,
        )

    normed_copies = seq_copies(0)
    for copy in normed_copies:
        copy.start()
    own_copy = pltpu.make_async_copy(cot_ref, cotg_ref.at[mine], own_sem.at[0])
    own_copy.start()
    own_start = pl.multiple_of(me * slab, slab)
    for way in (0, 1):
        cols_ref[0, way, 0] = normed_ref[way * half : (way + 1) * half, pl.ds(own_start, slab)]

    def in_step(step, carry):
        slot = lax.rem(step, 2)
        mode = lax.rem(step, modes)

        @pl.when(step + 1 < steps)
        def _():
            for b in (0, 1):
                in_copy(step + 1, b).start()

        for b in (0, 1):
            in_copy(step, b).wait()
        weights = jnp.concatenate([in_buf.at[slot, b].reshape(2 * width, 128)[...] for b in (0, 1)], axis=1)
        mask = jnp.concatenate([mask_ref[mode]] * 2, axis=1) > 0
        columns = pl.ds(pl.multiple_of(step // modes * 256, 256), 256)
        for j, target in enumerate((x_ref, z_ref)):
            found = jnp.dot(x2_ref[j], weights, preferred_element_type=jnp.float32).astype(jnp.bfloat16)
            target[:, columns] = jnp.where(mask, found, target[:, columns])
        return carry

    x_ref[...] = jnp.zeros_like(x_ref)
    z_ref[...] = jnp.zeros_like(z_ref)
    row = lax.broadcasted_iota(jnp.int32, (256, 512), 0)
    column = lax.broadcasted_iota(jnp.int32, (256, 512), 1)
    for j in (0, 1):
        spread = (column == 2 * row + j).astype(jnp.bfloat16)
        for block in range(width // 256):
            x2_ref[j, :, block * 512 : (block + 1) * 512] = jnp.dot(
                normed_ref[:, block * 256 : (block + 1) * 256], spread, preferred_element_type=jnp.float32
            ).astype(jnp.bfloat16)
    first = steps // 2
    lax.fori_loop(0, first, in_step, 0)
    own_copy.wait()
    for copy in cot_copies:
        copy.wait_recv()
    tail_copies = seq_copies(1)
    for copy in tail_copies:
        copy.start()
    own_slab = cotg_ref.at[me * slab // part]
    for way in (0, 1):
        cols_ref[1, way, 0] = own_slab[way * half : (way + 1) * half, pl.ds(pl.multiple_of(lax.rem(me * slab, part), slab), slab)]
    for copy in normed_copies:
        copy.wait_recv()
    twin_copy(0).start()
    lax.fori_loop(first, steps, in_step, 0)
    halo_copy = pltpu.make_async_remote_copy(
        src_ref=x_ref.at[pl.ds(rows - 16, 16)], dst_ref=halo_ref, send_sem=halo_send.at[0], recv_sem=halo_recv.at[0],
        device_id={"seq": lax.rem(me + 1, count)}, device_id_type=MESH,
    )
    halo_copy.start()

    def out_step(step, carry):
        slot = lax.rem(step, 2)
        mode = lax.rem(step, modes)

        @pl.when(step + 1 < out_steps)
        def _():
            out_copy(step + 1).start()

        out_copy(step).wait()
        mask = jnp.concatenate([mask_ref[mode]] * (wide // 128), axis=1) > 0
        columns = pl.ds(pl.multiple_of(step // modes * wide, wide), wide)
        found = jnp.zeros((rows, wide), jnp.float32)
        for c in range(twins):
            found = found + jnp.dot(
                cotg_ref[c], out_buf[slot, c * part : (c + 1) * part], preferred_element_type=jnp.float32
            )
        gated_ref[:, columns] = jnp.where(mask, found, gated_ref[:, columns])
        return carry

    gated_ref[...] = jnp.zeros_like(gated_ref)
    lax.fori_loop(0, out_steps, out_step, 0)
    for copy in tail_copies:
        copy.wait_recv()
    twin_copy(1).start()
    for kind in (0, 1):
        twin_copy(kind).wait_recv()
        twin_copy(kind).wait_send()
    halo_copy.wait_recv()
    for copy in cot_copies + normed_copies + tail_copies + [halo_copy]:
        copy.wait_send()


def front(normed, masks, cot, w_in, w_out):
    count, twins = lax.axis_size("seq"), lax.axis_size("ch")
    rows, width = normed.shape
    inner = w_out.shape[2]
    modes = w_out.shape[0]
    vmem = pl.BlockSpec(memory_space=pltpu.VMEM)
    hbm = pl.BlockSpec(memory_space=pl.ANY)
    wide = min(512, inner)
    return pl.pallas_call(
        functools.partial(front_kernel, (count, twins)),
        in_specs=[vmem, vmem, vmem, hbm, hbm],
        out_specs=[vmem] * 5,
        out_shape=[
            jax.ShapeDtypeStruct((rows, inner), jnp.bfloat16),
            jax.ShapeDtypeStruct((rows, inner), jnp.bfloat16),
            jax.ShapeDtypeStruct((rows, inner), jnp.float32),
            jax.ShapeDtypeStruct((2, 2, count, rows // 2, width // count), jnp.bfloat16),
            jax.ShapeDtypeStruct((16, inner), jnp.bfloat16),
        ],
        scratch_shapes=[
            pltpu.VMEM((2, rows, 2 * width), jnp.bfloat16),
            pltpu.SemaphoreType.DMA((1,)),
            pltpu.SemaphoreType.DMA((1,)),
            pltpu.VMEM((twins,) + cot.shape, jnp.bfloat16),
            pltpu.VMEM((2, 2, width, 2, 128), jnp.bfloat16),
            pltpu.VMEM((2, width, wide), jnp.bfloat16),
            pltpu.SemaphoreType.DMA((2, 2)),
            pltpu.SemaphoreType.DMA((2,)),
            pltpu.SemaphoreType.DMA((twins - 1,)),
            pltpu.SemaphoreType.DMA((twins - 1,)),
            pltpu.SemaphoreType.DMA((2, count - 1)),
            pltpu.SemaphoreType.DMA((2, count - 1)),
            pltpu.SemaphoreType.DMA((2,)),
            pltpu.SemaphoreType.DMA((2,)),
            pltpu.SemaphoreType.DMA((1,)),
        ],
        compiler_params=pltpu.CompilerParams(collective_id=1, has_side_effects=True, vmem_limit_bytes=56 << 20),
        name="front",
    )(normed, masks, cot, w_in, w_out)


def doc_tables(doc_lengths, positions):
    count = doc_lengths.shape[0]
    order = jnp.arange(count, dtype=jnp.int32)
    doc_ends = jnp.sum(jnp.where(order[:, None] >= order[None, :], doc_lengths[None, :], 0), axis=1)
    doc_starts = doc_ends - doc_lengths
    doc_index = jnp.sum((positions[:, None] >= doc_ends[None, :]).astype(jnp.int32), axis=1)
    begins = jnp.any(positions[:, None] == doc_starts[None, :], axis=1)
    return (doc_index, begins)


def tile_lanes(v, lanes):
    return jnp.concatenate([v] * (lanes // 128), axis=1)

def ring_places(count):
    ring = cycle_of(count)
    where = {s: i for i, s in enumerate(ring)}
    me = lax.axis_index("seq")
    onward = table_of(me, [ring[(where[s] + 1) % count] for s in range(count)])
    backward = table_of(me, [ring[(where[s] - 1) % count] for s in range(count)])
    place = table_of(me, [where[s] for s in range(count)])
    return ring, place, onward, backward


def add_products(acc_ref, kind, k, cols_ref, blocks, modes_ref, ring, place, count):
    parts = []
    for way in (0, 1):
        step = k if way else count - k
        source = table_of(lax.rem(place + step, count), ring)
        parts.append((jnp.transpose(cols_ref[kind, way, k]), modes_ref[pl.ds(2 * source + way, 1), :]))
    right = jnp.concatenate(blocks, axis=0)
    for m in range(acc_ref.shape[0]):
        left = jnp.concatenate(
            [part * jnp.where(row == m, 1.0, 0.0).astype(jnp.bfloat16) for part, row in parts], axis=1
        )
        acc_ref[m] += jnp.dot(left, right, preferred_element_type=jnp.float32)


def core_kernel(
    sizes, w_in_ref, w_out_ref, x_ref, halo_ref, z_ref, dgated_ref, same_ref, big_ref, taps_ref, cbias_ref, x_proj_ref,
    dt_proj_ref, dt_bias_ref, a_log_ref, skip_ref, cols_ref, modes_ref, mask_ref, pick_ref,
    dwo_ref, dwz_ref, gx_ref, zpart_ref, mix_ref, small_ref,
    ext_ref, pre_ref, conv_ref, g_ref, step_ref, dtd_ref, u_ref, sig_ref, low_t_ref, b_ref, c_ref, rate_ref, ends_ref,
    ends_sent, ends_got, steps_sent, steps_got, h0_ref, gz_ref,
    racc_ref, rows_ref, sum_ref, half_ref, half_got, four_ref, four_b16, four_got, in_buf, out_buf, mix_sent, mix_got,
    ring_ref, hist_ref, lam_ref, w_ref, pend_ref, gstep_ref, gscan_ref, part_ref, grad_ref, sent_ref, got_ref, gpre_ref, edge_ref,
    in_sem, out_sem, mix_send, mix_recv, half_send, half_recv, four_send, four_recv, last_send, last_recv, all_send, all_recv,
    ends_send, ends_recv, steps_send, steps_recv, low_send, low_recv,
    ring_send, ring_recv, ch_send, ch_recv, edge_send, edge_recv,
):
    count, twins = sizes
    chunks, _, chans = pre_ref.shape
    rows = chunks * 16
    n = a_log_ref.shape[0]
    half = rows // 2
    ring, place, onward, backward = ring_places(count)
    me = lax.axis_index("seq")
    mine = lax.axis_index("ch")
    before = lax.rem(me + count - 1, count)
    nt = (((1,), (1,)), ((), ()))
    f32, b16 = jnp.float32, jnp.bfloat16
    lb = min(512, chans)

    modes = mask_ref.shape[0]
    width = w_out_ref.shape[1]
    part = width // twins
    eighths = chans // 128
    across = half_ref.shape[1]
    tall = half_ref.shape[0]
    depth = half_ref.shape[2]
    z_at = me // across
    x_at = lax.rem(me, across)

    def chunk_of(step):
        return pl.ds(pl.multiple_of(lax.rem(mine + 1 + step // modes, twins) * part, part), part)

    def in_copy(step, b):
        slot = step % 2
        return pltpu.make_async_copy(w_in_ref.at[step % modes, chunk_of(step), b], in_buf.at[slot, b], in_sem.at[slot, b])

    def in_copies(step, wait):
        for b in range(eighths):
            if wait:
                in_copy(step, b).wait()
            else:
                in_copy(step, b).start()

    def out_copy(step):
        slot = step % 2
        return pltpu.make_async_copy(w_out_ref.at[step % modes, chunk_of(step)], out_buf.at[slot], out_sem.at[slot])

    barrier = pltpu.get_barrier_semaphore()
    for k in range(1, count):
        pl.semaphore_signal(barrier, inc=1, device_id={"seq": lax.rem(me + k, count)}, device_id_type=MESH)
    for k in range(1, twins):
        peer = {"ch": lax.rem(mine + k, twins)}
        pl.semaphore_signal(barrier, inc=1, device_id=peer, device_id_type=MESH)
    in_copies(0, 0)
    out_copy(0).start()
    pl.semaphore_wait(barrier, count - 1 + twins - 1)

    ext_ref[0:8] = halo_ref[8:16].astype(f32)
    ext_ref[8:] = x_ref[...].astype(f32)

    def conv_body(block, carry):
        cut = pl.ds(pl.multiple_of(block * 128, 128), 128)
        pre = jnp.zeros((rows, 128), f32) + cbias_ref[:, cut]
        for k in range(4):
            pre = pre + taps_ref[k : k + 1, cut] * ext_ref[5 + k : 5 + k + rows, cut] * same_ref[k].astype(f32)
        pre_ref[:, :, cut] = pre.reshape(chunks, 16, 128)
        conv_ref[:, :, cut] = (pre / (1.0 + jnp.exp(-pre))).astype(b16).reshape(chunks, 16, 128)
        return carry

    lax.fori_loop(0, chans // 128, conv_body, 0)
    part_ref[...] = lax.dot_general(
        conv_ref[...].reshape(rows, chans), x_proj_ref[...], nt, preferred_element_type=f32
    )
    sent_ref[0] = part_ref[...].astype(b16)

    def maps_copies(which, send, recv):
        return [
            pltpu.make_async_remote_copy(
                src_ref=sent_ref.at[which], dst_ref=got_ref.at[which, k - 1], send_sem=send.at[k - 1],
                recv_sem=recv.at[k - 1], device_id={"ch": lax.rem(mine + k, twins)}, device_id_type=MESH,
            )
            for k in range(1, twins)
        ]

    low_copies = maps_copies(0, low_send, low_recv)
    for copy in low_copies:
        copy.start()

    def gate_body(i, carry):
        z = z_ref[i].astype(f32)
        g_ref[i] = dgated_ref[i] * (z / (1.0 + jnp.exp(-z)))
        return carry

    lax.fori_loop(0, chunks, gate_body, 0)
    rate_ref[...] = -math.log2(math.e) * jnp.exp(a_log_ref[...])
    own = (
        lax.broadcasted_iota(jnp.int32, (16, 16 * n), 1) // n == lax.broadcasted_iota(jnp.int32, (16, 16 * n), 0)
    )
    ones = own.astype(b16)
    token_row = lax.broadcasted_iota(jnp.int32, (16 * n, 16), 0) // n
    repeat = (token_row == lax.broadcasted_iota(jnp.int32, (16 * n, 16), 1)).astype(b16)
    pick_row = lax.broadcasted_iota(jnp.int32, (16 * n, 128), 0)
    pick_col = lax.broadcasted_iota(jnp.int32, (16 * n, 128), 1)
    is_b = pick_row % n == pick_col
    is_c = pick_row % n + n == pick_col
    pick_b = is_b.astype(b16)
    pick_c = is_c.astype(b16)
    flat = jnp.ones((256, 128), b16)
    for copy in low_copies:
        copy.wait_recv()
    total = part_ref[...]
    for k in range(twins - 1):
        total = total + got_ref[0, k].astype(f32)
    part_ref[...] = total
    low_t_ref[...] = jnp.transpose(total[:, 0:128]).astype(b16)
    raw = jnp.dot(total[:, 0:128].astype(b16), dt_proj_ref[...], preferred_element_type=f32)
    step_ref[...] = raw.reshape(chunks, 16, chans)

    def step_body(i, carry):
        raw = step_ref[i] + dt_bias_ref[...]
        step = jnp.maximum(raw, 0.0) + jnp.log1p(jnp.exp(-jnp.abs(raw)))
        step_ref[i] = step
        sig_ref[i] = 1.0 / (1.0 + jnp.exp(-raw))
        dtd_ref[i] = step + jnp.concatenate([big_ref[i]] * (chans // 128), axis=1)
        u_ref[i] = step * conv_ref[i].astype(f32)
        maps = part_ref[pl.ds(pl.multiple_of(i * 16, 16), 16), 128:256]
        high = maps.astype(b16)
        low = (maps - high.astype(f32)).astype(b16)
        high = jnp.dot(repeat, high, preferred_element_type=f32)
        low = jnp.dot(repeat, low, preferred_element_type=f32)
        for target, chosen in ((b_ref, is_b), (c_ref, is_c)):
            terms = [jnp.where(chosen, term, 0.0).astype(b16) for term in (high, low)]
            found = jnp.dot(jnp.concatenate(terms, axis=1), flat, preferred_element_type=f32)
            target[pl.ds(i * 16, 16)] = found.reshape(16, n, 128)
        return carry

    lax.fori_loop(0, chunks, step_body, 0)

    def maps_block(chunk, pick):
        maps = part_ref[pl.ds(pl.multiple_of(chunk * 16, 16), 16), 128:256].astype(b16)
        found = lax.dot_general(maps, pick, nt, preferred_element_type=f32)
        return jnp.where(own, found, 0.0).astype(b16)

    ends_ref[0:n] = jnp.zeros((n, chans), f32)
    ends_ref[n : 2 * n] = jnp.ones((n, chans), f32)
    ends_ref[2 * n : 3 * n] = jnp.zeros((n, chans), f32)

    def ends_body(chunk, carry):
        for block in range(chans // lb):
            cut = slice(block * lb, (block + 1) * lb)
            rate = rate_ref[:, cut]
            h = ends_ref[0:n, cut]
            reach = ends_ref[n : 2 * n, cut]
            head = ends_ref[2 * n : 3 * n, cut]
            for t in range(16):
                decay = jnp.exp2(dtd_ref[chunk, t : t + 1, cut] * rate)
                h = decay * h + u_ref[chunk, t : t + 1, cut] * tile_lanes(b_ref[chunk * 16 + t], lb)
                reach = reach * decay
                head = head + reach * (g_ref[chunk, t : t + 1, cut] * tile_lanes(c_ref[chunk * 16 + t], lb))
            ends_ref[0:n, cut] = h
            ends_ref[n : 2 * n, cut] = reach
            ends_ref[2 * n : 3 * n, cut] = head
        return carry

    lax.fori_loop(0, chunks, ends_body, 0)
    ends_sent[0] = ends_ref[0:n].astype(b16)
    ends_sent[1] = ends_ref[2 * n : 3 * n].astype(b16)
    steps_sent[...] = jnp.sum(jnp.sum(dtd_ref[...], axis=0), axis=0, keepdims=True)
    ends_copies = []
    for k in range(1, count):
        peer = lax.rem(me + k, count)
        side = jnp.where(peer > me, 0, 1)
        ends_copies.append(
            pltpu.make_async_remote_copy(
                src_ref=ends_sent.at[side], dst_ref=ends_got.at[k - 1], send_sem=ends_send.at[k - 1],
                recv_sem=ends_recv.at[k - 1], device_id={"seq": peer}, device_id_type=MESH,
            )
        )
        ends_copies.append(
            pltpu.make_async_remote_copy(
                src_ref=steps_sent, dst_ref=steps_got.at[k - 1], send_sem=steps_send.at[k - 1],
                recv_sem=steps_recv.at[k - 1], device_id={"seq": peer}, device_id_type=MESH,
            )
        )
    for copy in ends_copies:
        copy.start()
    for copy in ends_copies:
        copy.wait_recv()

    def arrived(slots, valid):
        total = jnp.zeros((n, chans), f32)
        gap = jnp.zeros((1, chans), f32)
        for k, slot in enumerate(slots):
            term = ends_got[slot].astype(f32) * jnp.exp2(rate_ref[...] * gap)
            total = total + jnp.where(valid(k + 1), term, 0.0)
            gap = gap + steps_got[slot]
        return total

    h0_ref[...] = arrived(range(count - 1), lambda k: k <= me)
    pend_ref[...] = arrived(range(count - 2, -1, -1), lambda k: k + me < count)

    racc_ref[...] = h0_ref[...]

    def forward_body(chunk, carry):
        for block in range(chans // lb):
            cut = slice(block * lb, (block + 1) * lb)
            rate = rate_ref[:, cut]
            h = racc_ref[:, cut]
            for t in range(16):
                decay = jnp.exp2(dtd_ref[chunk, t : t + 1, cut] * rate)
                h = decay * h + u_ref[chunk, t : t + 1, cut] * tile_lanes(b_ref[chunk * 16 + t], lb)
                hist_ref[chunk, t * n : (t + 1) * n, cut] = h.astype(b16)
            racc_ref[:, cut] = h
        ssm = jnp.dot(maps_block(chunk, pick_c), hist_ref[chunk], preferred_element_type=f32)
        ssm = ssm + skip_ref[...] * conv_ref[chunk].astype(f32)
        z = z_ref[chunk].astype(f32)
        sig = 1.0 / (1.0 + jnp.exp(-z))
        rc = pl.ds(pl.multiple_of(chunk * 16, 16), 16)
        gz_ref[0, rc] = (ssm * (z * sig)).astype(b16)
        gz_ref[1, rc] = (dgated_ref[chunk] * ssm * (sig * (1.0 + z * (1.0 - sig)))).astype(b16)
        return carry

    lax.fori_loop(0, chunks, forward_body, 0)

    def ring_copy(kind, way, k):
        if k == 0:
            source = gz_ref.at[kind, pl.ds(way * half, half)]
        else:
            source = ring_ref.at[kind, way, k - 1]
        return pltpu.make_async_remote_copy(
            src_ref=source, dst_ref=ring_ref.at[kind, way, k], send_sem=ring_send.at[kind, way, k],
            recv_sem=ring_recv.at[kind, way, k], device_id={"seq": backward if way else onward}, device_id_type=MESH,
        )

    def relay(kind, k):
        for way in (0, 1):
            ring_copy(kind, way, k - 1).wait_recv()
            if k < count - 1:
                ring_copy(kind, way, k).start()

    for kind in (0, 1):
        for way in (0, 1):
            ring_copy(kind, way, 0).start()
    turns = [(kind, k) for k in range(1, count) for kind in (0, 1)]
    early = turns[:2]
    late = turns[2:]

    racc_ref[...] = jnp.zeros_like(racc_ref)

    def span_body(i, carry):
        at = spans - 1 - i
        for sub in reversed(range(span // 16)):
            chunk = at * (span // 16) + sub
            for block in range(chans // lb):
                cut = slice(block * lb, (block + 1) * lb)
                rate = rate_ref[:, cut]
                pend = pend_ref[:, cut]
                racc = racc_ref[:, cut]
                for t in reversed(range(16)):
                    decay = jnp.exp2(dtd_ref[chunk, t : t + 1, cut] * rate)
                    lam = g_ref[chunk, t : t + 1, cut] * tile_lanes(c_ref[chunk * 16 + t], lb) + pend
                    pend = decay * lam
                    if t:
                        prior = hist_ref[chunk, (t - 1) * n : t * n, cut].astype(jnp.float32)
                    else:
                        prior = hist_ref[jnp.maximum(chunk - 1, 0), 15 * n : 16 * n, cut].astype(jnp.float32)
                        prior = jnp.where(chunk == 0, h0_ref[:, cut], prior)
                    w = pend * prior
                    racc = racc + w * step_ref[chunk, t : t + 1, cut]
                    lam_ref[t * n : (t + 1) * n, cut] = lam.astype(jnp.bfloat16)
                    w_ref[t * n : (t + 1) * n, cut] = (w * rate).astype(jnp.bfloat16)
                pend_ref[:, cut] = pend
                racc_ref[:, cut] = racc
            step = step_ref[chunk]
            conv = conv_ref[chunk].astype(jnp.float32)
            adj = jnp.dot(maps_block(chunk, pick_b), lam_ref[...], preferred_element_type=jnp.float32)
            wsum = jnp.dot(ones, w_ref[...], preferred_element_type=jnp.float32)
            gstep_ref[chunk] = wsum * math.log(2.0) + adj * conv
            gscan_ref[chunk] = adj * step
            gb = lax.dot_general(u_ref[chunk].astype(jnp.bfloat16), lam_ref[...], nt, preferred_element_type=jnp.float32)
            gc = lax.dot_general(
                g_ref[chunk].astype(jnp.bfloat16), hist_ref[chunk], nt, preferred_element_type=jnp.float32
            )
            gb = jnp.where(own, gb, 0.0).astype(jnp.bfloat16)
            gc = jnp.where(own, gc, 0.0).astype(jnp.bfloat16)
            grad_ref[pl.ds(pl.multiple_of(chunk * 16, 16), 16), 128:256] = jnp.dot(
                gb, pick_b, preferred_element_type=jnp.float32
            ) + jnp.dot(gc, pick_c, preferred_element_type=jnp.float32)
        return carry

    span = 32
    spans = rows // span
    lax.fori_loop(0, spans // 2, span_body, 0)
    relay(*early[0])
    lax.fori_loop(spans // 2, spans, span_body, 0)
    relay(*early[1])

    rows_ref[...] = jnp.zeros_like(rows_ref)

    def raw_body(i, carry):
        full = gstep_ref[i] * sig_ref[i]
        rows_ref[5:6] += jnp.sum(full, axis=0, keepdims=True)
        rows_ref[6:7] += jnp.sum(g_ref[i] * conv_ref[i].astype(jnp.float32), axis=0, keepdims=True)
        gx_ref[pl.ds(pl.multiple_of(i * 16, 16), 16), :] = full.astype(jnp.bfloat16)
        return carry

    lax.fori_loop(0, chunks, raw_body, 0)
    grad_ref[:, 0:128] = lax.dot_general(gx_ref[...], dt_proj_ref[...], nt, preferred_element_type=jnp.float32)
    sent_ref[1] = grad_ref[...].astype(jnp.bfloat16)
    ch_copies = maps_copies(1, ch_send, ch_recv)
    for copy in ch_copies:
        copy.start()
    relay(*late[0])
    sum_ref[160:288] = jnp.dot(low_t_ref[...], gx_ref[...], preferred_element_type=jnp.float32)
    for copy in ch_copies:
        copy.wait_recv()
    total = grad_ref[...]
    for k in range(twins - 1):
        total = total + got_ref[1, k].astype(jnp.float32)
    grad_ref[...] = total
    relay(*late[1])

    skip = skip_ref[...]
    def pre_body(i, carry):
        rc = pl.ds(pl.multiple_of(i * 16, 16), 16)
        g_conv = jnp.dot(grad_ref[rc, :].astype(jnp.bfloat16), x_proj_ref[...], preferred_element_type=jnp.float32)
        g_conv = g_conv + skip * g_ref[i] + gscan_ref[i]
        pre = pre_ref[i]
        sig = 1.0 / (1.0 + jnp.exp(-pre))
        gpre = g_conv * sig * (1.0 + pre * (1.0 - sig))
        gpre_ref[rc, :] = gpre
        return carry

    pre_body(0, 0)
    edge_ref[...] = gpre_ref[0:8, :]
    edge_copy = pltpu.make_async_remote_copy(
        src_ref=edge_ref, dst_ref=gpre_ref.at[pl.ds(rows, 8)], send_sem=edge_send.at[0], recv_sem=edge_recv.at[0],
        device_id={"seq": before}, device_id_type=MESH,
    )
    edge_copy.start()
    lax.fori_loop(1, chunks, pre_body, 0)
    flipped = jnp.transpose(grad_ref[...]).astype(jnp.bfloat16)
    sum_ref[0:160] = jnp.dot(flipped[0:160], conv_ref[...].reshape(rows, chans), preferred_element_type=jnp.float32)
    relay(*late[2])
    edge_copy.wait_recv()

    def taps_body(block, carry):
        cut = pl.ds(pl.multiple_of(block * 128, 128), 128)
        gpre = gpre_ref[0:rows, cut]
        rows_ref[4:5, cut] = jnp.sum(gpre, axis=0, keepdims=True)
        total = jnp.zeros((rows, 128), jnp.float32)
        for k in range(4):
            lag = 3 - k
            total = total + gpre_ref[lag : lag + rows, cut] * taps_ref[k : k + 1, cut] * same_ref[3 + lag].astype(jnp.float32)
            rows_ref[k : k + 1, cut] = jnp.sum(
                gpre * ext_ref[5 + k : 5 + k + rows, cut] * same_ref[k].astype(jnp.float32), axis=0, keepdims=True
            )
        gx_ref[:, cut] = total.astype(jnp.bfloat16)
        return carry

    lax.fori_loop(0, chans // 128, taps_body, 0)
    sum_ref[288:304] = racc_ref[...] * rate_ref[...] * math.log(2.0)
    sum_ref[304:312] = rows_ref[...]
    if tall * across * depth > 312:
        sum_ref[312:] = jnp.zeros((tall * across * depth - 312, chans), jnp.float32)
    for z in range(tall):
        for x in range(across):
            first = (z * across + x) * depth
            half_ref[z, x] = sum_ref[first : first + depth].astype(jnp.bfloat16)

    def to(device):
        return dict(device_id={"seq": device}, device_id_type=MESH)

    half_copies = [
        pltpu.make_async_remote_copy(
            src_ref=half_ref.at[:, lax.rem(x_at + k, across)], dst_ref=half_got.at[k - 1], send_sem=half_send.at[k - 1],
            recv_sem=half_recv.at[k - 1], **to(z_at * across + lax.rem(x_at + k, across)),
        )
        for k in range(1, across)
    ]
    four_copies = [
        pltpu.make_async_remote_copy(
            src_ref=four_b16.at[lax.rem(z_at + k, tall)], dst_ref=four_got.at[k - 1], send_sem=four_send.at[k - 1],
            recv_sem=four_recv.at[k - 1], **to(lax.rem(z_at + k, tall) * across + x_at),
        )
        for k in range(1, tall)
    ]
    last_copies = [
        pltpu.make_async_remote_copy(
            src_ref=small_ref.at[z_at, x_at], dst_ref=small_ref.at[z_at, x_at], send_sem=last_send.at[k - 1],
            recv_sem=last_recv.at[k - 1], **to(lax.rem(z_at + k, tall) * across + x_at),
        )
        for k in range(1, tall)
    ]
    all_copies = [
        pltpu.make_async_remote_copy(
            src_ref=small_ref.at[:, x_at], dst_ref=small_ref.at[:, x_at], send_sem=all_send.at[k - 1],
            recv_sem=all_recv.at[k - 1], **to(z_at * across + lax.rem(x_at + k, across)),
        )
        for k in range(1, across)
    ]

    def small_phase(phase):
        if phase == 0:
            for copy in half_copies:
                copy.start()
        elif phase == 1:
            for copy in half_copies:
                copy.wait_recv()
            for z in range(tall):
                first = pl.multiple_of((z * across + x_at) * depth, depth)
                total = sum_ref[pl.ds(first, depth)]
                for k in range(across - 1):
                    total = total + half_got[k, z].astype(jnp.float32)
                four_ref[z] = total
                four_b16[z] = total.astype(jnp.bfloat16)
            for copy in four_copies:
                copy.start()
        elif phase == 2:
            for copy in four_copies:
                copy.wait_recv()
            total = four_ref[z_at]
            for k in range(tall - 1):
                total = total + four_got[k].astype(jnp.float32)
            small_ref[z_at, x_at] = total.astype(jnp.bfloat16)
            for copy in last_copies:
                copy.start()
        elif phase == 3:
            for copy in last_copies:
                copy.wait_recv()
            for copy in all_copies:
                copy.start()
        else:
            for copy in all_copies:
                copy.wait_recv()
            for copy in half_copies + four_copies + last_copies + all_copies:
                copy.wait_send()

    small_phase(0)
    dwo_ref[...] = jnp.zeros_like(dwo_ref)
    dwz_ref[...] = jnp.zeros_like(dwz_ref)

    def products(kind, k):
        if k == 0:
            blocks = [gz_ref[kind, way * half : (way + 1) * half] for way in (0, 1)]
        else:
            blocks = [ring_ref[kind, way, k - 1] for way in (0, 1)]
        add_products(dwz_ref if kind else dwo_ref, 1 - kind, k, cols_ref, blocks, modes_ref, ring, place, count)

    def mix_copy(j):
        return pltpu.make_async_remote_copy(
            src_ref=mix_sent.at[j], dst_ref=mix_got.at[j], send_sem=mix_send.at[j], recv_sem=mix_recv.at[j],
            device_id={"ch": lax.rem(mine + 1 + j, twins)}, device_id_type=MESH,
        )

    steps = twins * modes

    def normed_unit(j):
        for m in range(modes):
            step = j * modes + m
            if step + 1 < steps:
                in_copies(step + 1, 0)
            in_copies(step, 1)
            spread_products(in_buf.at[step % 2], gz_ref.at[1], mask_ref.at[m], pick_ref[1], gpre_ref, m, part)
        zpart_ref[j] = gpre_ref[0:rows, 0:part].astype(jnp.bfloat16)

    def mix_unit(j):
        for m in range(modes):
            step = j * modes + m
            if step + 1 < steps:
                out_copy(step + 1).start()
            out_copy(step).wait()
            mask = jnp.concatenate([mask_ref[m]] * (part // 128), axis=1) > 0
            found = lax.dot_general(gz_ref[0], out_buf[step % 2], nt, preferred_element_type=jnp.float32)
            mix_ref[...] = jnp.where(mask, found, mix_ref[...]) if m else found
        if j < twins - 1:
            mix_sent[j] = mix_ref[...].astype(jnp.bfloat16)
            mix_copy(j).start()

    edge_copy.wait_send()
    work = [lambda: small_phase(1)]
    for j in range(twins):
        work.append(functools.partial(normed_unit, j))
        work.append(functools.partial(mix_unit, j))
        if j < 3:
            work.append(functools.partial(small_phase, j + 2))
    ready = [(kind, 0) for kind in (0, 1)] + early + late[:3]
    per_turn = max(1, -(-len(work) // max(1, min(4, len(late) - 3))))
    for turn in late[3:]:
        for _ in range(per_turn):
            if work:
                work.pop(0)()
        relay(*turn)
        ready.append(turn)
        products(*ready.pop(0))
        if not work and len(ready) > 2:
            products(*ready.pop(0))
    for unit in work:
        unit()
    for turn in ready:
        products(*turn)
    for j in range(twins - 1):
        mix_copy(j).wait_recv()
        mix_ref[...] += mix_got[j].astype(jnp.float32)
    for j in range(twins - 1):
        mix_copy(j).wait_send()

    for kind in (0, 1):
        for way in (0, 1):
            for k in range(count - 1):
                ring_copy(kind, way, k).wait_send()
    for copy in ch_copies + low_copies + ends_copies:
        copy.wait_send()


def spread_products(buf, source, mask, pick, target, m, part):
    nt = (((1,), (1,)), ((), ()))
    rows = source.shape[0]
    chosen = mask[...] > 0
    for q in range(2 * part // 256):
        weights = jnp.concatenate(
            [buf.at[b].reshape(2 * part, 128)[q * 256 : (q + 1) * 256] for b in range(buf.shape[0])], axis=1
        )
        found = lax.dot_general(source[...], weights, nt, preferred_element_type=jnp.float32)
        found = jnp.dot(found.astype(jnp.bfloat16), pick, preferred_element_type=jnp.float32)
        cut = pl.ds(q * 128, 128)
        target[0:rows, cut] = jnp.where(chosen, found, target[0:rows, cut]) if m else found


def core(w_in, w_out, x, halo, z, dgated, same, big, taps, cbias, x_proj_t, dt_proj, dt_bias, a_log, skip, cols, modes, masks, pick):
    count, twins = lax.axis_size("seq"), lax.axis_size("ch")
    rows, chans = x.shape
    n = a_log.shape[0]
    chunks = rows // 16
    slab = cols.shape[4]
    width = w_out.shape[1]
    part = width // twins
    tall, across = 4, count // 4
    depth = -(-312 // (16 * count)) * 16
    vmem = pl.BlockSpec(memory_space=pltpu.VMEM)
    hbm = pl.BlockSpec(memory_space=pl.ANY)
    cube = lambda a: a.reshape((chunks, a.shape[0] // chunks) + a.shape[1:])
    f32, b16 = jnp.float32, jnp.bfloat16
    shape = jax.ShapeDtypeStruct
    dma = pltpu.SemaphoreType.DMA
    keep = pltpu.VMEM
    operands = [w_in, w_out, x, halo, cube(z), cube(dgated), same, cube(big), taps, cbias, x_proj_t, dt_proj, dt_bias, a_log,
                skip, cols, modes, masks, pick]
    block = (chunks, 16, chans)
    pair = lambda size: [dma((size,)), dma((size,))]
    return pl.pallas_call(
        functools.partial(core_kernel, (count, twins)),
        in_specs=[hbm, hbm] + [vmem] * (len(operands) - 2),
        out_specs=[vmem] * 6,
        out_shape=[
            shape((3, slab, chans), f32), shape((3, slab, chans), f32), shape((rows, chans), b16),
            shape((twins, rows, part), b16), shape((rows, part), f32), shape((tall, across, depth, chans), b16),
        ],
        scratch_shapes=[
            keep((rows + 8, chans), f32), keep(block, f32), keep(block, b16), keep(block, f32), keep(block, f32),
            keep(block, f32), keep(block, f32), keep(block, f32), keep((128, rows), b16), keep((rows, n, 128), f32),
            keep((rows, n, 128), f32), keep((n, chans), f32), keep((3 * n, chans), f32),
            keep((2, n, chans), b16), keep((count - 1, n, chans), b16), keep((1, chans), f32),
            keep((count - 1, 1, chans), f32), keep((n, chans), f32), keep((2, rows, chans), b16),
            keep((n, chans), f32), keep((8, chans), f32), keep((tall * across * depth, chans), f32),
            keep((tall, across, depth, chans), b16), keep((across - 1, tall, depth, chans), b16),
            keep((tall, depth, chans), f32), keep((tall, depth, chans), b16), keep((tall - 1, depth, chans), b16),
            keep((2, chans // 128, part, 2, 128), b16), keep((2, part, chans), b16), keep((twins - 1, rows, part), b16),
            keep((twins - 1, rows, part), b16),
            keep((2, 2, count - 1, rows // 2, chans), b16), keep((chunks, 16 * n, chans), b16), keep((16 * n, chans), b16),
            keep((16 * n, chans), b16), keep((n, chans), f32), keep(block, f32), keep(block, f32), keep((rows, 256), f32),
            keep((rows, 256), f32), keep((2, rows, 256), b16), keep((2, twins - 1, rows, 256), b16),
            keep((rows + 8, chans), f32), keep((8, chans), f32),
            dma((2, chans // 128)), dma((2,)), *pair(twins - 1), *pair(across - 1), *pair(tall - 1), *pair(tall - 1),
            *pair(across - 1), *pair(count - 1), *pair(count - 1), *pair(twins - 1),
            dma((2, 2, count - 1)), dma((2, 2, count - 1)), *pair(twins - 1), dma((1,)), dma((1,)),
        ],
        compiler_params=pltpu.CompilerParams(collective_id=2, has_side_effects=True, vmem_limit_bytes=63 << 20),
        name="core",
    )(*operands)


def tail_kernel(
    sizes, gx_ref, zpart_ref, x_ref, gain_ref, scaled_ref, mask_ref, cols_ref, modes_ref, pick_ref, w_in_ref,
    acc_ref, slice_ref, dots_ref, dgain_ref,
    ring_ref, in_buf, norm_sent, norm_got, dots_sent, dots_got, gain_sent, gain_got,
    in_sem, ring_send, ring_recv, norm_send, norm_recv, dots_send, dots_recv, gain_send, gain_recv,
):
    count, twins = sizes
    rows, chans = gx_ref.shape
    modes = mask_ref.shape[0]
    half = rows // 2
    quarter = half // 2
    width = x_ref.shape[1]
    part = width // twins
    eighths = chans // 128
    ring, place, onward, backward = ring_places(count)
    mine = lax.axis_index("ch")

    barrier = pltpu.get_barrier_semaphore()
    me = lax.axis_index("seq")
    for k in range(1, count):
        pl.semaphore_signal(barrier, inc=1, device_id={"seq": lax.rem(me + k, count)}, device_id_type=MESH)
    for k in range(1, twins):
        pl.semaphore_signal(barrier, inc=1, device_id={"ch": lax.rem(mine + k, twins)}, device_id_type=MESH)

    steps = twins * modes

    def chunk_of(step):
        return lax.rem(mine + 1 + step // modes, twins)

    def in_copy(step, b):
        slot = lax.rem(step, 2)
        features = pl.ds(pl.multiple_of(chunk_of(step) * part, part), part)
        return pltpu.make_async_copy(
            w_in_ref.at[lax.rem(step, modes), features, b], in_buf.at[slot, b], in_sem.at[slot, b]
        )

    for b in range(eighths):
        in_copy(0, b).start()
    pl.semaphore_wait(barrier, count - 1 + twins - 1)

    def ring_copy(way, piece, k):
        if k == 0:
            source = gx_ref.at[pl.ds(way * half + piece * quarter, quarter)]
        else:
            source = ring_ref.at[way, k - 1, pl.ds(piece * quarter, quarter)]
        return pltpu.make_async_remote_copy(
            src_ref=source, dst_ref=ring_ref.at[way, k, pl.ds(piece * quarter, quarter)],
            send_sem=ring_send.at[way, piece, k], recv_sem=ring_recv.at[way, piece, k],
            device_id={"seq": backward if way else onward}, device_id_type=MESH,
        )

    def relay(k):
        for piece in (0, 1):
            for way in (0, 1):
                ring_copy(way, piece, k - 1).wait_recv()
                if k < count - 1:
                    ring_copy(way, piece, k).start()

    for piece in (0, 1):
        for way in (0, 1):
            ring_copy(way, piece, 0).start()

    def peer_copy(j):
        return pltpu.make_async_remote_copy(
            src_ref=norm_sent.at[j], dst_ref=norm_got.at[j], send_sem=norm_send.at[j], recv_sem=norm_recv.at[j],
            device_id={"ch": lax.rem(mine + 1 + j, twins)}, device_id_type=MESH,
        )

    dots_ref[...] = jnp.zeros_like(dots_ref)
    for j in range(twins):
        for m in range(modes):
            step = j * modes + m
            if step + 1 < steps:
                for b in range(eighths):
                    in_copy(step + 1, b).start()
            for b in range(eighths):
                in_copy(step, b).wait()
            spread_products(in_buf.at[step % 2], gx_ref, mask_ref.at[m], pick_ref[0], slice_ref, m, part)
        for q in range(part // 128):
            lanes = slice(q * 128, (q + 1) * 128)
            cut = pl.ds(pl.multiple_of(lax.rem(mine + 1 + j, twins) * part + q * 128, 128), 128)
            found = slice_ref[:, lanes] + zpart_ref[j, :, lanes].astype(jnp.float32)
            slice_ref[:, lanes] = found
            dots_ref[...] += found * x_ref[:, cut].astype(jnp.float32) * gain_ref[:, cut]
        if j < twins - 1:
            norm_sent[j] = slice_ref[...].astype(jnp.bfloat16)
            peer_copy(j).start()
        if j < 3:
            relay(j + 1)
    dots_sent[...] = dots_ref[...].astype(jnp.bfloat16)
    dots_copies = [
        pltpu.make_async_remote_copy(
            src_ref=dots_sent, dst_ref=dots_got.at[k - 1], send_sem=dots_send.at[k - 1], recv_sem=dots_recv.at[k - 1],
            device_id={"ch": lax.rem(mine + k, twins)}, device_id_type=MESH,
        )
        for k in range(1, twins)
    ]
    for copy in dots_copies:
        copy.start()

    acc_ref[...] = jnp.zeros_like(acc_ref)

    def products(k):
        if k == 0:
            blocks = [gx_ref[way * half : (way + 1) * half] for way in (0, 1)]
        else:
            blocks = [ring_ref[way, k - 1] for way in (0, 1)]
        add_products(acc_ref, 0, k, cols_ref, blocks, modes_ref, ring, place, count)

    for k in range(min(3, twins) + 1):
        products(k)
    for j in range(twins - 1):
        peer_copy(j).wait_recv()
        slice_ref[...] += norm_got[j].astype(jnp.float32)
    dgain_ref[...] = jnp.zeros_like(dgain_ref) + jnp.sum(slice_ref[...] * scaled_ref[...], axis=0, keepdims=True)
    gain_sent[...] = dgain_ref[...]
    gain_copies = [
        pltpu.make_async_remote_copy(
            src_ref=gain_sent, dst_ref=gain_got.at[k - 1], send_sem=gain_send.at[k - 1], recv_sem=gain_recv.at[k - 1],
            device_id={"seq": lax.rem(me + k, count)}, device_id_type=MESH,
        )
        for k in range(1, count)
    ]
    for copy in gain_copies:
        copy.start()
    for k, copy in enumerate(dots_copies):
        copy.wait_recv()
        dots_ref[...] += dots_got[k].astype(jnp.float32)
    for k in range(min(3, twins) + 1, count):
        relay(k)
        products(k)

    for k, copy in enumerate(gain_copies):
        copy.wait_recv()
        dgain_ref[...] += gain_got[k]
    for way in (0, 1):
        for piece in (0, 1):
            for k in range(count - 1):
                ring_copy(way, piece, k).wait_send()
    for j in range(twins - 1):
        peer_copy(j).wait_send()
    for copy in dots_copies + gain_copies:
        copy.wait_send()


def picks():
    order = jnp.arange(256)
    return jnp.stack([order[:, None] == 2 * jnp.arange(128)[None] + j for j in (0, 1)]).astype(jnp.bfloat16)


def lane_blocks(w_in):
    kinds, width, _, chans = w_in.shape
    return w_in.reshape(kinds, width, 2, chans // 128, 128).transpose(0, 1, 3, 2, 4)


def tail(gx, zpart, x_in, gain, scaled, masks, cols, modes, pick, w_in):
    count, twins = lax.axis_size("seq"), lax.axis_size("ch")
    rows, chans = gx.shape
    width = x_in.shape[1]
    part = width // twins
    slab = cols.shape[4]
    kinds = w_in.shape[0]
    vmem = pl.BlockSpec(memory_space=pltpu.VMEM)
    hbm = pl.BlockSpec(memory_space=pl.ANY)
    f32, b16 = jnp.float32, jnp.bfloat16
    shape = jax.ShapeDtypeStruct
    dma = pltpu.SemaphoreType.DMA
    return pl.pallas_call(
        functools.partial(tail_kernel, (count, twins)),
        in_specs=[vmem] * 9 + [hbm],
        out_specs=[vmem] * 4,
        out_shape=[
            shape((kinds, slab, chans), f32), shape((rows, part), f32), shape((rows, 128), f32), shape((8, part), f32),
        ],
        scratch_shapes=[
            pltpu.VMEM((2, count - 1, rows // 2, chans), b16),
            pltpu.VMEM((2, chans // 128, part, 2, 128), b16),
            pltpu.VMEM((twins - 1, rows, part), b16),
            pltpu.VMEM((twins - 1, rows, part), b16),
            pltpu.VMEM((rows, 128), b16),
            pltpu.VMEM((twins - 1, rows, 128), b16),
            pltpu.VMEM((8, part), f32),
            pltpu.VMEM((count - 1, 8, part), f32),
            dma((2, chans // 128)), dma((2, 2, count - 1)), dma((2, 2, count - 1)), dma((twins - 1,)), dma((twins - 1,)),
            dma((twins - 1,)), dma((twins - 1,)), dma((count - 1,)), dma((count - 1,)),
        ],
        compiler_params=pltpu.CompilerParams(collective_id=3, has_side_effects=True, vmem_limit_bytes=60 << 20),
        name="tail",
    )(gx, zpart, x_in, gain.reshape(1, -1), scaled, masks, cols, modes, pick, w_in)


def weave_kernel(x_ref, z_ref, out_ref, sems):
    kinds, _, chans = x_ref.shape
    copies = []
    for m in range(kinds):
        for b in range(chans // 128):
            for j, source in enumerate((x_ref, z_ref)):
                copies.append(
                    pltpu.make_async_copy(
                        source.at[m, :, pl.ds(b * 128, 128)], out_ref.at[m, :, b, j], sems.at[len(copies)]
                    )
                )
    for copy in copies:
        copy.start()
    for copy in copies:
        copy.wait()


def weave(x_part, z_part):
    kinds, slab, chans = x_part.shape
    out = pl.pallas_call(
        weave_kernel,
        in_specs=[pl.BlockSpec(memory_space=pltpu.VMEM)] * 2,
        out_specs=pl.BlockSpec(memory_space=pl.ANY),
        out_shape=jax.ShapeDtypeStruct((kinds, slab, chans // 128, 2, 128), jnp.float32),
        scratch_shapes=[pltpu.SemaphoreType.DMA((kinds * chans // 64,))],
        compiler_params=pltpu.CompilerParams(vmem_limit_bytes=32 << 20),
        name="weave",
    )(x_part, z_part)
    return out.transpose(0, 1, 3, 2, 4).reshape(kinds, slab, 2, chans)


def shards(
    x_in,
    norm_gain,
    w_in,
    conv_weight,
    conv_bias,
    x_proj,
    dt_proj,
    dt_bias,
    a_log,
    d_skip,
    w_out,
    modes,
    doc_lengths,
    cotangent,
):
    tok_rows, model_width = x_in.shape
    mode_count = w_in.shape[0]
    seq_count = lax.axis_size("seq")
    inner_local = conv_bias.shape[0]
    conv_taps = conv_weight.shape[0]
    ch_count = lax.axis_size("ch")
    feat_part = model_width // ch_count
    seq_index = lax.axis_index("seq")
    ch_index = lax.axis_index("ch")
    first_pos = seq_index * tok_rows
    positions = first_pos + jnp.arange(tok_rows, dtype=jnp.int32)
    my_modes = lax.dynamic_slice_in_dim(modes, first_pos, tok_rows)
    onehot = (my_modes[:, None] == jnp.arange(mode_count, dtype=jnp.int32)[None]).astype(
        jnp.bfloat16
    )
    doc_index, begins = doc_tables(doc_lengths, positions)
    x_full = x_in.astype(jnp.float32)
    scale = lax.rsqrt(jnp.mean(x_full * x_full, axis=1, keepdims=True) + EPSILON)
    normed = (x_full * scale * norm_gain[None]).astype(jnp.bfloat16)
    masks = jnp.broadcast_to(onehot.T[:, :, None], (mode_count, tok_rows, 128))
    blocks = lane_blocks(w_in)
    pick = picks()
    x_branch, z_branch, d_gated, columns, halo = front(normed, masks, cotangent, blocks, w_out)
    around = jnp.arange(1 - conv_taps, tok_rows + conv_taps - 1, dtype=jnp.int32) + first_pos
    around_doc = jnp.where(around >= 0, doc_tables(doc_lengths, around)[0], -1)
    same = jnp.stack(
        [around_doc[k : k + tok_rows] == doc_index for k in range(2 * conv_taps - 1)]
    ).astype(jnp.bfloat16)
    same = jnp.broadcast_to(same[:, :, None], (2 * conv_taps - 1, tok_rows, 128))
    big = jnp.broadcast_to(jnp.where(begins, 1e30, 0.0)[:, None], (tok_rows, 128))
    mode_rows = modes.reshape(2 * seq_count, tok_rows // 2)
    x_proj_t = jnp.pad(x_proj.T, ((0, 256 - x_proj.shape[1]), (0, 0)))
    d_w_out, d_w_z, d_x_branch, zpart, mixer, smalls = core(
        blocks, w_out, x_branch, halo, z_branch, d_gated, same, big, conv_weight, conv_bias[None], x_proj_t, dt_proj,
        dt_bias[None], a_log, d_skip[None], columns, mode_rows, masks, pick,
    )
    x_slice = lax.dynamic_slice_in_dim(x_full, ch_index * feat_part, feat_part, 1)
    gain_slice = lax.dynamic_slice_in_dim(norm_gain, ch_index * feat_part, feat_part, 0)
    d_w_x, d_slice, dots, d_gain = tail(
        d_x_branch, zpart, x_in, norm_gain, x_slice * scale, masks, columns, mode_rows, pick, blocks
    )
    d_w_in = weave(d_w_x, d_w_z)
    block_out = (x_slice + mixer).astype(jnp.bfloat16)
    mean_term = (jnp.sum(dots, axis=1) / model_width)[:, None]
    weighted_slice = d_slice * gain_slice[None]
    d_x_in = cotangent.astype(jnp.float32) + scale * weighted_slice - x_slice * scale**3 * mean_term
    smalls = smalls.reshape(-1, inner_local).astype(jnp.float32)
    return (
        block_out,
        d_x_in,
        d_gain[0],
        d_w_in,
        smalls[304:308],
        smalls[308],
        smalls[:160].T,
        smalls[160:288],
        smalls[309],
        smalls[288:304],
        smalls[310],
        d_w_out,
    )


def solution(mesh):
    return jax.shard_map(
        shards,
        mesh=mesh,
        in_specs=(
            P("seq", None),
            P(),
            P(None, None, None, "ch"),
            P(None, "ch"),
            P("ch"),
            P("ch", None),
            P(None, "ch"),
            P("ch"),
            P(None, "ch"),
            P("ch"),
            P(None, None, "ch"),
            P(),
            P(),
            P("seq", "ch"),
        ),
        out_specs=(
            P("seq", "ch"),
            P("seq", "ch"),
            P("ch"),
            P(None, "seq", None, "ch"),
            P(None, "ch"),
            P("ch"),
            P("ch", None),
            P(None, "ch"),
            P("ch"),
            P(None, "ch"),
            P("ch"),
            P(None, "seq", "ch"),
        ),
        check_vma=False,
    )
```

```python
import functools
import math

import jax
import jax.numpy as jnp
from jax import lax
from jax.experimental import pallas as pl
from jax.experimental.pallas import tpu as pltpu
from jax.sharding import PartitionSpec as P

EPSILON = 1e-05


MESH = pl.DeviceIdType.MESH


def cycle_of(count):
    across = count // 4
    walk = [(0, x) for x in range(across)]
    for turn, x in enumerate(reversed(range(across))):
        column = [(z, x) for z in range(1, 4)]
        walk += column[::-1] if turn % 2 else column
    return [z * across + x for z, x in walk]


def table_of(index, values):
    picked = jnp.int32(values[0])
    for i in range(1, len(values)):
        picked = jnp.where(index == i, jnp.int32(values[i]), picked)
    return picked


def front_kernel(
    sizes, normed_ref, mask_ref, cot_ref, w_in_ref, w_out_ref,
    x_ref, z_ref, gated_ref, cotg_ref, halo_ref,
    x2_ref, halo_send, halo_recv, in_buf, out_buf, in_sem, out_sem, cot_send, cot_recv, own_sem,
):
    count, twins = sizes
    rows, width = normed_ref.shape
    modes = mask_ref.shape[0]
    part = cot_ref.shape[1]
    inner = x_ref.shape[1]
    me = lax.axis_index("seq")
    mine = lax.axis_index("ch")
    barrier = pltpu.get_barrier_semaphore()
    for peer in (lax.rem(me + 1, count), lax.rem(me + count - 1, count)):
        pl.semaphore_signal(barrier, inc=1, device_id={"seq": peer}, device_id_type=MESH)
    for k in range(1, twins):
        peer = {"ch": lax.rem(mine + k, twins)}
        pl.semaphore_signal(barrier, inc=1, device_id=peer, device_id_type=MESH)

    pairs = inner // 256
    steps = pairs * modes

    def in_copy(step, b):
        slot = lax.rem(step, 2)
        return pltpu.make_async_copy(
            w_in_ref.at[lax.rem(step, modes), :, step // modes * 2 + b], in_buf.at[slot, b], in_sem.at[slot, b]
        )

    wide = out_buf.shape[2]
    out_steps = inner // wide * modes

    def out_copy(step):
        slot = lax.rem(step, 2)
        columns = pl.ds(pl.multiple_of(step // modes * wide, wide), wide)
        return pltpu.make_async_copy(
            w_out_ref.at[lax.rem(step, modes), :, columns], out_buf.at[slot], out_sem.at[slot]
        )

    for b in (0, 1):
        in_copy(0, b).start()
    out_copy(0).start()
    pl.semaphore_wait(barrier, 2 + twins - 1)

    cot_copies = [
        pltpu.make_async_remote_copy(
            src_ref=cot_ref, dst_ref=cotg_ref.at[mine], send_sem=cot_send.at[k - 1], recv_sem=cot_recv.at[k - 1],
            device_id={"ch": lax.rem(mine + k, twins)}, device_id_type=MESH,
        )
        for k in range(1, twins)
    ]
    for copy in cot_copies:
        copy.start()
    own_copy = pltpu.make_async_copy(cot_ref, cotg_ref.at[mine], own_sem.at[0])
    own_copy.start()
    def in_step(step, carry):
        slot = lax.rem(step, 2)
        mode = lax.rem(step, modes)

        @pl.when(step + 1 < steps)
        def _():
            for b in (0, 1):
                in_copy(step + 1, b).start()

        for b in (0, 1):
            in_copy(step, b).wait()
        weights = jnp.concatenate([in_buf.at[slot, b].reshape(2 * width, 128)[...] for b in (0, 1)], axis=1)
        mask = jnp.concatenate([mask_ref[mode]] * 2, axis=1) > 0
        columns = pl.ds(pl.multiple_of(step // modes * 256, 256), 256)
        for j, target in enumerate((x_ref, z_ref)):
            found = jnp.dot(x2_ref[j], weights, preferred_element_type=jnp.float32).astype(jnp.bfloat16)
            target[:, columns] = jnp.where(mask, found, target[:, columns])
        return carry

    x_ref[...] = jnp.zeros_like(x_ref)
    z_ref[...] = jnp.zeros_like(z_ref)
    row = lax.broadcasted_iota(jnp.int32, (256, 512), 0)
    column = lax.broadcasted_iota(jnp.int32, (256, 512), 1)
    for j in (0, 1):
        spread = (column == 2 * row + j).astype(jnp.bfloat16)
        for block in range(width // 256):
            x2_ref[j, :, block * 512 : (block + 1) * 512] = jnp.dot(
                normed_ref[:, block * 256 : (block + 1) * 256], spread, preferred_element_type=jnp.float32
            ).astype(jnp.bfloat16)
    lax.fori_loop(0, steps, in_step, 0)
    halo_copy = pltpu.make_async_remote_copy(
        src_ref=x_ref.at[pl.ds(rows - 16, 16)], dst_ref=halo_ref, send_sem=halo_send.at[0], recv_sem=halo_recv.at[0],
        device_id={"seq": lax.rem(me + 1, count)}, device_id_type=MESH,
    )
    halo_copy.start()
    own_copy.wait()
    for copy in cot_copies:
        copy.wait_recv()

    def out_step(step, carry):
        slot = lax.rem(step, 2)
        mode = lax.rem(step, modes)

        @pl.when(step + 1 < out_steps)
        def _():
            out_copy(step + 1).start()

        out_copy(step).wait()
        mask = jnp.concatenate([mask_ref[mode]] * (wide // 128), axis=1) > 0
        columns = pl.ds(pl.multiple_of(step // modes * wide, wide), wide)
        found = jnp.zeros((rows, wide), jnp.float32)
        for c in range(twins):
            found = found + jnp.dot(
                cotg_ref[c], out_buf[slot, c * part : (c + 1) * part], preferred_element_type=jnp.float32
            )
        gated_ref[:, columns] = jnp.where(mask, found, gated_ref[:, columns])
        return carry

    gated_ref[...] = jnp.zeros_like(gated_ref)
    lax.fori_loop(0, out_steps, out_step, 0)
    halo_copy.wait_recv()
    for copy in cot_copies + [halo_copy]:
        copy.wait_send()


def front(normed, masks, cot, w_in, w_out):
    count, twins = lax.axis_size("seq"), lax.axis_size("ch")
    rows, width = normed.shape
    inner = w_out.shape[2]
    modes = w_out.shape[0]
    vmem = pl.BlockSpec(memory_space=pltpu.VMEM)
    hbm = pl.BlockSpec(memory_space=pl.ANY)
    wide = min(512, inner)
    return pl.pallas_call(
        functools.partial(front_kernel, (count, twins)),
        in_specs=[vmem, vmem, vmem, hbm, hbm],
        out_specs=[vmem] * 5,
        out_shape=[
            jax.ShapeDtypeStruct((rows, inner), jnp.bfloat16),
            jax.ShapeDtypeStruct((rows, inner), jnp.bfloat16),
            jax.ShapeDtypeStruct((rows, inner), jnp.float32),
            jax.ShapeDtypeStruct((twins,) + cot.shape, jnp.bfloat16),
            jax.ShapeDtypeStruct((16, inner), jnp.bfloat16),
        ],
        scratch_shapes=[
            pltpu.VMEM((2, rows, 2 * width), jnp.bfloat16),
            pltpu.SemaphoreType.DMA((1,)),
            pltpu.SemaphoreType.DMA((1,)),
            pltpu.VMEM((2, 2, width, 2, 128), jnp.bfloat16),
            pltpu.VMEM((2, width, wide), jnp.bfloat16),
            pltpu.SemaphoreType.DMA((2, 2)),
            pltpu.SemaphoreType.DMA((2,)),
            pltpu.SemaphoreType.DMA((twins - 1,)),
            pltpu.SemaphoreType.DMA((twins - 1,)),
            pltpu.SemaphoreType.DMA((1,)),
        ],
        compiler_params=pltpu.CompilerParams(collective_id=1, has_side_effects=True, vmem_limit_bytes=56 << 20),
        name="front",
    )(normed, masks, cot, w_in, w_out)


def doc_tables(doc_lengths, positions):
    count = doc_lengths.shape[0]
    order = jnp.arange(count, dtype=jnp.int32)
    doc_ends = jnp.sum(jnp.where(order[:, None] >= order[None, :], doc_lengths[None, :], 0), axis=1)
    doc_starts = doc_ends - doc_lengths
    doc_index = jnp.sum((positions[:, None] >= doc_ends[None, :]).astype(jnp.int32), axis=1)
    begins = jnp.any(positions[:, None] == doc_starts[None, :], axis=1)
    return (doc_index, begins)


def tile_lanes(v, lanes):
    return jnp.concatenate([v] * (lanes // 128), axis=1)

def ring_places(count):
    ring = cycle_of(count)
    where = {s: i for i, s in enumerate(ring)}
    me = lax.axis_index("seq")
    onward = table_of(me, [ring[(where[s] + 1) % count] for s in range(count)])
    backward = table_of(me, [ring[(where[s] - 1) % count] for s in range(count)])
    place = table_of(me, [where[s] for s in range(count)])
    return ring, place, onward, backward


def add_products(accs, kind, k, cols_ref, blocks, modes_ref, ring, place, count):
    parts = []
    for way in (0, 1):
        step = k if way else count - k
        source = table_of(lax.rem(place + step, count), ring)
        parts.append((jnp.transpose(cols_ref[kind, way, k]), modes_ref[pl.ds(2 * source + way, 1), :]))
    right = jnp.concatenate(blocks, axis=0)
    for m, acc in enumerate(accs):
        left = jnp.concatenate(
            [part * jnp.where(row == m, 1.0, 0.0).astype(jnp.bfloat16) for part, row in parts], axis=1
        )
        found = jnp.dot(left, right, preferred_element_type=jnp.float32)
        acc[...] += found.reshape(acc.shape)


def core_kernel(
    sizes, w_in_ref, w_out_ref, normed_ref, cotg_ref, x_ref, halo_ref, z_ref, dgated_ref, same_ref, big_ref, taps_ref,
    cbias_ref, x_proj_ref, dt_proj_ref, dt_bias_ref, a_log_ref, skip_ref, modes_ref, mask_ref, pick_ref, x_in_ref, gain_ref,
    scaled_ref,
    dwo_ref, dwz_ref, dwx_ref, mix_ref, small_ref, slice_ref, dots_ref, dgain_ref,
    free_sem, ext_ref, pre_ref, conv_ref, g_ref, step_ref, dtd_ref, u_ref, sig_ref, low_t_ref, b_ref, c_ref, rate_ref, ends_ref,
    ends_sent, ends_got, steps_sent, steps_got, h0_ref, gz_ref, gx_ref, cols_ref,
    racc_ref, rows_ref, sum_ref, half_ref, half_got, four_ref, four_b16, four_got, in_buf, out_buf, mix_sent, mix_got,
    norm_sent, norm_got, dots_sent, dots_got, gain_sent, gain_got,
    ring_ref, hist_ref, lam_ref, w_ref, pend_ref, gstep_ref, gscan_ref, part_ref, grad_ref, sent_ref, got_ref,
    gpre_ref, edge_ref,
    in_sem, out_sem, mix_send, mix_recv, half_send, half_recv, four_send, four_recv, last_send, last_recv, all_send, all_recv,
    ends_send, ends_recv, steps_send, steps_recv, low_send, low_recv, norm_send, norm_recv, dots_send, dots_recv,
    gain_send, gain_recv, seq_send, seq_recv, twin_send, twin_recv, own_sem, dwo_sem,
    ring_send, ring_recv, gx_send, gx_recv, ch_send, ch_recv, edge_send, edge_recv,
):
    count, twins = sizes
    chunks, _, chans = pre_ref.shape
    rows = chunks * 16
    n = a_log_ref.shape[0]
    half = rows // 2
    ring, place, onward, backward = ring_places(count)
    me = lax.axis_index("seq")
    mine = lax.axis_index("ch")
    before = lax.rem(me + count - 1, count)
    nt = (((1,), (1,)), ((), ()))
    f32, b16 = jnp.float32, jnp.bfloat16
    lb = min(512, chans)

    modes = mask_ref.shape[0]
    width = w_out_ref.shape[1]
    part = width // twins
    eighths = chans // 128
    across = half_ref.shape[1]
    tall = half_ref.shape[0]
    depth = half_ref.shape[2]
    z_at = me // across
    x_at = lax.rem(me, across)

    def chunk_of(step):
        return pl.ds(pl.multiple_of(lax.rem(mine + 1 + step // modes, twins) * part, part), part)

    def in_copy(step, b):
        slot = step % 2
        return pltpu.make_async_copy(w_in_ref.at[step % modes, chunk_of(step), b], in_buf.at[slot, b], in_sem.at[slot, b])

    def in_copies(step, wait):
        for b in range(eighths):
            if wait:
                in_copy(step, b).wait()
            else:
                in_copy(step, b).start()

    def out_copy(step):
        slot = step % 2
        return pltpu.make_async_copy(w_out_ref.at[step % modes, chunk_of(step)], out_buf.at[slot], out_sem.at[slot])

    barrier = pltpu.get_barrier_semaphore()
    for k in range(1, count):
        pl.semaphore_signal(barrier, inc=1, device_id={"seq": lax.rem(me + k, count)}, device_id_type=MESH)
    for k in range(1, twins):
        peer = {"ch": lax.rem(mine + k, twins)}
        pl.semaphore_signal(barrier, inc=1, device_id=peer, device_id_type=MESH)
    in_copies(0, 0)
    out_copy(0).start()
    pl.semaphore_wait(barrier, count - 1 + twins - 1)

    slab = cols_ref.shape[4]
    side = lax.rem(mine, 2)
    twin = mine + 1 - 2 * side
    side_rows = pl.ds(pl.multiple_of(side * half, half), half)

    def column_source(kind, owner, those):
        if kind == 0:
            return normed_ref.at[those, pl.ds(pl.multiple_of(owner * slab, slab), slab)]
        return cotg_ref.at[owner * slab // part, those, pl.ds(pl.multiple_of(lax.rem(owner * slab, part), slab), slab)]

    own_columns = [
        pltpu.make_async_copy(
            column_source(kind, me, pl.ds(way * half, half)), cols_ref.at[kind, way, 0], own_sem.at[kind, way]
        )
        for kind in (0, 1)
        for way in (0, 1)
    ]
    seq_copies = []
    for kind in (0, 1):
        for k in range(1, count):
            peer = table_of(lax.rem(place + jnp.where(side == 0, k, count - k), count), ring)
            seq_copies.append(
                pltpu.make_async_remote_copy(
                    src_ref=column_source(kind, peer, side_rows), dst_ref=cols_ref.at[kind, side, k],
                    send_sem=seq_send.at[kind, k - 1], recv_sem=seq_recv.at[kind, k - 1], device_id={"seq": peer},
                    device_id_type=MESH,
                )
            )
    for copy in own_columns + seq_copies:
        copy.start()
    twin_copies = [
        pltpu.make_async_remote_copy(
            src_ref=cols_ref.at[kind, side, pl.ds(1, count - 1)], dst_ref=cols_ref.at[kind, side, pl.ds(1, count - 1)],
            send_sem=twin_send.at[kind], recv_sem=twin_recv.at[kind], device_id={"ch": twin}, device_id_type=MESH,
        )
        for kind in (0, 1)
    ]

    ext_ref[0:8] = halo_ref[8:16].astype(f32)
    ext_ref[8:] = x_ref[...].astype(f32)

    def conv_body(block, carry):
        cut = pl.ds(pl.multiple_of(block * 128, 128), 128)
        pre = jnp.zeros((rows, 128), f32) + cbias_ref[:, cut]
        for k in range(4):
            pre = pre + taps_ref[k : k + 1, cut] * ext_ref[5 + k : 5 + k + rows, cut] * same_ref[k].astype(f32)
        pre_ref[:, :, cut] = pre.reshape(chunks, 16, 128)
        conv_ref[:, :, cut] = (pre / (1.0 + jnp.exp(-pre))).astype(b16).reshape(chunks, 16, 128)
        return carry

    lax.fori_loop(0, chans // 128, conv_body, 0)
    part_ref[...] = lax.dot_general(
        conv_ref[...].reshape(rows, chans), x_proj_ref[...], nt, preferred_element_type=f32
    )
    sent_ref[0] = part_ref[...].astype(b16)

    def maps_copies(which, send, recv):
        return [
            pltpu.make_async_remote_copy(
                src_ref=sent_ref.at[which], dst_ref=got_ref.at[which, k - 1], send_sem=send.at[k - 1],
                recv_sem=recv.at[k - 1], device_id={"ch": lax.rem(mine + k, twins)}, device_id_type=MESH,
            )
            for k in range(1, twins)
        ]

    low_copies = maps_copies(0, low_send, low_recv)
    for copy in low_copies:
        copy.start()

    def gate_body(i, carry):
        z = z_ref[i].astype(f32)
        g_ref[i] = dgated_ref[i] * (z / (1.0 + jnp.exp(-z)))
        return carry

    lax.fori_loop(0, chunks, gate_body, 0)
    rate_ref[...] = -math.log2(math.e) * jnp.exp(a_log_ref[...])
    own = (
        lax.broadcasted_iota(jnp.int32, (16, 16 * n), 1) // n == lax.broadcasted_iota(jnp.int32, (16, 16 * n), 0)
    )
    ones = own.astype(b16)
    token_row = lax.broadcasted_iota(jnp.int32, (16 * n, 16), 0) // n
    repeat = (token_row == lax.broadcasted_iota(jnp.int32, (16 * n, 16), 1)).astype(b16)
    pick_row = lax.broadcasted_iota(jnp.int32, (16 * n, 128), 0)
    pick_col = lax.broadcasted_iota(jnp.int32, (16 * n, 128), 1)
    is_b = pick_row % n == pick_col
    is_c = pick_row % n + n == pick_col
    pick_b = is_b.astype(b16)
    pick_c = is_c.astype(b16)
    flat = jnp.ones((256, 128), b16)
    for copy in low_copies:
        copy.wait_recv()
    total = part_ref[...]
    for k in range(twins - 1):
        total = total + got_ref[0, k].astype(f32)
    part_ref[...] = total
    low_t_ref[...] = jnp.transpose(total[:, 0:128]).astype(b16)
    raw = jnp.dot(total[:, 0:128].astype(b16), dt_proj_ref[...], preferred_element_type=f32)
    step_ref[...] = raw.reshape(chunks, 16, chans)

    def step_body(i, carry):
        raw = step_ref[i] + dt_bias_ref[...]
        step = jnp.maximum(raw, 0.0) + jnp.log1p(jnp.exp(-jnp.abs(raw)))
        step_ref[i] = step
        sig_ref[i] = 1.0 / (1.0 + jnp.exp(-raw))
        dtd_ref[i] = step + jnp.concatenate([big_ref[i]] * (chans // 128), axis=1)
        u_ref[i] = step * conv_ref[i].astype(f32)
        maps = part_ref[pl.ds(pl.multiple_of(i * 16, 16), 16), 128:256]
        high = maps.astype(b16)
        low = (maps - high.astype(f32)).astype(b16)
        high = jnp.dot(repeat, high, preferred_element_type=f32)
        low = jnp.dot(repeat, low, preferred_element_type=f32)
        for target, chosen in ((b_ref, is_b), (c_ref, is_c)):
            terms = [jnp.where(chosen, term, 0.0).astype(b16) for term in (high, low)]
            found = jnp.dot(jnp.concatenate(terms, axis=1), flat, preferred_element_type=f32)
            target[pl.ds(i * 16, 16)] = found.reshape(16, n, 128)
        return carry

    lax.fori_loop(0, chunks, step_body, 0)

    def maps_block(chunk, pick):
        maps = part_ref[pl.ds(pl.multiple_of(chunk * 16, 16), 16), 128:256].astype(b16)
        found = lax.dot_general(maps, pick, nt, preferred_element_type=f32)
        return jnp.where(own, found, 0.0).astype(b16)

    ends_ref[0:n] = jnp.zeros((n, chans), f32)
    ends_ref[n : 2 * n] = jnp.ones((n, chans), f32)
    ends_ref[2 * n : 3 * n] = jnp.zeros((n, chans), f32)

    def ends_body(chunk, carry):
        for block in range(chans // lb):
            cut = slice(block * lb, (block + 1) * lb)
            rate = rate_ref[:, cut]
            h = ends_ref[0:n, cut]
            reach = ends_ref[n : 2 * n, cut]
            head = ends_ref[2 * n : 3 * n, cut]
            for t in range(16):
                decay = jnp.exp2(dtd_ref[chunk, t : t + 1, cut] * rate)
                h = decay * h + u_ref[chunk, t : t + 1, cut] * tile_lanes(b_ref[chunk * 16 + t], lb)
                reach = reach * decay
                head = head + reach * (g_ref[chunk, t : t + 1, cut] * tile_lanes(c_ref[chunk * 16 + t], lb))
            ends_ref[0:n, cut] = h
            ends_ref[n : 2 * n, cut] = reach
            ends_ref[2 * n : 3 * n, cut] = head
        return carry

    lax.fori_loop(0, chunks, ends_body, 0)
    ends_sent[0] = ends_ref[0:n].astype(b16)
    ends_sent[1] = ends_ref[2 * n : 3 * n].astype(b16)
    steps_sent[...] = jnp.sum(jnp.sum(dtd_ref[...], axis=0), axis=0, keepdims=True)
    ends_copies = []
    for k in range(1, count):
        peer = lax.rem(me + k, count)
        side = jnp.where(peer > me, 0, 1)
        ends_copies.append(
            pltpu.make_async_remote_copy(
                src_ref=ends_sent.at[side], dst_ref=ends_got.at[k - 1], send_sem=ends_send.at[k - 1],
                recv_sem=ends_recv.at[k - 1], device_id={"seq": peer}, device_id_type=MESH,
            )
        )
        ends_copies.append(
            pltpu.make_async_remote_copy(
                src_ref=steps_sent, dst_ref=steps_got.at[k - 1], send_sem=steps_send.at[k - 1],
                recv_sem=steps_recv.at[k - 1], device_id={"seq": peer}, device_id_type=MESH,
            )
        )
    for copy in ends_copies:
        copy.start()
    for copy in ends_copies:
        copy.wait_recv()

    def arrived(slots, valid):
        total = jnp.zeros((n, chans), f32)
        gap = jnp.zeros((1, chans), f32)
        for k, slot in enumerate(slots):
            term = ends_got[slot].astype(f32) * jnp.exp2(rate_ref[...] * gap)
            total = total + jnp.where(valid(k + 1), term, 0.0)
            gap = gap + steps_got[slot]
        return total

    h0_ref[...] = arrived(range(count - 1), lambda k: k <= me)
    pend_ref[...] = arrived(range(count - 2, -1, -1), lambda k: k + me < count)

    racc_ref[...] = h0_ref[...]

    def forward_body(chunk, carry):
        for block in range(chans // lb):
            cut = slice(block * lb, (block + 1) * lb)
            rate = rate_ref[:, cut]
            h = racc_ref[:, cut]
            for t in range(16):
                decay = jnp.exp2(dtd_ref[chunk, t : t + 1, cut] * rate)
                h = decay * h + u_ref[chunk, t : t + 1, cut] * tile_lanes(b_ref[chunk * 16 + t], lb)
                hist_ref[chunk, t * n : (t + 1) * n, cut] = h.astype(b16)
            racc_ref[:, cut] = h
        ssm = jnp.dot(maps_block(chunk, pick_c), hist_ref[chunk], preferred_element_type=f32)
        ssm = ssm + skip_ref[...] * conv_ref[chunk].astype(f32)
        z = z_ref[chunk].astype(f32)
        sig = 1.0 / (1.0 + jnp.exp(-z))
        rc = pl.ds(pl.multiple_of(chunk * 16, 16), 16)
        gz_ref[0, rc] = (ssm * (z * sig)).astype(b16)
        gz_ref[1, rc] = (dgated_ref[chunk] * ssm * (sig * (1.0 + z * (1.0 - sig)))).astype(b16)
        return carry

    lax.fori_loop(0, chunks, forward_body, 0)

    def ring_copy(kind, way, k):
        if k == 0:
            source = gz_ref.at[kind, pl.ds(way * half, half)]
        else:
            source = ring_ref.at[kind, way, k - 1]
        return pltpu.make_async_remote_copy(
            src_ref=source, dst_ref=ring_ref.at[kind, way, k], send_sem=ring_send.at[kind, way, k],
            recv_sem=ring_recv.at[kind, way, k], device_id={"seq": backward if way else onward}, device_id_type=MESH,
        )

    def relay(kind, k):
        for way in (0, 1):
            if kind == 2:
                gx_copy(way, k - 1).wait_recv()
                if k < count - 1:
                    gx_copy(way, k).start()
            else:
                ring_copy(kind, way, k - 1).wait_recv()
                if k < count - 1:
                    ring_copy(kind, way, k).start()

    def gx_slot(way, k):
        slot = way * (count - 1) + k
        return hist_ref.at[slot // 2, pl.ds(slot % 2 * half, half)]

    def gx_copy(way, k):
        return pltpu.make_async_remote_copy(
            src_ref=gx_slot(way, k - 1) if k else gx_ref.at[pl.ds(way * half, half)], dst_ref=gx_slot(way, k),
            send_sem=gx_send.at[way, k], recv_sem=gx_recv.at[way, k], device_id={"seq": backward if way else onward},
            device_id_type=MESH,
        )

    for kind in (0, 1):
        for way in (0, 1):
            ring_copy(kind, way, 0).start()
    turns = [(kind, k) for k in range(1, count) for kind in (0, 1)]
    early = turns[:2]
    late = turns[2:]

    racc_ref[...] = jnp.zeros_like(racc_ref)

    def span_body(i, carry):
        at = spans - 1 - i
        for sub in reversed(range(span // 16)):
            chunk = at * (span // 16) + sub
            for block in range(chans // lb):
                cut = slice(block * lb, (block + 1) * lb)
                rate = rate_ref[:, cut]
                pend = pend_ref[:, cut]
                racc = racc_ref[:, cut]
                for t in reversed(range(16)):
                    decay = jnp.exp2(dtd_ref[chunk, t : t + 1, cut] * rate)
                    lam = g_ref[chunk, t : t + 1, cut] * tile_lanes(c_ref[chunk * 16 + t], lb) + pend
                    pend = decay * lam
                    if t:
                        prior = hist_ref[chunk, (t - 1) * n : t * n, cut].astype(jnp.float32)
                    else:
                        prior = hist_ref[jnp.maximum(chunk - 1, 0), 15 * n : 16 * n, cut].astype(jnp.float32)
                        prior = jnp.where(chunk == 0, h0_ref[:, cut], prior)
                    w = pend * prior
                    racc = racc + w * step_ref[chunk, t : t + 1, cut]
                    lam_ref[t * n : (t + 1) * n, cut] = lam.astype(jnp.bfloat16)
                    w_ref[t * n : (t + 1) * n, cut] = (w * rate).astype(jnp.bfloat16)
                pend_ref[:, cut] = pend
                racc_ref[:, cut] = racc
            step = step_ref[chunk]
            conv = conv_ref[chunk].astype(jnp.float32)
            adj = jnp.dot(maps_block(chunk, pick_b), lam_ref[...], preferred_element_type=jnp.float32)
            wsum = jnp.dot(ones, w_ref[...], preferred_element_type=jnp.float32)
            gstep_ref[chunk] = wsum * math.log(2.0) + adj * conv
            gscan_ref[chunk] = adj * step
            gb = lax.dot_general(u_ref[chunk].astype(jnp.bfloat16), lam_ref[...], nt, preferred_element_type=jnp.float32)
            gc = lax.dot_general(
                g_ref[chunk].astype(jnp.bfloat16), hist_ref[chunk], nt, preferred_element_type=jnp.float32
            )
            gb = jnp.where(own, gb, 0.0).astype(jnp.bfloat16)
            gc = jnp.where(own, gc, 0.0).astype(jnp.bfloat16)
            grad_ref[pl.ds(pl.multiple_of(chunk * 16, 16), 16), 128:256] = jnp.dot(
                gb, pick_b, preferred_element_type=jnp.float32
            ) + jnp.dot(gc, pick_c, preferred_element_type=jnp.float32)
        return carry

    span = 32
    spans = rows // span
    lax.fori_loop(0, spans // 2, span_body, 0)
    relay(*early[0])
    for copy in seq_copies:
        copy.wait_recv()
    for copy in twin_copies:
        copy.start()
    lax.fori_loop(spans // 2, spans, span_body, 0)
    for peer in (onward, backward):
        pl.semaphore_signal(free_sem, inc=1, device_id={"seq": peer}, device_id_type=MESH)
    relay(*early[1])

    rows_ref[...] = jnp.zeros_like(rows_ref)

    def raw_body(i, carry):
        full = gstep_ref[i] * sig_ref[i]
        rows_ref[5:6] += jnp.sum(full, axis=0, keepdims=True)
        rows_ref[6:7] += jnp.sum(g_ref[i] * conv_ref[i].astype(jnp.float32), axis=0, keepdims=True)
        gx_ref[pl.ds(pl.multiple_of(i * 16, 16), 16), :] = full.astype(jnp.bfloat16)
        return carry

    lax.fori_loop(0, chunks, raw_body, 0)
    grad_ref[:, 0:128] = lax.dot_general(gx_ref[...], dt_proj_ref[...], nt, preferred_element_type=jnp.float32)
    sent_ref[1] = grad_ref[...].astype(jnp.bfloat16)
    ch_copies = maps_copies(1, ch_send, ch_recv)
    for copy in ch_copies:
        copy.start()
    relay(*late[0])
    sum_ref[160:288] = jnp.dot(low_t_ref[...], gx_ref[...], preferred_element_type=jnp.float32)
    for copy in ch_copies:
        copy.wait_recv()
    total = grad_ref[...]
    for k in range(twins - 1):
        total = total + got_ref[1, k].astype(jnp.float32)
    grad_ref[...] = total
    relay(*late[1])

    skip = skip_ref[...]
    def pre_body(i, carry):
        rc = pl.ds(pl.multiple_of(i * 16, 16), 16)
        g_conv = jnp.dot(grad_ref[rc, :].astype(jnp.bfloat16), x_proj_ref[...], preferred_element_type=jnp.float32)
        g_conv = g_conv + skip * g_ref[i] + gscan_ref[i]
        pre = pre_ref[i]
        sig = 1.0 / (1.0 + jnp.exp(-pre))
        gpre = g_conv * sig * (1.0 + pre * (1.0 - sig))
        gpre_ref[rc, :] = gpre
        return carry

    pre_body(0, 0)
    edge_ref[...] = gpre_ref[0:8, :]
    edge_copy = pltpu.make_async_remote_copy(
        src_ref=edge_ref, dst_ref=gpre_ref.at[pl.ds(rows, 8)], send_sem=edge_send.at[0], recv_sem=edge_recv.at[0],
        device_id={"seq": before}, device_id_type=MESH,
    )
    edge_copy.start()
    lax.fori_loop(1, chunks, pre_body, 0)
    flipped = jnp.transpose(grad_ref[...]).astype(jnp.bfloat16)
    sum_ref[0:160] = jnp.dot(flipped[0:160], conv_ref[...].reshape(rows, chans), preferred_element_type=jnp.float32)
    relay(*late[2])
    edge_copy.wait_recv()

    def taps_body(block, carry):
        cut = pl.ds(pl.multiple_of(block * 128, 128), 128)
        gpre = gpre_ref[0:rows, cut]
        rows_ref[4:5, cut] = jnp.sum(gpre, axis=0, keepdims=True)
        total = jnp.zeros((rows, 128), jnp.float32)
        for k in range(4):
            lag = 3 - k
            total = total + gpre_ref[lag : lag + rows, cut] * taps_ref[k : k + 1, cut] * same_ref[3 + lag].astype(jnp.float32)
            rows_ref[k : k + 1, cut] = jnp.sum(
                gpre * ext_ref[5 + k : 5 + k + rows, cut] * same_ref[k].astype(jnp.float32), axis=0, keepdims=True
            )
        gx_ref[:, cut] = total.astype(jnp.bfloat16)
        return carry

    lax.fori_loop(0, chans // 128, taps_body, 0)
    pl.semaphore_wait(free_sem, 2)
    for way in (0, 1):
        gx_copy(way, 0).start()
    sum_ref[288:304] = racc_ref[...] * rate_ref[...] * math.log(2.0)
    sum_ref[304:312] = rows_ref[...]
    if tall * across * depth > 312:
        sum_ref[312:] = jnp.zeros((tall * across * depth - 312, chans), jnp.float32)
    for z in range(tall):
        for x in range(across):
            first = (z * across + x) * depth
            half_ref[z, x] = sum_ref[first : first + depth].astype(jnp.bfloat16)

    def to(device):
        return dict(device_id={"seq": device}, device_id_type=MESH)

    half_copies = [
        pltpu.make_async_remote_copy(
            src_ref=half_ref.at[:, lax.rem(x_at + k, across)], dst_ref=half_got.at[k - 1], send_sem=half_send.at[k - 1],
            recv_sem=half_recv.at[k - 1], **to(z_at * across + lax.rem(x_at + k, across)),
        )
        for k in range(1, across)
    ]
    four_copies = [
        pltpu.make_async_remote_copy(
            src_ref=four_b16.at[lax.rem(z_at + k, tall)], dst_ref=four_got.at[k - 1], send_sem=four_send.at[k - 1],
            recv_sem=four_recv.at[k - 1], **to(lax.rem(z_at + k, tall) * across + x_at),
        )
        for k in range(1, tall)
    ]
    last_copies = [
        pltpu.make_async_remote_copy(
            src_ref=small_ref.at[z_at, x_at], dst_ref=small_ref.at[z_at, x_at], send_sem=last_send.at[k - 1],
            recv_sem=last_recv.at[k - 1], **to(lax.rem(z_at + k, tall) * across + x_at),
        )
        for k in range(1, tall)
    ]
    all_copies = [
        pltpu.make_async_remote_copy(
            src_ref=small_ref.at[:, x_at], dst_ref=small_ref.at[:, x_at], send_sem=all_send.at[k - 1],
            recv_sem=all_recv.at[k - 1], **to(z_at * across + lax.rem(x_at + k, across)),
        )
        for k in range(1, across)
    ]

    def small_phase(phase):
        if phase == 0:
            for copy in half_copies:
                copy.start()
        elif phase == 1:
            for copy in half_copies:
                copy.wait_recv()
            for z in range(tall):
                first = pl.multiple_of((z * across + x_at) * depth, depth)
                total = sum_ref[pl.ds(first, depth)]
                for k in range(across - 1):
                    total = total + half_got[k, z].astype(jnp.float32)
                four_ref[z] = total
                four_b16[z] = total.astype(jnp.bfloat16)
            for copy in four_copies:
                copy.start()
        elif phase == 2:
            for copy in four_copies:
                copy.wait_recv()
            total = four_ref[z_at]
            for k in range(tall - 1):
                total = total + four_got[k].astype(jnp.float32)
            small_ref[z_at, x_at] = total.astype(jnp.bfloat16)
            for copy in last_copies:
                copy.start()
        elif phase == 3:
            for copy in last_copies:
                copy.wait_recv()
            for copy in all_copies:
                copy.start()
        else:
            for copy in all_copies:
                copy.wait_recv()
            for copy in half_copies + four_copies + last_copies + all_copies:
                copy.wait_send()

    small_phase(0)
    dwo_accs = [ref.at[0 : slab // 16] for ref in (dtd_ref, u_ref, sig_ref)]
    dwz_accs = [ref.at[0 : slab // 16] for ref in (step_ref, g_ref, gscan_ref)]
    dwx_accs = [dwx_ref.at[m] for m in range(modes)]
    for acc in dwo_accs + dwz_accs + dwx_accs:
        acc[...] = jnp.zeros_like(acc)

    def products(kind, k):
        if k == 0:
            source = gx_ref if kind == 2 else gz_ref.at[kind]
            blocks = [source[way * half : (way + 1) * half] for way in (0, 1)]
        else:
            blocks = [gx_slot(way, k - 1)[...] if kind == 2 else ring_ref[kind, way, k - 1] for way in (0, 1)]
        accs = (dwo_accs, dwz_accs, dwx_accs)[kind]
        add_products(accs, 0 if kind else 1, k, cols_ref, blocks, modes_ref, ring, place, count)
        if kind < 2 and k == count - 1:
            for copy in out_copies[kind]:
                copy.start()

    out_copies = [
        [pltpu.make_async_copy(acc, target.at[m], dwo_sem.at[kind, m]) for m, acc in enumerate(accs)]
        for kind, (accs, target) in enumerate(((dwo_accs, dwo_ref), (dwz_accs, dwz_ref)))
    ]

    def mix_copy(j):
        return pltpu.make_async_remote_copy(
            src_ref=mix_sent.at[j], dst_ref=mix_got.at[j], send_sem=mix_send.at[j], recv_sem=mix_recv.at[j],
            device_id={"ch": lax.rem(mine + 1 + j, twins)}, device_id_type=MESH,
        )

    steps = twins * modes

    def norm_copy(j):
        return pltpu.make_async_remote_copy(
            src_ref=norm_sent.at[j], dst_ref=norm_got.at[j], send_sem=norm_send.at[j], recv_sem=norm_recv.at[j],
            device_id={"ch": lax.rem(mine + 1 + j, twins)}, device_id_type=MESH,
        )

    def normed_unit(j, m):
        step = j * modes + m
        if step + 1 < steps:
            in_copies(step + 1, 0)
        in_copies(step, 1)
        spread_products(in_buf.at[step % 2], (gx_ref, gz_ref.at[1]), mask_ref.at[m], pick_ref, slice_ref, m, part)

    def normed_end(j):
        for q in range(part // 128):
            lanes = slice(q * 128, (q + 1) * 128)
            cut = pl.ds(pl.multiple_of(lax.rem(mine + 1 + j, twins) * part + q * 128, 128), 128)
            dots_ref[...] += slice_ref[:, lanes] * x_in_ref[:, cut].astype(f32) * gain_ref[:, cut]
        if j < twins - 1:
            norm_sent[j] = slice_ref[...].astype(b16)
            norm_copy(j).start()

    def mix_unit(j):
        for m in range(modes):
            step = j * modes + m
            if step + 1 < steps:
                out_copy(step + 1).start()
            out_copy(step).wait()
            mask = jnp.concatenate([mask_ref[m]] * (part // 128), axis=1) > 0
            found = lax.dot_general(gz_ref[0], out_buf[step % 2], nt, preferred_element_type=jnp.float32)
            mix_ref[...] = jnp.where(mask, found, mix_ref[...]) if m else found
        if j < twins - 1:
            mix_sent[j] = mix_ref[...].astype(jnp.bfloat16)
            mix_copy(j).start()

    dots_copies = [
        pltpu.make_async_remote_copy(
            src_ref=dots_sent, dst_ref=dots_got.at[k - 1], send_sem=dots_send.at[k - 1], recv_sem=dots_recv.at[k - 1],
            device_id={"ch": lax.rem(mine + k, twins)}, device_id_type=MESH,
        )
        for k in range(1, twins)
    ]
    gain_copies = [
        pltpu.make_async_remote_copy(
            src_ref=gain_sent, dst_ref=gain_got.at[k - 1], send_sem=gain_send.at[k - 1], recv_sem=gain_recv.at[k - 1],
            device_id={"seq": lax.rem(me + k, count)}, device_id_type=MESH,
        )
        for k in range(1, count)
    ]

    def dots_unit():
        dots_sent[...] = dots_ref[...].astype(b16)
        for copy in dots_copies:
            copy.start()

    def slice_unit():
        for j in range(twins - 1):
            norm_copy(j).wait_recv()
            slice_ref[...] += norm_got[j].astype(f32)
        gain_sent[...] = jnp.zeros_like(gain_sent) + jnp.sum(slice_ref[...] * scaled_ref[...], axis=0, keepdims=True)
        for copy in gain_copies:
            copy.start()

    def gain_unit():
        total = gain_sent[...]
        for k, copy in enumerate(gain_copies):
            copy.wait_recv()
            total = total + gain_got[k]
        dgain_ref[...] = total
        for k, copy in enumerate(dots_copies):
            copy.wait_recv()
            dots_ref[...] += dots_got[k].astype(f32)
        for j in range(twins - 1):
            mix_copy(j).wait_recv()
            mix_ref[...] += mix_got[j].astype(f32)

    edge_copy.wait_send()
    dots_ref[...] = jnp.zeros_like(dots_ref)
    work = []
    for j in range(twins):
        for m in range(modes):
            work.append(functools.partial(normed_unit, j, m))
        work.append(functools.partial(normed_end, j))
        if j < 4:
            work.append(functools.partial(small_phase, j + 1))
    work.append(dots_unit)
    for j in range(twins):
        work.append(functools.partial(mix_unit, j))
    work += [slice_unit, gain_unit]
    for copy in own_columns:
        copy.wait()
    for copy in twin_copies:
        copy.wait_recv()
    ready = [(0, 0), (1, 0), (2, 0)] + early + late[:3]
    rest, last = late[3:], [(2, k) for k in range(1, count)]
    turns = []
    while rest or last:
        turns += rest[:2] + last[:1]
        rest, last = rest[2:], last[1:]
    for i, turn in enumerate(turns):
        left = len(turns) - i
        for _ in range(min(len(work), max(2, -(-len(work) // left)))):
            work.pop(0)()
        relay(*turn)
        ready.append(turn)
        for _ in range(2 if len(ready) > left else 1):
            if len(ready) > 1:
                products(*ready.pop(0))
    for unit in work:
        unit()
    for turn in ready:
        products(*turn)
    for copy in out_copies[0] + out_copies[1]:
        copy.wait()
    for j in range(twins - 1):
        mix_copy(j).wait_send()
        norm_copy(j).wait_send()
    for copy in dots_copies + gain_copies + seq_copies + twin_copies:
        copy.wait_send()
    for way in (0, 1):
        for k in range(count - 1):
            gx_copy(way, k).wait_send()

    for kind in (0, 1):
        for way in (0, 1):
            for k in range(count - 1):
                ring_copy(kind, way, k).wait_send()
    for copy in ch_copies + low_copies + ends_copies:
        copy.wait_send()


def spread_products(buf, sources, mask, picks_ref, target, m, part):
    nt = (((1,), (1,)), ((), ()))
    chosen = mask[...] > 0
    for q in range(2 * part // 256):
        weights = jnp.concatenate(
            [buf.at[b].reshape(2 * part, 128)[q * 256 : (q + 1) * 256] for b in range(buf.shape[0])], axis=1
        )
        total = None
        for j, source in enumerate(sources):
            found = lax.dot_general(source[...], weights, nt, preferred_element_type=jnp.float32)
            found = jnp.dot(found.astype(jnp.bfloat16), picks_ref[j], preferred_element_type=jnp.float32)
            total = found if total is None else total + found
        cut = pl.ds(q * 128, 128)
        target[:, cut] = jnp.where(chosen, total, target[:, cut]) if m else total


def core(
    w_in, w_out, normed, cotg, x, halo, z, dgated, same, big, taps, cbias, x_proj_t, dt_proj, dt_bias, a_log, skip, modes,
    masks, pick, x_in, gain, scaled,
):
    count, twins = lax.axis_size("seq"), lax.axis_size("ch")
    rows, chans = x.shape
    n = a_log.shape[0]
    chunks = rows // 16
    width = w_out.shape[1]
    slab = width // count
    part = width // twins
    tall, across = 4, count // 4
    depth = -(-312 // (16 * count)) * 16
    vmem = pl.BlockSpec(memory_space=pltpu.VMEM)
    hbm = pl.BlockSpec(memory_space=pl.ANY)
    cube = lambda a: a.reshape((chunks, a.shape[0] // chunks) + a.shape[1:])
    f32, b16 = jnp.float32, jnp.bfloat16
    shape = jax.ShapeDtypeStruct
    dma = pltpu.SemaphoreType.DMA
    keep = pltpu.VMEM
    operands = [w_in, w_out, normed, cotg, x, halo, cube(z), cube(dgated), same, cube(big), taps, cbias, x_proj_t, dt_proj, dt_bias, a_log,
                skip, modes, masks, pick, x_in, gain, scaled]
    block = (chunks, 16, chans)
    pair = lambda size: [dma((size,)), dma((size,))]
    return pl.pallas_call(
        functools.partial(core_kernel, (count, twins)),
        in_specs=[hbm] * 4 + [vmem] * (len(operands) - 4),
        out_specs=[hbm] * 2 + [vmem] * 6,
        out_shape=[
            shape((3, slab // 16, 16, chans), f32), shape((3, slab // 16, 16, chans), f32), shape((3, slab, chans), f32),
            shape((rows, part), f32), shape((tall, across, depth, chans), b16), shape((rows, part), f32),
            shape((rows, 128), f32), shape((8, part), f32),
        ],
        scratch_shapes=[
            pltpu.SemaphoreType.REGULAR, keep((rows + 8, chans), f32), keep(block, f32), keep(block, b16), keep(block, f32), keep(block, f32),
            keep(block, f32), keep(block, f32), keep(block, f32), keep((128, rows), b16), keep((rows, n, 128), f32),
            keep((rows, n, 128), f32), keep((n, chans), f32), keep((3 * n, chans), f32),
            keep((2, n, chans), b16), keep((count - 1, n, chans), b16), keep((1, chans), f32),
            keep((count - 1, 1, chans), f32), keep((n, chans), f32), keep((2, rows, chans), b16), keep((rows, chans), b16),
            keep((2, 2, count, rows // 2, slab), b16),
            keep((n, chans), f32), keep((8, chans), f32), keep((tall * across * depth, chans), f32),
            keep((tall, across, depth, chans), b16), keep((across - 1, tall, depth, chans), b16),
            keep((tall, depth, chans), f32), keep((tall, depth, chans), b16), keep((tall - 1, depth, chans), b16),
            keep((2, chans // 128, part, 2, 128), b16), keep((2, part, chans), b16), keep((twins - 1, rows, part), b16),
            keep((twins - 1, rows, part), b16),
            keep((twins - 1, rows, part), b16), keep((twins - 1, rows, part), b16), keep((rows, 128), b16),
            keep((twins - 1, rows, 128), b16), keep((8, part), f32), keep((count - 1, 8, part), f32),
            keep((2, 2, count - 1, rows // 2, chans), b16),
            keep((chunks, 16 * n, chans), b16), keep((16 * n, chans), b16),
            keep((16 * n, chans), b16), keep((n, chans), f32), keep(block, f32), keep(block, f32), keep((rows, 256), f32),
            keep((rows, 256), f32), keep((2, rows, 256), b16), keep((2, twins - 1, rows, 256), b16),
            keep((rows + 8, chans), f32), keep((8, chans), f32),
            dma((2, chans // 128)), dma((2,)), *pair(twins - 1), *pair(across - 1), *pair(tall - 1), *pair(tall - 1),
            *pair(across - 1), *pair(count - 1), *pair(count - 1), *pair(twins - 1), *pair(twins - 1), *pair(twins - 1),
            *pair(count - 1), dma((2, count - 1)), dma((2, count - 1)), dma((2,)), dma((2,)), dma((2, 2)), dma((2, 3)),
            dma((2, 2, count - 1)), dma((2, 2, count - 1)), dma((2, count - 1)), dma((2, count - 1)), *pair(twins - 1), dma((1,)), dma((1,)),
        ],
        compiler_params=pltpu.CompilerParams(collective_id=2, has_side_effects=True, vmem_limit_bytes=63 << 20),
        name="core",
    )(*operands)


def picks():
    order = jnp.arange(256)
    return jnp.stack([order[:, None] == 2 * jnp.arange(128)[None] + j for j in (0, 1)]).astype(jnp.bfloat16)


def lane_blocks(w_in):
    kinds, width, _, chans = w_in.shape
    return w_in.reshape(kinds, width, 2, chans // 128, 128).transpose(0, 1, 3, 2, 4)


def weave_kernel(x_ref, z_ref, out_ref, sems):
    kinds, _, chans = x_ref.shape
    copies = []
    for m in range(kinds):
        for b in range(chans // 128):
            for j, source in enumerate((x_ref, z_ref)):
                copies.append(
                    pltpu.make_async_copy(
                        source.at[m, :, pl.ds(b * 128, 128)], out_ref.at[m, :, b, j], sems.at[len(copies)]
                    )
                )
    for copy in copies:
        copy.start()
    for copy in copies:
        copy.wait()


def weave(x_part, z_part):
    kinds, slab, chans = x_part.shape
    out = pl.pallas_call(
        weave_kernel,
        in_specs=[pl.BlockSpec(memory_space=pltpu.VMEM)] * 2,
        out_specs=pl.BlockSpec(memory_space=pl.ANY),
        out_shape=jax.ShapeDtypeStruct((kinds, slab, chans // 128, 2, 128), jnp.float32),
        scratch_shapes=[pltpu.SemaphoreType.DMA((kinds * chans // 64,))],
        compiler_params=pltpu.CompilerParams(vmem_limit_bytes=32 << 20),
        name="weave",
    )(x_part, z_part)
    return out.transpose(0, 1, 3, 2, 4).reshape(kinds, slab, 2, chans)


def shards(
    x_in,
    norm_gain,
    w_in,
    conv_weight,
    conv_bias,
    x_proj,
    dt_proj,
    dt_bias,
    a_log,
    d_skip,
    w_out,
    modes,
    doc_lengths,
    cotangent,
):
    tok_rows, model_width = x_in.shape
    mode_count = w_in.shape[0]
    seq_count = lax.axis_size("seq")
    inner_local = conv_bias.shape[0]
    conv_taps = conv_weight.shape[0]
    ch_count = lax.axis_size("ch")
    feat_part = model_width // ch_count
    seq_index = lax.axis_index("seq")
    ch_index = lax.axis_index("ch")
    first_pos = seq_index * tok_rows
    positions = first_pos + jnp.arange(tok_rows, dtype=jnp.int32)
    my_modes = lax.dynamic_slice_in_dim(modes, first_pos, tok_rows)
    onehot = (my_modes[:, None] == jnp.arange(mode_count, dtype=jnp.int32)[None]).astype(
        jnp.bfloat16
    )
    doc_index, begins = doc_tables(doc_lengths, positions)
    x_full = x_in.astype(jnp.float32)
    scale = lax.rsqrt(jnp.mean(x_full * x_full, axis=1, keepdims=True) + EPSILON)
    normed = (x_full * scale * norm_gain[None]).astype(jnp.bfloat16)
    masks = jnp.broadcast_to(onehot.T[:, :, None], (mode_count, tok_rows, 128))
    blocks = lane_blocks(w_in)
    pick = picks()
    x_branch, z_branch, d_gated, cotg, halo = front(normed, masks, cotangent, blocks, w_out)
    around = jnp.arange(1 - conv_taps, tok_rows + conv_taps - 1, dtype=jnp.int32) + first_pos
    around_doc = jnp.where(around >= 0, doc_tables(doc_lengths, around)[0], -1)
    same = jnp.stack(
        [around_doc[k : k + tok_rows] == doc_index for k in range(2 * conv_taps - 1)]
    ).astype(jnp.bfloat16)
    same = jnp.broadcast_to(same[:, :, None], (2 * conv_taps - 1, tok_rows, 128))
    big = jnp.broadcast_to(jnp.where(begins, 1e30, 0.0)[:, None], (tok_rows, 128))
    mode_rows = modes.reshape(2 * seq_count, tok_rows // 2)
    x_proj_t = jnp.pad(x_proj.T, ((0, 256 - x_proj.shape[1]), (0, 0)))
    x_slice = lax.dynamic_slice_in_dim(x_full, ch_index * feat_part, feat_part, 1)
    gain_slice = lax.dynamic_slice_in_dim(norm_gain, ch_index * feat_part, feat_part, 0)
    d_w_out, d_w_z, d_w_x, mixer, smalls, d_slice, dots, d_gain = core(
        blocks, w_out, normed, cotg, x_branch, halo, z_branch, d_gated, same, big, conv_weight, conv_bias[None], x_proj_t,
        dt_proj, dt_bias[None], a_log, d_skip[None], mode_rows, masks, pick, x_in, norm_gain[None], x_slice * scale,
    )
    d_w_out = d_w_out.reshape(mode_count, -1, inner_local)
    d_w_in = weave(d_w_x, d_w_z.reshape(d_w_x.shape))
    block_out = (x_slice + mixer).astype(jnp.bfloat16)
    mean_term = (jnp.sum(dots, axis=1) / model_width)[:, None]
    weighted_slice = d_slice * gain_slice[None]
    d_x_in = cotangent.astype(jnp.float32) + scale * weighted_slice - x_slice * scale**3 * mean_term
    smalls = smalls.reshape(-1, inner_local).astype(jnp.float32)
    return (
        block_out,
        d_x_in,
        d_gain[0],
        d_w_in,
        smalls[304:308],
        smalls[308],
        smalls[:160].T,
        smalls[160:288],
        smalls[309],
        smalls[288:304],
        smalls[310],
        d_w_out,
    )


def solution(mesh):
    return jax.shard_map(
        shards,
        mesh=mesh,
        in_specs=(
            P("seq", None),
            P(),
            P(None, None, None, "ch"),
            P(None, "ch"),
            P("ch"),
            P("ch", None),
            P(None, "ch"),
            P("ch"),
            P(None, "ch"),
            P("ch"),
            P(None, None, "ch"),
            P(),
            P(),
            P("seq", "ch"),
        ),
        out_specs=(
            P("seq", "ch"),
            P("seq", "ch"),
            P("ch"),
            P(None, "seq", None, "ch"),
            P(None, "ch"),
            P("ch"),
            P("ch", None),
            P(None, "ch"),
            P("ch"),
            P(None, "ch"),
            P("ch"),
            P(None, "seq", "ch"),
        ),
        check_vma=False,
    )
```

```python
import functools
import math

import jax
import jax.numpy as jnp
from jax import lax
from jax.experimental import pallas as pl
from jax.experimental.pallas import tpu as pltpu
from jax.sharding import PartitionSpec as P

EPSILON = 1e-05


MESH = pl.DeviceIdType.MESH


def cycle_of(count):
    across = count // 4
    walk = [(0, x) for x in range(across)]
    for turn, x in enumerate(reversed(range(across))):
        column = [(z, x) for z in range(1, 4)]
        walk += column[::-1] if turn % 2 else column
    return [z * across + x for z, x in walk]


def table_of(index, values):
    picked = jnp.int32(values[0])
    for i in range(1, len(values)):
        picked = jnp.where(index == i, jnp.int32(values[i]), picked)
    return picked


def mode_columns(modes_ref, target_ref):
    half = target_ref.shape[0] // 2
    for way in (0, 1):
        row = modes_ref[pl.ds(2 * lax.axis_index("seq") + way, 1), :].astype(jnp.float32)
        target_ref[way * half : (way + 1) * half] = jnp.transpose(jnp.broadcast_to(row, (128, half)))


def row_scale(x):
    return lax.rsqrt(jnp.mean(x * x, axis=1, keepdims=True) + EPSILON)


def front_kernel(
    sizes, x_in_ref, gain_ref, modes_ref, cot_ref, w_in_ref, w_out_ref,
    x_ref, z_ref, gated_ref, cotg_ref, halo_ref, normed_ref,
    mode_ref, x2_ref, halo_send, halo_recv, in_buf, out_buf, in_sem, out_sem, cot_send, cot_recv, own_sem,
):
    count, twins = sizes
    rows, width = x_in_ref.shape
    modes = w_out_ref.shape[0]
    part = cot_ref.shape[1]
    inner = x_ref.shape[1]
    me = lax.axis_index("seq")
    mine = lax.axis_index("ch")
    barrier = pltpu.get_barrier_semaphore()
    for peer in (lax.rem(me + 1, count), lax.rem(me + count - 1, count)):
        pl.semaphore_signal(barrier, inc=1, device_id={"seq": peer}, device_id_type=MESH)
    for k in range(1, twins):
        peer = {"ch": lax.rem(mine + k, twins)}
        pl.semaphore_signal(barrier, inc=1, device_id=peer, device_id_type=MESH)

    pairs = inner // 256
    steps = pairs * modes

    def in_copy(step, b):
        slot = lax.rem(step, 2)
        return pltpu.make_async_copy(
            w_in_ref.at[lax.rem(step, modes), :, step // modes * 2 + b], in_buf.at[slot, b], in_sem.at[slot, b]
        )

    wide = out_buf.shape[2]
    out_steps = inner // wide * modes

    def out_copy(step):
        slot = lax.rem(step, 2)
        columns = pl.ds(pl.multiple_of(step // modes * wide, wide), wide)
        return pltpu.make_async_copy(
            w_out_ref.at[lax.rem(step, modes), :, columns], out_buf.at[slot], out_sem.at[slot]
        )

    for b in (0, 1):
        in_copy(0, b).start()
    out_copy(0).start()
    mode_columns(modes_ref, mode_ref)

    def norm_body(i, carry):
        rc = pl.ds(pl.multiple_of(i * 16, 16), 16)
        x = x_in_ref[rc, :].astype(jnp.float32)
        normed_ref[rc, :] = (x * row_scale(x) * gain_ref[...]).astype(jnp.bfloat16)
        return carry

    pl.semaphore_wait(barrier, 2 + twins - 1)

    cot_copies = [
        pltpu.make_async_remote_copy(
            src_ref=cot_ref, dst_ref=cotg_ref.at[mine], send_sem=cot_send.at[k - 1], recv_sem=cot_recv.at[k - 1],
            device_id={"ch": lax.rem(mine + k, twins)}, device_id_type=MESH,
        )
        for k in range(1, twins)
    ]
    for copy in cot_copies:
        copy.start()
    own_copy = pltpu.make_async_copy(cot_ref, cotg_ref.at[mine], own_sem.at[0])
    own_copy.start()
    def in_step(step, carry):
        slot = lax.rem(step, 2)
        mode = lax.rem(step, modes)

        @pl.when(step + 1 < steps)
        def _():
            for b in (0, 1):
                in_copy(step + 1, b).start()

        for b in (0, 1):
            in_copy(step, b).wait()
        weights = jnp.concatenate([in_buf.at[slot, b].reshape(2 * width, 128)[...] for b in (0, 1)], axis=1)
        mask = jnp.concatenate([mode_ref[...]] * 2, axis=1) == mode.astype(jnp.float32)
        columns = pl.ds(pl.multiple_of(step // modes * 256, 256), 256)
        for j, target in enumerate((x_ref, z_ref)):
            found = jnp.dot(x2_ref[j], weights, preferred_element_type=jnp.float32)
            found = jnp.where(mask, found, target[:, columns].astype(jnp.float32))
            target[:, columns] = found.astype(jnp.bfloat16)
        return carry

    lax.fori_loop(0, rows // 16, norm_body, 0)
    x_ref[...] = jnp.zeros_like(x_ref)
    z_ref[...] = jnp.zeros_like(z_ref)
    row = lax.broadcasted_iota(jnp.int32, (256, 512), 0)
    column = lax.broadcasted_iota(jnp.int32, (256, 512), 1)
    for j in (0, 1):
        spread = (column == 2 * row + j).astype(jnp.bfloat16)
        for block in range(width // 256):
            x2_ref[j, :, block * 512 : (block + 1) * 512] = jnp.dot(
                normed_ref[:, block * 256 : (block + 1) * 256], spread, preferred_element_type=jnp.float32
            ).astype(jnp.bfloat16)
    lax.fori_loop(0, steps, in_step, 0)
    halo_copy = pltpu.make_async_remote_copy(
        src_ref=x_ref.at[pl.ds(rows - 16, 16)], dst_ref=halo_ref, send_sem=halo_send.at[0], recv_sem=halo_recv.at[0],
        device_id={"seq": lax.rem(me + 1, count)}, device_id_type=MESH,
    )
    halo_copy.start()
    own_copy.wait()
    for copy in cot_copies:
        copy.wait_recv()

    def out_step(step, carry):
        slot = lax.rem(step, 2)
        mode = lax.rem(step, modes)

        @pl.when(step + 1 < out_steps)
        def _():
            out_copy(step + 1).start()

        out_copy(step).wait()
        mask = jnp.concatenate([mode_ref[...]] * (wide // 128), axis=1) == mode.astype(jnp.float32)
        columns = pl.ds(pl.multiple_of(step // modes * wide, wide), wide)
        found = jnp.zeros((rows, wide), jnp.float32)
        for c in range(twins):
            found = found + jnp.dot(
                cotg_ref[c], out_buf[slot, c * part : (c + 1) * part], preferred_element_type=jnp.float32
            )
        gated_ref[:, columns] = jnp.where(mask, found, gated_ref[:, columns])
        return carry

    gated_ref[...] = jnp.zeros_like(gated_ref)
    lax.fori_loop(0, out_steps, out_step, 0)
    halo_copy.wait_recv()
    for copy in cot_copies + [halo_copy]:
        copy.wait_send()


def front(x_in, gain, modes, cot, w_in, w_out):
    count, twins = lax.axis_size("seq"), lax.axis_size("ch")
    rows, width = x_in.shape
    inner = w_out.shape[2]
    vmem = pl.BlockSpec(memory_space=pltpu.VMEM)
    hbm = pl.BlockSpec(memory_space=pl.ANY)
    wide = min(512, inner)
    return pl.pallas_call(
        functools.partial(front_kernel, (count, twins)),
        in_specs=[vmem] * 4 + [hbm] * 2,
        out_specs=[vmem] * 6,
        out_shape=[
            jax.ShapeDtypeStruct((rows, inner), jnp.bfloat16),
            jax.ShapeDtypeStruct((rows, inner), jnp.bfloat16),
            jax.ShapeDtypeStruct((rows, inner), jnp.float32),
            jax.ShapeDtypeStruct((twins,) + cot.shape, jnp.bfloat16),
            jax.ShapeDtypeStruct((16, inner), jnp.bfloat16),
            jax.ShapeDtypeStruct((rows, width), jnp.bfloat16),
        ],
        scratch_shapes=[
            pltpu.VMEM((rows, 128), jnp.float32),
            pltpu.VMEM((2, rows, 2 * width), jnp.bfloat16),
            pltpu.SemaphoreType.DMA((1,)),
            pltpu.SemaphoreType.DMA((1,)),
            pltpu.VMEM((2, 2, width, 2, 128), jnp.bfloat16),
            pltpu.VMEM((2, width, wide), jnp.bfloat16),
            pltpu.SemaphoreType.DMA((2, 2)),
            pltpu.SemaphoreType.DMA((2,)),
            pltpu.SemaphoreType.DMA((twins - 1,)),
            pltpu.SemaphoreType.DMA((twins - 1,)),
            pltpu.SemaphoreType.DMA((1,)),
        ],
        compiler_params=pltpu.CompilerParams(collective_id=1, has_side_effects=True, vmem_limit_bytes=56 << 20),
        name="front",
    )(x_in, gain, modes, cot, w_in, w_out)


def tile_lanes(v, lanes):
    return jnp.concatenate([v] * (lanes // 128), axis=1)

def ring_places(count):
    ring = cycle_of(count)
    where = {s: i for i, s in enumerate(ring)}
    me = lax.axis_index("seq")
    onward = table_of(me, [ring[(where[s] + 1) % count] for s in range(count)])
    backward = table_of(me, [ring[(where[s] - 1) % count] for s in range(count)])
    place = table_of(me, [where[s] for s in range(count)])
    return ring, place, onward, backward


def add_products(accs, kind, k, cols_ref, blocks, modes_ref, ring, place, count):
    parts = []
    for way in (0, 1):
        step = k if way else count - k
        source = table_of(lax.rem(place + step, count), ring)
        parts.append((jnp.transpose(cols_ref[kind, way, k]), modes_ref[pl.ds(2 * source + way, 1), :]))
    right = jnp.concatenate(blocks, axis=0)
    for m, acc in enumerate(accs):
        left = jnp.concatenate(
            [part * jnp.where(row == m, 1.0, 0.0).astype(jnp.bfloat16) for part, row in parts], axis=1
        )
        found = jnp.dot(left, right, preferred_element_type=jnp.float32)
        acc[...] += found.reshape(acc.shape)


def core_kernel(
    sizes, w_in_ref, w_out_ref, normed_ref, cotg_ref, x_ref, halo_ref, z_ref, dgated_ref, starts_ref, taps_ref,
    cbias_ref, x_proj_ref, dt_proj_ref, dt_bias_ref, a_log_ref, skip_ref, modes_ref, x_in_ref, gain_ref,
    dwo_ref, dwz_ref, dwx_ref, mix_ref, small_ref, slice_ref, dots_ref, dgain_ref, scale_ref,
    same_ref, mode_ref,     free_sem, ext_ref, pre_ref, conv_ref, g_ref, step_ref, dtd_ref, u_ref, sig_ref, low_t_ref, b_ref, c_ref, rate_ref, ends_ref,
    ends_sent, ends_got, steps_sent, steps_got, h0_ref, gz_ref, gx_ref, cols_ref,
    racc_ref, rows_ref, sum_ref, half_ref, half_got, four_ref, four_b16, four_got, in_buf, out_buf, mix_sent, mix_got,
    norm_sent, norm_got, dots_sent, dots_got, gain_sent, gain_got,
    ring_ref, hist_ref, lam_ref, w_ref, pend_ref, gstep_ref, gscan_ref, part_ref, grad_ref, sent_ref, got_ref,
    gpre_ref, edge_ref,
    in_sem, out_sem, mix_send, mix_recv, half_send, half_recv, four_send, four_recv, last_send, last_recv, all_send, all_recv,
    ends_send, ends_recv, steps_send, steps_recv, low_send, low_recv, norm_send, norm_recv, dots_send, dots_recv,
    gain_send, gain_recv, seq_send, seq_recv, twin_send, twin_recv, own_sem, dwo_sem,
    ring_send, ring_recv, gx_send, gx_recv, ch_send, ch_recv, edge_send, edge_recv,
):
    count, twins = sizes
    chunks, _, chans = pre_ref.shape
    rows = chunks * 16
    n = a_log_ref.shape[0]
    half = rows // 2
    ring, place, onward, backward = ring_places(count)
    me = lax.axis_index("seq")
    mine = lax.axis_index("ch")
    before = lax.rem(me + count - 1, count)
    nt = (((1,), (1,)), ((), ()))
    f32, b16 = jnp.float32, jnp.bfloat16
    lb = min(512, chans)

    modes, width = w_out_ref.shape[:2]
    part = width // twins
    eighths = chans // 128
    across = half_ref.shape[1]
    tall = half_ref.shape[0]
    depth = half_ref.shape[2]
    z_at = me // across
    x_at = lax.rem(me, across)

    def chunk_of(step):
        return pl.ds(pl.multiple_of(lax.rem(mine + 1 + step // modes, twins) * part, part), part)

    def in_copy(step, b):
        slot = step % 2
        return pltpu.make_async_copy(w_in_ref.at[step % modes, chunk_of(step), b], in_buf.at[slot, b], in_sem.at[slot, b])

    def in_copies(step, wait):
        for b in range(eighths):
            if wait:
                in_copy(step, b).wait()
            else:
                in_copy(step, b).start()

    def out_copy(step):
        slot = step % 2
        return pltpu.make_async_copy(w_out_ref.at[step % modes, chunk_of(step)], out_buf.at[slot], out_sem.at[slot])

    barrier = pltpu.get_barrier_semaphore()
    for k in range(1, count):
        pl.semaphore_signal(barrier, inc=1, device_id={"seq": lax.rem(me + k, count)}, device_id_type=MESH)
    for k in range(1, twins):
        peer = {"ch": lax.rem(mine + k, twins)}
        pl.semaphore_signal(barrier, inc=1, device_id=peer, device_id_type=MESH)
    in_copies(0, 0)
    out_copy(0).start()
    pl.semaphore_wait(barrier, count - 1 + twins - 1)

    slab = cols_ref.shape[4]
    side = lax.rem(mine, 2)
    twin = mine + 1 - 2 * side
    side_rows = pl.ds(pl.multiple_of(side * half, half), half)

    def column_source(kind, owner, those):
        if kind == 0:
            return normed_ref.at[those, pl.ds(pl.multiple_of(owner * slab, slab), slab)]
        return cotg_ref.at[owner * slab // part, those, pl.ds(pl.multiple_of(lax.rem(owner * slab, part), slab), slab)]

    own_columns = [
        pltpu.make_async_copy(
            column_source(kind, me, pl.ds(way * half, half)), cols_ref.at[kind, way, 0], own_sem.at[kind, way]
        )
        for kind in (0, 1)
        for way in (0, 1)
    ]
    seq_copies = []
    for kind in (0, 1):
        for k in range(1, count):
            peer = table_of(lax.rem(place + jnp.where(side == 0, k, count - k), count), ring)
            seq_copies.append(
                pltpu.make_async_remote_copy(
                    src_ref=column_source(kind, peer, side_rows), dst_ref=cols_ref.at[kind, side, k],
                    send_sem=seq_send.at[kind, k - 1], recv_sem=seq_recv.at[kind, k - 1], device_id={"seq": peer},
                    device_id_type=MESH,
                )
            )
    for copy in own_columns + seq_copies:
        copy.start()
    twin_copies = [
        pltpu.make_async_remote_copy(
            src_ref=cols_ref.at[kind, side, pl.ds(1, count - 1)], dst_ref=cols_ref.at[kind, side, pl.ds(1, count - 1)],
            send_sem=twin_send.at[kind], recv_sem=twin_recv.at[kind], device_id={"ch": twin}, device_id_type=MESH,
        )
        for kind in (0, 1)
    ]

    mode_columns(modes_ref, mode_ref)
    spot = lax.broadcasted_iota(jnp.int32, (rows, 128), 0) + me * rows

    def passed(at):
        total = jnp.zeros(at.shape, f32)
        for i in range(starts_ref.shape[0]):
            total = total + jnp.where(at >= starts_ref[i : i + 1], 1.0, 0.0)
        return jnp.where(at >= count * rows, -1.0, total)

    here = passed(spot)
    for i in range(7):
        same_ref[i] = jnp.where(passed(spot + (i - 3)) == here, 1.0, 0.0).astype(b16)
    ext_ref[0:8] = halo_ref[8:16].astype(f32)
    ext_ref[8:] = x_ref[...].astype(f32)

    def conv_body(block, carry):
        cut = pl.ds(pl.multiple_of(block * 128, 128), 128)
        pre = jnp.zeros((rows, 128), f32) + cbias_ref[:, cut]
        for k in range(4):
            pre = pre + taps_ref[k : k + 1, cut] * ext_ref[5 + k : 5 + k + rows, cut] * same_ref[k].astype(f32)
        pre_ref[:, :, cut] = pre.reshape(chunks, 16, 128)
        conv_ref[:, :, cut] = (pre / (1.0 + jnp.exp(-pre))).astype(b16).reshape(chunks, 16, 128)
        return carry

    lax.fori_loop(0, chans // 128, conv_body, 0)
    part_ref[...] = lax.dot_general(
        conv_ref[...].reshape(rows, chans), x_proj_ref[...], nt, preferred_element_type=f32
    )
    sent_ref[0] = part_ref[...].astype(b16)

    def maps_copies(which, send, recv):
        return [
            pltpu.make_async_remote_copy(
                src_ref=sent_ref.at[which], dst_ref=got_ref.at[which, k - 1], send_sem=send.at[k - 1],
                recv_sem=recv.at[k - 1], device_id={"ch": lax.rem(mine + k, twins)}, device_id_type=MESH,
            )
            for k in range(1, twins)
        ]

    low_copies = maps_copies(0, low_send, low_recv)
    for copy in low_copies:
        copy.start()

    def gate_body(i, carry):
        z = z_ref[i].astype(f32)
        g_ref[i] = dgated_ref[i] * (z / (1.0 + jnp.exp(-z)))
        return carry

    lax.fori_loop(0, chunks, gate_body, 0)
    rate_ref[...] = -math.log2(math.e) * jnp.exp(a_log_ref[...])
    own = (
        lax.broadcasted_iota(jnp.int32, (16, 16 * n), 1) // n == lax.broadcasted_iota(jnp.int32, (16, 16 * n), 0)
    )
    ones = own.astype(b16)
    token_row = lax.broadcasted_iota(jnp.int32, (16 * n, 16), 0) // n
    repeat = (token_row == lax.broadcasted_iota(jnp.int32, (16 * n, 16), 1)).astype(b16)
    pick_row = lax.broadcasted_iota(jnp.int32, (16 * n, 128), 0)
    pick_col = lax.broadcasted_iota(jnp.int32, (16 * n, 128), 1)
    is_b = pick_row % n == pick_col
    is_c = pick_row % n + n == pick_col
    pick_b = is_b.astype(b16)
    pick_c = is_c.astype(b16)
    flat = jnp.ones((256, 128), b16)
    for copy in low_copies:
        copy.wait_recv()
    total = part_ref[...]
    for k in range(twins - 1):
        total = total + got_ref[0, k].astype(f32)
    part_ref[...] = total
    low_t_ref[...] = jnp.transpose(total[:, 0:128]).astype(b16)
    raw = jnp.dot(total[:, 0:128].astype(b16), dt_proj_ref[...], preferred_element_type=f32)
    step_ref[...] = raw.reshape(chunks, 16, chans)

    def step_body(i, carry):
        raw = step_ref[i] + dt_bias_ref[...]
        step = jnp.maximum(raw, 0.0) + jnp.log1p(jnp.exp(-jnp.abs(raw)))
        step_ref[i] = step
        sig_ref[i] = 1.0 / (1.0 + jnp.exp(-raw))
        at = lax.broadcasted_iota(jnp.int32, (16, 128), 0) + (me * rows + i * 16)
        big = jnp.where(passed(at) == passed(at - 1), 0.0, 1e30)
        dtd_ref[i] = step + jnp.concatenate([big] * (chans // 128), axis=1)
        u_ref[i] = step * conv_ref[i].astype(f32)
        maps = part_ref[pl.ds(pl.multiple_of(i * 16, 16), 16), 128:256]
        high = maps.astype(b16)
        low = (maps - high.astype(f32)).astype(b16)
        high = jnp.dot(repeat, high, preferred_element_type=f32)
        low = jnp.dot(repeat, low, preferred_element_type=f32)
        for target, chosen in ((b_ref, is_b), (c_ref, is_c)):
            terms = [jnp.where(chosen, term, 0.0).astype(b16) for term in (high, low)]
            found = jnp.dot(jnp.concatenate(terms, axis=1), flat, preferred_element_type=f32)
            target[pl.ds(i * 16, 16)] = found.reshape(16, n, 128)
        return carry

    lax.fori_loop(0, chunks, step_body, 0)

    def maps_block(chunk, pick):
        maps = part_ref[pl.ds(pl.multiple_of(chunk * 16, 16), 16), 128:256].astype(b16)
        found = lax.dot_general(maps, pick, nt, preferred_element_type=f32)
        return jnp.where(own, found, 0.0).astype(b16)

    ends_ref[0:n] = jnp.zeros((n, chans), f32)
    ends_ref[n : 2 * n] = jnp.ones((n, chans), f32)
    ends_ref[2 * n : 3 * n] = jnp.zeros((n, chans), f32)

    def ends_body(chunk, carry):
        for block in range(chans // lb):
            cut = slice(block * lb, (block + 1) * lb)
            rate = rate_ref[:, cut]
            h = ends_ref[0:n, cut]
            reach = ends_ref[n : 2 * n, cut]
            head = ends_ref[2 * n : 3 * n, cut]
            for t in range(16):
                decay = jnp.exp2(dtd_ref[chunk, t : t + 1, cut] * rate)
                h = decay * h + u_ref[chunk, t : t + 1, cut] * tile_lanes(b_ref[chunk * 16 + t], lb)
                reach = reach * decay
                head = head + reach * (g_ref[chunk, t : t + 1, cut] * tile_lanes(c_ref[chunk * 16 + t], lb))
            ends_ref[0:n, cut] = h
            ends_ref[n : 2 * n, cut] = reach
            ends_ref[2 * n : 3 * n, cut] = head
        return carry

    lax.fori_loop(0, chunks, ends_body, 0)
    ends_sent[0] = ends_ref[0:n].astype(b16)
    ends_sent[1] = ends_ref[2 * n : 3 * n].astype(b16)
    steps_sent[...] = jnp.sum(jnp.sum(dtd_ref[...], axis=0), axis=0, keepdims=True)
    ends_copies = []
    for k in range(1, count):
        peer = lax.rem(me + k, count)
        side = jnp.where(peer > me, 0, 1)
        ends_copies.append(
            pltpu.make_async_remote_copy(
                src_ref=ends_sent.at[side], dst_ref=ends_got.at[k - 1], send_sem=ends_send.at[k - 1],
                recv_sem=ends_recv.at[k - 1], device_id={"seq": peer}, device_id_type=MESH,
            )
        )
        ends_copies.append(
            pltpu.make_async_remote_copy(
                src_ref=steps_sent, dst_ref=steps_got.at[k - 1], send_sem=steps_send.at[k - 1],
                recv_sem=steps_recv.at[k - 1], device_id={"seq": peer}, device_id_type=MESH,
            )
        )
    for copy in ends_copies:
        copy.start()
    for copy in ends_copies:
        copy.wait_recv()

    def arrived(slots, valid):
        total = jnp.zeros((n, chans), f32)
        gap = jnp.zeros((1, chans), f32)
        for k, slot in enumerate(slots):
            term = ends_got[slot].astype(f32) * jnp.exp2(rate_ref[...] * gap)
            total = total + jnp.where(valid(k + 1), term, 0.0)
            gap = gap + steps_got[slot]
        return total

    h0_ref[...] = arrived(range(count - 1), lambda k: k <= me)
    pend_ref[...] = arrived(range(count - 2, -1, -1), lambda k: k + me < count)

    racc_ref[...] = h0_ref[...]

    def forward_body(chunk, carry):
        for block in range(chans // lb):
            cut = slice(block * lb, (block + 1) * lb)
            rate = rate_ref[:, cut]
            h = racc_ref[:, cut]
            for t in range(16):
                decay = jnp.exp2(dtd_ref[chunk, t : t + 1, cut] * rate)
                h = decay * h + u_ref[chunk, t : t + 1, cut] * tile_lanes(b_ref[chunk * 16 + t], lb)
                hist_ref[chunk, t * n : (t + 1) * n, cut] = h.astype(b16)
            racc_ref[:, cut] = h
        ssm = jnp.dot(maps_block(chunk, pick_c), hist_ref[chunk], preferred_element_type=f32)
        ssm = ssm + skip_ref[...] * conv_ref[chunk].astype(f32)
        z = z_ref[chunk].astype(f32)
        sig = 1.0 / (1.0 + jnp.exp(-z))
        rc = pl.ds(pl.multiple_of(chunk * 16, 16), 16)
        gz_ref[0, rc] = (ssm * (z * sig)).astype(b16)
        gz_ref[1, rc] = (dgated_ref[chunk] * ssm * (sig * (1.0 + z * (1.0 - sig)))).astype(b16)
        return carry

    lax.fori_loop(0, chunks, forward_body, 0)

    def ring_copy(kind, way, k):
        if k == 0:
            source = gz_ref.at[kind, pl.ds(way * half, half)]
        else:
            source = ring_ref.at[kind, way, k - 1]
        return pltpu.make_async_remote_copy(
            src_ref=source, dst_ref=ring_ref.at[kind, way, k], send_sem=ring_send.at[kind, way, k],
            recv_sem=ring_recv.at[kind, way, k], device_id={"seq": backward if way else onward}, device_id_type=MESH,
        )

    def relay(kind, k):
        for way in (0, 1):
            if kind == 2:
                gx_copy(way, k - 1).wait_recv()
                if k < count - 1:
                    gx_copy(way, k).start()
            else:
                ring_copy(kind, way, k - 1).wait_recv()
                if k < count - 1:
                    ring_copy(kind, way, k).start()

    def gx_slot(way, k):
        slot = way * (count - 1) + k
        return hist_ref.at[slot // 2, pl.ds(slot % 2 * half, half)]

    def gx_copy(way, k):
        return pltpu.make_async_remote_copy(
            src_ref=gx_slot(way, k - 1) if k else gx_ref.at[pl.ds(way * half, half)], dst_ref=gx_slot(way, k),
            send_sem=gx_send.at[way, k], recv_sem=gx_recv.at[way, k], device_id={"seq": backward if way else onward},
            device_id_type=MESH,
        )

    for kind in (0, 1):
        for way in (0, 1):
            ring_copy(kind, way, 0).start()
    turns = [(kind, k) for k in range(1, count) for kind in (0, 1)]
    early = turns[:2]
    late = turns[2:]

    racc_ref[...] = jnp.zeros_like(racc_ref)

    def span_body(i, carry):
        at = spans - 1 - i
        for sub in reversed(range(span // 16)):
            chunk = at * (span // 16) + sub
            for block in range(chans // lb):
                cut = slice(block * lb, (block + 1) * lb)
                rate = rate_ref[:, cut]
                pend = pend_ref[:, cut]
                racc = racc_ref[:, cut]
                for t in reversed(range(16)):
                    decay = jnp.exp2(dtd_ref[chunk, t : t + 1, cut] * rate)
                    lam = g_ref[chunk, t : t + 1, cut] * tile_lanes(c_ref[chunk * 16 + t], lb) + pend
                    pend = decay * lam
                    if t:
                        prior = hist_ref[chunk, (t - 1) * n : t * n, cut].astype(jnp.float32)
                    else:
                        prior = hist_ref[jnp.maximum(chunk - 1, 0), 15 * n : 16 * n, cut].astype(jnp.float32)
                        prior = jnp.where(chunk == 0, h0_ref[:, cut], prior)
                    w = pend * prior
                    racc = racc + w * step_ref[chunk, t : t + 1, cut]
                    lam_ref[t * n : (t + 1) * n, cut] = lam.astype(jnp.bfloat16)
                    w_ref[t * n : (t + 1) * n, cut] = (w * rate).astype(jnp.bfloat16)
                pend_ref[:, cut] = pend
                racc_ref[:, cut] = racc
            step = step_ref[chunk]
            conv = conv_ref[chunk].astype(jnp.float32)
            adj = jnp.dot(maps_block(chunk, pick_b), lam_ref[...], preferred_element_type=jnp.float32)
            wsum = jnp.dot(ones, w_ref[...], preferred_element_type=jnp.float32)
            gstep_ref[chunk] = wsum * math.log(2.0) + adj * conv
            gscan_ref[chunk] = adj * step
            gb = lax.dot_general(u_ref[chunk].astype(jnp.bfloat16), lam_ref[...], nt, preferred_element_type=jnp.float32)
            gc = lax.dot_general(
                g_ref[chunk].astype(jnp.bfloat16), hist_ref[chunk], nt, preferred_element_type=jnp.float32
            )
            gb = jnp.where(own, gb, 0.0).astype(jnp.bfloat16)
            gc = jnp.where(own, gc, 0.0).astype(jnp.bfloat16)
            grad_ref[pl.ds(pl.multiple_of(chunk * 16, 16), 16), 128:256] = jnp.dot(
                gb, pick_b, preferred_element_type=jnp.float32
            ) + jnp.dot(gc, pick_c, preferred_element_type=jnp.float32)
        return carry

    span = 32
    spans = rows // span
    lax.fori_loop(0, spans // 2, span_body, 0)
    relay(*early[0])
    for copy in seq_copies:
        copy.wait_recv()
    for copy in twin_copies:
        copy.start()
    lax.fori_loop(spans // 2, spans, span_body, 0)
    for peer in (onward, backward):
        pl.semaphore_signal(free_sem, inc=1, device_id={"seq": peer}, device_id_type=MESH)
    relay(*early[1])

    rows_ref[...] = jnp.zeros_like(rows_ref)

    def raw_body(i, carry):
        full = gstep_ref[i] * sig_ref[i]
        rows_ref[5:6] += jnp.sum(full, axis=0, keepdims=True)
        rows_ref[6:7] += jnp.sum(g_ref[i] * conv_ref[i].astype(jnp.float32), axis=0, keepdims=True)
        gx_ref[pl.ds(pl.multiple_of(i * 16, 16), 16), :] = full.astype(jnp.bfloat16)
        return carry

    lax.fori_loop(0, chunks, raw_body, 0)
    grad_ref[:, 0:128] = lax.dot_general(gx_ref[...], dt_proj_ref[...], nt, preferred_element_type=jnp.float32)
    sent_ref[1] = grad_ref[...].astype(jnp.bfloat16)
    ch_copies = maps_copies(1, ch_send, ch_recv)
    for copy in ch_copies:
        copy.start()
    relay(*late[0])
    sum_ref[160:288] = jnp.dot(low_t_ref[...], gx_ref[...], preferred_element_type=jnp.float32)
    for copy in ch_copies:
        copy.wait_recv()
    total = grad_ref[...]
    for k in range(twins - 1):
        total = total + got_ref[1, k].astype(jnp.float32)
    grad_ref[...] = total
    relay(*late[1])

    skip = skip_ref[...]
    def pre_body(i, carry):
        rc = pl.ds(pl.multiple_of(i * 16, 16), 16)
        g_conv = jnp.dot(grad_ref[rc, :].astype(jnp.bfloat16), x_proj_ref[...], preferred_element_type=jnp.float32)
        g_conv = g_conv + skip * g_ref[i] + gscan_ref[i]
        pre = pre_ref[i]
        sig = 1.0 / (1.0 + jnp.exp(-pre))
        gpre = g_conv * sig * (1.0 + pre * (1.0 - sig))
        gpre_ref[rc, :] = gpre
        return carry

    pre_body(0, 0)
    edge_ref[...] = gpre_ref[0:8, :]
    edge_copy = pltpu.make_async_remote_copy(
        src_ref=edge_ref, dst_ref=gpre_ref.at[pl.ds(rows, 8)], send_sem=edge_send.at[0], recv_sem=edge_recv.at[0],
        device_id={"seq": before}, device_id_type=MESH,
    )
    edge_copy.start()
    lax.fori_loop(1, chunks, pre_body, 0)
    flipped = jnp.transpose(grad_ref[...]).astype(jnp.bfloat16)
    sum_ref[0:160] = jnp.dot(flipped[0:160], conv_ref[...].reshape(rows, chans), preferred_element_type=jnp.float32)
    relay(*late[2])
    edge_copy.wait_recv()

    def taps_body(block, carry):
        cut = pl.ds(pl.multiple_of(block * 128, 128), 128)
        gpre = gpre_ref[0:rows, cut]
        rows_ref[4:5, cut] = jnp.sum(gpre, axis=0, keepdims=True)
        total = jnp.zeros((rows, 128), jnp.float32)
        for k in range(4):
            lag = 3 - k
            total = total + gpre_ref[lag : lag + rows, cut] * taps_ref[k : k + 1, cut] * same_ref[3 + lag].astype(jnp.float32)
            rows_ref[k : k + 1, cut] = jnp.sum(
                gpre * ext_ref[5 + k : 5 + k + rows, cut] * same_ref[k].astype(jnp.float32), axis=0, keepdims=True
            )
        gx_ref[:, cut] = total.astype(jnp.bfloat16)
        return carry

    lax.fori_loop(0, chans // 128, taps_body, 0)
    pl.semaphore_wait(free_sem, 2)
    for way in (0, 1):
        gx_copy(way, 0).start()
    sum_ref[288:304] = racc_ref[...] * rate_ref[...] * math.log(2.0)
    sum_ref[304:312] = rows_ref[...]
    if tall * across * depth > 312:
        sum_ref[312:] = jnp.zeros((tall * across * depth - 312, chans), jnp.float32)
    for z in range(tall):
        for x in range(across):
            first = (z * across + x) * depth
            half_ref[z, x] = sum_ref[first : first + depth].astype(jnp.bfloat16)

    def to(device):
        return dict(device_id={"seq": device}, device_id_type=MESH)

    half_copies = [
        pltpu.make_async_remote_copy(
            src_ref=half_ref.at[:, lax.rem(x_at + k, across)], dst_ref=half_got.at[k - 1], send_sem=half_send.at[k - 1],
            recv_sem=half_recv.at[k - 1], **to(z_at * across + lax.rem(x_at + k, across)),
        )
        for k in range(1, across)
    ]
    four_copies = [
        pltpu.make_async_remote_copy(
            src_ref=four_b16.at[lax.rem(z_at + k, tall)], dst_ref=four_got.at[k - 1], send_sem=four_send.at[k - 1],
            recv_sem=four_recv.at[k - 1], **to(lax.rem(z_at + k, tall) * across + x_at),
        )
        for k in range(1, tall)
    ]
    last_copies = [
        pltpu.make_async_remote_copy(
            src_ref=small_ref.at[z_at, x_at], dst_ref=small_ref.at[z_at, x_at], send_sem=last_send.at[k - 1],
            recv_sem=last_recv.at[k - 1], **to(lax.rem(z_at + k, tall) * across + x_at),
        )
        for k in range(1, tall)
    ]
    all_copies = [
        pltpu.make_async_remote_copy(
            src_ref=small_ref.at[:, x_at], dst_ref=small_ref.at[:, x_at], send_sem=all_send.at[k - 1],
            recv_sem=all_recv.at[k - 1], **to(z_at * across + lax.rem(x_at + k, across)),
        )
        for k in range(1, across)
    ]

    def small_phase(phase):
        if phase == 0:
            for copy in half_copies:
                copy.start()
        elif phase == 1:
            for copy in half_copies:
                copy.wait_recv()
            for z in range(tall):
                first = pl.multiple_of((z * across + x_at) * depth, depth)
                total = sum_ref[pl.ds(first, depth)]
                for k in range(across - 1):
                    total = total + half_got[k, z].astype(jnp.float32)
                four_ref[z] = total
                four_b16[z] = total.astype(jnp.bfloat16)
            for copy in four_copies:
                copy.start()
        elif phase == 2:
            for copy in four_copies:
                copy.wait_recv()
            total = four_ref[z_at]
            for k in range(tall - 1):
                total = total + four_got[k].astype(jnp.float32)
            small_ref[z_at, x_at] = total.astype(jnp.bfloat16)
            for copy in last_copies:
                copy.start()
        elif phase == 3:
            for copy in last_copies:
                copy.wait_recv()
            for copy in all_copies:
                copy.start()
        else:
            for copy in all_copies:
                copy.wait_recv()
            for copy in half_copies + four_copies + last_copies + all_copies:
                copy.wait_send()

    small_phase(0)
    dwo_accs = [ref.at[0 : slab // 16] for ref in (dtd_ref, u_ref, sig_ref)]
    dwz_accs = [ref.at[0 : slab // 16] for ref in (step_ref, g_ref, gscan_ref)]
    dwx_accs = [dwx_ref.at[m] for m in range(modes)]
    for acc in dwo_accs + dwz_accs + dwx_accs:
        acc[...] = jnp.zeros_like(acc)

    def products(kind, k):
        if k == 0:
            source = gx_ref if kind == 2 else gz_ref.at[kind]
            blocks = [source[way * half : (way + 1) * half] for way in (0, 1)]
        else:
            blocks = [gx_slot(way, k - 1)[...] if kind == 2 else ring_ref[kind, way, k - 1] for way in (0, 1)]
        accs = (dwo_accs, dwz_accs, dwx_accs)[kind]
        add_products(accs, 0 if kind else 1, k, cols_ref, blocks, modes_ref, ring, place, count)
        if kind < 2 and k == count - 1:
            for copy in out_copies[kind]:
                copy.start()

    out_copies = [
        [pltpu.make_async_copy(acc, target.at[m], dwo_sem.at[kind, m]) for m, acc in enumerate(accs)]
        for kind, (accs, target) in enumerate(((dwo_accs, dwo_ref), (dwz_accs, dwz_ref)))
    ]

    def mix_copy(j):
        return pltpu.make_async_remote_copy(
            src_ref=mix_sent.at[j], dst_ref=mix_got.at[j], send_sem=mix_send.at[j], recv_sem=mix_recv.at[j],
            device_id={"ch": lax.rem(mine + 1 + j, twins)}, device_id_type=MESH,
        )

    steps = twins * modes

    def norm_copy(j):
        return pltpu.make_async_remote_copy(
            src_ref=norm_sent.at[j], dst_ref=norm_got.at[j], send_sem=norm_send.at[j], recv_sem=norm_recv.at[j],
            device_id={"ch": lax.rem(mine + 1 + j, twins)}, device_id_type=MESH,
        )

    def normed_unit(j, m):
        step = j * modes + m
        if step + 1 < steps:
            in_copies(step + 1, 0)
        in_copies(step, 1)
        spread_products(in_buf.at[step % 2], (gx_ref, gz_ref.at[1]), mode_ref, slice_ref, m, part)

    def normed_end(j):
        for q in range(part // 128):
            lanes = slice(q * 128, (q + 1) * 128)
            cut = pl.ds(pl.multiple_of(lax.rem(mine + 1 + j, twins) * part + q * 128, 128), 128)
            dots_ref[...] += slice_ref[:, lanes] * x_in_ref[:, cut].astype(f32) * gain_ref[:, cut]
        if j < twins - 1:
            norm_sent[j] = slice_ref[...].astype(b16)
            norm_copy(j).start()

    def mix_unit(j):
        for m in range(modes):
            step = j * modes + m
            if step + 1 < steps:
                out_copy(step + 1).start()
            out_copy(step).wait()
            mask = jnp.concatenate([mode_ref[...]] * (part // 128), axis=1) == float(m)
            found = lax.dot_general(gz_ref[0], out_buf[step % 2], nt, preferred_element_type=jnp.float32)
            mix_ref[...] = jnp.where(mask, found, mix_ref[...]) if m else found
        if j < twins - 1:
            mix_sent[j] = mix_ref[...].astype(jnp.bfloat16)
            mix_copy(j).start()

    dots_copies = [
        pltpu.make_async_remote_copy(
            src_ref=dots_sent, dst_ref=dots_got.at[k - 1], send_sem=dots_send.at[k - 1], recv_sem=dots_recv.at[k - 1],
            device_id={"ch": lax.rem(mine + k, twins)}, device_id_type=MESH,
        )
        for k in range(1, twins)
    ]
    gain_copies = [
        pltpu.make_async_remote_copy(
            src_ref=gain_sent, dst_ref=gain_got.at[k - 1], send_sem=gain_send.at[k - 1], recv_sem=gain_recv.at[k - 1],
            device_id={"seq": lax.rem(me + k, count)}, device_id_type=MESH,
        )
        for k in range(1, count)
    ]

    def scale_body(i, carry):
        rc = pl.ds(pl.multiple_of(i * 16, 16), 16)
        scale_ref[rc] = jnp.broadcast_to(row_scale(x_in_ref[rc].astype(f32)), (16, 128))
        return carry

    def dots_unit():
        lax.fori_loop(0, chunks, scale_body, 0)
        dots_sent[...] = dots_ref[...].astype(b16)
        for copy in dots_copies:
            copy.start()

    def slice_unit():
        for j in range(twins - 1):
            norm_copy(j).wait_recv()
            slice_ref[...] += norm_got[j].astype(f32)
        for q in range(part // 128):
            lanes = slice(q * 128, (q + 1) * 128)
            cut = pl.ds(pl.multiple_of(mine * part + q * 128, 128), 128)
            terms = slice_ref[:, lanes] * x_in_ref[:, cut].astype(f32) * scale_ref[...]
            gain_sent[:, lanes] = jnp.broadcast_to(jnp.sum(terms, axis=0, keepdims=True), (8, 128))
        for copy in gain_copies:
            copy.start()

    def gain_unit():
        total = gain_sent[...]
        for k, copy in enumerate(gain_copies):
            copy.wait_recv()
            total = total + gain_got[k]
        dgain_ref[...] = total
        for k, copy in enumerate(dots_copies):
            copy.wait_recv()
            dots_ref[...] += dots_got[k].astype(f32)
        mean = jnp.sum(dots_ref[...], axis=1, keepdims=True) / width
        dots_ref[...] = jnp.broadcast_to(mean, (rows, 128))
        for j in range(twins - 1):
            mix_copy(j).wait_recv()
            mix_ref[...] += mix_got[j].astype(f32)

    edge_copy.wait_send()
    dots_ref[...] = jnp.zeros_like(dots_ref)
    work = []
    for j in range(twins):
        for m in range(modes):
            work.append(functools.partial(normed_unit, j, m))
        work.append(functools.partial(normed_end, j))
        if j < 4:
            work.append(functools.partial(small_phase, j + 1))
    work.append(dots_unit)
    for j in range(twins):
        work.append(functools.partial(mix_unit, j))
    work += [slice_unit, gain_unit]
    for copy in own_columns:
        copy.wait()
    for copy in twin_copies:
        copy.wait_recv()
    ready = [(0, 0), (1, 0), (2, 0)] + early + late[:3]
    rest, last = late[3:], [(2, k) for k in range(1, count)]
    turns = []
    while rest or last:
        turns += rest[:2] + last[:1]
        rest, last = rest[2:], last[1:]
    for i, turn in enumerate(turns):
        left = len(turns) - i
        for _ in range(min(len(work), max(2, -(-len(work) // left)))):
            work.pop(0)()
        relay(*turn)
        ready.append(turn)
        for _ in range(2 if len(ready) > left else 1):
            if len(ready) > 1:
                products(*ready.pop(0))
    for unit in work:
        unit()
    for turn in ready:
        products(*turn)
    for copy in out_copies[0] + out_copies[1]:
        copy.wait()
    for j in range(twins - 1):
        mix_copy(j).wait_send()
        norm_copy(j).wait_send()
    for copy in dots_copies + gain_copies + seq_copies + twin_copies:
        copy.wait_send()
    for way in (0, 1):
        for k in range(count - 1):
            gx_copy(way, k).wait_send()

    for kind in (0, 1):
        for way in (0, 1):
            for k in range(count - 1):
                ring_copy(kind, way, k).wait_send()
    for copy in ch_copies + low_copies + ends_copies:
        copy.wait_send()


def spread_products(buf, sources, mode_ref, target, m, part):
    nt = (((1,), (1,)), ((), ()))
    chosen = mode_ref[...] == float(m)
    row = lax.broadcasted_iota(jnp.int32, (256, 128), 0)
    column = lax.broadcasted_iota(jnp.int32, (256, 128), 1)
    picks = [(row == 2 * column + j).astype(jnp.bfloat16) for j in (0, 1)]
    for q in range(2 * part // 256):
        weights = jnp.concatenate(
            [buf.at[b].reshape(2 * part, 128)[q * 256 : (q + 1) * 256] for b in range(buf.shape[0])], axis=1
        )
        total = None
        for j, source in enumerate(sources):
            found = lax.dot_general(source[...], weights, nt, preferred_element_type=jnp.float32)
            found = jnp.dot(found.astype(jnp.bfloat16), picks[j], preferred_element_type=jnp.float32)
            total = found if total is None else total + found
        cut = pl.ds(q * 128, 128)
        target[:, cut] = jnp.where(chosen, total, target[:, cut]) if m else total


def core(
    w_in, w_out, normed, cotg, x, halo, z, dgated, starts, taps, cbias, x_proj_t, dt_proj, dt_bias, a_log, skip, modes, x_in,
    gain,
):
    count, twins = lax.axis_size("seq"), lax.axis_size("ch")
    rows, chans = x.shape
    n = a_log.shape[0]
    chunks = rows // 16
    width = w_out.shape[1]
    slab = width // count
    part = width // twins
    tall, across = 4, count // 4
    depth = -(-312 // (16 * count)) * 16
    vmem = pl.BlockSpec(memory_space=pltpu.VMEM)
    hbm = pl.BlockSpec(memory_space=pl.ANY)
    cube = lambda a: a.reshape((chunks, a.shape[0] // chunks) + a.shape[1:])
    f32, b16 = jnp.float32, jnp.bfloat16
    shape = jax.ShapeDtypeStruct
    dma = pltpu.SemaphoreType.DMA
    keep = pltpu.VMEM
    operands = [w_in, w_out, normed, cotg, x, halo, cube(z), cube(dgated), starts, taps, cbias, x_proj_t, dt_proj, dt_bias,
                a_log, skip, modes, x_in, gain]
    block = (chunks, 16, chans)
    pair = lambda size: [dma((size,)), dma((size,))]
    return pl.pallas_call(
        functools.partial(core_kernel, (count, twins)),
        in_specs=[hbm] * 4 + [vmem] * (len(operands) - 4),
        out_specs=[hbm] * 2 + [vmem] * 7,
        out_shape=[
            shape((3, slab // 16, 16, chans), f32), shape((3, slab // 16, 16, chans), f32), shape((3, slab, chans), f32),
            shape((rows, part), f32), shape((tall, across, depth, chans), b16), shape((rows, part), f32),
            shape((rows, 128), f32), shape((8, part), f32), shape((rows, 128), f32),
        ],
        scratch_shapes=[
            keep((7, rows, 128), b16), keep((rows, 128), f32), pltpu.SemaphoreType.REGULAR, keep((rows + 8, chans), f32), keep(block, f32), keep(block, b16), keep(block, f32), keep(block, f32),
            keep(block, f32), keep(block, f32), keep(block, f32), keep((128, rows), b16), keep((rows, n, 128), f32),
            keep((rows, n, 128), f32), keep((n, chans), f32), keep((3 * n, chans), f32),
            keep((2, n, chans), b16), keep((count - 1, n, chans), b16), keep((1, chans), f32),
            keep((count - 1, 1, chans), f32), keep((n, chans), f32), keep((2, rows, chans), b16), keep((rows, chans), b16),
            keep((2, 2, count, rows // 2, slab), b16),
            keep((n, chans), f32), keep((8, chans), f32), keep((tall * across * depth, chans), f32),
            keep((tall, across, depth, chans), b16), keep((across - 1, tall, depth, chans), b16),
            keep((tall, depth, chans), f32), keep((tall, depth, chans), b16), keep((tall - 1, depth, chans), b16),
            keep((2, chans // 128, part, 2, 128), b16), keep((2, part, chans), b16), keep((twins - 1, rows, part), b16),
            keep((twins - 1, rows, part), b16),
            keep((twins - 1, rows, part), b16), keep((twins - 1, rows, part), b16), keep((rows, 128), b16),
            keep((twins - 1, rows, 128), b16), keep((8, part), f32), keep((count - 1, 8, part), f32),
            keep((2, 2, count - 1, rows // 2, chans), b16),
            keep((chunks, 16 * n, chans), b16), keep((16 * n, chans), b16),
            keep((16 * n, chans), b16), keep((n, chans), f32), keep(block, f32), keep(block, f32), keep((rows, 256), f32),
            keep((rows, 256), f32), keep((2, rows, 256), b16), keep((2, twins - 1, rows, 256), b16),
            keep((rows + 8, chans), f32), keep((8, chans), f32),
            dma((2, chans // 128)), dma((2,)), *pair(twins - 1), *pair(across - 1), *pair(tall - 1), *pair(tall - 1),
            *pair(across - 1), *pair(count - 1), *pair(count - 1), *pair(twins - 1), *pair(twins - 1), *pair(twins - 1),
            *pair(count - 1), dma((2, count - 1)), dma((2, count - 1)), dma((2,)), dma((2,)), dma((2, 2)), dma((2, 3)),
            dma((2, 2, count - 1)), dma((2, 2, count - 1)), dma((2, count - 1)), dma((2, count - 1)), *pair(twins - 1), dma((1,)), dma((1,)),
        ],
        compiler_params=pltpu.CompilerParams(collective_id=2, has_side_effects=True, vmem_limit_bytes=63 << 20),
        name="core",
    )(*operands)


def lane_blocks(w_in):
    kinds, width, _, chans = w_in.shape
    return w_in.reshape(kinds, width, 2, chans // 128, 128).transpose(0, 1, 3, 2, 4)


def finish_kernel(
    x_part_ref, z_part_ref, out_part_ref, small_ref, slice_ref, mix_ref, mean_ref, scale_ref, cot_ref, x_in_ref, gain_ref,
    dgain_ref,
    dw_in_ref, dw_out_ref, block_ref, dx_ref, gain_out_ref, taps_ref, cbias_ref, x_proj_ref, dt_proj_ref, dt_bias_ref, a_log_ref,
    skip_ref,
    sems, out_sem,
):
    kinds, _, chans = x_part_ref.shape
    part = slice_ref.shape[1]
    mine = lax.axis_index("ch")
    copies = [pltpu.make_async_copy(out_part_ref, dw_out_ref, out_sem.at[0])]
    for m in range(kinds):
        for b in range(chans // 128):
            for j, source in enumerate((x_part_ref, z_part_ref)):
                copies.append(
                    pltpu.make_async_copy(
                        source.at[m, :, pl.ds(b * 128, 128)], dw_in_ref.at[m, :, b, j], sems.at[len(copies) - 1]
                    )
                )
    for copy in copies:
        copy.start()
    scale = scale_ref[...]
    bent = scale * scale * scale * mean_ref[...]
    for q in range(part // 128):
        lanes = slice(q * 128, (q + 1) * 128)
        cut = pl.ds(pl.multiple_of(mine * part + q * 128, 128), 128)
        x = x_in_ref[:, cut].astype(jnp.float32)
        block_ref[:, lanes] = (x + mix_ref[:, lanes]).astype(jnp.bfloat16)
        weighted = slice_ref[:, lanes] * gain_ref[:, cut]
        dx_ref[:, lanes] = cot_ref[:, lanes].astype(jnp.float32) + scale * weighted - x * bent
    gain_out_ref[...] = dgain_ref[0:1]
    x_proj_ref[...] = small_ref[0:160].astype(jnp.float32)
    dt_proj_ref[...] = small_ref[160:288].astype(jnp.float32)
    a_log_ref[...] = small_ref[288:304].astype(jnp.float32)
    rest = small_ref[304:320].astype(jnp.float32)
    taps_ref[...] = rest[0:4]
    cbias_ref[...] = rest[4:5]
    dt_bias_ref[...] = rest[5:6]
    skip_ref[...] = rest[6:7]
    for copy in copies:
        copy.wait()


def finish(x_part, z_part, out_part, small, total, mix, mean, scale, cot, x_in, gain, dgain):
    kinds, slab, chans = x_part.shape
    rows, part = total.shape
    vmem = pl.BlockSpec(memory_space=pltpu.VMEM)
    hbm = pl.BlockSpec(memory_space=pl.ANY)
    f32 = jnp.float32
    shape = jax.ShapeDtypeStruct
    outs = pl.pallas_call(
        finish_kernel,
        in_specs=[hbm] * 3 + [vmem] * 9,
        out_specs=[hbm] * 2 + [vmem] * 10,
        out_shape=[
            shape((kinds, slab, chans // 128, 2, 128), f32), shape((kinds, slab, chans), f32),
            shape((rows, part), jnp.bfloat16), shape((rows, part), f32), shape((1, part), f32), shape((4, chans), f32),
            shape((1, chans), f32), shape((160, chans), f32), shape((128, chans), f32), shape((1, chans), f32),
            shape((16, chans), f32), shape((1, chans), f32),
        ],
        scratch_shapes=[pltpu.SemaphoreType.DMA((kinds * chans // 64,)), pltpu.SemaphoreType.DMA((1,))],
        compiler_params=pltpu.CompilerParams(vmem_limit_bytes=32 << 20),
        name="finish",
    )(x_part, z_part, out_part, small, total, mix, mean, scale, cot, x_in, gain, dgain)
    dw_in = outs[0].transpose(0, 1, 3, 2, 4).reshape(kinds, slab, 2, chans)
    return (outs[2], outs[3], outs[4][0], dw_in, outs[5], outs[6][0], outs[7].T, outs[8], outs[9][0], outs[10], outs[11][0], outs[1])


def shards(
    x_in,
    norm_gain,
    w_in,
    conv_weight,
    conv_bias,
    x_proj,
    dt_proj,
    dt_bias,
    a_log,
    d_skip,
    w_out,
    modes,
    doc_lengths,
    cotangent,
):
    seq_count = lax.axis_size("seq")
    tok_rows = x_in.shape[0]
    inner_local = conv_bias.shape[0]
    docs = doc_lengths.shape[0]
    order = jnp.arange(docs, dtype=jnp.int32)
    starts = jnp.sum(jnp.where(order[:, None] > order[None, :], doc_lengths[None, :], 0), axis=1)
    starts = jnp.broadcast_to(starts[:, None], (docs, 128))
    mode_rows = modes.reshape(2 * seq_count, tok_rows // 2)
    blocks = lane_blocks(w_in)
    gain = norm_gain[None]
    x_branch, z_branch, d_gated, cotg, halo, normed = front(x_in, gain, mode_rows, cotangent, blocks, w_out)
    x_proj_t = jnp.pad(x_proj.T, ((0, 256 - x_proj.shape[1]), (0, 0)))
    d_w_out, d_w_z, d_w_x, mixer, smalls, d_slice, mean, d_gain, scale = core(
        blocks, w_out, normed, cotg, x_branch, halo, z_branch, d_gated, starts, conv_weight, conv_bias[None], x_proj_t,
        dt_proj, dt_bias[None], a_log, d_skip[None], mode_rows, x_in, gain,
    )
    return finish(
        d_w_x, d_w_z.reshape(d_w_x.shape), d_w_out.reshape(d_w_x.shape), smalls.reshape(-1, inner_local), d_slice, mixer,
        mean, scale, cotangent, x_in, gain, d_gain,
    )


def solution(mesh):
    return jax.shard_map(
        shards,
        mesh=mesh,
        in_specs=(
            P("seq", None),
            P(),
            P(None, None, None, "ch"),
            P(None, "ch"),
            P("ch"),
            P("ch", None),
            P(None, "ch"),
            P("ch"),
            P(None, "ch"),
            P("ch"),
            P(None, None, "ch"),
            P(),
            P(),
            P("seq", "ch"),
        ),
        out_specs=(
            P("seq", "ch"),
            P("seq", "ch"),
            P("ch"),
            P(None, "seq", None, "ch"),
            P(None, "ch"),
            P("ch"),
            P("ch", None),
            P(None, "ch"),
            P("ch"),
            P(None, "ch"),
            P("ch"),
            P(None, "seq", "ch"),
        ),
        check_vma=False,
    )
```

```python
import functools
import math

import jax
import jax.numpy as jnp
from jax import lax
from jax.experimental import pallas as pl
from jax.experimental.pallas import tpu as pltpu
from jax.sharding import PartitionSpec as P

EPSILON = 1e-05


MESH = pl.DeviceIdType.MESH


def cycle_of(count):
    across = count // 4
    walk = [(0, x) for x in range(across)]
    for turn, x in enumerate(reversed(range(across))):
        column = [(z, x) for z in range(1, 4)]
        walk += column[::-1] if turn % 2 else column
    return [z * across + x for z, x in walk]


def table_of(index, values):
    picked = jnp.int32(values[0])
    for i in range(1, len(values)):
        picked = jnp.where(index == i, jnp.int32(values[i]), picked)
    return picked


def mode_columns(modes_ref, target_ref):
    half = target_ref.shape[0] // 2
    for way in (0, 1):
        row = modes_ref[pl.ds(2 * lax.axis_index("seq") + way, 1), :].astype(jnp.float32)
        target_ref[way * half : (way + 1) * half] = jnp.transpose(jnp.broadcast_to(row, (128, half)))


def row_scale(x):
    return lax.rsqrt(jnp.mean(x * x, axis=1, keepdims=True) + EPSILON)


def documents(starts_ref, tokens):
    def passed(at):
        total = jnp.zeros(at.shape, jnp.float32)
        for i in range(starts_ref.shape[0]):
            total = total + jnp.where(at >= starts_ref[i : i + 1], 1.0, 0.0)
        return jnp.where(at >= tokens, -1.0, total)

    return passed


def padded(x_proj_ref, target_ref):
    tall = x_proj_ref.shape[0]
    target_ref[0:tall] = x_proj_ref[...]
    target_ref[tall:] = jnp.zeros((target_ref.shape[0] - tall, target_ref.shape[1]), target_ref.dtype)


def front_kernel(
    sizes, x_in_ref, gain_ref, modes_ref, cot_ref, starts_ref, taps_ref, cbias_ref, x_proj_ref, w_in_ref, w_out_ref,
    z_ref, gated_ref, cotg_ref, normed_ref, ext_ref, pre_ref, conv_ref, part_ref,
    x_ref, halo_ref, padded_ref, sent_ref, got_ref, low_send, low_recv, mode_ref, x2_ref, halo_send, halo_recv, in_buf, out_buf, in_sem, out_sem, cot_send, cot_recv, own_sem,
):
    count, twins = sizes
    rows, width = x_in_ref.shape
    modes = w_out_ref.shape[0]
    part = cot_ref.shape[1]
    inner = x_ref.shape[1]
    me = lax.axis_index("seq")
    mine = lax.axis_index("ch")
    barrier = pltpu.get_barrier_semaphore()
    for peer in (lax.rem(me + 1, count), lax.rem(me + count - 1, count)):
        pl.semaphore_signal(barrier, inc=1, device_id={"seq": peer}, device_id_type=MESH)
    for k in range(1, twins):
        peer = {"ch": lax.rem(mine + k, twins)}
        pl.semaphore_signal(barrier, inc=1, device_id=peer, device_id_type=MESH)

    pairs = inner // 256
    steps = pairs * modes

    def in_copy(step, b):
        slot = lax.rem(step, 2)
        return pltpu.make_async_copy(
            w_in_ref.at[lax.rem(step, modes), :, step // modes * 2 + b], in_buf.at[slot, b], in_sem.at[slot, b]
        )

    wide = out_buf.shape[2]
    out_steps = inner // wide * modes

    def out_copy(step):
        slot = lax.rem(step, 2)
        columns = pl.ds(pl.multiple_of(step // modes * wide, wide), wide)
        return pltpu.make_async_copy(
            w_out_ref.at[lax.rem(step, modes), :, columns], out_buf.at[slot], out_sem.at[slot]
        )

    for b in (0, 1):
        in_copy(0, b).start()
    out_copy(0).start()
    mode_columns(modes_ref, mode_ref)

    def norm_body(i, carry):
        rc = pl.ds(pl.multiple_of(i * 16, 16), 16)
        x = x_in_ref[rc, :].astype(jnp.float32)
        normed_ref[rc, :] = (x * row_scale(x) * gain_ref[...]).astype(jnp.bfloat16)
        return carry

    pl.semaphore_wait(barrier, 2 + twins - 1)

    own_part = pl.ds(pl.multiple_of(mine * part, part), part)
    cot_copies = [
        pltpu.make_async_remote_copy(
            src_ref=cot_ref, dst_ref=cotg_ref.at[:, own_part], send_sem=cot_send.at[k - 1], recv_sem=cot_recv.at[k - 1],
            device_id={"ch": lax.rem(mine + k, twins)}, device_id_type=MESH,
        )
        for k in range(1, twins)
    ]
    for copy in cot_copies:
        copy.start()
    own_copy = pltpu.make_async_copy(cot_ref, cotg_ref.at[:, own_part], own_sem.at[0])
    own_copy.start()
    def in_step(step, carry):
        slot = lax.rem(step, 2)
        mode = lax.rem(step, modes)

        @pl.when(step + 1 < steps)
        def _():
            for b in (0, 1):
                in_copy(step + 1, b).start()

        for b in (0, 1):
            in_copy(step, b).wait()
        weights = jnp.concatenate([in_buf.at[slot, b].reshape(2 * width, 128)[...] for b in (0, 1)], axis=1)
        mask = jnp.concatenate([mode_ref[...]] * 2, axis=1) == mode.astype(jnp.float32)
        columns = pl.ds(pl.multiple_of(step // modes * 256, 256), 256)
        both = jnp.dot(x2_ref[...], weights, preferred_element_type=jnp.float32)
        for j, target in enumerate((x_ref, z_ref)):
            found = jnp.where(mask, both[j * rows : (j + 1) * rows], target[:, columns].astype(jnp.float32))
            target[:, columns] = found.astype(jnp.bfloat16)
        return carry

    lax.fori_loop(0, rows // 16, norm_body, 0)
    x_ref[...] = jnp.zeros_like(x_ref)
    z_ref[...] = jnp.zeros_like(z_ref)
    row = lax.broadcasted_iota(jnp.int32, (256, 512), 0)
    column = lax.broadcasted_iota(jnp.int32, (256, 512), 1)
    for j in (0, 1):
        spread = (column == 2 * row + j).astype(jnp.bfloat16)
        for block in range(width // 256):
            x2_ref[j * rows : (j + 1) * rows, block * 512 : (block + 1) * 512] = jnp.dot(
                normed_ref[:, block * 256 : (block + 1) * 256], spread, preferred_element_type=jnp.float32
            ).astype(jnp.bfloat16)
    lax.fori_loop(0, steps, in_step, 0)
    halo_copy = pltpu.make_async_remote_copy(
        src_ref=x_ref.at[pl.ds(rows - 16, 16)], dst_ref=halo_ref, send_sem=halo_send.at[0], recv_sem=halo_recv.at[0],
        device_id={"seq": lax.rem(me + 1, count)}, device_id_type=MESH,
    )
    halo_copy.start()
    own_copy.wait()
    for copy in cot_copies:
        copy.wait_recv()

    def out_step(step, carry):
        slot = lax.rem(step, 2)
        mode = lax.rem(step, modes)

        @pl.when(step + 1 < out_steps)
        def _():
            out_copy(step + 1).start()

        out_copy(step).wait()
        mask = jnp.concatenate([mode_ref[...]] * (wide // 128), axis=1) == mode.astype(jnp.float32)
        columns = pl.ds(pl.multiple_of(step // modes * wide, wide), wide)
        found = jnp.dot(cotg_ref[...], out_buf[slot], preferred_element_type=jnp.float32)
        gated_ref[:, columns] = jnp.where(mask, found, gated_ref[:, columns])
        return carry

    gated_ref[...] = jnp.zeros_like(gated_ref)
    lax.fori_loop(0, out_steps // 2, out_step, 0)

    chunks, _, inner = pre_ref.shape
    padded(x_proj_ref, padded_ref)
    passed = documents(starts_ref, count * rows)
    spot = lax.broadcasted_iota(jnp.int32, (rows, 128), 0) + me * rows
    here = passed(spot)
    same = [jnp.where(passed(spot - lag) == here, 1.0, 0.0) for lag in (3, 2, 1, 0)]
    halo_copy.wait_recv()
    ext_ref[0:8] = halo_ref[8:16].astype(jnp.float32)
    ext_ref[8:] = x_ref[...].astype(jnp.float32)

    def conv_body(block, carry):
        cut = pl.ds(pl.multiple_of(block * 128, 128), 128)
        pre = jnp.zeros((rows, 128), jnp.float32) + cbias_ref[:, cut]
        for k in range(4):
            pre = pre + taps_ref[k : k + 1, cut] * ext_ref[5 + k : 5 + k + rows, cut] * same[k]
        pre_ref[:, :, cut] = pre.reshape(chunks, 16, 128)
        conv_ref[:, :, cut] = (pre / (1.0 + jnp.exp(-pre))).astype(jnp.bfloat16).reshape(chunks, 16, 128)
        return carry

    lax.fori_loop(0, inner // 128, conv_body, 0)
    part_ref[...] = lax.dot_general(
        conv_ref[...].reshape(rows, inner), padded_ref[...], (((1,), (1,)), ((), ())), preferred_element_type=jnp.float32
    )
    sent_ref[...] = part_ref[...].astype(jnp.bfloat16)
    low_copies = [
        pltpu.make_async_remote_copy(
            src_ref=sent_ref, dst_ref=got_ref.at[k - 1], send_sem=low_send.at[k - 1], recv_sem=low_recv.at[k - 1],
            device_id={"ch": lax.rem(mine + k, twins)}, device_id_type=MESH,
        )
        for k in range(1, twins)
    ]
    for copy in low_copies:
        copy.start()
    lax.fori_loop(out_steps // 2, out_steps, out_step, 0)
    for k, copy in enumerate(low_copies):
        copy.wait_recv()
        part_ref[...] += got_ref[k].astype(jnp.float32)
    for copy in cot_copies + low_copies + [halo_copy]:
        copy.wait_send()


def front(x_in, gain, modes, cot, starts, taps, cbias, x_proj_t, w_in, w_out):
    count, twins = lax.axis_size("seq"), lax.axis_size("ch")
    rows, width = x_in.shape
    inner = w_out.shape[2]
    f32, b16 = jnp.float32, jnp.bfloat16
    shape = jax.ShapeDtypeStruct
    vmem = pl.BlockSpec(memory_space=pltpu.VMEM)
    hbm = pl.BlockSpec(memory_space=pl.ANY)
    wide = min(512, inner)
    return pl.pallas_call(
        functools.partial(front_kernel, (count, twins)),
        in_specs=[vmem] * 8 + [hbm] * 2,
        out_specs=[vmem] * 8,
        out_shape=[
            shape((rows, inner), b16), shape((rows, inner), f32), shape((rows, width), b16), shape((rows, width), b16),
            shape((rows + 8, inner), f32), shape((rows // 16, 16, inner), f32), shape((rows // 16, 16, inner), b16),
            shape((rows, 256), f32),
        ],
        scratch_shapes=[
            pltpu.VMEM((rows, inner), b16), pltpu.VMEM((16, inner), b16), pltpu.VMEM((256, inner), b16),
            pltpu.VMEM((rows, 256), b16), pltpu.VMEM((twins - 1, rows, 256), b16),
            pltpu.SemaphoreType.DMA((twins - 1,)), pltpu.SemaphoreType.DMA((twins - 1,)),
            pltpu.VMEM((rows, 128), jnp.float32),
            pltpu.VMEM((2 * rows, 2 * width), jnp.bfloat16),
            pltpu.SemaphoreType.DMA((1,)),
            pltpu.SemaphoreType.DMA((1,)),
            pltpu.VMEM((2, 2, width, 2, 128), jnp.bfloat16),
            pltpu.VMEM((2, width, wide), jnp.bfloat16),
            pltpu.SemaphoreType.DMA((2, 2)),
            pltpu.SemaphoreType.DMA((2,)),
            pltpu.SemaphoreType.DMA((twins - 1,)),
            pltpu.SemaphoreType.DMA((twins - 1,)),
            pltpu.SemaphoreType.DMA((1,)),
        ],
        compiler_params=pltpu.CompilerParams(collective_id=1, has_side_effects=True, vmem_limit_bytes=56 << 20),
        name="front",
    )(x_in, gain, modes, cot, starts, taps, cbias, x_proj_t, w_in, w_out)


def tile_lanes(v, lanes):
    return jnp.concatenate([v] * (lanes // 128), axis=1)

def ring_places(count):
    ring = cycle_of(count)
    where = {s: i for i, s in enumerate(ring)}
    me = lax.axis_index("seq")
    onward = table_of(me, [ring[(where[s] + 1) % count] for s in range(count)])
    backward = table_of(me, [ring[(where[s] - 1) % count] for s in range(count)])
    place = table_of(me, [where[s] for s in range(count)])
    return ring, place, onward, backward


def add_products(accs, kind, k, cols_ref, blocks, modes_ref, ring, place, count):
    parts = []
    for way in (0, 1):
        step = k if way else count - k
        source = table_of(lax.rem(place + step, count), ring)
        parts.append((jnp.transpose(cols_ref[kind, way, k]), modes_ref[pl.ds(2 * source + way, 1), :]))
    right = jnp.concatenate(blocks, axis=0)
    for m, acc in enumerate(accs):
        left = jnp.concatenate(
            [part * jnp.where(row == m, 1.0, 0.0).astype(jnp.bfloat16) for part, row in parts], axis=1
        )
        found = jnp.dot(left, right, preferred_element_type=jnp.float32)
        acc[...] += found.reshape(acc.shape)


def core_kernel(
    sizes, w_in_ref, w_out_ref, normed_ref, cotg_ref, ext_ref, pre_ref, conv_ref, part_ref, z_ref, dgated_ref, starts_ref,
    taps_ref, x_t_ref, dt_proj_ref, dt_bias_ref, a_log_ref, skip_ref, modes_ref, x_in_ref, gain_ref,
    dwo_ref, dwz_ref, dwx_ref, mix_ref, small_ref, slice_ref, dots_ref, dgain_ref, scale_ref,
    x_proj_ref, same_ref, mode_ref, free_sem, g_ref, step_ref, dtd_ref, u_ref, sig_ref, low_t_ref, b_ref, c_ref, rate_ref, ends_ref,
    ends_sent, ends_got, steps_sent, steps_got, h0_ref, gz_ref, cols_ref,
    racc_ref, rows_ref, sum_ref, half_ref, half_got, four_ref, four_b16, four_got, in_buf, out_buf, mix_sent, mix_got,
    norm_sent, norm_got, dots_sent, dots_got, gain_sent, gain_got,
    ring_ref, hist_ref, lam_ref, w_ref, pend_ref, gstep_ref, gscan_ref, grad_ref, sent_ref, got_ref,
    gpre_ref, edge_ref,
    in_sem, out_sem, mix_send, mix_recv, half_send, half_recv, four_send, four_recv, last_send, last_recv, all_send, all_recv,
    ends_send, ends_recv, steps_send, steps_recv, norm_send, norm_recv, dots_send, dots_recv,
    gain_send, gain_recv, seq_send, seq_recv, twin_send, twin_recv, own_sem, dwo_sem,
    ring_send, ring_recv, gx_send, gx_recv, ch_send, ch_recv, edge_send, edge_recv,
):
    count, twins = sizes
    chunks, _, chans = pre_ref.shape
    rows = chunks * 16
    gx_ref = gz_ref.at[2]
    n = a_log_ref.shape[0]
    half = rows // 2
    ring, place, onward, backward = ring_places(count)
    me = lax.axis_index("seq")
    mine = lax.axis_index("ch")
    before = lax.rem(me + count - 1, count)
    nt = (((1,), (1,)), ((), ()))
    f32, b16 = jnp.float32, jnp.bfloat16
    lb = min(512, chans)

    modes, width = w_out_ref.shape[:2]
    part = width // twins
    eighths = chans // 128
    across = half_ref.shape[1]
    tall = half_ref.shape[0]
    depth = half_ref.shape[2]
    z_at = me // across
    x_at = lax.rem(me, across)

    def chunk_of(step):
        return pl.ds(pl.multiple_of(lax.rem(mine + 1 + step // modes, twins) * part, part), part)

    def in_copy(step, b):
        slot = step % 2
        return pltpu.make_async_copy(w_in_ref.at[step % modes, chunk_of(step), b], in_buf.at[slot, b], in_sem.at[slot, b])

    def in_copies(step, wait):
        for b in range(eighths):
            if wait:
                in_copy(step, b).wait()
            else:
                in_copy(step, b).start()

    def out_copy(step):
        slot = step % 2
        return pltpu.make_async_copy(w_out_ref.at[step % modes, chunk_of(step)], out_buf.at[slot], out_sem.at[slot])

    barrier = pltpu.get_barrier_semaphore()
    for k in range(1, count):
        pl.semaphore_signal(barrier, inc=1, device_id={"seq": lax.rem(me + k, count)}, device_id_type=MESH)
    for k in range(1, twins):
        peer = {"ch": lax.rem(mine + k, twins)}
        pl.semaphore_signal(barrier, inc=1, device_id=peer, device_id_type=MESH)
    in_copies(0, 0)
    out_copy(0).start()
    pl.semaphore_wait(barrier, count - 1 + twins - 1)

    slab = cols_ref.shape[4]
    side = lax.rem(mine, 2)
    twin = mine + 1 - 2 * side
    side_rows = pl.ds(pl.multiple_of(side * half, half), half)

    def column_source(kind, owner, those):
        return (normed_ref, cotg_ref)[kind].at[those, pl.ds(pl.multiple_of(owner * slab, slab), slab)]

    own_columns = [
        pltpu.make_async_copy(
            column_source(kind, me, pl.ds(way * half, half)), cols_ref.at[kind, way, 0], own_sem.at[kind, way]
        )
        for kind in (0, 1)
        for way in (0, 1)
    ]
    seq_copies = []
    for kind in (0, 1):
        for k in range(1, count):
            peer = table_of(lax.rem(place + jnp.where(side == 0, k, count - k), count), ring)
            seq_copies.append(
                pltpu.make_async_remote_copy(
                    src_ref=column_source(kind, peer, side_rows), dst_ref=cols_ref.at[kind, side, k],
                    send_sem=seq_send.at[kind, k - 1], recv_sem=seq_recv.at[kind, k - 1], device_id={"seq": peer},
                    device_id_type=MESH,
                )
            )
    for copy in own_columns + seq_copies:
        copy.start()
    twin_copies = [
        pltpu.make_async_remote_copy(
            src_ref=cols_ref.at[kind, side, pl.ds(1, count - 1)], dst_ref=cols_ref.at[kind, side, pl.ds(1, count - 1)],
            send_sem=twin_send.at[kind], recv_sem=twin_recv.at[kind], device_id={"ch": twin}, device_id_type=MESH,
        )
        for kind in (0, 1)
    ]

    passed = documents(starts_ref, count * rows)

    def maps_copies(send, recv):
        return [
            pltpu.make_async_remote_copy(
                src_ref=sent_ref, dst_ref=got_ref.at[k - 1], send_sem=send.at[k - 1],
                recv_sem=recv.at[k - 1], device_id={"ch": lax.rem(mine + k, twins)}, device_id_type=MESH,
            )
            for k in range(1, twins)
        ]


    def gate_body(i, carry):
        z = z_ref[i].astype(f32)
        g_ref[i] = dgated_ref[i] * (z / (1.0 + jnp.exp(-z)))
        return carry

    lax.fori_loop(0, chunks, gate_body, 0)
    rate_ref[...] = -math.log2(math.e) * jnp.exp(a_log_ref[...])
    own = (
        lax.broadcasted_iota(jnp.int32, (16, 16 * n), 1) // n == lax.broadcasted_iota(jnp.int32, (16, 16 * n), 0)
    )
    ones = own.astype(b16)
    token_row = lax.broadcasted_iota(jnp.int32, (16 * n, 16), 0) // n
    repeat = (token_row == lax.broadcasted_iota(jnp.int32, (16 * n, 16), 1)).astype(b16)
    pick_row = lax.broadcasted_iota(jnp.int32, (16 * n, 128), 0)
    pick_col = lax.broadcasted_iota(jnp.int32, (16 * n, 128), 1)
    is_b = pick_row % n == pick_col
    is_c = pick_row % n + n == pick_col
    pick_b = is_b.astype(b16)
    pick_c = is_c.astype(b16)
    flat = jnp.ones((256, 128), b16)
    total = part_ref[...]
    low_t_ref[...] = jnp.transpose(total[:, 0:128]).astype(b16)
    raw = jnp.dot(total[:, 0:128].astype(b16), dt_proj_ref[...], preferred_element_type=f32)
    step_ref[...] = raw.reshape(chunks, 16, chans)

    def step_body(i, carry):
        raw = step_ref[i] + dt_bias_ref[...]
        step = jnp.maximum(raw, 0.0) + jnp.log1p(jnp.exp(-jnp.abs(raw)))
        step_ref[i] = step
        sig_ref[i] = 1.0 / (1.0 + jnp.exp(-raw))
        at = lax.broadcasted_iota(jnp.int32, (16, 128), 0) + (me * rows + i * 16)
        big = jnp.where(passed(at) == passed(at - 1), 0.0, 1e30)
        dtd_ref[i] = step + jnp.concatenate([big] * (chans // 128), axis=1)
        u_ref[i] = step * conv_ref[i].astype(f32)
        maps = part_ref[pl.ds(pl.multiple_of(i * 16, 16), 16), 128:256]
        high = maps.astype(b16)
        low = (maps - high.astype(f32)).astype(b16)
        high = jnp.dot(repeat, high, preferred_element_type=f32)
        low = jnp.dot(repeat, low, preferred_element_type=f32)
        for target, chosen in ((b_ref, is_b), (c_ref, is_c)):
            terms = [jnp.where(chosen, term, 0.0).astype(b16) for term in (high, low)]
            found = jnp.dot(jnp.concatenate(terms, axis=1), flat, preferred_element_type=f32)
            target[pl.ds(i * 16, 16)] = found.reshape(16, n, 128)
        return carry

    lax.fori_loop(0, chunks, step_body, 0)

    def maps_block(chunk, pick):
        maps = part_ref[pl.ds(pl.multiple_of(chunk * 16, 16), 16), 128:256].astype(b16)
        found = lax.dot_general(maps, pick, nt, preferred_element_type=f32)
        return jnp.where(own, found, 0.0).astype(b16)

    ends_ref[0:n] = jnp.zeros((n, chans), f32)
    ends_ref[n : 2 * n] = jnp.ones((n, chans), f32)
    ends_ref[2 * n : 3 * n] = jnp.zeros((n, chans), f32)

    def ends_body(chunk, carry):
        for block in range(chans // lb):
            cut = slice(block * lb, (block + 1) * lb)
            rate = rate_ref[:, cut]
            h = ends_ref[0:n, cut]
            reach = ends_ref[n : 2 * n, cut]
            head = ends_ref[2 * n : 3 * n, cut]
            for t in range(16):
                decay = jnp.exp2(dtd_ref[chunk, t : t + 1, cut] * rate)
                h = decay * h + u_ref[chunk, t : t + 1, cut] * tile_lanes(b_ref[chunk * 16 + t], lb)
                reach = reach * decay
                head = head + reach * (g_ref[chunk, t : t + 1, cut] * tile_lanes(c_ref[chunk * 16 + t], lb))
            ends_ref[0:n, cut] = h
            ends_ref[n : 2 * n, cut] = reach
            ends_ref[2 * n : 3 * n, cut] = head
        return carry

    lax.fori_loop(0, chunks, ends_body, 0)
    ends_sent[0] = ends_ref[0:n].astype(b16)
    ends_sent[1] = ends_ref[2 * n : 3 * n].astype(b16)
    steps_sent[...] = jnp.sum(jnp.sum(dtd_ref[...], axis=0), axis=0, keepdims=True)
    ends_copies = []
    for k in range(1, count):
        peer = lax.rem(me + k, count)
        side = jnp.where(peer > me, 0, 1)
        ends_copies.append(
            pltpu.make_async_remote_copy(
                src_ref=ends_sent.at[side], dst_ref=ends_got.at[k - 1], send_sem=ends_send.at[k - 1],
                recv_sem=ends_recv.at[k - 1], device_id={"seq": peer}, device_id_type=MESH,
            )
        )
        ends_copies.append(
            pltpu.make_async_remote_copy(
                src_ref=steps_sent, dst_ref=steps_got.at[k - 1], send_sem=steps_send.at[k - 1],
                recv_sem=steps_recv.at[k - 1], device_id={"seq": peer}, device_id_type=MESH,
            )
        )
    for copy in ends_copies:
        copy.start()
    for copy in ends_copies:
        copy.wait_recv()

    def arrived(slots, valid):
        total = jnp.zeros((n, chans), f32)
        gap = jnp.zeros((1, chans), f32)
        for k, slot in enumerate(slots):
            term = ends_got[slot].astype(f32) * jnp.exp2(rate_ref[...] * gap)
            total = total + jnp.where(valid(k + 1), term, 0.0)
            gap = gap + steps_got[slot]
        return total

    h0_ref[...] = arrived(range(count - 1), lambda k: k <= me)
    pend_ref[...] = arrived(range(count - 2, -1, -1), lambda k: k + me < count)

    racc_ref[...] = h0_ref[...]

    def forward_body(chunk, carry):
        for block in range(chans // lb):
            cut = slice(block * lb, (block + 1) * lb)
            rate = rate_ref[:, cut]
            h = racc_ref[:, cut]
            for t in range(16):
                decay = jnp.exp2(dtd_ref[chunk, t : t + 1, cut] * rate)
                h = decay * h + u_ref[chunk, t : t + 1, cut] * tile_lanes(b_ref[chunk * 16 + t], lb)
                hist_ref[chunk, t * n : (t + 1) * n, cut] = h.astype(b16)
            racc_ref[:, cut] = h
        ssm = jnp.dot(maps_block(chunk, pick_c), hist_ref[chunk], preferred_element_type=f32)
        ssm = ssm + skip_ref[...] * conv_ref[chunk].astype(f32)
        z = z_ref[chunk].astype(f32)
        sig = 1.0 / (1.0 + jnp.exp(-z))
        rc = pl.ds(pl.multiple_of(chunk * 16, 16), 16)
        gz_ref[0, rc] = (ssm * (z * sig)).astype(b16)
        gz_ref[1, rc] = (dgated_ref[chunk] * ssm * (sig * (1.0 + z * (1.0 - sig)))).astype(b16)
        return carry

    lax.fori_loop(0, chunks, forward_body, 0)

    def ring_copy(kind, way, k):
        if k == 0:
            source = gz_ref.at[kind, pl.ds(way * half, half)]
        else:
            source = ring_ref.at[kind, way, k - 1]
        return pltpu.make_async_remote_copy(
            src_ref=source, dst_ref=ring_ref.at[kind, way, k], send_sem=ring_send.at[kind, way, k],
            recv_sem=ring_recv.at[kind, way, k], device_id={"seq": backward if way else onward}, device_id_type=MESH,
        )

    def relay(kind, k):
        for way in (0, 1):
            if kind == 2:
                gx_copy(way, k - 1).wait_recv()
                if k < count - 1:
                    gx_copy(way, k).start()
            else:
                ring_copy(kind, way, k - 1).wait_recv()
                if k < count - 1:
                    ring_copy(kind, way, k).start()

    def gx_slot(way, k):
        slot = way * (count - 1) + k
        return hist_ref.at[slot // 2, pl.ds(slot % 2 * half, half)]

    def gx_copy(way, k):
        return pltpu.make_async_remote_copy(
            src_ref=gx_slot(way, k - 1) if k else gx_ref.at[pl.ds(way * half, half)], dst_ref=gx_slot(way, k),
            send_sem=gx_send.at[way, k], recv_sem=gx_recv.at[way, k], device_id={"seq": backward if way else onward},
            device_id_type=MESH,
        )

    for kind in (0, 1):
        for way in (0, 1):
            ring_copy(kind, way, 0).start()
    turns = [(kind, k) for k in range(1, count) for kind in (0, 1)]
    early = turns[:2]
    late = turns[2:]

    racc_ref[...] = jnp.zeros_like(racc_ref)

    def span_body(i, carry):
        at = spans - 1 - i
        for sub in reversed(range(span // 16)):
            chunk = at * (span // 16) + sub
            for block in range(chans // lb):
                cut = slice(block * lb, (block + 1) * lb)
                rate = rate_ref[:, cut]
                pend = pend_ref[:, cut]
                racc = racc_ref[:, cut]
                for t in reversed(range(16)):
                    decay = jnp.exp2(dtd_ref[chunk, t : t + 1, cut] * rate)
                    lam = g_ref[chunk, t : t + 1, cut] * tile_lanes(c_ref[chunk * 16 + t], lb) + pend
                    pend = decay * lam
                    if t:
                        prior = hist_ref[chunk, (t - 1) * n : t * n, cut].astype(jnp.float32)
                    else:
                        prior = hist_ref[jnp.maximum(chunk - 1, 0), 15 * n : 16 * n, cut].astype(jnp.float32)
                        prior = jnp.where(chunk == 0, h0_ref[:, cut], prior)
                    w = pend * prior
                    racc = racc + w * step_ref[chunk, t : t + 1, cut]
                    lam_ref[t * n : (t + 1) * n, cut] = lam.astype(jnp.bfloat16)
                    w_ref[t * n : (t + 1) * n, cut] = (w * rate).astype(jnp.bfloat16)
                pend_ref[:, cut] = pend
                racc_ref[:, cut] = racc
            step = step_ref[chunk]
            conv = conv_ref[chunk].astype(jnp.float32)
            adj = jnp.dot(maps_block(chunk, pick_b), lam_ref[...], preferred_element_type=jnp.float32)
            wsum = jnp.dot(ones, w_ref[...], preferred_element_type=jnp.float32)
            gstep_ref[chunk] = wsum * math.log(2.0) + adj * conv
            gscan_ref[chunk] = adj * step
            gb = lax.dot_general(u_ref[chunk].astype(jnp.bfloat16), lam_ref[...], nt, preferred_element_type=jnp.float32)
            gc = lax.dot_general(
                g_ref[chunk].astype(jnp.bfloat16), hist_ref[chunk], nt, preferred_element_type=jnp.float32
            )
            gb = jnp.where(own, gb, 0.0).astype(jnp.bfloat16)
            gc = jnp.where(own, gc, 0.0).astype(jnp.bfloat16)
            grad_ref[pl.ds(pl.multiple_of(chunk * 16, 16), 16), 128:256] = jnp.dot(
                gb, pick_b, preferred_element_type=jnp.float32
            ) + jnp.dot(gc, pick_c, preferred_element_type=jnp.float32)
        return carry

    span = 32
    spans = rows // span
    mode_columns(modes_ref, mode_ref)
    padded(x_t_ref, x_proj_ref)
    passed = documents(starts_ref, count * rows)
    spot = lax.broadcasted_iota(jnp.int32, (rows, 128), 0) + me * rows
    here = passed(spot)
    for i in range(7):
        same_ref[i] = jnp.where(passed(spot + (i - 3)) == here, 1.0, 0.0).astype(b16)
    lax.fori_loop(0, spans // 2, span_body, 0)
    relay(*early[0])
    for copy in seq_copies:
        copy.wait_recv()
    for copy in twin_copies:
        copy.start()
    lax.fori_loop(spans // 2, spans, span_body, 0)
    for peer in (onward, backward):
        pl.semaphore_signal(free_sem, inc=1, device_id={"seq": peer}, device_id_type=MESH)
    relay(*early[1])

    rows_ref[...] = jnp.zeros_like(rows_ref)

    def raw_body(i, carry):
        full = gstep_ref[i] * sig_ref[i]
        rows_ref[5:6] += jnp.sum(full, axis=0, keepdims=True)
        rows_ref[6:7] += jnp.sum(g_ref[i] * conv_ref[i].astype(jnp.float32), axis=0, keepdims=True)
        gx_ref[pl.ds(pl.multiple_of(i * 16, 16), 16), :] = full.astype(jnp.bfloat16)
        return carry

    lax.fori_loop(0, chunks, raw_body, 0)
    grad_ref[:, 0:128] = lax.dot_general(gx_ref[...], dt_proj_ref[...], nt, preferred_element_type=jnp.float32)
    sent_ref[...] = grad_ref[...].astype(jnp.bfloat16)
    ch_copies = maps_copies(ch_send, ch_recv)
    for copy in ch_copies:
        copy.start()
    relay(*late[0])
    sum_ref[160:288] = jnp.dot(low_t_ref[...], gx_ref[...], preferred_element_type=jnp.float32)
    for copy in ch_copies:
        copy.wait_recv()
    total = grad_ref[...]
    for k in range(twins - 1):
        total = total + got_ref[k].astype(jnp.float32)
    grad_ref[...] = total
    relay(*late[1])

    skip = skip_ref[...]
    def pre_body(i, carry):
        rc = pl.ds(pl.multiple_of(i * 16, 16), 16)
        g_conv = jnp.dot(grad_ref[rc, :].astype(jnp.bfloat16), x_proj_ref[...], preferred_element_type=jnp.float32)
        g_conv = g_conv + skip * g_ref[i] + gscan_ref[i]
        pre = pre_ref[i]
        sig = 1.0 / (1.0 + jnp.exp(-pre))
        gpre = g_conv * sig * (1.0 + pre * (1.0 - sig))
        gpre_ref[rc, :] = gpre
        return carry

    pre_body(0, 0)
    edge_ref[...] = gpre_ref[0:8, :]
    edge_copy = pltpu.make_async_remote_copy(
        src_ref=edge_ref, dst_ref=gpre_ref.at[pl.ds(rows, 8)], send_sem=edge_send.at[0], recv_sem=edge_recv.at[0],
        device_id={"seq": before}, device_id_type=MESH,
    )
    edge_copy.start()
    lax.fori_loop(1, chunks, pre_body, 0)
    flipped = jnp.transpose(grad_ref[...]).astype(jnp.bfloat16)
    sum_ref[0:160] = jnp.dot(flipped[0:160], conv_ref[...].reshape(rows, chans), preferred_element_type=jnp.float32)
    relay(*late[2])
    edge_copy.wait_recv()

    def taps_body(block, carry):
        cut = pl.ds(pl.multiple_of(block * 128, 128), 128)
        gpre = gpre_ref[0:rows, cut]
        rows_ref[4:5, cut] = jnp.sum(gpre, axis=0, keepdims=True)
        total = jnp.zeros((rows, 128), jnp.float32)
        for k in range(4):
            lag = 3 - k
            total = total + gpre_ref[lag : lag + rows, cut] * taps_ref[k : k + 1, cut] * same_ref[3 + lag].astype(jnp.float32)
            rows_ref[k : k + 1, cut] = jnp.sum(
                gpre * ext_ref[5 + k : 5 + k + rows, cut] * same_ref[k].astype(jnp.float32), axis=0, keepdims=True
            )
        gx_ref[:, cut] = total.astype(jnp.bfloat16)
        return carry

    lax.fori_loop(0, chans // 128, taps_body, 0)
    pl.semaphore_wait(free_sem, 2)
    for way in (0, 1):
        gx_copy(way, 0).start()
    sum_ref[288:304] = racc_ref[...] * rate_ref[...] * math.log(2.0)
    sum_ref[304:312] = rows_ref[...]
    if tall * across * depth > 312:
        sum_ref[312:] = jnp.zeros((tall * across * depth - 312, chans), jnp.float32)
    for z in range(tall):
        for x in range(across):
            first = (z * across + x) * depth
            half_ref[z, x] = sum_ref[first : first + depth].astype(jnp.bfloat16)

    def to(device):
        return dict(device_id={"seq": device}, device_id_type=MESH)

    half_copies = [
        pltpu.make_async_remote_copy(
            src_ref=half_ref.at[:, lax.rem(x_at + k, across)], dst_ref=half_got.at[k - 1], send_sem=half_send.at[k - 1],
            recv_sem=half_recv.at[k - 1], **to(z_at * across + lax.rem(x_at + k, across)),
        )
        for k in range(1, across)
    ]
    four_copies = [
        pltpu.make_async_remote_copy(
            src_ref=four_b16.at[lax.rem(z_at + k, tall)], dst_ref=four_got.at[k - 1], send_sem=four_send.at[k - 1],
            recv_sem=four_recv.at[k - 1], **to(lax.rem(z_at + k, tall) * across + x_at),
        )
        for k in range(1, tall)
    ]
    last_copies = [
        pltpu.make_async_remote_copy(
            src_ref=small_ref.at[z_at, x_at], dst_ref=small_ref.at[z_at, x_at], send_sem=last_send.at[k - 1],
            recv_sem=last_recv.at[k - 1], **to(lax.rem(z_at + k, tall) * across + x_at),
        )
        for k in range(1, tall)
    ]
    all_copies = [
        pltpu.make_async_remote_copy(
            src_ref=small_ref.at[:, x_at], dst_ref=small_ref.at[:, x_at], send_sem=all_send.at[k - 1],
            recv_sem=all_recv.at[k - 1], **to(z_at * across + lax.rem(x_at + k, across)),
        )
        for k in range(1, across)
    ]

    def small_phase(phase):
        if phase == 0:
            for copy in half_copies:
                copy.start()
        elif phase == 1:
            for copy in half_copies:
                copy.wait_recv()
            for z in range(tall):
                first = pl.multiple_of((z * across + x_at) * depth, depth)
                total = sum_ref[pl.ds(first, depth)]
                for k in range(across - 1):
                    total = total + half_got[k, z].astype(jnp.float32)
                four_ref[z] = total
                four_b16[z] = total.astype(jnp.bfloat16)
            for copy in four_copies:
                copy.start()
        elif phase == 2:
            for copy in four_copies:
                copy.wait_recv()
            total = four_ref[z_at]
            for k in range(tall - 1):
                total = total + four_got[k].astype(jnp.float32)
            small_ref[z_at, x_at] = total.astype(jnp.bfloat16)
            for copy in last_copies:
                copy.start()
        elif phase == 3:
            for copy in last_copies:
                copy.wait_recv()
            for copy in all_copies:
                copy.start()
        else:
            for copy in all_copies:
                copy.wait_recv()
            for copy in half_copies + four_copies + last_copies + all_copies:
                copy.wait_send()

    small_phase(0)
    dwo_accs = [ref.at[0 : slab // 16] for ref in (dtd_ref, u_ref, sig_ref)]
    dwz_accs = [ref.at[0 : slab // 16] for ref in (step_ref, g_ref, gscan_ref)]
    dwx_accs = [dwx_ref.at[m] for m in range(modes)]
    for acc in dwo_accs + dwz_accs + dwx_accs:
        acc[...] = jnp.zeros_like(acc)

    def products(kind, k):
        if k == 0:
            source = gx_ref if kind == 2 else gz_ref.at[kind]
            blocks = [source[way * half : (way + 1) * half] for way in (0, 1)]
        else:
            blocks = [gx_slot(way, k - 1)[...] if kind == 2 else ring_ref[kind, way, k - 1] for way in (0, 1)]
        accs = (dwo_accs, dwz_accs, dwx_accs)[kind]
        add_products(accs, 0 if kind else 1, k, cols_ref, blocks, modes_ref, ring, place, count)
        if kind < 2 and k == count - 1:
            for copy in out_copies[kind]:
                copy.start()

    out_copies = [
        [pltpu.make_async_copy(acc, target.at[m], dwo_sem.at[kind, m]) for m, acc in enumerate(accs)]
        for kind, (accs, target) in enumerate(((dwo_accs, dwo_ref), (dwz_accs, dwz_ref)))
    ]

    def mix_copy(j):
        return pltpu.make_async_remote_copy(
            src_ref=mix_sent.at[j], dst_ref=mix_got.at[j], send_sem=mix_send.at[j], recv_sem=mix_recv.at[j],
            device_id={"ch": lax.rem(mine + 1 + j, twins)}, device_id_type=MESH,
        )

    steps = twins * modes

    def norm_copy(j):
        return pltpu.make_async_remote_copy(
            src_ref=norm_sent.at[j], dst_ref=norm_got.at[j], send_sem=norm_send.at[j], recv_sem=norm_recv.at[j],
            device_id={"ch": lax.rem(mine + 1 + j, twins)}, device_id_type=MESH,
        )

    def normed_unit(j, m):
        step = j * modes + m
        if step + 1 < steps:
            in_copies(step + 1, 0)
        in_copies(step, 1)
        spread_products(in_buf.at[step % 2], gz_ref, mode_ref, slice_ref, m, part)

    def normed_end(j):
        for q in range(part // 128):
            lanes = slice(q * 128, (q + 1) * 128)
            cut = pl.ds(pl.multiple_of(lax.rem(mine + 1 + j, twins) * part + q * 128, 128), 128)
            dots_ref[...] += slice_ref[:, lanes] * x_in_ref[:, cut].astype(f32) * gain_ref[:, cut]
        if j < twins - 1:
            norm_sent[j] = slice_ref[...].astype(b16)
            norm_copy(j).start()

    def mix_unit(j):
        for m in range(modes):
            step = j * modes + m
            if step + 1 < steps:
                out_copy(step + 1).start()
            out_copy(step).wait()
            mask = jnp.concatenate([mode_ref[...]] * (part // 128), axis=1) == float(m)
            found = lax.dot_general(gz_ref[0], out_buf[step % 2], nt, preferred_element_type=jnp.float32)
            mix_ref[...] = jnp.where(mask, found, mix_ref[...]) if m else found
        if j < twins - 1:
            mix_sent[j] = mix_ref[...].astype(jnp.bfloat16)
            mix_copy(j).start()

    dots_copies = [
        pltpu.make_async_remote_copy(
            src_ref=dots_sent, dst_ref=dots_got.at[k - 1], send_sem=dots_send.at[k - 1], recv_sem=dots_recv.at[k - 1],
            device_id={"ch": lax.rem(mine + k, twins)}, device_id_type=MESH,
        )
        for k in range(1, twins)
    ]
    gain_copies = [
        pltpu.make_async_remote_copy(
            src_ref=gain_sent, dst_ref=gain_got.at[k - 1], send_sem=gain_send.at[k - 1], recv_sem=gain_recv.at[k - 1],
            device_id={"seq": lax.rem(me + k, count)}, device_id_type=MESH,
        )
        for k in range(1, count)
    ]

    def scale_body(i, carry):
        rc = pl.ds(pl.multiple_of(i * 16, 16), 16)
        scale_ref[rc] = jnp.broadcast_to(row_scale(x_in_ref[rc].astype(f32)), (16, 128))
        return carry

    def dots_unit():
        lax.fori_loop(0, chunks, scale_body, 0)
        dots_sent[...] = dots_ref[...].astype(b16)
        for copy in dots_copies:
            copy.start()

    def slice_unit():
        for j in range(twins - 1):
            norm_copy(j).wait_recv()
            slice_ref[...] += norm_got[j].astype(f32)
        for q in range(part // 128):
            lanes = slice(q * 128, (q + 1) * 128)
            cut = pl.ds(pl.multiple_of(mine * part + q * 128, 128), 128)
            terms = slice_ref[:, lanes] * x_in_ref[:, cut].astype(f32) * scale_ref[...]
            gain_sent[:, lanes] = jnp.broadcast_to(jnp.sum(terms, axis=0, keepdims=True), (8, 128))
        for copy in gain_copies:
            copy.start()

    def gain_unit():
        total = gain_sent[...]
        for k, copy in enumerate(gain_copies):
            copy.wait_recv()
            total = total + gain_got[k]
        dgain_ref[...] = total
        for k, copy in enumerate(dots_copies):
            copy.wait_recv()
            dots_ref[...] += dots_got[k].astype(f32)
        mean = jnp.sum(dots_ref[...], axis=1, keepdims=True) / width
        dots_ref[...] = jnp.broadcast_to(mean, (rows, 128))
        for j in range(twins - 1):
            mix_copy(j).wait_recv()
            mix_ref[...] += mix_got[j].astype(f32)

    edge_copy.wait_send()
    dots_ref[...] = jnp.zeros_like(dots_ref)
    work = []
    for j in range(twins):
        for m in range(modes):
            work.append(functools.partial(normed_unit, j, m))
        work.append(functools.partial(normed_end, j))
        if j < 4:
            work.append(functools.partial(small_phase, j + 1))
    work.append(dots_unit)
    for j in range(twins):
        work.append(functools.partial(mix_unit, j))
    work += [slice_unit, gain_unit]
    for copy in own_columns:
        copy.wait()
    for copy in twin_copies:
        copy.wait_recv()
    ready = [(0, 0), (1, 0), (2, 0)] + early + late[:3]
    rest, last = late[3:], [(2, k) for k in range(1, count)]
    turns = []
    while rest or last:
        turns += rest[:2] + last[:1]
        rest, last = rest[2:], last[1:]
    for i, turn in enumerate(turns):
        left = len(turns) - i
        for _ in range(min(len(work), max(2, -(-len(work) // left)))):
            work.pop(0)()
        relay(*turn)
        ready.append(turn)
        for _ in range(2 if len(ready) > left else 1):
            if len(ready) > 1:
                products(*ready.pop(0))
    for unit in work:
        unit()
    for turn in ready:
        products(*turn)
    for copy in out_copies[0] + out_copies[1]:
        copy.wait()
    for j in range(twins - 1):
        mix_copy(j).wait_send()
        norm_copy(j).wait_send()
    for copy in dots_copies + gain_copies + seq_copies + twin_copies:
        copy.wait_send()
    for way in (0, 1):
        for k in range(count - 1):
            gx_copy(way, k).wait_send()

    for kind in (0, 1):
        for way in (0, 1):
            for k in range(count - 1):
                ring_copy(kind, way, k).wait_send()
    for copy in ch_copies + ends_copies:
        copy.wait_send()


def spread_products(buf, trio_ref, mode_ref, target, m, part):
    nt = (((1,), (1,)), ((), ()))
    chosen = mode_ref[...] == float(m)
    row = lax.broadcasted_iota(jnp.int32, (256, 128), 0)
    column = lax.broadcasted_iota(jnp.int32, (256, 128), 1)
    picks = [(row == 2 * column + j).astype(jnp.bfloat16) for j in (1, 0)]
    rows = trio_ref.shape[1]
    stacked = trio_ref[1:3].reshape(2 * rows, trio_ref.shape[2])
    for q in range(2 * part // 256):
        weights = jnp.concatenate(
            [buf.at[b].reshape(2 * part, 128)[q * 256 : (q + 1) * 256] for b in range(buf.shape[0])], axis=1
        )
        found = lax.dot_general(stacked, weights, nt, preferred_element_type=jnp.float32).astype(jnp.bfloat16)
        total = jnp.dot(found[:rows], picks[0], preferred_element_type=jnp.float32)
        total = total + jnp.dot(found[rows:], picks[1], preferred_element_type=jnp.float32)
        cut = pl.ds(q * 128, 128)
        target[:, cut] = jnp.where(chosen, total, target[:, cut]) if m else total


def core(
    w_in, w_out, normed, cotg, ext, pre, conv, maps, z, dgated, starts, taps, x_proj_t, dt_proj, dt_bias, a_log, skip, modes,
    x_in, gain,
):
    count, twins = lax.axis_size("seq"), lax.axis_size("ch")
    rows, chans = z.shape
    n = a_log.shape[0]
    chunks = rows // 16
    width = w_out.shape[1]
    slab = width // count
    part = width // twins
    tall, across = 4, count // 4
    depth = -(-312 // (16 * count)) * 16
    vmem = pl.BlockSpec(memory_space=pltpu.VMEM)
    hbm = pl.BlockSpec(memory_space=pl.ANY)
    cube = lambda a: a.reshape((chunks, a.shape[0] // chunks) + a.shape[1:])
    f32, b16 = jnp.float32, jnp.bfloat16
    shape = jax.ShapeDtypeStruct
    dma = pltpu.SemaphoreType.DMA
    keep = pltpu.VMEM
    operands = [w_in, w_out, normed, cotg, ext, pre, conv, maps, cube(z), cube(dgated), starts, taps, x_proj_t, dt_proj, dt_bias,
                a_log, skip, modes, x_in, gain]
    block = (chunks, 16, chans)
    pair = lambda size: [dma((size,)), dma((size,))]
    return pl.pallas_call(
        functools.partial(core_kernel, (count, twins)),
        in_specs=[hbm] * 4 + [vmem] * (len(operands) - 4),
        out_specs=[hbm] * 2 + [vmem] * 7,
        out_shape=[
            shape((3, slab // 16, 16, chans), f32), shape((3, slab // 16, 16, chans), f32), shape((3, slab, chans), f32),
            shape((rows, part), f32), shape((tall, across, depth, chans), b16), shape((rows, part), f32),
            shape((rows, 128), f32), shape((8, part), f32), shape((rows, 128), f32),
        ],
        scratch_shapes=[
            keep((256, chans), b16), keep((7, rows, 128), b16), keep((rows, 128), f32), pltpu.SemaphoreType.REGULAR, keep(block, f32), keep(block, f32),
            keep(block, f32), keep(block, f32), keep(block, f32), keep((128, rows), b16), keep((rows, n, 128), f32),
            keep((rows, n, 128), f32), keep((n, chans), f32), keep((3 * n, chans), f32),
            keep((2, n, chans), b16), keep((count - 1, n, chans), b16), keep((1, chans), f32),
            keep((count - 1, 1, chans), f32), keep((n, chans), f32), keep((3, rows, chans), b16),
            keep((2, 2, count, rows // 2, slab), b16),
            keep((n, chans), f32), keep((8, chans), f32), keep((tall * across * depth, chans), f32),
            keep((tall, across, depth, chans), b16), keep((across - 1, tall, depth, chans), b16),
            keep((tall, depth, chans), f32), keep((tall, depth, chans), b16), keep((tall - 1, depth, chans), b16),
            keep((2, chans // 128, part, 2, 128), b16), keep((2, part, chans), b16), keep((twins - 1, rows, part), b16),
            keep((twins - 1, rows, part), b16),
            keep((twins - 1, rows, part), b16), keep((twins - 1, rows, part), b16), keep((rows, 128), b16),
            keep((twins - 1, rows, 128), b16), keep((8, part), f32), keep((count - 1, 8, part), f32),
            keep((2, 2, count - 1, rows // 2, chans), b16),
            keep((chunks, 16 * n, chans), b16), keep((16 * n, chans), b16),
            keep((16 * n, chans), b16), keep((n, chans), f32), keep(block, f32), keep(block, f32), keep((rows, 256), f32), keep((rows, 256), b16), keep((twins - 1, rows, 256), b16),
            keep((rows + 8, chans), f32), keep((8, chans), f32),
            dma((2, chans // 128)), dma((2,)), *pair(twins - 1), *pair(across - 1), *pair(tall - 1), *pair(tall - 1),
            *pair(across - 1), *pair(count - 1), *pair(count - 1), *pair(twins - 1), *pair(twins - 1),
            *pair(count - 1), dma((2, count - 1)), dma((2, count - 1)), dma((2,)), dma((2,)), dma((2, 2)), dma((2, 3)),
            dma((2, 2, count - 1)), dma((2, 2, count - 1)), dma((2, count - 1)), dma((2, count - 1)), *pair(twins - 1), dma((1,)), dma((1,)),
        ],
        compiler_params=pltpu.CompilerParams(collective_id=2, has_side_effects=True, vmem_limit_bytes=63 << 20),
        name="core",
    )(*operands)


def lane_blocks(w_in):
    kinds, width, _, chans = w_in.shape
    return w_in.reshape(kinds, width, 2, chans // 128, 128).transpose(0, 1, 3, 2, 4)


def finish_kernel(
    x_part_ref, z_part_ref, out_part_ref, *refs,
):
    sources, refs = refs[:9], refs[9:]
    (
        dw_in_ref, dw_out_ref, block_ref, dx_ref, gain_out_ref, taps_ref, cbias_ref, x_proj_ref, dt_proj_ref, dt_bias_ref,
        a_log_ref, skip_ref,
    ) = refs[:12]
    buffers, (sems, out_sem, in_sem) = refs[12:21], refs[21:]
    small_ref, slice_ref, mix_ref, mean_ref, scale_ref, cot_ref, x_ref, gain_ref, dgain_ref = buffers
    kinds, _, chans = x_part_ref.shape
    part = slice_ref.shape[1]
    mine = lax.axis_index("ch")
    own_part = pl.ds(pl.multiple_of(mine * part, part), part)
    fetches = [
        pltpu.make_async_copy(source.at[:, own_part] if i in (6, 7) else source, buffer, in_sem.at[i])
        for i, (source, buffer) in enumerate(zip(sources, buffers))
    ]
    for copy in fetches:
        copy.start()
    copies = [pltpu.make_async_copy(out_part_ref, dw_out_ref, out_sem.at[0])]
    for m in range(kinds):
        for b in range(chans // 128):
            for j, source in enumerate((x_part_ref, z_part_ref)):
                copies.append(
                    pltpu.make_async_copy(
                        source.at[m, :, pl.ds(b * 128, 128)], dw_in_ref.at[m, :, b, j], sems.at[len(copies) - 1]
                    )
                )
    for copy in copies:
        copy.start()
    for copy in fetches:
        copy.wait()
    scale = scale_ref[...]
    bent = scale * scale * scale * mean_ref[...]
    for q in range(part // 128):
        lanes = slice(q * 128, (q + 1) * 128)
        x = x_ref[:, lanes].astype(jnp.float32)
        block_ref[:, lanes] = (x + mix_ref[:, lanes]).astype(jnp.bfloat16)
        weighted = slice_ref[:, lanes] * gain_ref[:, lanes]
        dx_ref[:, lanes] = cot_ref[:, lanes].astype(jnp.float32) + scale * weighted - x * bent
    gain_out_ref[...] = dgain_ref[0:1]
    x_proj_ref[...] = small_ref[0:160].astype(jnp.float32)
    dt_proj_ref[...] = small_ref[160:288].astype(jnp.float32)
    a_log_ref[...] = small_ref[288:304].astype(jnp.float32)
    rest = small_ref[304:320].astype(jnp.float32)
    taps_ref[...] = rest[0:4]
    cbias_ref[...] = rest[4:5]
    dt_bias_ref[...] = rest[5:6]
    skip_ref[...] = rest[6:7]
    for copy in copies:
        copy.wait()


def finish(x_part, z_part, out_part, small, total, mix, mean, scale, cot, x_in, gain, dgain):
    kinds, slab, chans = x_part.shape
    rows, part = total.shape
    vmem = pl.BlockSpec(memory_space=pltpu.VMEM)
    hbm = pl.BlockSpec(memory_space=pl.ANY)
    f32 = jnp.float32
    shape = jax.ShapeDtypeStruct
    outs = pl.pallas_call(
        finish_kernel,
        in_specs=[hbm] * 12,
        out_specs=[hbm] * 2 + [vmem] * 10,
        out_shape=[
            shape((kinds, slab, chans // 128, 2, 128), f32), shape((kinds, slab, chans), f32),
            shape((rows, part), jnp.bfloat16), shape((rows, part), f32), shape((1, part), f32), shape((4, chans), f32),
            shape((1, chans), f32), shape((160, chans), f32), shape((128, chans), f32), shape((1, chans), f32),
            shape((16, chans), f32), shape((1, chans), f32),
        ],
        scratch_shapes=[
            pltpu.VMEM(small.shape, small.dtype), pltpu.VMEM((rows, part), f32), pltpu.VMEM((rows, part), f32),
            pltpu.VMEM((rows, 128), f32), pltpu.VMEM((rows, 128), f32), pltpu.VMEM((rows, part), cot.dtype),
            pltpu.VMEM((rows, part), x_in.dtype), pltpu.VMEM((1, part), f32), pltpu.VMEM(dgain.shape, f32),
            pltpu.SemaphoreType.DMA((kinds * chans // 64,)), pltpu.SemaphoreType.DMA((1,)), pltpu.SemaphoreType.DMA((9,)),
        ],
        compiler_params=pltpu.CompilerParams(vmem_limit_bytes=60 << 20),
        name="finish",
    )(x_part, z_part, out_part, small, total, mix, mean, scale, cot, x_in, gain, dgain)
    dw_in = outs[0].transpose(0, 1, 3, 2, 4).reshape(kinds, slab, 2, chans)
    return (outs[2], outs[3], outs[4][0], dw_in, outs[5], outs[6][0], outs[7].T, outs[8], outs[9][0], outs[10], outs[11][0], outs[1])


def shards(
    x_in,
    norm_gain,
    w_in,
    conv_weight,
    conv_bias,
    x_proj,
    dt_proj,
    dt_bias,
    a_log,
    d_skip,
    w_out,
    modes,
    doc_lengths,
    cotangent,
):
    seq_count = lax.axis_size("seq")
    tok_rows = x_in.shape[0]
    inner_local = conv_bias.shape[0]
    docs = doc_lengths.shape[0]
    order = jnp.arange(docs, dtype=jnp.int32)
    starts = jnp.sum(jnp.where(order[:, None] > order[None, :], doc_lengths[None, :], 0), axis=1)
    starts = jnp.broadcast_to(starts[:, None], (docs, 128))
    mode_rows = modes.reshape(2 * seq_count, tok_rows // 2)
    blocks = lane_blocks(w_in)
    gain = norm_gain[None]
    x_proj_t = x_proj.T
    z_branch, d_gated, cotg, normed, extended, conv_pre, conv_out, maps = front(
        x_in, gain, mode_rows, cotangent, starts, conv_weight, conv_bias[None], x_proj_t, blocks, w_out
    )
    d_w_out, d_w_z, d_w_x, mixer, smalls, d_slice, mean, d_gain, scale = core(
        blocks, w_out, normed, cotg, extended, conv_pre, conv_out, maps, z_branch, d_gated, starts, conv_weight, x_proj_t,
        dt_proj, dt_bias[None], a_log, d_skip[None], mode_rows, x_in, gain,
    )
    return finish(
        d_w_x, d_w_z.reshape(d_w_x.shape), d_w_out.reshape(d_w_x.shape), smalls.reshape(-1, inner_local), d_slice, mixer,
        mean, scale, cotangent, x_in, gain, d_gain,
    )


def solution(mesh):
    return jax.shard_map(
        shards,
        mesh=mesh,
        in_specs=(
            P("seq", None),
            P(),
            P(None, None, None, "ch"),
            P(None, "ch"),
            P("ch"),
            P("ch", None),
            P(None, "ch"),
            P("ch"),
            P(None, "ch"),
            P("ch"),
            P(None, None, "ch"),
            P(),
            P(),
            P("seq", "ch"),
        ),
        out_specs=(
            P("seq", "ch"),
            P("seq", "ch"),
            P("ch"),
            P(None, "seq", None, "ch"),
            P(None, "ch"),
            P("ch"),
            P("ch", None),
            P(None, "ch"),
            P("ch"),
            P(None, "ch"),
            P("ch"),
            P(None, "seq", "ch"),
        ),
        check_vma=False,
    )
```

```python
import functools
import math

import jax
import jax.numpy as jnp
from jax import lax
from jax.experimental import pallas as pl
from jax.experimental.pallas import tpu as pltpu
from jax.sharding import PartitionSpec as P

EPSILON = 1e-05


MESH = pl.DeviceIdType.MESH


def cycle_of(count):
    across = count // 4
    walk = [(0, x) for x in range(across)]
    for turn, x in enumerate(reversed(range(across))):
        column = [(z, x) for z in range(1, 4)]
        walk += column[::-1] if turn % 2 else column
    return [z * across + x for z, x in walk]


def table_of(index, values):
    picked = jnp.int32(values[0])
    for i in range(1, len(values)):
        picked = jnp.where(index == i, jnp.int32(values[i]), picked)
    return picked


def mode_columns(modes_ref, target_ref):
    half = target_ref.shape[0] // 2
    for way in (0, 1):
        row = modes_ref[pl.ds(2 * lax.axis_index("seq") + way, 1), :].astype(jnp.float32)
        target_ref[way * half : (way + 1) * half] = jnp.transpose(jnp.broadcast_to(row, (128, half)))


def row_scale(x):
    return lax.rsqrt(jnp.mean(x * x, axis=1, keepdims=True) + EPSILON)


def documents(starts_ref, tokens):
    def passed(at):
        total = jnp.zeros(at.shape, jnp.float32)
        for i in range(starts_ref.shape[0]):
            total = total + jnp.where(at >= starts_ref[i : i + 1], 1.0, 0.0)
        return jnp.where(at >= tokens, -1.0, total)

    return passed


def padded(x_proj_ref, target_ref):
    tall = x_proj_ref.shape[0]
    target_ref[0:tall] = x_proj_ref[...]
    target_ref[tall:] = jnp.zeros((target_ref.shape[0] - tall, target_ref.shape[1]), target_ref.dtype)


def front_kernel(
    sizes, x_in_ref, gain_ref, modes_ref, cot_ref, starts_ref, taps_ref, cbias_ref, x_proj_ref, w_in_ref, w_out_ref,
    z_ref, gated_ref, cols_ref, ext_ref, pre_ref, conv_ref, part_ref,
    cotg_ref, normed_ref, cols_sem, seq_send, seq_recv, twin_send, twin_recv, x_ref, halo_ref, padded_ref, sent_ref, got_ref, low_send, low_recv, mode_ref, x2_ref, halo_send, halo_recv, in_buf, out_buf, in_sem, out_sem, cot_send, cot_recv, own_sem,
):
    count, twins = sizes
    rows, width = x_in_ref.shape
    modes = w_out_ref.shape[0]
    part = cot_ref.shape[1]
    inner = x_ref.shape[1]
    me = lax.axis_index("seq")
    mine = lax.axis_index("ch")
    barrier = pltpu.get_barrier_semaphore()
    for k in range(1, count):
        pl.semaphore_signal(barrier, inc=1, device_id={"seq": lax.rem(me + k, count)}, device_id_type=MESH)
    for k in range(1, twins):
        peer = {"ch": lax.rem(mine + k, twins)}
        pl.semaphore_signal(barrier, inc=1, device_id=peer, device_id_type=MESH)

    pairs = inner // 256
    steps = pairs * modes

    def in_copy(step, b):
        slot = lax.rem(step, 2)
        return pltpu.make_async_copy(
            w_in_ref.at[lax.rem(step, modes), :, step // modes * 2 + b], in_buf.at[slot, b], in_sem.at[slot, b]
        )

    wide = out_buf.shape[2]
    out_steps = inner // wide * modes

    def out_copy(step):
        slot = lax.rem(step, 2)
        columns = pl.ds(pl.multiple_of(step // modes * wide, wide), wide)
        return pltpu.make_async_copy(
            w_out_ref.at[lax.rem(step, modes), :, columns], out_buf.at[slot], out_sem.at[slot]
        )

    for b in (0, 1):
        in_copy(0, b).start()
    out_copy(0).start()
    mode_columns(modes_ref, mode_ref)

    def norm_body(i, carry):
        rc = pl.ds(pl.multiple_of(i * 16, 16), 16)
        x = x_in_ref[rc, :].astype(jnp.float32)
        normed_ref[rc, :] = (x * row_scale(x) * gain_ref[...]).astype(jnp.bfloat16)
        return carry

    lax.fori_loop(0, rows // 16, norm_body, 0)
    pl.semaphore_wait(barrier, count - 1 + twins - 1)
    slab = cols_ref.shape[4]
    half = rows // 2
    ring = cycle_of(count)
    where = {s: i for i, s in enumerate(ring)}
    place = table_of(me, [where[s] for s in range(count)])
    side = lax.rem(mine, 2)
    twin = mine + 1 - 2 * side
    side_rows = pl.ds(pl.multiple_of(side * half, half), half)

    def column_source(kind, owner, those):
        return (normed_ref, cotg_ref)[kind].at[those, pl.ds(pl.multiple_of(owner * slab, slab), slab)]

    own_columns = [
        pltpu.make_async_copy(
            column_source(kind, me, pl.ds(way * half, half)), cols_ref.at[kind, way, 0], cols_sem.at[kind, way]
        )
        for kind in (0, 1)
        for way in (0, 1)
    ]
    seq_copies = []
    for kind in (0, 1):
        for k in range(1, count):
            peer = table_of(lax.rem(place + jnp.where(side == 0, k, count - k), count), ring)
            seq_copies.append(
                pltpu.make_async_remote_copy(
                    src_ref=column_source(kind, peer, side_rows), dst_ref=cols_ref.at[kind, side, k],
                    send_sem=seq_send.at[kind, k - 1], recv_sem=seq_recv.at[kind, k - 1], device_id={"seq": peer},
                    device_id_type=MESH,
                )
            )
    twin_copies = [
        pltpu.make_async_remote_copy(
            src_ref=cols_ref.at[kind, side, pl.ds(1, count - 1)], dst_ref=cols_ref.at[kind, side, pl.ds(1, count - 1)],
            send_sem=twin_send.at[kind], recv_sem=twin_recv.at[kind], device_id={"ch": twin}, device_id_type=MESH,
        )
        for kind in (0, 1)
    ]


    own_part = pl.ds(pl.multiple_of(mine * part, part), part)
    cot_copies = [
        pltpu.make_async_remote_copy(
            src_ref=cot_ref, dst_ref=cotg_ref.at[:, own_part], send_sem=cot_send.at[k - 1], recv_sem=cot_recv.at[k - 1],
            device_id={"ch": lax.rem(mine + k, twins)}, device_id_type=MESH,
        )
        for k in range(1, twins)
    ]
    for copy in cot_copies:
        copy.start()
    own_copy = pltpu.make_async_copy(cot_ref, cotg_ref.at[:, own_part], own_sem.at[0])
    own_copy.start()
    for copy in seq_copies[: count - 1] + own_columns[:2]:
        copy.start()

    def in_step(step, carry):
        slot = lax.rem(step, 2)
        mode = lax.rem(step, modes)

        @pl.when(step + 1 < steps)
        def _():
            for b in (0, 1):
                in_copy(step + 1, b).start()

        for b in (0, 1):
            in_copy(step, b).wait()
        weights = jnp.concatenate([in_buf.at[slot, b].reshape(2 * width, 128)[...] for b in (0, 1)], axis=1)
        mask = jnp.concatenate([mode_ref[...]] * 2, axis=1) == mode.astype(jnp.float32)
        columns = pl.ds(pl.multiple_of(step // modes * 256, 256), 256)
        both = jnp.dot(x2_ref[...], weights, preferred_element_type=jnp.float32)
        for j, target in enumerate((x_ref, z_ref)):
            found = jnp.where(mask, both[j * rows : (j + 1) * rows], target[:, columns].astype(jnp.float32))
            target[:, columns] = found.astype(jnp.bfloat16)
        return carry

    x_ref[...] = jnp.zeros_like(x_ref)
    z_ref[...] = jnp.zeros_like(z_ref)
    row = lax.broadcasted_iota(jnp.int32, (256, 512), 0)
    column = lax.broadcasted_iota(jnp.int32, (256, 512), 1)
    for j in (0, 1):
        spread = (column == 2 * row + j).astype(jnp.bfloat16)
        for block in range(width // 256):
            x2_ref[j * rows : (j + 1) * rows, block * 512 : (block + 1) * 512] = jnp.dot(
                normed_ref[:, block * 256 : (block + 1) * 256], spread, preferred_element_type=jnp.float32
            ).astype(jnp.bfloat16)
    lax.fori_loop(0, steps // 2, in_step, 0)
    own_copy.wait()
    for copy in cot_copies:
        copy.wait_recv()
    for copy in seq_copies[count - 1 :] + own_columns[2:]:
        copy.start()
    lax.fori_loop(steps // 2, steps, in_step, 0)
    halo_copy = pltpu.make_async_remote_copy(
        src_ref=x_ref.at[pl.ds(rows - 16, 16)], dst_ref=halo_ref, send_sem=halo_send.at[0], recv_sem=halo_recv.at[0],
        device_id={"seq": lax.rem(me + 1, count)}, device_id_type=MESH,
    )
    halo_copy.start()
    for copy in seq_copies[: count - 1]:
        copy.wait_recv()
    twin_copies[0].start()

    def out_step(step, carry):
        slot = lax.rem(step, 2)
        mode = lax.rem(step, modes)

        @pl.when(step + 1 < out_steps)
        def _():
            out_copy(step + 1).start()

        out_copy(step).wait()
        mask = jnp.concatenate([mode_ref[...]] * (wide // 128), axis=1) == mode.astype(jnp.float32)
        columns = pl.ds(pl.multiple_of(step // modes * wide, wide), wide)
        found = jnp.dot(cotg_ref[...], out_buf[slot], preferred_element_type=jnp.float32)
        gated_ref[:, columns] = jnp.where(mask, found, gated_ref[:, columns])
        return carry

    gated_ref[...] = jnp.zeros_like(gated_ref)
    lax.fori_loop(0, out_steps // 2, out_step, 0)

    chunks, _, inner = pre_ref.shape
    padded(x_proj_ref, padded_ref)
    passed = documents(starts_ref, count * rows)
    spot = lax.broadcasted_iota(jnp.int32, (rows, 128), 0) + me * rows
    here = passed(spot)
    same = [jnp.where(passed(spot - lag) == here, 1.0, 0.0) for lag in (3, 2, 1, 0)]
    halo_copy.wait_recv()
    ext_ref[0:8] = halo_ref[8:16].astype(jnp.float32)
    ext_ref[8:] = x_ref[...].astype(jnp.float32)

    def conv_body(block, carry):
        cut = pl.ds(pl.multiple_of(block * 128, 128), 128)
        pre = jnp.zeros((rows, 128), jnp.float32) + cbias_ref[:, cut]
        for k in range(4):
            pre = pre + taps_ref[k : k + 1, cut] * ext_ref[5 + k : 5 + k + rows, cut] * same[k]
        pre_ref[:, :, cut] = pre.reshape(chunks, 16, 128)
        conv_ref[:, :, cut] = (pre / (1.0 + jnp.exp(-pre))).astype(jnp.bfloat16).reshape(chunks, 16, 128)
        return carry

    lax.fori_loop(0, inner // 128, conv_body, 0)
    part_ref[...] = lax.dot_general(
        conv_ref[...].reshape(rows, inner), padded_ref[...], (((1,), (1,)), ((), ())), preferred_element_type=jnp.float32
    )
    sent_ref[...] = part_ref[...].astype(jnp.bfloat16)
    low_copies = [
        pltpu.make_async_remote_copy(
            src_ref=sent_ref, dst_ref=got_ref.at[k - 1], send_sem=low_send.at[k - 1], recv_sem=low_recv.at[k - 1],
            device_id={"ch": lax.rem(mine + k, twins)}, device_id_type=MESH,
        )
        for k in range(1, twins)
    ]
    for copy in low_copies:
        copy.start()
    for copy in seq_copies[count - 1 :]:
        copy.wait_recv()
    twin_copies[1].start()
    lax.fori_loop(out_steps // 2, out_steps, out_step, 0)
    for k, copy in enumerate(low_copies):
        copy.wait_recv()
        part_ref[...] += got_ref[k].astype(jnp.float32)
    for copy in own_columns:
        copy.wait()
    for copy in twin_copies:
        copy.wait_recv()
    for copy in cot_copies + low_copies + seq_copies + twin_copies + [halo_copy]:
        copy.wait_send()


def front(x_in, gain, modes, cot, starts, taps, cbias, x_proj_t, w_in, w_out):
    count, twins = lax.axis_size("seq"), lax.axis_size("ch")
    rows, width = x_in.shape
    inner = w_out.shape[2]
    f32, b16 = jnp.float32, jnp.bfloat16
    shape = jax.ShapeDtypeStruct
    vmem = pl.BlockSpec(memory_space=pltpu.VMEM)
    hbm = pl.BlockSpec(memory_space=pl.ANY)
    wide = min(512, inner)
    return pl.pallas_call(
        functools.partial(front_kernel, (count, twins)),
        in_specs=[vmem] * 8 + [hbm] * 2,
        out_specs=[vmem] * 7,
        out_shape=[
            shape((rows, inner), b16), shape((rows, inner), f32), shape((2, 2, count, rows // 2, width // count), b16),
            shape((rows + 8, inner), f32), shape((rows // 16, 16, inner), f32), shape((rows // 16, 16, inner), b16),
            shape((rows, 256), f32),
        ],
        scratch_shapes=[
            pltpu.VMEM((rows, width), b16), pltpu.VMEM((rows, width), b16), pltpu.SemaphoreType.DMA((2, 2)),
            pltpu.SemaphoreType.DMA((2, count - 1)), pltpu.SemaphoreType.DMA((2, count - 1)),
            pltpu.SemaphoreType.DMA((2,)), pltpu.SemaphoreType.DMA((2,)),
            pltpu.VMEM((rows, inner), b16), pltpu.VMEM((16, inner), b16), pltpu.VMEM((256, inner), b16),
            pltpu.VMEM((rows, 256), b16), pltpu.VMEM((twins - 1, rows, 256), b16),
            pltpu.SemaphoreType.DMA((twins - 1,)), pltpu.SemaphoreType.DMA((twins - 1,)),
            pltpu.VMEM((rows, 128), jnp.float32),
            pltpu.VMEM((2 * rows, 2 * width), jnp.bfloat16),
            pltpu.SemaphoreType.DMA((1,)),
            pltpu.SemaphoreType.DMA((1,)),
            pltpu.VMEM((2, 2, width, 2, 128), jnp.bfloat16),
            pltpu.VMEM((2, width, wide), jnp.bfloat16),
            pltpu.SemaphoreType.DMA((2, 2)),
            pltpu.SemaphoreType.DMA((2,)),
            pltpu.SemaphoreType.DMA((twins - 1,)),
            pltpu.SemaphoreType.DMA((twins - 1,)),
            pltpu.SemaphoreType.DMA((1,)),
        ],
        compiler_params=pltpu.CompilerParams(collective_id=1, has_side_effects=True, vmem_limit_bytes=56 << 20),
        name="front",
    )(x_in, gain, modes, cot, starts, taps, cbias, x_proj_t, w_in, w_out)


def tile_lanes(v, lanes):
    return jnp.concatenate([v] * (lanes // 128), axis=1)

def ring_places(count):
    ring = cycle_of(count)
    where = {s: i for i, s in enumerate(ring)}
    me = lax.axis_index("seq")
    onward = table_of(me, [ring[(where[s] + 1) % count] for s in range(count)])
    backward = table_of(me, [ring[(where[s] - 1) % count] for s in range(count)])
    place = table_of(me, [where[s] for s in range(count)])
    return ring, place, onward, backward


def add_products(accs, kind, k, cols_ref, blocks, modes_ref, ring, place, count):
    parts = []
    for way in (0, 1):
        step = k if way else count - k
        source = table_of(lax.rem(place + step, count), ring)
        parts.append((jnp.transpose(cols_ref[kind, way, k]), modes_ref[pl.ds(2 * source + way, 1), :]))
    right = jnp.concatenate(blocks, axis=0)
    for m, acc in enumerate(accs):
        left = jnp.concatenate(
            [part * jnp.where(row == m, 1.0, 0.0).astype(jnp.bfloat16) for part, row in parts], axis=1
        )
        found = jnp.dot(left, right, preferred_element_type=jnp.float32)
        acc[...] += found.reshape(acc.shape)


def core_kernel(
    sizes, w_in_ref, w_out_ref, cols_ref, ext_ref, pre_ref, conv_ref, part_ref, z_ref, dgated_ref, starts_ref,
    taps_ref, x_t_ref, dt_proj_ref, dt_bias_ref, a_log_ref, skip_ref, modes_ref, x_in_ref, gain_ref,
    dwo_ref, dwz_ref, dwx_ref, mix_ref, small_ref, slice_ref, dots_ref, dgain_ref, scale_ref,
    x_proj_ref, same_ref, mode_ref, free_sem, g_ref, step_ref, dtd_ref, u_ref, sig_ref, low_t_ref, b_ref, c_ref, rate_ref, ends_ref,
    ends_sent, ends_got, steps_sent, steps_got, h0_ref, gz_ref,
    racc_ref, rows_ref, sum_ref, half_ref, half_got, four_ref, four_b16, four_got, in_buf, out_buf, mix_sent, mix_got,
    norm_sent, norm_got, dots_sent, dots_got, gain_sent, gain_got,
    ring_ref, hist_ref, lam_ref, w_ref, pend_ref, gstep_ref, gscan_ref, grad_ref, sent_ref, got_ref,
    gpre_ref, edge_ref,
    in_sem, out_sem, mix_send, mix_recv, half_send, half_recv, four_send, four_recv, last_send, last_recv, all_send, all_recv,
    ends_send, ends_recv, steps_send, steps_recv, norm_send, norm_recv, dots_send, dots_recv,
    gain_send, gain_recv, dwo_sem,
    ring_send, ring_recv, gx_send, gx_recv, ch_send, ch_recv, edge_send, edge_recv,
):
    count, twins = sizes
    chunks, _, chans = pre_ref.shape
    rows = chunks * 16
    gx_ref = gz_ref.at[2]
    slab = cols_ref.shape[4]
    n = a_log_ref.shape[0]
    half = rows // 2
    ring, place, onward, backward = ring_places(count)
    me = lax.axis_index("seq")
    mine = lax.axis_index("ch")
    before = lax.rem(me + count - 1, count)
    nt = (((1,), (1,)), ((), ()))
    f32, b16 = jnp.float32, jnp.bfloat16
    lb = min(512, chans)

    modes, width = w_out_ref.shape[:2]
    part = width // twins
    eighths = chans // 128
    across = half_ref.shape[1]
    tall = half_ref.shape[0]
    depth = half_ref.shape[2]
    z_at = me // across
    x_at = lax.rem(me, across)

    def chunk_of(step):
        return pl.ds(pl.multiple_of(lax.rem(mine + 1 + step // modes, twins) * part, part), part)

    def in_copy(step, b):
        slot = step % 2
        return pltpu.make_async_copy(w_in_ref.at[step % modes, chunk_of(step), b], in_buf.at[slot, b], in_sem.at[slot, b])

    def in_copies(step, wait):
        for b in range(eighths):
            if wait:
                in_copy(step, b).wait()
            else:
                in_copy(step, b).start()

    def out_copy(step):
        slot = step % 2
        return pltpu.make_async_copy(w_out_ref.at[step % modes, chunk_of(step)], out_buf.at[slot], out_sem.at[slot])

    barrier = pltpu.get_barrier_semaphore()
    for k in range(1, count):
        pl.semaphore_signal(barrier, inc=1, device_id={"seq": lax.rem(me + k, count)}, device_id_type=MESH)
    for k in range(1, twins):
        peer = {"ch": lax.rem(mine + k, twins)}
        pl.semaphore_signal(barrier, inc=1, device_id=peer, device_id_type=MESH)
    in_copies(0, 0)
    out_copy(0).start()
    pl.semaphore_wait(barrier, count - 1 + twins - 1)

    passed = documents(starts_ref, count * rows)

    def maps_copies(send, recv):
        return [
            pltpu.make_async_remote_copy(
                src_ref=sent_ref, dst_ref=got_ref.at[k - 1], send_sem=send.at[k - 1],
                recv_sem=recv.at[k - 1], device_id={"ch": lax.rem(mine + k, twins)}, device_id_type=MESH,
            )
            for k in range(1, twins)
        ]


    def gate_body(i, carry):
        z = z_ref[i].astype(f32)
        g_ref[i] = dgated_ref[i] * (z / (1.0 + jnp.exp(-z)))
        return carry

    lax.fori_loop(0, chunks, gate_body, 0)
    rate_ref[...] = -math.log2(math.e) * jnp.exp(a_log_ref[...])
    own = (
        lax.broadcasted_iota(jnp.int32, (16, 16 * n), 1) // n == lax.broadcasted_iota(jnp.int32, (16, 16 * n), 0)
    )
    ones = own.astype(b16)
    token_row = lax.broadcasted_iota(jnp.int32, (16 * n, 16), 0) // n
    repeat = (token_row == lax.broadcasted_iota(jnp.int32, (16 * n, 16), 1)).astype(b16)
    pick_row = lax.broadcasted_iota(jnp.int32, (16 * n, 128), 0)
    pick_col = lax.broadcasted_iota(jnp.int32, (16 * n, 128), 1)
    is_b = pick_row % n == pick_col
    is_c = pick_row % n + n == pick_col
    pick_b = is_b.astype(b16)
    pick_c = is_c.astype(b16)
    flat = jnp.ones((256, 128), b16)
    total = part_ref[...]
    low_t_ref[...] = jnp.transpose(total[:, 0:128]).astype(b16)
    raw = jnp.dot(total[:, 0:128].astype(b16), dt_proj_ref[...], preferred_element_type=f32)
    step_ref[...] = raw.reshape(chunks, 16, chans)

    def step_body(i, carry):
        raw = step_ref[i] + dt_bias_ref[...]
        step = jnp.maximum(raw, 0.0) + jnp.log1p(jnp.exp(-jnp.abs(raw)))
        step_ref[i] = step
        sig_ref[i] = 1.0 / (1.0 + jnp.exp(-raw))
        at = lax.broadcasted_iota(jnp.int32, (16, 128), 0) + (me * rows + i * 16)
        big = jnp.where(passed(at) == passed(at - 1), 0.0, 1e30)
        dtd_ref[i] = step + jnp.concatenate([big] * (chans // 128), axis=1)
        u_ref[i] = step * conv_ref[i].astype(f32)
        maps = part_ref[pl.ds(pl.multiple_of(i * 16, 16), 16), 128:256]
        high = maps.astype(b16)
        low = (maps - high.astype(f32)).astype(b16)
        high = jnp.dot(repeat, high, preferred_element_type=f32)
        low = jnp.dot(repeat, low, preferred_element_type=f32)
        for target, chosen in ((b_ref, is_b), (c_ref, is_c)):
            terms = [jnp.where(chosen, term, 0.0).astype(b16) for term in (high, low)]
            found = jnp.dot(jnp.concatenate(terms, axis=1), flat, preferred_element_type=f32)
            target[pl.ds(i * 16, 16)] = found.reshape(16, n, 128)
        return carry

    lax.fori_loop(0, chunks, step_body, 0)

    def maps_block(chunk, pick):
        maps = part_ref[pl.ds(pl.multiple_of(chunk * 16, 16), 16), 128:256].astype(b16)
        found = lax.dot_general(maps, pick, nt, preferred_element_type=f32)
        return jnp.where(own, found, 0.0).astype(b16)

    ends_ref[0:n] = jnp.zeros((n, chans), f32)
    ends_ref[n : 2 * n] = jnp.ones((n, chans), f32)
    ends_ref[2 * n : 3 * n] = jnp.zeros((n, chans), f32)

    def ends_body(chunk, carry):
        for block in range(chans // lb):
            cut = slice(block * lb, (block + 1) * lb)
            rate = rate_ref[:, cut]
            h = ends_ref[0:n, cut]
            reach = ends_ref[n : 2 * n, cut]
            head = ends_ref[2 * n : 3 * n, cut]
            for t in range(16):
                decay = jnp.exp2(dtd_ref[chunk, t : t + 1, cut] * rate)
                h = decay * h + u_ref[chunk, t : t + 1, cut] * tile_lanes(b_ref[chunk * 16 + t], lb)
                reach = reach * decay
                head = head + reach * (g_ref[chunk, t : t + 1, cut] * tile_lanes(c_ref[chunk * 16 + t], lb))
            ends_ref[0:n, cut] = h
            ends_ref[n : 2 * n, cut] = reach
            ends_ref[2 * n : 3 * n, cut] = head
        return carry

    lax.fori_loop(0, chunks, ends_body, 0)
    ends_sent[0] = ends_ref[0:n].astype(b16)
    ends_sent[1] = ends_ref[2 * n : 3 * n].astype(b16)
    steps_sent[...] = jnp.sum(jnp.sum(dtd_ref[...], axis=0), axis=0, keepdims=True)
    ends_copies = []
    for k in range(1, count):
        peer = lax.rem(me + k, count)
        side = jnp.where(peer > me, 0, 1)
        ends_copies.append(
            pltpu.make_async_remote_copy(
                src_ref=ends_sent.at[side], dst_ref=ends_got.at[k - 1], send_sem=ends_send.at[k - 1],
                recv_sem=ends_recv.at[k - 1], device_id={"seq": peer}, device_id_type=MESH,
            )
        )
        ends_copies.append(
            pltpu.make_async_remote_copy(
                src_ref=steps_sent, dst_ref=steps_got.at[k - 1], send_sem=steps_send.at[k - 1],
                recv_sem=steps_recv.at[k - 1], device_id={"seq": peer}, device_id_type=MESH,
            )
        )
    for copy in ends_copies:
        copy.start()
    for copy in ends_copies:
        copy.wait_recv()

    def arrived(slots, valid):
        total = jnp.zeros((n, chans), f32)
        gap = jnp.zeros((1, chans), f32)
        for k, slot in enumerate(slots):
            term = ends_got[slot].astype(f32) * jnp.exp2(rate_ref[...] * gap)
            total = total + jnp.where(valid(k + 1), term, 0.0)
            gap = gap + steps_got[slot]
        return total

    h0_ref[...] = arrived(range(count - 1), lambda k: k <= me)
    pend_ref[...] = arrived(range(count - 2, -1, -1), lambda k: k + me < count)

    racc_ref[...] = h0_ref[...]

    def forward_body(chunk, carry):
        for block in range(chans // lb):
            cut = slice(block * lb, (block + 1) * lb)
            rate = rate_ref[:, cut]
            h = racc_ref[:, cut]
            for t in range(16):
                decay = jnp.exp2(dtd_ref[chunk, t : t + 1, cut] * rate)
                h = decay * h + u_ref[chunk, t : t + 1, cut] * tile_lanes(b_ref[chunk * 16 + t], lb)
                hist_ref[chunk, t * n : (t + 1) * n, cut] = h.astype(b16)
            racc_ref[:, cut] = h
        ssm = jnp.dot(maps_block(chunk, pick_c), hist_ref[chunk], preferred_element_type=f32)
        ssm = ssm + skip_ref[...] * conv_ref[chunk].astype(f32)
        z = z_ref[chunk].astype(f32)
        sig = 1.0 / (1.0 + jnp.exp(-z))
        rc = pl.ds(pl.multiple_of(chunk * 16, 16), 16)
        gz_ref[0, rc] = (ssm * (z * sig)).astype(b16)
        gz_ref[1, rc] = (dgated_ref[chunk] * ssm * (sig * (1.0 + z * (1.0 - sig)))).astype(b16)
        return carry

    lax.fori_loop(0, chunks, forward_body, 0)

    def ring_copy(kind, way, k):
        if k == 0:
            source = gz_ref.at[kind, pl.ds(way * half, half)]
        else:
            source = ring_ref.at[kind, way, k - 1]
        return pltpu.make_async_remote_copy(
            src_ref=source, dst_ref=ring_ref.at[kind, way, k], send_sem=ring_send.at[kind, way, k],
            recv_sem=ring_recv.at[kind, way, k], device_id={"seq": backward if way else onward}, device_id_type=MESH,
        )

    def relay(kind, k):
        for way in (0, 1):
            if kind == 2:
                gx_copy(way, k - 1).wait_recv()
                if k < count - 1:
                    gx_copy(way, k).start()
            else:
                ring_copy(kind, way, k - 1).wait_recv()
                if k < count - 1:
                    ring_copy(kind, way, k).start()

    def gx_slot(way, k):
        slot = way * (count - 1) + k
        return hist_ref.at[slot // 2, pl.ds(slot % 2 * half, half)]

    def gx_copy(way, k):
        return pltpu.make_async_remote_copy(
            src_ref=gx_slot(way, k - 1) if k else gx_ref.at[pl.ds(way * half, half)], dst_ref=gx_slot(way, k),
            send_sem=gx_send.at[way, k], recv_sem=gx_recv.at[way, k], device_id={"seq": backward if way else onward},
            device_id_type=MESH,
        )

    for kind in (0, 1):
        for way in (0, 1):
            ring_copy(kind, way, 0).start()
    turns = [(kind, k) for k in range(1, count) for kind in (0, 1)]
    early = turns[:2]
    late = turns[2:]

    racc_ref[...] = jnp.zeros_like(racc_ref)

    def span_body(i, carry):
        at = spans - 1 - i
        for sub in reversed(range(span // 16)):
            chunk = at * (span // 16) + sub
            for block in range(chans // lb):
                cut = slice(block * lb, (block + 1) * lb)
                rate = rate_ref[:, cut]
                pend = pend_ref[:, cut]
                racc = racc_ref[:, cut]
                for t in reversed(range(16)):
                    decay = jnp.exp2(dtd_ref[chunk, t : t + 1, cut] * rate)
                    lam = g_ref[chunk, t : t + 1, cut] * tile_lanes(c_ref[chunk * 16 + t], lb) + pend
                    pend = decay * lam
                    if t:
                        prior = hist_ref[chunk, (t - 1) * n : t * n, cut].astype(jnp.float32)
                    else:
                        prior = hist_ref[jnp.maximum(chunk - 1, 0), 15 * n : 16 * n, cut].astype(jnp.float32)
                        prior = jnp.where(chunk == 0, h0_ref[:, cut], prior)
                    w = pend * prior
                    racc = racc + w * step_ref[chunk, t : t + 1, cut]
                    lam_ref[t * n : (t + 1) * n, cut] = lam.astype(jnp.bfloat16)
                    w_ref[t * n : (t + 1) * n, cut] = (w * rate).astype(jnp.bfloat16)
                pend_ref[:, cut] = pend
                racc_ref[:, cut] = racc
            step = step_ref[chunk]
            conv = conv_ref[chunk].astype(jnp.float32)
            adj = jnp.dot(maps_block(chunk, pick_b), lam_ref[...], preferred_element_type=jnp.float32)
            wsum = jnp.dot(ones, w_ref[...], preferred_element_type=jnp.float32)
            gstep_ref[chunk] = wsum * math.log(2.0) + adj * conv
            gscan_ref[chunk] = adj * step
            gb = lax.dot_general(u_ref[chunk].astype(jnp.bfloat16), lam_ref[...], nt, preferred_element_type=jnp.float32)
            gc = lax.dot_general(
                g_ref[chunk].astype(jnp.bfloat16), hist_ref[chunk], nt, preferred_element_type=jnp.float32
            )
            gb = jnp.where(own, gb, 0.0).astype(jnp.bfloat16)
            gc = jnp.where(own, gc, 0.0).astype(jnp.bfloat16)
            grad_ref[pl.ds(pl.multiple_of(chunk * 16, 16), 16), 128:256] = jnp.dot(
                gb, pick_b, preferred_element_type=jnp.float32
            ) + jnp.dot(gc, pick_c, preferred_element_type=jnp.float32)
        return carry

    span = 32
    spans = rows // span
    mode_columns(modes_ref, mode_ref)
    padded(x_t_ref, x_proj_ref)
    passed = documents(starts_ref, count * rows)
    spot = lax.broadcasted_iota(jnp.int32, (rows, 128), 0) + me * rows
    here = passed(spot)
    for i in range(7):
        same_ref[i] = jnp.where(passed(spot + (i - 3)) == here, 1.0, 0.0).astype(b16)
    lax.fori_loop(0, spans // 2, span_body, 0)
    relay(*early[0])
    lax.fori_loop(spans // 2, spans, span_body, 0)
    for peer in (onward, backward):
        pl.semaphore_signal(free_sem, inc=1, device_id={"seq": peer}, device_id_type=MESH)
    relay(*early[1])

    rows_ref[...] = jnp.zeros_like(rows_ref)

    def raw_body(i, carry):
        full = gstep_ref[i] * sig_ref[i]
        rows_ref[5:6] += jnp.sum(full, axis=0, keepdims=True)
        rows_ref[6:7] += jnp.sum(g_ref[i] * conv_ref[i].astype(jnp.float32), axis=0, keepdims=True)
        gx_ref[pl.ds(pl.multiple_of(i * 16, 16), 16), :] = full.astype(jnp.bfloat16)
        return carry

    lax.fori_loop(0, chunks, raw_body, 0)
    grad_ref[:, 0:128] = lax.dot_general(gx_ref[...], dt_proj_ref[...], nt, preferred_element_type=jnp.float32)
    sent_ref[...] = grad_ref[...].astype(jnp.bfloat16)
    ch_copies = maps_copies(ch_send, ch_recv)
    for copy in ch_copies:
        copy.start()
    relay(*late[0])
    sum_ref[160:288] = jnp.dot(low_t_ref[...], gx_ref[...], preferred_element_type=jnp.float32)
    for copy in ch_copies:
        copy.wait_recv()
    total = grad_ref[...]
    for k in range(twins - 1):
        total = total + got_ref[k].astype(jnp.float32)
    grad_ref[...] = total
    relay(*late[1])

    skip = skip_ref[...]
    def pre_body(i, carry):
        rc = pl.ds(pl.multiple_of(i * 16, 16), 16)
        g_conv = jnp.dot(grad_ref[rc, :].astype(jnp.bfloat16), x_proj_ref[...], preferred_element_type=jnp.float32)
        g_conv = g_conv + skip * g_ref[i] + gscan_ref[i]
        pre = pre_ref[i]
        sig = 1.0 / (1.0 + jnp.exp(-pre))
        gpre = g_conv * sig * (1.0 + pre * (1.0 - sig))
        gpre_ref[rc, :] = gpre
        return carry

    pre_body(0, 0)
    edge_ref[...] = gpre_ref[0:8, :]
    edge_copy = pltpu.make_async_remote_copy(
        src_ref=edge_ref, dst_ref=gpre_ref.at[pl.ds(rows, 8)], send_sem=edge_send.at[0], recv_sem=edge_recv.at[0],
        device_id={"seq": before}, device_id_type=MESH,
    )
    edge_copy.start()
    lax.fori_loop(1, chunks, pre_body, 0)
    flipped = jnp.transpose(grad_ref[...]).astype(jnp.bfloat16)
    sum_ref[0:160] = jnp.dot(flipped[0:160], conv_ref[...].reshape(rows, chans), preferred_element_type=jnp.float32)
    relay(*late[2])
    edge_copy.wait_recv()

    def taps_body(block, carry):
        cut = pl.ds(pl.multiple_of(block * 128, 128), 128)
        gpre = gpre_ref[0:rows, cut]
        rows_ref[4:5, cut] = jnp.sum(gpre, axis=0, keepdims=True)
        total = jnp.zeros((rows, 128), jnp.float32)
        for k in range(4):
            lag = 3 - k
            total = total + gpre_ref[lag : lag + rows, cut] * taps_ref[k : k + 1, cut] * same_ref[3 + lag].astype(jnp.float32)
            rows_ref[k : k + 1, cut] = jnp.sum(
                gpre * ext_ref[5 + k : 5 + k + rows, cut] * same_ref[k].astype(jnp.float32), axis=0, keepdims=True
            )
        gx_ref[:, cut] = total.astype(jnp.bfloat16)
        return carry

    lax.fori_loop(0, chans // 128, taps_body, 0)
    pl.semaphore_wait(free_sem, 2)
    for way in (0, 1):
        gx_copy(way, 0).start()
    sum_ref[288:304] = racc_ref[...] * rate_ref[...] * math.log(2.0)
    sum_ref[304:312] = rows_ref[...]
    if tall * across * depth > 312:
        sum_ref[312:] = jnp.zeros((tall * across * depth - 312, chans), jnp.float32)
    for z in range(tall):
        for x in range(across):
            first = (z * across + x) * depth
            half_ref[z, x] = sum_ref[first : first + depth].astype(jnp.bfloat16)

    def to(device):
        return dict(device_id={"seq": device}, device_id_type=MESH)

    half_copies = [
        pltpu.make_async_remote_copy(
            src_ref=half_ref.at[:, lax.rem(x_at + k, across)], dst_ref=half_got.at[k - 1], send_sem=half_send.at[k - 1],
            recv_sem=half_recv.at[k - 1], **to(z_at * across + lax.rem(x_at + k, across)),
        )
        for k in range(1, across)
    ]
    four_copies = [
        pltpu.make_async_remote_copy(
            src_ref=four_b16.at[lax.rem(z_at + k, tall)], dst_ref=four_got.at[k - 1], send_sem=four_send.at[k - 1],
            recv_sem=four_recv.at[k - 1], **to(lax.rem(z_at + k, tall) * across + x_at),
        )
        for k in range(1, tall)
    ]
    last_copies = [
        pltpu.make_async_remote_copy(
            src_ref=small_ref.at[z_at, x_at], dst_ref=small_ref.at[z_at, x_at], send_sem=last_send.at[k - 1],
            recv_sem=last_recv.at[k - 1], **to(lax.rem(z_at + k, tall) * across + x_at),
        )
        for k in range(1, tall)
    ]
    all_copies = [
        pltpu.make_async_remote_copy(
            src_ref=small_ref.at[:, x_at], dst_ref=small_ref.at[:, x_at], send_sem=all_send.at[k - 1],
            recv_sem=all_recv.at[k - 1], **to(z_at * across + lax.rem(x_at + k, across)),
        )
        for k in range(1, across)
    ]

    def small_phase(phase):
        if phase == 0:
            for copy in half_copies:
                copy.start()
        elif phase == 1:
            for copy in half_copies:
                copy.wait_recv()
            for z in range(tall):
                first = pl.multiple_of((z * across + x_at) * depth, depth)
                total = sum_ref[pl.ds(first, depth)]
                for k in range(across - 1):
                    total = total + half_got[k, z].astype(jnp.float32)
                four_ref[z] = total
                four_b16[z] = total.astype(jnp.bfloat16)
            for copy in four_copies:
                copy.start()
        elif phase == 2:
            for copy in four_copies:
                copy.wait_recv()
            total = four_ref[z_at]
            for k in range(tall - 1):
                total = total + four_got[k].astype(jnp.float32)
            small_ref[z_at, x_at] = total.astype(jnp.bfloat16)
            for copy in last_copies:
                copy.start()
        elif phase == 3:
            for copy in last_copies:
                copy.wait_recv()
            for copy in all_copies:
                copy.start()
        else:
            for copy in all_copies:
                copy.wait_recv()
            for copy in half_copies + four_copies + last_copies + all_copies:
                copy.wait_send()

    small_phase(0)
    dwo_accs = [ref.at[0 : slab // 16] for ref in (dtd_ref, u_ref, sig_ref)]
    dwz_accs = [ref.at[0 : slab // 16] for ref in (step_ref, g_ref, gscan_ref)]
    dwx_accs = [dwx_ref.at[m] for m in range(modes)]
    for acc in dwo_accs + dwz_accs + dwx_accs:
        acc[...] = jnp.zeros_like(acc)

    def products(kind, k):
        if k == 0:
            source = gx_ref if kind == 2 else gz_ref.at[kind]
            blocks = [source[way * half : (way + 1) * half] for way in (0, 1)]
        else:
            blocks = [gx_slot(way, k - 1)[...] if kind == 2 else ring_ref[kind, way, k - 1] for way in (0, 1)]
        accs = (dwo_accs, dwz_accs, dwx_accs)[kind]
        add_products(accs, 0 if kind else 1, k, cols_ref, blocks, modes_ref, ring, place, count)
        if kind < 2 and k == count - 1:
            for copy in out_copies[kind]:
                copy.start()

    out_copies = [
        [pltpu.make_async_copy(acc, target.at[m], dwo_sem.at[kind, m]) for m, acc in enumerate(accs)]
        for kind, (accs, target) in enumerate(((dwo_accs, dwo_ref), (dwz_accs, dwz_ref)))
    ]

    def mix_copy(j):
        return pltpu.make_async_remote_copy(
            src_ref=mix_sent.at[j], dst_ref=mix_got.at[j], send_sem=mix_send.at[j], recv_sem=mix_recv.at[j],
            device_id={"ch": lax.rem(mine + 1 + j, twins)}, device_id_type=MESH,
        )

    steps = twins * modes

    def norm_copy(j):
        return pltpu.make_async_remote_copy(
            src_ref=norm_sent.at[j], dst_ref=norm_got.at[j], send_sem=norm_send.at[j], recv_sem=norm_recv.at[j],
            device_id={"ch": lax.rem(mine + 1 + j, twins)}, device_id_type=MESH,
        )

    def normed_unit(j, m):
        step = j * modes + m
        if step + 1 < steps:
            in_copies(step + 1, 0)
        in_copies(step, 1)
        spread_products(in_buf.at[step % 2], gz_ref, mode_ref, slice_ref, m, part)

    def normed_end(j):
        for q in range(part // 128):
            lanes = slice(q * 128, (q + 1) * 128)
            cut = pl.ds(pl.multiple_of(lax.rem(mine + 1 + j, twins) * part + q * 128, 128), 128)
            dots_ref[...] += slice_ref[:, lanes] * x_in_ref[:, cut].astype(f32) * gain_ref[:, cut]
        if j < twins - 1:
            norm_sent[j] = slice_ref[...].astype(b16)
            norm_copy(j).start()

    def mix_unit(j):
        for m in range(modes):
            step = j * modes + m
            if step + 1 < steps:
                out_copy(step + 1).start()
            out_copy(step).wait()
            mask = jnp.concatenate([mode_ref[...]] * (part // 128), axis=1) == float(m)
            found = lax.dot_general(gz_ref[0], out_buf[step % 2], nt, preferred_element_type=jnp.float32)
            mix_ref[...] = jnp.where(mask, found, mix_ref[...]) if m else found
        if j < twins - 1:
            mix_sent[j] = mix_ref[...].astype(jnp.bfloat16)
            mix_copy(j).start()

    dots_copies = [
        pltpu.make_async_remote_copy(
            src_ref=dots_sent, dst_ref=dots_got.at[k - 1], send_sem=dots_send.at[k - 1], recv_sem=dots_recv.at[k - 1],
            device_id={"ch": lax.rem(mine + k, twins)}, device_id_type=MESH,
        )
        for k in range(1, twins)
    ]
    gain_copies = [
        pltpu.make_async_remote_copy(
            src_ref=gain_sent, dst_ref=gain_got.at[k - 1], send_sem=gain_send.at[k - 1], recv_sem=gain_recv.at[k - 1],
            device_id={"seq": lax.rem(me + k, count)}, device_id_type=MESH,
        )
        for k in range(1, count)
    ]

    def scale_body(i, carry):
        rc = pl.ds(pl.multiple_of(i * 16, 16), 16)
        scale_ref[rc] = jnp.broadcast_to(row_scale(x_in_ref[rc].astype(f32)), (16, 128))
        return carry

    def dots_unit():
        lax.fori_loop(0, chunks, scale_body, 0)
        dots_sent[...] = dots_ref[...].astype(b16)
        for copy in dots_copies:
            copy.start()

    def slice_unit():
        for j in range(twins - 1):
            norm_copy(j).wait_recv()
            slice_ref[...] += norm_got[j].astype(f32)
        for q in range(part // 128):
            lanes = slice(q * 128, (q + 1) * 128)
            cut = pl.ds(pl.multiple_of(mine * part + q * 128, 128), 128)
            terms = slice_ref[:, lanes] * x_in_ref[:, cut].astype(f32) * scale_ref[...]
            gain_sent[:, lanes] = jnp.broadcast_to(jnp.sum(terms, axis=0, keepdims=True), (8, 128))
        for copy in gain_copies:
            copy.start()

    def gain_unit():
        total = gain_sent[...]
        for k, copy in enumerate(gain_copies):
            copy.wait_recv()
            total = total + gain_got[k]
        dgain_ref[...] = total
        for k, copy in enumerate(dots_copies):
            copy.wait_recv()
            dots_ref[...] += dots_got[k].astype(f32)
        mean = jnp.sum(dots_ref[...], axis=1, keepdims=True) / width
        dots_ref[...] = jnp.broadcast_to(mean, (rows, 128))
        for j in range(twins - 1):
            mix_copy(j).wait_recv()
            mix_ref[...] += mix_got[j].astype(f32)

    edge_copy.wait_send()
    dots_ref[...] = jnp.zeros_like(dots_ref)
    work = []
    for j in range(twins):
        for m in range(modes):
            work.append(functools.partial(normed_unit, j, m))
        work.append(functools.partial(normed_end, j))
        if j < 4:
            work.append(functools.partial(small_phase, j + 1))
    work.append(dots_unit)
    for j in range(twins):
        work.append(functools.partial(mix_unit, j))
    work += [slice_unit, gain_unit]
    ready = [(0, 0), (1, 0), (2, 0)] + early + late[:3]
    rest, last = late[3:], [(2, k) for k in range(1, count)]
    turns = []
    while rest or last:
        turns += rest[:2] + last[:1]
        rest, last = rest[2:], last[1:]
    for i, turn in enumerate(turns):
        left = len(turns) - i
        for _ in range(min(len(work), max(2, -(-len(work) // left)))):
            work.pop(0)()
        relay(*turn)
        ready.append(turn)
        for _ in range(2 if len(ready) > left else 1):
            if len(ready) > 1:
                products(*ready.pop(0))
    for unit in work:
        unit()
    for turn in ready:
        products(*turn)
    for copy in out_copies[0] + out_copies[1]:
        copy.wait()
    for j in range(twins - 1):
        mix_copy(j).wait_send()
        norm_copy(j).wait_send()
    for copy in dots_copies + gain_copies:
        copy.wait_send()
    for way in (0, 1):
        for k in range(count - 1):
            gx_copy(way, k).wait_send()

    for kind in (0, 1):
        for way in (0, 1):
            for k in range(count - 1):
                ring_copy(kind, way, k).wait_send()
    for copy in ch_copies + ends_copies:
        copy.wait_send()


def spread_products(buf, trio_ref, mode_ref, target, m, part):
    nt = (((1,), (1,)), ((), ()))
    chosen = mode_ref[...] == float(m)
    row = lax.broadcasted_iota(jnp.int32, (256, 128), 0)
    column = lax.broadcasted_iota(jnp.int32, (256, 128), 1)
    picks = [(row == 2 * column + j).astype(jnp.bfloat16) for j in (1, 0)]
    rows = trio_ref.shape[1]
    stacked = trio_ref[1:3].reshape(2 * rows, trio_ref.shape[2])
    for q in range(2 * part // 256):
        weights = jnp.concatenate(
            [buf.at[b].reshape(2 * part, 128)[q * 256 : (q + 1) * 256] for b in range(buf.shape[0])], axis=1
        )
        found = lax.dot_general(stacked, weights, nt, preferred_element_type=jnp.float32).astype(jnp.bfloat16)
        total = jnp.dot(found[:rows], picks[0], preferred_element_type=jnp.float32)
        total = total + jnp.dot(found[rows:], picks[1], preferred_element_type=jnp.float32)
        cut = pl.ds(q * 128, 128)
        target[:, cut] = jnp.where(chosen, total, target[:, cut]) if m else total


def core(
    w_in, w_out, cols, ext, pre, conv, maps, z, dgated, starts, taps, x_proj_t, dt_proj, dt_bias, a_log, skip, modes,
    x_in, gain,
):
    count, twins = lax.axis_size("seq"), lax.axis_size("ch")
    rows, chans = z.shape
    n = a_log.shape[0]
    chunks = rows // 16
    width = w_out.shape[1]
    slab = width // count
    part = width // twins
    tall, across = 4, count // 4
    depth = -(-312 // (16 * count)) * 16
    vmem = pl.BlockSpec(memory_space=pltpu.VMEM)
    hbm = pl.BlockSpec(memory_space=pl.ANY)
    cube = lambda a: a.reshape((chunks, a.shape[0] // chunks) + a.shape[1:])
    f32, b16 = jnp.float32, jnp.bfloat16
    shape = jax.ShapeDtypeStruct
    dma = pltpu.SemaphoreType.DMA
    keep = pltpu.VMEM
    operands = [w_in, w_out, cols, ext, pre, conv, maps, cube(z), cube(dgated), starts, taps, x_proj_t, dt_proj, dt_bias,
                a_log, skip, modes, x_in, gain]
    block = (chunks, 16, chans)
    pair = lambda size: [dma((size,)), dma((size,))]
    return pl.pallas_call(
        functools.partial(core_kernel, (count, twins)),
        in_specs=[hbm] * 2 + [vmem] * (len(operands) - 2),
        out_specs=[hbm] * 2 + [vmem] * 7,
        out_shape=[
            shape((3, slab // 16, 16, chans), f32), shape((3, slab // 16, 16, chans), f32), shape((3, slab, chans), f32),
            shape((rows, part), f32), shape((tall, across, depth, chans), b16), shape((rows, part), f32),
            shape((rows, 128), f32), shape((8, part), f32), shape((rows, 128), f32),
        ],
        scratch_shapes=[
            keep((256, chans), b16), keep((7, rows, 128), b16), keep((rows, 128), f32), pltpu.SemaphoreType.REGULAR, keep(block, f32), keep(block, f32),
            keep(block, f32), keep(block, f32), keep(block, f32), keep((128, rows), b16), keep((rows, n, 128), f32),
            keep((rows, n, 128), f32), keep((n, chans), f32), keep((3 * n, chans), f32),
            keep((2, n, chans), b16), keep((count - 1, n, chans), b16), keep((1, chans), f32),
            keep((count - 1, 1, chans), f32), keep((n, chans), f32), keep((3, rows, chans), b16),
            keep((n, chans), f32), keep((8, chans), f32), keep((tall * across * depth, chans), f32),
            keep((tall, across, depth, chans), b16), keep((across - 1, tall, depth, chans), b16),
            keep((tall, depth, chans), f32), keep((tall, depth, chans), b16), keep((tall - 1, depth, chans), b16),
            keep((2, chans // 128, part, 2, 128), b16), keep((2, part, chans), b16), keep((twins - 1, rows, part), b16),
            keep((twins - 1, rows, part), b16),
            keep((twins - 1, rows, part), b16), keep((twins - 1, rows, part), b16), keep((rows, 128), b16),
            keep((twins - 1, rows, 128), b16), keep((8, part), f32), keep((count - 1, 8, part), f32),
            keep((2, 2, count - 1, rows // 2, chans), b16),
            keep((chunks, 16 * n, chans), b16), keep((16 * n, chans), b16),
            keep((16 * n, chans), b16), keep((n, chans), f32), keep(block, f32), keep(block, f32), keep((rows, 256), f32), keep((rows, 256), b16), keep((twins - 1, rows, 256), b16),
            keep((rows + 8, chans), f32), keep((8, chans), f32),
            dma((2, chans // 128)), dma((2,)), *pair(twins - 1), *pair(across - 1), *pair(tall - 1), *pair(tall - 1),
            *pair(across - 1), *pair(count - 1), *pair(count - 1), *pair(twins - 1), *pair(twins - 1),
            *pair(count - 1), dma((2, 3)),
            dma((2, 2, count - 1)), dma((2, 2, count - 1)), dma((2, count - 1)), dma((2, count - 1)), *pair(twins - 1), dma((1,)), dma((1,)),
        ],
        compiler_params=pltpu.CompilerParams(collective_id=2, has_side_effects=True, vmem_limit_bytes=63 << 20),
        name="core",
    )(*operands)


def lane_blocks(w_in):
    kinds, width, _, chans = w_in.shape
    return w_in.reshape(kinds, width, 2, chans // 128, 128).transpose(0, 1, 3, 2, 4)


def finish_kernel(
    x_part_ref, z_part_ref, out_part_ref, *refs,
):
    sources, refs = refs[:9], refs[9:]
    (
        dw_in_ref, dw_out_ref, block_ref, dx_ref, gain_out_ref, taps_ref, cbias_ref, x_proj_ref, dt_proj_ref, dt_bias_ref,
        a_log_ref, skip_ref,
    ) = refs[:12]
    buffers, (x_buf, z_buf, out_buf, sems, out_sem, in_sem, big_sem) = refs[12:21], refs[21:]
    small_ref, slice_ref, mix_ref, mean_ref, scale_ref, cot_ref, x_ref, gain_ref, dgain_ref = buffers
    kinds, _, chans = x_part_ref.shape
    part = slice_ref.shape[1]
    mine = lax.axis_index("ch")
    own_part = pl.ds(pl.multiple_of(mine * part, part), part)
    fetches = [
        pltpu.make_async_copy(source.at[:, own_part] if i in (6, 7) else source, buffer, in_sem.at[i])
        for i, (source, buffer) in enumerate(zip(sources, buffers))
    ]
    large = [
        [
            pltpu.make_async_copy(source.at[m], target.at[m], big_sem.at[i, m])
            for i, (source, target) in enumerate(((x_part_ref, x_buf), (z_part_ref, z_buf), (out_part_ref, out_buf)))
        ]
        for m in range(kinds)
    ]
    for copy in sum(large, []) + fetches:
        copy.start()
    copies = []
    for m in range(kinds):
        for copy in large[m]:
            copy.wait()
        first = len(copies)
        copies.append(pltpu.make_async_copy(out_buf.at[m], dw_out_ref.at[m], out_sem.at[m]))
        for b in range(chans // 128):
            for j, source in enumerate((x_buf, z_buf)):
                slot = (m * (chans // 128) + b) * 2 + j
                copies.append(
                    pltpu.make_async_copy(source.at[m, :, pl.ds(b * 128, 128)], dw_in_ref.at[m, :, b, j], sems.at[slot])
                )
        for copy in copies[first:]:
            copy.start()
    for copy in fetches:
        copy.wait()
    scale = scale_ref[...]
    bent = scale * scale * scale * mean_ref[...]
    for q in range(part // 128):
        lanes = slice(q * 128, (q + 1) * 128)
        x = x_ref[:, lanes].astype(jnp.float32)
        block_ref[:, lanes] = (x + mix_ref[:, lanes]).astype(jnp.bfloat16)
        weighted = slice_ref[:, lanes] * gain_ref[:, lanes]
        dx_ref[:, lanes] = cot_ref[:, lanes].astype(jnp.float32) + scale * weighted - x * bent
    gain_out_ref[...] = dgain_ref[0:1]
    x_proj_ref[...] = small_ref[0:160].astype(jnp.float32)
    dt_proj_ref[...] = small_ref[160:288].astype(jnp.float32)
    a_log_ref[...] = small_ref[288:304].astype(jnp.float32)
    rest = small_ref[304:320].astype(jnp.float32)
    taps_ref[...] = rest[0:4]
    cbias_ref[...] = rest[4:5]
    dt_bias_ref[...] = rest[5:6]
    skip_ref[...] = rest[6:7]
    for copy in copies:
        copy.wait()


def finish(x_part, z_part, out_part, small, total, mix, mean, scale, cot, x_in, gain, dgain):
    kinds, slab, chans = x_part.shape
    rows, part = total.shape
    vmem = pl.BlockSpec(memory_space=pltpu.VMEM)
    hbm = pl.BlockSpec(memory_space=pl.ANY)
    f32 = jnp.float32
    shape = jax.ShapeDtypeStruct
    outs = pl.pallas_call(
        finish_kernel,
        in_specs=[hbm] * 12,
        out_specs=[hbm] * 2 + [vmem] * 10,
        out_shape=[
            shape((kinds, slab, chans // 128, 2, 128), f32), shape((kinds, slab, chans), f32),
            shape((rows, part), jnp.bfloat16), shape((rows, part), f32), shape((1, part), f32), shape((4, chans), f32),
            shape((1, chans), f32), shape((160, chans), f32), shape((128, chans), f32), shape((1, chans), f32),
            shape((16, chans), f32), shape((1, chans), f32),
        ],
        scratch_shapes=[
            pltpu.VMEM(small.shape, small.dtype), pltpu.VMEM((rows, part), f32), pltpu.VMEM((rows, part), f32),
            pltpu.VMEM((rows, 128), f32), pltpu.VMEM((rows, 128), f32), pltpu.VMEM((rows, part), cot.dtype),
            pltpu.VMEM((rows, part), x_in.dtype), pltpu.VMEM((1, part), f32), pltpu.VMEM(dgain.shape, f32),
            pltpu.VMEM(x_part.shape, f32), pltpu.VMEM(x_part.shape, f32), pltpu.VMEM(x_part.shape, f32),
            pltpu.SemaphoreType.DMA((kinds * chans // 64,)), pltpu.SemaphoreType.DMA((kinds,)), pltpu.SemaphoreType.DMA((9,)),
            pltpu.SemaphoreType.DMA((3, kinds)),
        ],
        compiler_params=pltpu.CompilerParams(vmem_limit_bytes=60 << 20),
        name="finish",
    )(x_part, z_part, out_part, small, total, mix, mean, scale, cot, x_in, gain, dgain)
    dw_in = outs[0].transpose(0, 1, 3, 2, 4).reshape(kinds, slab, 2, chans)
    return (outs[2], outs[3], outs[4][0], dw_in, outs[5], outs[6][0], outs[7].T, outs[8], outs[9][0], outs[10], outs[11][0], outs[1])


def shards(
    x_in,
    norm_gain,
    w_in,
    conv_weight,
    conv_bias,
    x_proj,
    dt_proj,
    dt_bias,
    a_log,
    d_skip,
    w_out,
    modes,
    doc_lengths,
    cotangent,
):
    seq_count = lax.axis_size("seq")
    tok_rows = x_in.shape[0]
    inner_local = conv_bias.shape[0]
    docs = doc_lengths.shape[0]
    order = jnp.arange(docs, dtype=jnp.int32)
    starts = jnp.sum(jnp.where(order[:, None] > order[None, :], doc_lengths[None, :], 0), axis=1)
    starts = jnp.broadcast_to(starts[:, None], (docs, 128))
    mode_rows = modes.reshape(2 * seq_count, tok_rows // 2)
    blocks = lane_blocks(w_in)
    gain = norm_gain[None]
    x_proj_t = x_proj.T
    z_branch, d_gated, columns, extended, conv_pre, conv_out, maps = front(
        x_in, gain, mode_rows, cotangent, starts, conv_weight, conv_bias[None], x_proj_t, blocks, w_out
    )
    d_w_out, d_w_z, d_w_x, mixer, smalls, d_slice, mean, d_gain, scale = core(
        blocks, w_out, columns, extended, conv_pre, conv_out, maps, z_branch, d_gated, starts, conv_weight, x_proj_t,
        dt_proj, dt_bias[None], a_log, d_skip[None], mode_rows, x_in, gain,
    )
    return finish(
        d_w_x, d_w_z.reshape(d_w_x.shape), d_w_out.reshape(d_w_x.shape), smalls.reshape(-1, inner_local), d_slice, mixer,
        mean, scale, cotangent, x_in, gain, d_gain,
    )


def solution(mesh):
    return jax.shard_map(
        shards,
        mesh=mesh,
        in_specs=(
            P("seq", None),
            P(),
            P(None, None, None, "ch"),
            P(None, "ch"),
            P("ch"),
            P("ch", None),
            P(None, "ch"),
            P("ch"),
            P(None, "ch"),
            P("ch"),
            P(None, None, "ch"),
            P(),
            P(),
            P("seq", "ch"),
        ),
        out_specs=(
            P("seq", "ch"),
            P("seq", "ch"),
            P("ch"),
            P(None, "seq", None, "ch"),
            P(None, "ch"),
            P("ch"),
            P("ch", None),
            P(None, "ch"),
            P("ch"),
            P(None, "ch"),
            P("ch"),
            P(None, "seq", "ch"),
        ),
        check_vma=False,
    )
```

```python
import functools
import math

import jax
import jax.numpy as jnp
from jax import lax
from jax.experimental import pallas as pl
from jax.experimental.pallas import tpu as pltpu
from jax.sharding import PartitionSpec as P

EPSILON = 1e-05


MESH = pl.DeviceIdType.MESH


def cycle_of(count):
    across = count // 4
    walk = [(0, x) for x in range(across)]
    for turn, x in enumerate(reversed(range(across))):
        column = [(z, x) for z in range(1, 4)]
        walk += column[::-1] if turn % 2 else column
    return [z * across + x for z, x in walk]


def table_of(index, values):
    picked = jnp.int32(values[0])
    for i in range(1, len(values)):
        picked = jnp.where(index == i, jnp.int32(values[i]), picked)
    return picked


def mode_columns(modes_ref, target_ref):
    half = target_ref.shape[0] // 2
    for way in (0, 1):
        row = modes_ref[pl.ds(2 * lax.axis_index("seq") + way, 1), :].astype(jnp.float32)
        target_ref[way * half : (way + 1) * half] = jnp.transpose(jnp.broadcast_to(row, (128, half)))


def row_scale(x):
    return lax.rsqrt(jnp.mean(x * x, axis=1, keepdims=True) + EPSILON)


def documents(starts_ref, tokens):
    def passed(at):
        total = jnp.zeros(at.shape, jnp.float32)
        for i in range(starts_ref.shape[0]):
            total = total + jnp.where(at >= starts_ref[i : i + 1], 1.0, 0.0)
        return jnp.where(at >= tokens, -1.0, total)

    return passed


def padded(x_proj_ref, target_ref):
    tall = x_proj_ref.shape[0]
    target_ref[0:tall] = x_proj_ref[...]
    target_ref[tall:] = jnp.zeros((target_ref.shape[0] - tall, target_ref.shape[1]), target_ref.dtype)


def front_kernel(
    sizes, x_in_ref, gain_ref, modes_ref, cot_ref, starts_ref, taps_ref, cbias_ref, x_proj_ref, w_in_ref, w_out_ref,
    z_ref, gated_ref, cols_ref, ext_ref, pre_ref, conv_ref, part_ref,
    cotg_ref, normed_ref, cols_sem, seq_send, seq_recv, twin_send, twin_recv, x_ref, halo_ref, padded_ref, sent_ref, got_ref, low_send, low_recv, mode_ref, x2_ref, halo_send, halo_recv, in_buf, out_buf, in_sem, out_sem, cot_send, cot_recv, own_sem,
):
    count, twins = sizes
    rows, width = x_in_ref.shape
    modes = w_out_ref.shape[0]
    part = cot_ref.shape[1]
    inner = x_ref.shape[1]
    me = lax.axis_index("seq")
    mine = lax.axis_index("ch")
    barrier = pltpu.get_barrier_semaphore()
    for k in range(1, count):
        pl.semaphore_signal(barrier, inc=1, device_id={"seq": lax.rem(me + k, count)}, device_id_type=MESH)
    for k in range(1, twins):
        peer = {"ch": lax.rem(mine + k, twins)}
        pl.semaphore_signal(barrier, inc=1, device_id=peer, device_id_type=MESH)

    pairs = inner // 256
    steps = pairs * modes

    def in_copy(step, b):
        slot = lax.rem(step, 2)
        return pltpu.make_async_copy(
            w_in_ref.at[lax.rem(step, modes), :, step // modes * 2 + b], in_buf.at[slot, b], in_sem.at[slot, b]
        )

    wide = out_buf.shape[2]
    out_steps = inner // wide * modes

    def out_copy(step):
        slot = lax.rem(step, 2)
        columns = pl.ds(pl.multiple_of(step // modes * wide, wide), wide)
        return pltpu.make_async_copy(
            w_out_ref.at[lax.rem(step, modes), :, columns], out_buf.at[slot], out_sem.at[slot]
        )

    for b in (0, 1):
        in_copy(0, b).start()
    out_copy(0).start()
    mode_columns(modes_ref, mode_ref)

    def norm_body(i, carry):
        rc = pl.ds(pl.multiple_of(i * 16, 16), 16)
        x = x_in_ref[rc, :].astype(jnp.float32)
        normed_ref[rc, :] = (x * row_scale(x) * gain_ref[...]).astype(jnp.bfloat16)
        return carry

    lax.fori_loop(0, rows // 16, norm_body, 0)
    pl.semaphore_wait(barrier, count - 1 + twins - 1)
    slab = cols_ref.shape[4]
    half = rows // 2
    ring = cycle_of(count)
    where = {s: i for i, s in enumerate(ring)}
    place = table_of(me, [where[s] for s in range(count)])
    side = lax.rem(mine, 2)
    twin = mine + 1 - 2 * side
    side_rows = pl.ds(pl.multiple_of(side * half, half), half)

    def column_source(kind, owner, those):
        return (normed_ref, cotg_ref)[kind].at[those, pl.ds(pl.multiple_of(owner * slab, slab), slab)]

    own_columns = [
        pltpu.make_async_copy(
            column_source(kind, me, pl.ds(way * half, half)), cols_ref.at[kind, way, 0], cols_sem.at[kind, way]
        )
        for kind in (0, 1)
        for way in (0, 1)
    ]
    seq_copies = []
    for kind in (0, 1):
        for k in range(1, count):
            peer = table_of(lax.rem(place + jnp.where(side == 0, k, count - k), count), ring)
            seq_copies.append(
                pltpu.make_async_remote_copy(
                    src_ref=column_source(kind, peer, side_rows), dst_ref=cols_ref.at[kind, side, k],
                    send_sem=seq_send.at[kind, k - 1], recv_sem=seq_recv.at[kind, k - 1], device_id={"seq": peer},
                    device_id_type=MESH,
                )
            )
    twin_copies = [
        pltpu.make_async_remote_copy(
            src_ref=cols_ref.at[kind, side, pl.ds(1, count - 1)], dst_ref=cols_ref.at[kind, side, pl.ds(1, count - 1)],
            send_sem=twin_send.at[kind], recv_sem=twin_recv.at[kind], device_id={"ch": twin}, device_id_type=MESH,
        )
        for kind in (0, 1)
    ]


    own_part = pl.ds(pl.multiple_of(mine * part, part), part)
    cot_copies = [
        pltpu.make_async_remote_copy(
            src_ref=cot_ref, dst_ref=cotg_ref.at[:, own_part], send_sem=cot_send.at[k - 1], recv_sem=cot_recv.at[k - 1],
            device_id={"ch": lax.rem(mine + k, twins)}, device_id_type=MESH,
        )
        for k in range(1, twins)
    ]
    for copy in cot_copies:
        copy.start()
    own_copy = pltpu.make_async_copy(cot_ref, cotg_ref.at[:, own_part], own_sem.at[0])
    own_copy.start()
    for copy in seq_copies[: count - 1] + own_columns[:2]:
        copy.start()

    def in_step(step, carry):
        slot = lax.rem(step, 2)
        mode = lax.rem(step, modes)

        @pl.when(step + 1 < steps)
        def _():
            for b in (0, 1):
                in_copy(step + 1, b).start()

        for b in (0, 1):
            in_copy(step, b).wait()
        weights = jnp.concatenate([in_buf.at[slot, b].reshape(2 * width, 128)[...] for b in (0, 1)], axis=1)
        mask = jnp.concatenate([mode_ref[...]] * 2, axis=1) == mode.astype(jnp.float32)
        columns = pl.ds(pl.multiple_of(step // modes * 256, 256), 256)
        both = jnp.dot(x2_ref[...], weights, preferred_element_type=jnp.float32)
        for j, target in enumerate((x_ref, z_ref)):
            found = jnp.where(mask, both[j * rows : (j + 1) * rows], target[:, columns].astype(jnp.float32))
            target[:, columns] = found.astype(jnp.bfloat16)
        return carry

    x_ref[...] = jnp.zeros_like(x_ref)
    z_ref[...] = jnp.zeros_like(z_ref)
    row = lax.broadcasted_iota(jnp.int32, (256, 512), 0)
    column = lax.broadcasted_iota(jnp.int32, (256, 512), 1)
    for j in (0, 1):
        spread = (column == 2 * row + j).astype(jnp.bfloat16)
        for block in range(width // 256):
            x2_ref[j * rows : (j + 1) * rows, block * 512 : (block + 1) * 512] = jnp.dot(
                normed_ref[:, block * 256 : (block + 1) * 256], spread, preferred_element_type=jnp.float32
            ).astype(jnp.bfloat16)
    lax.fori_loop(0, steps // 2, in_step, 0)
    own_copy.wait()
    for copy in cot_copies:
        copy.wait_recv()
    for copy in seq_copies[count - 1 :] + own_columns[2:]:
        copy.start()
    lax.fori_loop(steps // 2, steps, in_step, 0)
    halo_copy = pltpu.make_async_remote_copy(
        src_ref=x_ref.at[pl.ds(rows - 16, 16)], dst_ref=halo_ref, send_sem=halo_send.at[0], recv_sem=halo_recv.at[0],
        device_id={"seq": lax.rem(me + 1, count)}, device_id_type=MESH,
    )
    halo_copy.start()
    for copy in seq_copies[: count - 1]:
        copy.wait_recv()
    twin_copies[0].start()

    def out_step(step, carry):
        slot = lax.rem(step, 2)
        mode = lax.rem(step, modes)

        @pl.when(step + 1 < out_steps)
        def _():
            out_copy(step + 1).start()

        out_copy(step).wait()
        mask = jnp.concatenate([mode_ref[...]] * (wide // 128), axis=1) == mode.astype(jnp.float32)
        columns = pl.ds(pl.multiple_of(step // modes * wide, wide), wide)
        found = jnp.dot(cotg_ref[...], out_buf[slot], preferred_element_type=jnp.float32)
        gated_ref[:, columns] = jnp.where(mask, found, gated_ref[:, columns])
        return carry

    gated_ref[...] = jnp.zeros_like(gated_ref)
    lax.fori_loop(0, out_steps // 2, out_step, 0)

    chunks, _, inner = pre_ref.shape
    padded(x_proj_ref, padded_ref)
    passed = documents(starts_ref, count * rows)
    spot = lax.broadcasted_iota(jnp.int32, (rows, 128), 0) + me * rows
    here = passed(spot)
    same = [jnp.where(passed(spot - lag) == here, 1.0, 0.0) for lag in (3, 2, 1, 0)]
    halo_copy.wait_recv()
    ext_ref[0:8] = halo_ref[8:16].astype(jnp.float32)
    ext_ref[8:] = x_ref[...].astype(jnp.float32)

    def conv_body(block, carry):
        cut = pl.ds(pl.multiple_of(block * 128, 128), 128)
        pre = jnp.zeros((rows, 128), jnp.float32) + cbias_ref[:, cut]
        for k in range(4):
            pre = pre + taps_ref[k : k + 1, cut] * ext_ref[5 + k : 5 + k + rows, cut] * same[k]
        pre_ref[:, :, cut] = pre.reshape(chunks, 16, 128)
        conv_ref[:, :, cut] = (pre / (1.0 + jnp.exp(-pre))).astype(jnp.bfloat16).reshape(chunks, 16, 128)
        return carry

    lax.fori_loop(0, inner // 128, conv_body, 0)
    part_ref[...] = lax.dot_general(
        conv_ref[...].reshape(rows, inner), padded_ref[...], (((1,), (1,)), ((), ())), preferred_element_type=jnp.float32
    )
    sent_ref[...] = part_ref[...].astype(jnp.bfloat16)
    low_copies = [
        pltpu.make_async_remote_copy(
            src_ref=sent_ref, dst_ref=got_ref.at[k - 1], send_sem=low_send.at[k - 1], recv_sem=low_recv.at[k - 1],
            device_id={"ch": lax.rem(mine + k, twins)}, device_id_type=MESH,
        )
        for k in range(1, twins)
    ]
    for copy in low_copies:
        copy.start()
    for copy in seq_copies[count - 1 :]:
        copy.wait_recv()
    twin_copies[1].start()
    lax.fori_loop(out_steps // 2, out_steps, out_step, 0)
    for k, copy in enumerate(low_copies):
        copy.wait_recv()
        part_ref[...] += got_ref[k].astype(jnp.float32)
    for copy in own_columns:
        copy.wait()
    for copy in twin_copies:
        copy.wait_recv()
    for copy in cot_copies + low_copies + seq_copies + twin_copies + [halo_copy]:
        copy.wait_send()


def front(x_in, gain, modes, cot, starts, taps, cbias, x_proj_t, w_in, w_out):
    count, twins = lax.axis_size("seq"), lax.axis_size("ch")
    rows, width = x_in.shape
    inner = w_out.shape[2]
    f32, b16 = jnp.float32, jnp.bfloat16
    shape = jax.ShapeDtypeStruct
    vmem = pl.BlockSpec(memory_space=pltpu.VMEM)
    hbm = pl.BlockSpec(memory_space=pl.ANY)
    wide = min(512, inner)
    return pl.pallas_call(
        functools.partial(front_kernel, (count, twins)),
        in_specs=[vmem] * 8 + [hbm] * 2,
        out_specs=[vmem] * 7,
        out_shape=[
            shape((rows, inner), b16), shape((rows, inner), f32), shape((2, 2, count, rows // 2, width // count), b16),
            shape((rows + 8, inner), f32), shape((rows // 16, 16, inner), f32), shape((rows // 16, 16, inner), b16),
            shape((rows, 256), f32),
        ],
        scratch_shapes=[
            pltpu.VMEM((rows, width), b16), pltpu.VMEM((rows, width), b16), pltpu.SemaphoreType.DMA((2, 2)),
            pltpu.SemaphoreType.DMA((2, count - 1)), pltpu.SemaphoreType.DMA((2, count - 1)),
            pltpu.SemaphoreType.DMA((2,)), pltpu.SemaphoreType.DMA((2,)),
            pltpu.VMEM((rows, inner), b16), pltpu.VMEM((16, inner), b16), pltpu.VMEM((256, inner), b16),
            pltpu.VMEM((rows, 256), b16), pltpu.VMEM((twins - 1, rows, 256), b16),
            pltpu.SemaphoreType.DMA((twins - 1,)), pltpu.SemaphoreType.DMA((twins - 1,)),
            pltpu.VMEM((rows, 128), jnp.float32),
            pltpu.VMEM((2 * rows, 2 * width), jnp.bfloat16),
            pltpu.SemaphoreType.DMA((1,)),
            pltpu.SemaphoreType.DMA((1,)),
            pltpu.VMEM((2, 2, width, 2, 128), jnp.bfloat16),
            pltpu.VMEM((2, width, wide), jnp.bfloat16),
            pltpu.SemaphoreType.DMA((2, 2)),
            pltpu.SemaphoreType.DMA((2,)),
            pltpu.SemaphoreType.DMA((twins - 1,)),
            pltpu.SemaphoreType.DMA((twins - 1,)),
            pltpu.SemaphoreType.DMA((1,)),
        ],
        compiler_params=pltpu.CompilerParams(collective_id=1, has_side_effects=True, vmem_limit_bytes=56 << 20),
        name="front",
    )(x_in, gain, modes, cot, starts, taps, cbias, x_proj_t, w_in, w_out)


def tile_lanes(v, lanes):
    return jnp.concatenate([v] * (lanes // 128), axis=1)

def ring_places(count):
    ring = cycle_of(count)
    where = {s: i for i, s in enumerate(ring)}
    me = lax.axis_index("seq")
    onward = table_of(me, [ring[(where[s] + 1) % count] for s in range(count)])
    backward = table_of(me, [ring[(where[s] - 1) % count] for s in range(count)])
    place = table_of(me, [where[s] for s in range(count)])
    return ring, place, onward, backward


def add_products(accs, kind, k, cols_ref, blocks, modes_ref, ring, place, count):
    parts = []
    for way in (0, 1):
        step = k if way else count - k
        source = table_of(lax.rem(place + step, count), ring)
        parts.append((jnp.transpose(cols_ref[kind, way, k]), modes_ref[pl.ds(2 * source + way, 1), :]))
    right = jnp.concatenate(blocks, axis=0)
    for m, acc in enumerate(accs):
        left = jnp.concatenate(
            [part * jnp.where(row == m, 1.0, 0.0).astype(jnp.bfloat16) for part, row in parts], axis=1
        )
        found = jnp.dot(left, right, preferred_element_type=jnp.float32)
        acc[...] += found.reshape(acc.shape)


def core_kernel(
    sizes, w_in_ref, w_out_ref, cols_hbm, ext_hbm, pre_hbm, x_in_hbm, conv_ref, part_ref, z_ref, dgated_ref, starts_ref,
    taps_ref, x_t_ref, dt_proj_ref, dt_bias_ref, a_log_ref, skip_ref, modes_ref, gain_ref,
    dwo_ref, dwz_ref, dwx_ref, mix_ref, small_ref, slice_ref, dots_ref, dgain_ref, scale_ref,
    cols_ref, ext_ref, pre_ref, x_in_ref, late_sem, x_proj_ref, same_ref, mode_ref, free_sem, g_ref, step_ref, dtd_ref, u_ref, sig_ref, low_t_ref, b_ref, c_ref, rate_ref, ends_ref,
    ends_sent, ends_got, steps_sent, steps_got, gap_ref, h0_ref, gz_ref,
    racc_ref, rows_ref, sum_ref, half_ref, half_got, four_ref, four_b16, four_got, in_buf, out_buf, mix_sent, mix_got,
    norm_sent, norm_got, dots_sent, dots_got, gain_sent, gain_got,
    ring_ref, hist_ref, lam_ref, w_ref, pend_ref, gstep_ref, gscan_ref, grad_ref, sent_ref, got_ref,
    gpre_ref, edge_ref,
    in_sem, out_sem, mix_send, mix_recv, half_send, half_recv, four_send, four_recv, last_send, last_recv, all_send, all_recv,
    ends_send, ends_recv, steps_send, steps_recv, norm_send, norm_recv, dots_send, dots_recv,
    gain_send, gain_recv, dwo_sem,
    ring_send, ring_recv, gx_send, gx_recv, ch_send, ch_recv, edge_send, edge_recv,
):
    count, twins = sizes
    chunks, _, chans = pre_ref.shape
    rows = chunks * 16
    gx_ref = gz_ref.at[2]
    slab = cols_ref.shape[4]
    n = a_log_ref.shape[0]
    half = rows // 2
    ring, place, onward, backward = ring_places(count)
    me = lax.axis_index("seq")
    mine = lax.axis_index("ch")
    before = lax.rem(me + count - 1, count)
    nt = (((1,), (1,)), ((), ()))
    f32, b16 = jnp.float32, jnp.bfloat16
    lb = min(512, chans)

    modes, width = w_out_ref.shape[:2]
    part = width // twins
    eighths = chans // 128
    across = half_ref.shape[1]
    tall = half_ref.shape[0]
    depth = half_ref.shape[2]
    z_at = me // across
    x_at = lax.rem(me, across)

    def chunk_of(step):
        return pl.ds(pl.multiple_of(lax.rem(mine + 1 + step // modes, twins) * part, part), part)

    def in_copy(step, b):
        slot = step % 2
        return pltpu.make_async_copy(w_in_ref.at[step % modes, chunk_of(step), b], in_buf.at[slot, b], in_sem.at[slot, b])

    def in_copies(step, wait):
        for b in range(eighths):
            if wait:
                in_copy(step, b).wait()
            else:
                in_copy(step, b).start()

    def out_copy(step):
        slot = step % 2
        return pltpu.make_async_copy(w_out_ref.at[step % modes, chunk_of(step)], out_buf.at[slot], out_sem.at[slot])

    barrier = pltpu.get_barrier_semaphore()
    for k in range(1, count):
        pl.semaphore_signal(barrier, inc=1, device_id={"seq": lax.rem(me + k, count)}, device_id_type=MESH)
    for k in range(1, twins):
        peer = {"ch": lax.rem(mine + k, twins)}
        pl.semaphore_signal(barrier, inc=1, device_id=peer, device_id_type=MESH)
    in_copies(0, 0)
    out_copy(0).start()
    late_operands = ((cols_hbm, cols_ref), (ext_hbm, ext_ref), (pre_hbm, pre_ref), (x_in_hbm, x_in_ref))
    late_fetches = [
        pltpu.make_async_copy(source, target, late_sem.at[i]) for i, (source, target) in enumerate(late_operands)
    ]
    for copy in late_fetches:
        copy.start()
    pl.semaphore_wait(barrier, count - 1 + twins - 1)

    passed = documents(starts_ref, count * rows)

    def maps_copies(send, recv):
        return [
            pltpu.make_async_remote_copy(
                src_ref=sent_ref, dst_ref=got_ref.at[k - 1], send_sem=send.at[k - 1],
                recv_sem=recv.at[k - 1], device_id={"ch": lax.rem(mine + k, twins)}, device_id_type=MESH,
            )
            for k in range(1, twins)
        ]


    def gate_body(i, carry):
        z = z_ref[i].astype(f32)
        g_ref[i] = dgated_ref[i] * (z / (1.0 + jnp.exp(-z)))
        return carry

    lax.fori_loop(0, chunks, gate_body, 0)
    rate_ref[...] = -math.log2(math.e) * jnp.exp(a_log_ref[...])
    own = (
        lax.broadcasted_iota(jnp.int32, (16, 16 * n), 1) // n == lax.broadcasted_iota(jnp.int32, (16, 16 * n), 0)
    )
    ones = own.astype(b16)
    token_row = lax.broadcasted_iota(jnp.int32, (16 * n, 16), 0) // n
    repeat = (token_row == lax.broadcasted_iota(jnp.int32, (16 * n, 16), 1)).astype(b16)
    pick_row = lax.broadcasted_iota(jnp.int32, (16 * n, 128), 0)
    pick_col = lax.broadcasted_iota(jnp.int32, (16 * n, 128), 1)
    is_b = pick_row % n == pick_col
    is_c = pick_row % n + n == pick_col
    pick_b = is_b.astype(b16)
    pick_c = is_c.astype(b16)
    flat = jnp.ones((256, 128), b16)
    total = part_ref[...]
    low_t_ref[...] = jnp.transpose(total[:, 0:128]).astype(b16)
    raw = jnp.dot(total[:, 0:128].astype(b16), dt_proj_ref[...], preferred_element_type=f32)
    step_ref[...] = raw.reshape(chunks, 16, chans)

    def step_body(i, carry):
        raw = step_ref[i] + dt_bias_ref[...]
        step = jnp.maximum(raw, 0.0) + jnp.log1p(jnp.exp(-jnp.abs(raw)))
        step_ref[i] = step
        sig_ref[i] = 1.0 / (1.0 + jnp.exp(-raw))
        at = lax.broadcasted_iota(jnp.int32, (16, 128), 0) + (me * rows + i * 16)
        big = jnp.where(passed(at) == passed(at - 1), 0.0, 1e30)
        dtd_ref[i] = step + jnp.concatenate([big] * (chans // 128), axis=1)
        u_ref[i] = step * conv_ref[i].astype(f32)
        maps = part_ref[pl.ds(pl.multiple_of(i * 16, 16), 16), 128:256]
        high = maps.astype(b16)
        low = (maps - high.astype(f32)).astype(b16)
        high = jnp.dot(repeat, high, preferred_element_type=f32)
        low = jnp.dot(repeat, low, preferred_element_type=f32)
        for target, chosen in ((b_ref, is_b), (c_ref, is_c)):
            terms = [jnp.where(chosen, term, 0.0).astype(b16) for term in (high, low)]
            found = jnp.dot(jnp.concatenate(terms, axis=1), flat, preferred_element_type=f32)
            target[pl.ds(i * 16, 16)] = found.reshape(16, n, 128)
        return carry

    lax.fori_loop(0, chunks, step_body, 0, unroll=2)

    def maps_block(chunk, pick):
        maps = part_ref[pl.ds(pl.multiple_of(chunk * 16, 16), 16), 128:256].astype(b16)
        found = lax.dot_general(maps, pick, nt, preferred_element_type=f32)
        return jnp.where(own, found, 0.0).astype(b16)

    ends_ref[0:n] = jnp.zeros((n, chans), f32)
    ends_ref[n : 2 * n] = jnp.ones((n, chans), f32)
    ends_ref[2 * n : 3 * n] = jnp.zeros((n, chans), f32)

    def end_body(chunk, carry):
        for block in range(chans // lb):
            cut = slice(block * lb, (block + 1) * lb)
            rate = rate_ref[:, cut]
            h = ends_ref[0:n, cut]
            for t in range(16):
                decay = jnp.exp2(dtd_ref[chunk, t : t + 1, cut] * rate)
                h = decay * h + u_ref[chunk, t : t + 1, cut] * tile_lanes(b_ref[chunk * 16 + t], lb)
            ends_ref[0:n, cut] = h
        return carry

    def head_body(chunk, carry):
        for block in range(chans // lb):
            cut = slice(block * lb, (block + 1) * lb)
            rate = rate_ref[:, cut]
            reach = ends_ref[n : 2 * n, cut]
            head = ends_ref[2 * n : 3 * n, cut]
            for t in range(16):
                reach = reach * jnp.exp2(dtd_ref[chunk, t : t + 1, cut] * rate)
                head = head + reach * (g_ref[chunk, t : t + 1, cut] * tile_lanes(c_ref[chunk * 16 + t], lb))
            ends_ref[n : 2 * n, cut] = reach
            ends_ref[2 * n : 3 * n, cut] = head
        return carry

    def state_copy(side, k):
        return pltpu.make_async_remote_copy(
            src_ref=ends_sent.at[side], dst_ref=ends_got.at[k - 1], send_sem=ends_send.at[k - 1],
            recv_sem=ends_recv.at[k - 1], device_id={"seq": lax.rem(me + k, count)}, device_id_type=MESH,
        )

    steps_copies = [
        pltpu.make_async_remote_copy(
            src_ref=steps_sent, dst_ref=steps_got.at[k - 1], send_sem=steps_send.at[k - 1],
            recv_sem=steps_recv.at[k - 1], device_id={"seq": lax.rem(me + k, count)}, device_id_type=MESH,
        )
        for k in range(1, count)
    ]
    steps_sent[...] = jnp.sum(jnp.sum(dtd_ref[...], axis=0), axis=0, keepdims=True)
    for copy in steps_copies:
        copy.start()
    lax.fori_loop(0, chunks, end_body, 0, unroll=2)
    ends_sent[0] = ends_ref[0:n].astype(b16)
    for k in range(1, count):

        @pl.when(me + k < count)
        def _():
            state_copy(0, k).start()

    lax.fori_loop(0, chunks, head_body, 0, unroll=2)
    ends_sent[1] = ends_ref[2 * n : 3 * n].astype(b16)
    for k in range(1, count):

        @pl.when(me + k >= count)
        def _():
            state_copy(1, k).start()

    for copy in steps_copies:
        copy.wait_recv()
    for k in range(1, count):

        @pl.when(me >= k)
        def _():
            state_copy(0, k).wait_recv()

    h0_ref[...] = jnp.zeros_like(h0_ref)
    gap_ref[...] = jnp.zeros_like(gap_ref)
    for k in range(1, count):

        @pl.when(me >= k)
        def _():
            h0_ref[...] += ends_got[k - 1].astype(f32) * jnp.exp2(rate_ref[...] * gap_ref[...])

        gap_ref[...] += steps_got[k - 1]

    racc_ref[...] = h0_ref[...]

    def forward_body(chunk, carry):
        for block in range(chans // lb):
            cut = slice(block * lb, (block + 1) * lb)
            rate = rate_ref[:, cut]
            h = racc_ref[:, cut]
            for t in range(16):
                decay = jnp.exp2(dtd_ref[chunk, t : t + 1, cut] * rate)
                h = decay * h + u_ref[chunk, t : t + 1, cut] * tile_lanes(b_ref[chunk * 16 + t], lb)
                hist_ref[chunk, t * n : (t + 1) * n, cut] = h.astype(b16)
            racc_ref[:, cut] = h
        ssm = jnp.dot(maps_block(chunk, pick_c), hist_ref[chunk], preferred_element_type=f32)
        ssm = ssm + skip_ref[...] * conv_ref[chunk].astype(f32)
        z = z_ref[chunk].astype(f32)
        sig = 1.0 / (1.0 + jnp.exp(-z))
        rc = pl.ds(pl.multiple_of(chunk * 16, 16), 16)
        gz_ref[0, rc] = (ssm * (z * sig)).astype(b16)
        gz_ref[1, rc] = (dgated_ref[chunk] * ssm * (sig * (1.0 + z * (1.0 - sig)))).astype(b16)
        return carry

    lax.fori_loop(0, chunks, forward_body, 0, unroll=2)

    def ring_copy(kind, way, k):
        if k == 0:
            source = gz_ref.at[kind, pl.ds(way * half, half)]
        else:
            source = ring_ref.at[kind, way, k - 1]
        return pltpu.make_async_remote_copy(
            src_ref=source, dst_ref=ring_ref.at[kind, way, k], send_sem=ring_send.at[kind, way, k],
            recv_sem=ring_recv.at[kind, way, k], device_id={"seq": backward if way else onward}, device_id_type=MESH,
        )

    def relay(kind, k):
        for way in (0, 1):
            if kind == 2:
                gx_copy(way, k - 1).wait_recv()
                if k < count - 1:
                    gx_copy(way, k).start()
            else:
                ring_copy(kind, way, k - 1).wait_recv()
                if k < count - 1:
                    ring_copy(kind, way, k).start()

    def gx_slot(way, k):
        slot = way * (count - 1) + k
        return hist_ref.at[slot // 2, pl.ds(slot % 2 * half, half)]

    def gx_copy(way, k):
        return pltpu.make_async_remote_copy(
            src_ref=gx_slot(way, k - 1) if k else gx_ref.at[pl.ds(way * half, half)], dst_ref=gx_slot(way, k),
            send_sem=gx_send.at[way, k], recv_sem=gx_recv.at[way, k], device_id={"seq": backward if way else onward},
            device_id_type=MESH,
        )

    for kind in (0, 1):
        for way in (0, 1):
            ring_copy(kind, way, 0).start()
    for copy in late_fetches:
        copy.wait()
    for k in range(1, count):

        @pl.when(me < k)
        def _():
            state_copy(1, k).wait_recv()

    pend_ref[...] = jnp.zeros_like(pend_ref)
    gap_ref[...] = jnp.zeros_like(gap_ref)
    for k in range(1, count):
        slot = count - 1 - k

        @pl.when(me + k < count)
        def _():
            pend_ref[...] += ends_got[slot].astype(f32) * jnp.exp2(rate_ref[...] * gap_ref[...])

        gap_ref[...] += steps_got[slot]

    turns = [(kind, k) for k in range(1, count) for kind in (0, 1)]
    early = turns[:2]
    late = turns[2:]

    racc_ref[...] = jnp.zeros_like(racc_ref)

    def span_body(i, carry):
        at = spans - 1 - i
        for sub in reversed(range(span // 16)):
            chunk = at * (span // 16) + sub
            for block in range(chans // lb):
                cut = slice(block * lb, (block + 1) * lb)
                rate = rate_ref[:, cut]
                pend = pend_ref[:, cut]
                racc = racc_ref[:, cut]
                for t in reversed(range(16)):
                    decay = jnp.exp2(dtd_ref[chunk, t : t + 1, cut] * rate)
                    lam = g_ref[chunk, t : t + 1, cut] * tile_lanes(c_ref[chunk * 16 + t], lb) + pend
                    pend = decay * lam
                    if t:
                        prior = hist_ref[chunk, (t - 1) * n : t * n, cut].astype(jnp.float32)
                    else:
                        prior = hist_ref[jnp.maximum(chunk - 1, 0), 15 * n : 16 * n, cut].astype(jnp.float32)
                        prior = jnp.where(chunk == 0, h0_ref[:, cut], prior)
                    w = pend * prior
                    racc = racc + w * step_ref[chunk, t : t + 1, cut]
                    lam_ref[t * n : (t + 1) * n, cut] = lam.astype(jnp.bfloat16)
                    w_ref[t * n : (t + 1) * n, cut] = (w * rate).astype(jnp.bfloat16)
                pend_ref[:, cut] = pend
                racc_ref[:, cut] = racc
            step = step_ref[chunk]
            conv = conv_ref[chunk].astype(jnp.float32)
            adj = jnp.dot(maps_block(chunk, pick_b), lam_ref[...], preferred_element_type=jnp.float32)
            wsum = jnp.dot(ones, w_ref[...], preferred_element_type=jnp.float32)
            gstep_ref[chunk] = wsum * math.log(2.0) + adj * conv
            gscan_ref[chunk] = adj * step
            gb = lax.dot_general(u_ref[chunk].astype(jnp.bfloat16), lam_ref[...], nt, preferred_element_type=jnp.float32)
            gc = lax.dot_general(
                g_ref[chunk].astype(jnp.bfloat16), hist_ref[chunk], nt, preferred_element_type=jnp.float32
            )
            gb = jnp.where(own, gb, 0.0).astype(jnp.bfloat16)
            gc = jnp.where(own, gc, 0.0).astype(jnp.bfloat16)
            grad_ref[pl.ds(pl.multiple_of(chunk * 16, 16), 16), 128:256] = jnp.dot(
                gb, pick_b, preferred_element_type=jnp.float32
            ) + jnp.dot(gc, pick_c, preferred_element_type=jnp.float32)
        return carry

    span = 32
    spans = rows // span
    mode_columns(modes_ref, mode_ref)
    padded(x_t_ref, x_proj_ref)
    passed = documents(starts_ref, count * rows)
    spot = lax.broadcasted_iota(jnp.int32, (rows, 128), 0) + me * rows
    here = passed(spot)
    for i in range(7):
        same_ref[i] = jnp.where(passed(spot + (i - 3)) == here, 1.0, 0.0).astype(b16)
    lax.fori_loop(0, spans // 2, span_body, 0)
    relay(*early[0])
    lax.fori_loop(spans // 2, spans, span_body, 0)
    for peer in (onward, backward):
        pl.semaphore_signal(free_sem, inc=1, device_id={"seq": peer}, device_id_type=MESH)
    relay(*early[1])

    rows_ref[...] = jnp.zeros_like(rows_ref)

    def raw_body(i, carry):
        full = gstep_ref[i] * sig_ref[i]
        rows_ref[5:6] += jnp.sum(full, axis=0, keepdims=True)
        rows_ref[6:7] += jnp.sum(g_ref[i] * conv_ref[i].astype(jnp.float32), axis=0, keepdims=True)
        gx_ref[pl.ds(pl.multiple_of(i * 16, 16), 16), :] = full.astype(jnp.bfloat16)
        return carry

    lax.fori_loop(0, chunks, raw_body, 0)
    grad_ref[:, 0:128] = lax.dot_general(gx_ref[...], dt_proj_ref[...], nt, preferred_element_type=jnp.float32)
    sent_ref[...] = grad_ref[...].astype(jnp.bfloat16)
    ch_copies = maps_copies(ch_send, ch_recv)
    for copy in ch_copies:
        copy.start()
    relay(*late[0])
    sum_ref[160:288] = jnp.dot(low_t_ref[...], gx_ref[...], preferred_element_type=jnp.float32)
    for copy in ch_copies:
        copy.wait_recv()
    total = grad_ref[...]
    for k in range(twins - 1):
        total = total + got_ref[k].astype(jnp.float32)
    grad_ref[...] = total
    relay(*late[1])

    skip = skip_ref[...]
    def pre_body(i, carry):
        rc = pl.ds(pl.multiple_of(i * 16, 16), 16)
        g_conv = jnp.dot(grad_ref[rc, :].astype(jnp.bfloat16), x_proj_ref[...], preferred_element_type=jnp.float32)
        g_conv = g_conv + skip * g_ref[i] + gscan_ref[i]
        pre = pre_ref[i]
        sig = 1.0 / (1.0 + jnp.exp(-pre))
        gpre = g_conv * sig * (1.0 + pre * (1.0 - sig))
        gpre_ref[rc, :] = gpre
        return carry

    pre_body(0, 0)
    edge_ref[...] = gpre_ref[0:8, :]
    edge_copy = pltpu.make_async_remote_copy(
        src_ref=edge_ref, dst_ref=gpre_ref.at[pl.ds(rows, 8)], send_sem=edge_send.at[0], recv_sem=edge_recv.at[0],
        device_id={"seq": before}, device_id_type=MESH,
    )
    edge_copy.start()
    lax.fori_loop(1, chunks, pre_body, 0)
    flipped = jnp.transpose(grad_ref[...]).astype(jnp.bfloat16)
    sum_ref[0:160] = jnp.dot(flipped[0:160], conv_ref[...].reshape(rows, chans), preferred_element_type=jnp.float32)
    relay(*late[2])
    edge_copy.wait_recv()

    def taps_body(block, carry):
        cut = pl.ds(pl.multiple_of(block * 128, 128), 128)
        gpre = gpre_ref[0:rows, cut]
        rows_ref[4:5, cut] = jnp.sum(gpre, axis=0, keepdims=True)
        total = jnp.zeros((rows, 128), jnp.float32)
        for k in range(4):
            lag = 3 - k
            total = total + gpre_ref[lag : lag + rows, cut] * taps_ref[k : k + 1, cut] * same_ref[3 + lag].astype(jnp.float32)
            rows_ref[k : k + 1, cut] = jnp.sum(
                gpre * ext_ref[5 + k : 5 + k + rows, cut] * same_ref[k].astype(jnp.float32), axis=0, keepdims=True
            )
        gx_ref[:, cut] = total.astype(jnp.bfloat16)
        return carry

    lax.fori_loop(0, chans // 128, taps_body, 0)
    pl.semaphore_wait(free_sem, 2)
    for way in (0, 1):
        gx_copy(way, 0).start()
    sum_ref[288:304] = racc_ref[...] * rate_ref[...] * math.log(2.0)
    sum_ref[304:312] = rows_ref[...]
    if tall * across * depth > 312:
        sum_ref[312:] = jnp.zeros((tall * across * depth - 312, chans), jnp.float32)
    for z in range(tall):
        for x in range(across):
            first = (z * across + x) * depth
            half_ref[z, x] = sum_ref[first : first + depth].astype(jnp.bfloat16)

    def to(device):
        return dict(device_id={"seq": device}, device_id_type=MESH)

    half_copies = [
        pltpu.make_async_remote_copy(
            src_ref=half_ref.at[:, lax.rem(x_at + k, across)], dst_ref=half_got.at[k - 1], send_sem=half_send.at[k - 1],
            recv_sem=half_recv.at[k - 1], **to(z_at * across + lax.rem(x_at + k, across)),
        )
        for k in range(1, across)
    ]
    four_copies = [
        pltpu.make_async_remote_copy(
            src_ref=four_b16.at[lax.rem(z_at + k, tall)], dst_ref=four_got.at[k - 1], send_sem=four_send.at[k - 1],
            recv_sem=four_recv.at[k - 1], **to(lax.rem(z_at + k, tall) * across + x_at),
        )
        for k in range(1, tall)
    ]
    last_copies = [
        pltpu.make_async_remote_copy(
            src_ref=small_ref.at[z_at, x_at], dst_ref=small_ref.at[z_at, x_at], send_sem=last_send.at[k - 1],
            recv_sem=last_recv.at[k - 1], **to(lax.rem(z_at + k, tall) * across + x_at),
        )
        for k in range(1, tall)
    ]
    all_copies = [
        pltpu.make_async_remote_copy(
            src_ref=small_ref.at[:, x_at], dst_ref=small_ref.at[:, x_at], send_sem=all_send.at[k - 1],
            recv_sem=all_recv.at[k - 1], **to(z_at * across + lax.rem(x_at + k, across)),
        )
        for k in range(1, across)
    ]

    def small_phase(phase):
        if phase == 0:
            for copy in half_copies:
                copy.start()
        elif phase == 1:
            for copy in half_copies:
                copy.wait_recv()
            for z in range(tall):
                first = pl.multiple_of((z * across + x_at) * depth, depth)
                total = sum_ref[pl.ds(first, depth)]
                for k in range(across - 1):
                    total = total + half_got[k, z].astype(jnp.float32)
                four_ref[z] = total
                four_b16[z] = total.astype(jnp.bfloat16)
            for copy in four_copies:
                copy.start()
        elif phase == 2:
            for copy in four_copies:
                copy.wait_recv()
            total = four_ref[z_at]
            for k in range(tall - 1):
                total = total + four_got[k].astype(jnp.float32)
            small_ref[z_at, x_at] = total.astype(jnp.bfloat16)
            for copy in last_copies:
                copy.start()
        elif phase == 3:
            for copy in last_copies:
                copy.wait_recv()
            for copy in all_copies:
                copy.start()
        else:
            for copy in all_copies:
                copy.wait_recv()
            for copy in half_copies + four_copies + last_copies + all_copies:
                copy.wait_send()

    small_phase(0)
    dwo_accs = [ref.at[0 : slab // 16] for ref in (dtd_ref, u_ref, sig_ref)]
    dwz_accs = [ref.at[0 : slab // 16] for ref in (step_ref, g_ref, gscan_ref)]
    dwx_accs = [dwx_ref.at[m] for m in range(modes)]
    for acc in dwo_accs + dwz_accs + dwx_accs:
        acc[...] = jnp.zeros_like(acc)

    def products(kind, k):
        if k == 0:
            source = gx_ref if kind == 2 else gz_ref.at[kind]
            blocks = [source[way * half : (way + 1) * half] for way in (0, 1)]
        else:
            blocks = [gx_slot(way, k - 1)[...] if kind == 2 else ring_ref[kind, way, k - 1] for way in (0, 1)]
        accs = (dwo_accs, dwz_accs, dwx_accs)[kind]
        add_products(accs, 0 if kind else 1, k, cols_ref, blocks, modes_ref, ring, place, count)
        if kind < 2 and k == count - 1:
            for copy in out_copies[kind]:
                copy.start()

    out_copies = [
        [pltpu.make_async_copy(acc, target.at[m], dwo_sem.at[kind, m]) for m, acc in enumerate(accs)]
        for kind, (accs, target) in enumerate(((dwo_accs, dwo_ref), (dwz_accs, dwz_ref)))
    ]

    def mix_copy(j):
        return pltpu.make_async_remote_copy(
            src_ref=mix_sent.at[j], dst_ref=mix_got.at[j], send_sem=mix_send.at[j], recv_sem=mix_recv.at[j],
            device_id={"ch": lax.rem(mine + 1 + j, twins)}, device_id_type=MESH,
        )

    steps = twins * modes

    def norm_copy(j):
        return pltpu.make_async_remote_copy(
            src_ref=norm_sent.at[j], dst_ref=norm_got.at[j], send_sem=norm_send.at[j], recv_sem=norm_recv.at[j],
            device_id={"ch": lax.rem(mine + 1 + j, twins)}, device_id_type=MESH,
        )

    def normed_unit(j, m):
        step = j * modes + m
        if step + 1 < steps:
            in_copies(step + 1, 0)
        in_copies(step, 1)
        spread_products(in_buf.at[step % 2], gz_ref, mode_ref, slice_ref, m, part)

    def normed_end(j):
        for q in range(part // 128):
            lanes = slice(q * 128, (q + 1) * 128)
            cut = pl.ds(pl.multiple_of(lax.rem(mine + 1 + j, twins) * part + q * 128, 128), 128)
            dots_ref[...] += slice_ref[:, lanes] * x_in_ref[:, cut].astype(f32) * gain_ref[:, cut]
        if j < twins - 1:
            norm_sent[j] = slice_ref[...].astype(b16)
            norm_copy(j).start()

    def mix_unit(j):
        for m in range(modes):
            step = j * modes + m
            if step + 1 < steps:
                out_copy(step + 1).start()
            out_copy(step).wait()
            mask = jnp.concatenate([mode_ref[...]] * (part // 128), axis=1) == float(m)
            found = lax.dot_general(gz_ref[0], out_buf[step % 2], nt, preferred_element_type=jnp.float32)
            mix_ref[...] = jnp.where(mask, found, mix_ref[...]) if m else found
        if j < twins - 1:
            mix_sent[j] = mix_ref[...].astype(jnp.bfloat16)
            mix_copy(j).start()

    dots_copies = [
        pltpu.make_async_remote_copy(
            src_ref=dots_sent, dst_ref=dots_got.at[k - 1], send_sem=dots_send.at[k - 1], recv_sem=dots_recv.at[k - 1],
            device_id={"ch": lax.rem(mine + k, twins)}, device_id_type=MESH,
        )
        for k in range(1, twins)
    ]
    gain_copies = [
        pltpu.make_async_remote_copy(
            src_ref=gain_sent, dst_ref=gain_got.at[k - 1], send_sem=gain_send.at[k - 1], recv_sem=gain_recv.at[k - 1],
            device_id={"seq": lax.rem(me + k, count)}, device_id_type=MESH,
        )
        for k in range(1, count)
    ]

    def scale_body(i, carry):
        rc = pl.ds(pl.multiple_of(i * 16, 16), 16)
        scale_ref[rc] = jnp.broadcast_to(row_scale(x_in_ref[rc].astype(f32)), (16, 128))
        return carry

    def dots_unit():
        lax.fori_loop(0, chunks, scale_body, 0)
        dots_sent[...] = dots_ref[...].astype(b16)
        for copy in dots_copies:
            copy.start()

    def slice_unit():
        for j in range(twins - 1):
            norm_copy(j).wait_recv()
            slice_ref[...] += norm_got[j].astype(f32)
        for q in range(part // 128):
            lanes = slice(q * 128, (q + 1) * 128)
            cut = pl.ds(pl.multiple_of(mine * part + q * 128, 128), 128)
            terms = slice_ref[:, lanes] * x_in_ref[:, cut].astype(f32) * scale_ref[...]
            gain_sent[:, lanes] = jnp.broadcast_to(jnp.sum(terms, axis=0, keepdims=True), (8, 128))
        for copy in gain_copies:
            copy.start()

    def gain_unit():
        total = gain_sent[...]
        for k, copy in enumerate(gain_copies):
            copy.wait_recv()
            total = total + gain_got[k]
        dgain_ref[...] = total
        for k, copy in enumerate(dots_copies):
            copy.wait_recv()
            dots_ref[...] += dots_got[k].astype(f32)
        mean = jnp.sum(dots_ref[...], axis=1, keepdims=True) / width
        dots_ref[...] = jnp.broadcast_to(mean, (rows, 128))
        for j in range(twins - 1):
            mix_copy(j).wait_recv()
            mix_ref[...] += mix_got[j].astype(f32)

    edge_copy.wait_send()
    dots_ref[...] = jnp.zeros_like(dots_ref)
    work = []
    for j in range(twins):
        for m in range(modes):
            work.append(functools.partial(normed_unit, j, m))
        work.append(functools.partial(normed_end, j))
        if j < 4:
            work.append(functools.partial(small_phase, j + 1))
    work.append(dots_unit)
    for j in range(twins):
        work.append(functools.partial(mix_unit, j))
    work += [slice_unit, gain_unit]
    ready = [(0, 0), (1, 0), (2, 0)] + early + late[:3]
    rest, last = late[3:], [(2, k) for k in range(1, count)]
    turns = []
    while rest or last:
        turns += rest[:2] + last[:1]
        rest, last = rest[2:], last[1:]
    for i, turn in enumerate(turns):
        left = len(turns) - i
        for _ in range(min(len(work), max(2, -(-len(work) // left)))):
            work.pop(0)()
        relay(*turn)
        ready.append(turn)
        for _ in range(2 if len(ready) > left else 1):
            if len(ready) > 1:
                products(*ready.pop(0))
    for unit in work:
        unit()
    for turn in ready:
        products(*turn)
    for copy in out_copies[0] + out_copies[1]:
        copy.wait()
    for j in range(twins - 1):
        mix_copy(j).wait_send()
        norm_copy(j).wait_send()
    for copy in dots_copies + gain_copies:
        copy.wait_send()
    for way in (0, 1):
        for k in range(count - 1):
            gx_copy(way, k).wait_send()

    for kind in (0, 1):
        for way in (0, 1):
            for k in range(count - 1):
                ring_copy(kind, way, k).wait_send()
    for copy in ch_copies + steps_copies:
        copy.wait_send()
    for k in range(1, count):
        state_copy(0, k).wait_send()


def spread_products(buf, trio_ref, mode_ref, target, m, part):
    nt = (((1,), (1,)), ((), ()))
    chosen = mode_ref[...] == float(m)
    row = lax.broadcasted_iota(jnp.int32, (256, 128), 0)
    column = lax.broadcasted_iota(jnp.int32, (256, 128), 1)
    picks = [(row == 2 * column + j).astype(jnp.bfloat16) for j in (1, 0)]
    rows = trio_ref.shape[1]
    stacked = trio_ref[1:3].reshape(2 * rows, trio_ref.shape[2])
    for q in range(2 * part // 256):
        weights = jnp.concatenate(
            [buf.at[b].reshape(2 * part, 128)[q * 256 : (q + 1) * 256] for b in range(buf.shape[0])], axis=1
        )
        found = lax.dot_general(stacked, weights, nt, preferred_element_type=jnp.float32).astype(jnp.bfloat16)
        total = jnp.dot(found[:rows], picks[0], preferred_element_type=jnp.float32)
        total = total + jnp.dot(found[rows:], picks[1], preferred_element_type=jnp.float32)
        cut = pl.ds(q * 128, 128)
        target[:, cut] = jnp.where(chosen, total, target[:, cut]) if m else total


def core(
    w_in, w_out, cols, ext, pre, conv, maps, z, dgated, starts, taps, x_proj_t, dt_proj, dt_bias, a_log, skip, modes,
    x_in, gain,
):
    count, twins = lax.axis_size("seq"), lax.axis_size("ch")
    rows, chans = z.shape
    n = a_log.shape[0]
    chunks = rows // 16
    width = w_out.shape[1]
    slab = width // count
    part = width // twins
    tall, across = 4, count // 4
    depth = -(-312 // (16 * count)) * 16
    vmem = pl.BlockSpec(memory_space=pltpu.VMEM)
    hbm = pl.BlockSpec(memory_space=pl.ANY)
    cube = lambda a: a.reshape((chunks, a.shape[0] // chunks) + a.shape[1:])
    f32, b16 = jnp.float32, jnp.bfloat16
    shape = jax.ShapeDtypeStruct
    dma = pltpu.SemaphoreType.DMA
    keep = pltpu.VMEM
    operands = [w_in, w_out, cols, ext, pre, x_in, conv, maps, cube(z), cube(dgated), starts, taps, x_proj_t, dt_proj, dt_bias,
                a_log, skip, modes, gain]
    block = (chunks, 16, chans)
    pair = lambda size: [dma((size,)), dma((size,))]
    return pl.pallas_call(
        functools.partial(core_kernel, (count, twins)),
        in_specs=[hbm] * 6 + [vmem] * (len(operands) - 6),
        out_specs=[hbm] * 2 + [vmem] * 7,
        out_shape=[
            shape((3, slab // 16, 16, chans), f32), shape((3, slab // 16, 16, chans), f32), shape((3, slab, chans), f32),
            shape((rows, part), f32), shape((tall, across, depth, chans), b16), shape((rows, part), f32),
            shape((rows, 128), f32), shape((8, part), f32), shape((rows, 128), f32),
        ],
        scratch_shapes=[
            keep(cols.shape, b16), keep(ext.shape, f32), keep(pre.shape, f32), keep(x_in.shape, b16), dma((4,)),
            keep((256, chans), b16), keep((7, rows, 128), b16), keep((rows, 128), f32), pltpu.SemaphoreType.REGULAR, keep(block, f32), keep(block, f32),
            keep(block, f32), keep(block, f32), keep(block, f32), keep((128, rows), b16), keep((rows, n, 128), f32),
            keep((rows, n, 128), f32), keep((n, chans), f32), keep((3 * n, chans), f32),
            keep((2, n, chans), b16), keep((count - 1, n, chans), b16), keep((1, chans), f32),
            keep((count - 1, 1, chans), f32), keep((1, chans), f32), keep((n, chans), f32), keep((3, rows, chans), b16),
            keep((n, chans), f32), keep((8, chans), f32), keep((tall * across * depth, chans), f32),
            keep((tall, across, depth, chans), b16), keep((across - 1, tall, depth, chans), b16),
            keep((tall, depth, chans), f32), keep((tall, depth, chans), b16), keep((tall - 1, depth, chans), b16),
            keep((2, chans // 128, part, 2, 128), b16), keep((2, part, chans), b16), keep((twins - 1, rows, part), b16),
            keep((twins - 1, rows, part), b16),
            keep((twins - 1, rows, part), b16), keep((twins - 1, rows, part), b16), keep((rows, 128), b16),
            keep((twins - 1, rows, 128), b16), keep((8, part), f32), keep((count - 1, 8, part), f32),
            keep((2, 2, count - 1, rows // 2, chans), b16),
            keep((chunks, 16 * n, chans), b16), keep((16 * n, chans), b16),
            keep((16 * n, chans), b16), keep((n, chans), f32), keep(block, f32), keep(block, f32), keep((rows, 256), f32), keep((rows, 256), b16), keep((twins - 1, rows, 256), b16),
            keep((rows + 8, chans), f32), keep((8, chans), f32),
            dma((2, chans // 128)), dma((2,)), *pair(twins - 1), *pair(across - 1), *pair(tall - 1), *pair(tall - 1),
            *pair(across - 1), *pair(count - 1), *pair(count - 1), *pair(twins - 1), *pair(twins - 1),
            *pair(count - 1), dma((2, 3)),
            dma((2, 2, count - 1)), dma((2, 2, count - 1)), dma((2, count - 1)), dma((2, count - 1)), *pair(twins - 1), dma((1,)), dma((1,)),
        ],
        compiler_params=pltpu.CompilerParams(collective_id=2, has_side_effects=True, vmem_limit_bytes=63 << 20),
        name="core",
    )(*operands)


def lane_blocks(w_in):
    kinds, width, _, chans = w_in.shape
    return w_in.reshape(kinds, width, 2, chans // 128, 128).transpose(0, 1, 3, 2, 4)


def finish_kernel(
    x_part_ref, z_part_ref, out_part_ref, *refs,
):
    sources, refs = refs[:9], refs[9:]
    (
        dw_in_ref, dw_out_ref, block_ref, dx_ref, gain_out_ref, taps_ref, cbias_ref, x_proj_ref, dt_proj_ref, dt_bias_ref,
        a_log_ref, skip_ref,
    ) = refs[:12]
    buffers, (x_buf, z_buf, out_buf, sems, out_sem, in_sem, big_sem) = refs[12:21], refs[21:]
    small_ref, slice_ref, mix_ref, mean_ref, scale_ref, cot_ref, x_ref, gain_ref, dgain_ref = buffers
    kinds, _, chans = x_part_ref.shape
    part = slice_ref.shape[1]
    mine = lax.axis_index("ch")
    own_part = pl.ds(pl.multiple_of(mine * part, part), part)
    fetches = [
        pltpu.make_async_copy(source.at[:, own_part] if i in (6, 7) else source, buffer, in_sem.at[i])
        for i, (source, buffer) in enumerate(zip(sources, buffers))
    ]
    large = [
        [
            pltpu.make_async_copy(source.at[m], target.at[m], big_sem.at[i, m])
            for i, (source, target) in enumerate(((x_part_ref, x_buf), (z_part_ref, z_buf), (out_part_ref, out_buf)))
        ]
        for m in range(kinds)
    ]
    for copy in sum(large, []) + fetches:
        copy.start()
    copies = []
    for m in range(kinds):
        for copy in large[m]:
            copy.wait()
        first = len(copies)
        copies.append(pltpu.make_async_copy(out_buf.at[m], dw_out_ref.at[m], out_sem.at[m]))
        for b in range(chans // 128):
            for j, source in enumerate((x_buf, z_buf)):
                slot = (m * (chans // 128) + b) * 2 + j
                copies.append(
                    pltpu.make_async_copy(source.at[m, :, pl.ds(b * 128, 128)], dw_in_ref.at[m, :, b, j], sems.at[slot])
                )
        for copy in copies[first:]:
            copy.start()
    for copy in fetches:
        copy.wait()
    scale = scale_ref[...]
    bent = scale * scale * scale * mean_ref[...]
    for q in range(part // 128):
        lanes = slice(q * 128, (q + 1) * 128)
        x = x_ref[:, lanes].astype(jnp.float32)
        block_ref[:, lanes] = (x + mix_ref[:, lanes]).astype(jnp.bfloat16)
        weighted = slice_ref[:, lanes] * gain_ref[:, lanes]
        dx_ref[:, lanes] = cot_ref[:, lanes].astype(jnp.float32) + scale * weighted - x * bent
    gain_out_ref[...] = dgain_ref[0:1]
    x_proj_ref[...] = small_ref[0:160].astype(jnp.float32)
    dt_proj_ref[...] = small_ref[160:288].astype(jnp.float32)
    a_log_ref[...] = small_ref[288:304].astype(jnp.float32)
    rest = small_ref[304:320].astype(jnp.float32)
    taps_ref[...] = rest[0:4]
    cbias_ref[...] = rest[4:5]
    dt_bias_ref[...] = rest[5:6]
    skip_ref[...] = rest[6:7]
    for copy in copies:
        copy.wait()


def finish(x_part, z_part, out_part, small, total, mix, mean, scale, cot, x_in, gain, dgain):
    kinds, slab, chans = x_part.shape
    rows, part = total.shape
    vmem = pl.BlockSpec(memory_space=pltpu.VMEM)
    hbm = pl.BlockSpec(memory_space=pl.ANY)
    f32 = jnp.float32
    shape = jax.ShapeDtypeStruct
    outs = pl.pallas_call(
        finish_kernel,
        in_specs=[hbm] * 12,
        out_specs=[hbm] * 2 + [vmem] * 10,
        out_shape=[
            shape((kinds, slab, chans // 128, 2, 128), f32), shape((kinds, slab, chans), f32),
            shape((rows, part), jnp.bfloat16), shape((rows, part), f32), shape((1, part), f32), shape((4, chans), f32),
            shape((1, chans), f32), shape((160, chans), f32), shape((128, chans), f32), shape((1, chans), f32),
            shape((16, chans), f32), shape((1, chans), f32),
        ],
        scratch_shapes=[
            pltpu.VMEM(small.shape, small.dtype), pltpu.VMEM((rows, part), f32), pltpu.VMEM((rows, part), f32),
            pltpu.VMEM((rows, 128), f32), pltpu.VMEM((rows, 128), f32), pltpu.VMEM((rows, part), cot.dtype),
            pltpu.VMEM((rows, part), x_in.dtype), pltpu.VMEM((1, part), f32), pltpu.VMEM(dgain.shape, f32),
            pltpu.VMEM(x_part.shape, f32), pltpu.VMEM(x_part.shape, f32), pltpu.VMEM(x_part.shape, f32),
            pltpu.SemaphoreType.DMA((kinds * chans // 64,)), pltpu.SemaphoreType.DMA((kinds,)), pltpu.SemaphoreType.DMA((9,)),
            pltpu.SemaphoreType.DMA((3, kinds)),
        ],
        compiler_params=pltpu.CompilerParams(vmem_limit_bytes=60 << 20),
        name="finish",
    )(x_part, z_part, out_part, small, total, mix, mean, scale, cot, x_in, gain, dgain)
    dw_in = outs[0].transpose(0, 1, 3, 2, 4).reshape(kinds, slab, 2, chans)
    return (outs[2], outs[3], outs[4][0], dw_in, outs[5], outs[6][0], outs[7].T, outs[8], outs[9][0], outs[10], outs[11][0], outs[1])


def shards(
    x_in,
    norm_gain,
    w_in,
    conv_weight,
    conv_bias,
    x_proj,
    dt_proj,
    dt_bias,
    a_log,
    d_skip,
    w_out,
    modes,
    doc_lengths,
    cotangent,
):
    seq_count = lax.axis_size("seq")
    tok_rows = x_in.shape[0]
    inner_local = conv_bias.shape[0]
    docs = doc_lengths.shape[0]
    order = jnp.arange(docs, dtype=jnp.int32)
    starts = jnp.sum(jnp.where(order[:, None] > order[None, :], doc_lengths[None, :], 0), axis=1)
    starts = jnp.broadcast_to(starts[:, None], (docs, 128))
    mode_rows = modes.reshape(2 * seq_count, tok_rows // 2)
    blocks = lane_blocks(w_in)
    gain = norm_gain[None]
    x_proj_t = x_proj.T
    z_branch, d_gated, columns, extended, conv_pre, conv_out, maps = front(
        x_in, gain, mode_rows, cotangent, starts, conv_weight, conv_bias[None], x_proj_t, blocks, w_out
    )
    d_w_out, d_w_z, d_w_x, mixer, smalls, d_slice, mean, d_gain, scale = core(
        blocks, w_out, columns, extended, conv_pre, conv_out, maps, z_branch, d_gated, starts, conv_weight, x_proj_t,
        dt_proj, dt_bias[None], a_log, d_skip[None], mode_rows, x_in, gain,
    )
    return finish(
        d_w_x, d_w_z.reshape(d_w_x.shape), d_w_out.reshape(d_w_x.shape), smalls.reshape(-1, inner_local), d_slice, mixer,
        mean, scale, cotangent, x_in, gain, d_gain,
    )


def solution(mesh):
    return jax.shard_map(
        shards,
        mesh=mesh,
        in_specs=(
            P("seq", None),
            P(),
            P(None, None, None, "ch"),
            P(None, "ch"),
            P("ch"),
            P("ch", None),
            P(None, "ch"),
            P("ch"),
            P(None, "ch"),
            P("ch"),
            P(None, None, "ch"),
            P(),
            P(),
            P("seq", "ch"),
        ),
        out_specs=(
            P("seq", "ch"),
            P("seq", "ch"),
            P("ch"),
            P(None, "seq", None, "ch"),
            P(None, "ch"),
            P("ch"),
            P("ch", None),
            P(None, "ch"),
            P("ch"),
            P(None, "ch"),
            P("ch"),
            P(None, "seq", "ch"),
        ),
        check_vma=False,
    )
```

```python
import functools
import math

import jax
import jax.numpy as jnp
from jax import lax
from jax.experimental import pallas as pl
from jax.experimental.pallas import tpu as pltpu
from jax.sharding import PartitionSpec as P

EPSILON = 1e-05


MESH = pl.DeviceIdType.MESH


def cycle_of(count):
    across = count // 4
    walk = [(0, x) for x in range(across)]
    for turn, x in enumerate(reversed(range(across))):
        column = [(z, x) for z in range(1, 4)]
        walk += column[::-1] if turn % 2 else column
    return [z * across + x for z, x in walk]


def table_of(index, values):
    picked = jnp.int32(values[0])
    for i in range(1, len(values)):
        picked = jnp.where(index == i, jnp.int32(values[i]), picked)
    return picked


def mode_columns(modes_ref, target_ref):
    half = target_ref.shape[0] // 2
    for way in (0, 1):
        row = modes_ref[pl.ds(2 * lax.axis_index("seq") + way, 1), :].astype(jnp.float32)
        target_ref[way * half : (way + 1) * half] = jnp.transpose(jnp.broadcast_to(row, (128, half)))


def row_scale(x):
    return lax.rsqrt(jnp.mean(x * x, axis=1, keepdims=True) + EPSILON)


def documents(starts_ref, tokens):
    def passed(at):
        total = jnp.zeros(at.shape, jnp.float32)
        for i in range(starts_ref.shape[0]):
            total = total + jnp.where(at >= starts_ref[i : i + 1], 1.0, 0.0)
        return jnp.where(at >= tokens, -1.0, total)

    return passed


def padded(x_proj_ref, target_ref):
    tall = x_proj_ref.shape[0]
    target_ref[0:tall] = x_proj_ref[...]
    target_ref[tall:] = jnp.zeros((target_ref.shape[0] - tall, target_ref.shape[1]), target_ref.dtype)


def front_kernel(
    sizes, x_in_ref, gain_ref, modes_ref, cot_ref, starts_ref, taps_ref, cbias_ref, x_proj_ref, w_in_ref, w_out_ref,
    z_ref, gated_ref, cols_ref, ext_ref, pre_ref, conv_ref, part_ref,
    cotg_ref, normed_ref, cols_sem, seq_send, seq_recv, twin_send, twin_recv, x_ref, halo_ref, padded_ref, sent_ref, got_ref, low_send, low_recv, mode_ref, x2_ref, halo_send, halo_recv, in_buf, out_buf, in_sem, out_sem, cot_send, cot_recv, own_sem,
):
    count, twins = sizes
    rows, width = x_in_ref.shape
    modes = w_out_ref.shape[0]
    part = cot_ref.shape[1]
    inner = x_ref.shape[1]
    me = lax.axis_index("seq")
    mine = lax.axis_index("ch")
    barrier = pltpu.get_barrier_semaphore()
    for k in range(1, count):
        pl.semaphore_signal(barrier, inc=1, device_id={"seq": lax.rem(me + k, count)}, device_id_type=MESH)
    for k in range(1, twins):
        peer = {"ch": lax.rem(mine + k, twins)}
        pl.semaphore_signal(barrier, inc=1, device_id=peer, device_id_type=MESH)

    pairs = inner // 256
    steps = pairs * modes

    def in_copy(step, b):
        slot = lax.rem(step, 2)
        return pltpu.make_async_copy(
            w_in_ref.at[lax.rem(step, modes), :, step // modes * 2 + b], in_buf.at[slot, b], in_sem.at[slot, b]
        )

    wide = out_buf.shape[2]
    out_steps = inner // wide * modes

    def out_copy(step):
        slot = lax.rem(step, 2)
        columns = pl.ds(pl.multiple_of(step // modes * wide, wide), wide)
        return pltpu.make_async_copy(
            w_out_ref.at[lax.rem(step, modes), :, columns], out_buf.at[slot], out_sem.at[slot]
        )

    for b in (0, 1):
        in_copy(0, b).start()
    out_copy(0).start()
    mode_columns(modes_ref, mode_ref)

    def norm_body(i, carry):
        rc = pl.ds(pl.multiple_of(i * 16, 16), 16)
        x = x_in_ref[rc, :].astype(jnp.float32)
        normed_ref[rc, :] = (x * row_scale(x) * gain_ref[...]).astype(jnp.bfloat16)
        return carry

    lax.fori_loop(0, rows // 16, norm_body, 0, unroll=4)
    pl.semaphore_wait(barrier, count - 1 + twins - 1)
    slab = cols_ref.shape[4]
    half = rows // 2
    ring = cycle_of(count)
    where = {s: i for i, s in enumerate(ring)}
    place = table_of(me, [where[s] for s in range(count)])
    side = lax.rem(mine, 2)
    twin = mine + 1 - 2 * side
    side_rows = pl.ds(pl.multiple_of(side * half, half), half)

    def column_source(kind, owner, those):
        return (normed_ref, cotg_ref)[kind].at[those, pl.ds(pl.multiple_of(owner * slab, slab), slab)]

    own_columns = [
        pltpu.make_async_copy(
            column_source(kind, me, pl.ds(way * half, half)), cols_ref.at[kind, way, 0], cols_sem.at[kind, way]
        )
        for kind in (0, 1)
        for way in (0, 1)
    ]
    seq_copies = []
    for kind in (0, 1):
        for k in range(1, count):
            peer = table_of(lax.rem(place + jnp.where(side == 0, k, count - k), count), ring)
            seq_copies.append(
                pltpu.make_async_remote_copy(
                    src_ref=column_source(kind, peer, side_rows), dst_ref=cols_ref.at[kind, side, k],
                    send_sem=seq_send.at[kind, k - 1], recv_sem=seq_recv.at[kind, k - 1], device_id={"seq": peer},
                    device_id_type=MESH,
                )
            )
    twin_copies = [
        pltpu.make_async_remote_copy(
            src_ref=cols_ref.at[kind, side, pl.ds(1, count - 1)], dst_ref=cols_ref.at[kind, side, pl.ds(1, count - 1)],
            send_sem=twin_send.at[kind], recv_sem=twin_recv.at[kind], device_id={"ch": twin}, device_id_type=MESH,
        )
        for kind in (0, 1)
    ]


    own_part = pl.ds(pl.multiple_of(mine * part, part), part)
    cot_copies = [
        pltpu.make_async_remote_copy(
            src_ref=cot_ref, dst_ref=cotg_ref.at[:, own_part], send_sem=cot_send.at[k - 1], recv_sem=cot_recv.at[k - 1],
            device_id={"ch": lax.rem(mine + k, twins)}, device_id_type=MESH,
        )
        for k in range(1, twins)
    ]
    for copy in cot_copies:
        copy.start()
    own_copy = pltpu.make_async_copy(cot_ref, cotg_ref.at[:, own_part], own_sem.at[0])
    own_copy.start()
    for copy in seq_copies[: count - 1] + own_columns[:2]:
        copy.start()

    def in_step(step, carry):
        slot = lax.rem(step, 2)
        mode = lax.rem(step, modes)

        @pl.when(step + 1 < steps)
        def _():
            for b in (0, 1):
                in_copy(step + 1, b).start()

        for b in (0, 1):
            in_copy(step, b).wait()
        weights = jnp.concatenate([in_buf.at[slot, b].reshape(2 * width, 128)[...] for b in (0, 1)], axis=1)
        mask = jnp.concatenate([mode_ref[...]] * 2, axis=1) == mode.astype(jnp.float32)
        columns = pl.ds(pl.multiple_of(step // modes * 256, 256), 256)
        both = jnp.dot(x2_ref[...], weights, preferred_element_type=jnp.float32)
        for j, target in enumerate((x_ref, z_ref)):
            found = jnp.where(mask, both[j * rows : (j + 1) * rows], target[:, columns].astype(jnp.float32))
            target[:, columns] = found.astype(jnp.bfloat16)
        return carry

    x_ref[...] = jnp.zeros_like(x_ref)
    z_ref[...] = jnp.zeros_like(z_ref)
    row = lax.broadcasted_iota(jnp.int32, (256, 512), 0)
    column = lax.broadcasted_iota(jnp.int32, (256, 512), 1)
    for j in (0, 1):
        spread = (column == 2 * row + j).astype(jnp.bfloat16)
        for block in range(width // 256):
            x2_ref[j * rows : (j + 1) * rows, block * 512 : (block + 1) * 512] = jnp.dot(
                normed_ref[:, block * 256 : (block + 1) * 256], spread, preferred_element_type=jnp.float32
            ).astype(jnp.bfloat16)
    lax.fori_loop(0, steps // 2, in_step, 0)
    own_copy.wait()
    for copy in cot_copies:
        copy.wait_recv()
    for copy in seq_copies[count - 1 :] + own_columns[2:]:
        copy.start()
    lax.fori_loop(steps // 2, steps, in_step, 0)
    halo_copy = pltpu.make_async_remote_copy(
        src_ref=x_ref.at[pl.ds(rows - 16, 16)], dst_ref=halo_ref, send_sem=halo_send.at[0], recv_sem=halo_recv.at[0],
        device_id={"seq": lax.rem(me + 1, count)}, device_id_type=MESH,
    )
    halo_copy.start()
    for copy in seq_copies[: count - 1]:
        copy.wait_recv()
    twin_copies[0].start()

    def out_step(step, carry):
        slot = lax.rem(step, 2)
        mode = lax.rem(step, modes)

        @pl.when(step + 1 < out_steps)
        def _():
            out_copy(step + 1).start()

        out_copy(step).wait()
        mask = jnp.concatenate([mode_ref[...]] * (wide // 128), axis=1) == mode.astype(jnp.float32)
        columns = pl.ds(pl.multiple_of(step // modes * wide, wide), wide)
        found = jnp.dot(cotg_ref[...], out_buf[slot], preferred_element_type=jnp.float32)
        gated_ref[:, columns] = jnp.where(mask, found, gated_ref[:, columns])
        return carry

    gated_ref[...] = jnp.zeros_like(gated_ref)
    lax.fori_loop(0, out_steps // 2, out_step, 0)

    chunks, _, inner = pre_ref.shape
    padded(x_proj_ref, padded_ref)
    passed = documents(starts_ref, count * rows)
    spot = lax.broadcasted_iota(jnp.int32, (rows, 128), 0) + me * rows
    here = passed(spot)
    same = [jnp.where(passed(spot - lag) == here, 1.0, 0.0) for lag in (3, 2, 1, 0)]
    halo_copy.wait_recv()
    ext_ref[0:8] = halo_ref[8:16].astype(jnp.float32)
    ext_ref[8:] = x_ref[...].astype(jnp.float32)

    def conv_body(block, carry):
        cut = pl.ds(pl.multiple_of(block * 128, 128), 128)
        pre = jnp.zeros((rows, 128), jnp.float32) + cbias_ref[:, cut]
        for k in range(4):
            pre = pre + taps_ref[k : k + 1, cut] * ext_ref[5 + k : 5 + k + rows, cut] * same[k]
        pre_ref[:, :, cut] = pre.reshape(chunks, 16, 128)
        conv_ref[:, :, cut] = (pre / (1.0 + jnp.exp(-pre))).astype(jnp.bfloat16).reshape(chunks, 16, 128)
        return carry

    lax.fori_loop(0, inner // 128, conv_body, 0, unroll=2)
    part_ref[...] = lax.dot_general(
        conv_ref[...].reshape(rows, inner), padded_ref[...], (((1,), (1,)), ((), ())), preferred_element_type=jnp.float32
    )
    sent_ref[...] = part_ref[...].astype(jnp.bfloat16)
    low_copies = [
        pltpu.make_async_remote_copy(
            src_ref=sent_ref, dst_ref=got_ref.at[k - 1], send_sem=low_send.at[k - 1], recv_sem=low_recv.at[k - 1],
            device_id={"ch": lax.rem(mine + k, twins)}, device_id_type=MESH,
        )
        for k in range(1, twins)
    ]
    for copy in low_copies:
        copy.start()
    for copy in seq_copies[count - 1 :]:
        copy.wait_recv()
    twin_copies[1].start()
    lax.fori_loop(out_steps // 2, out_steps, out_step, 0)
    for k, copy in enumerate(low_copies):
        copy.wait_recv()
        part_ref[...] += got_ref[k].astype(jnp.float32)
    for copy in own_columns:
        copy.wait()
    for copy in twin_copies:
        copy.wait_recv()
    for copy in cot_copies + low_copies + seq_copies + twin_copies + [halo_copy]:
        copy.wait_send()


def front(x_in, gain, modes, cot, starts, taps, cbias, x_proj_t, w_in, w_out):
    count, twins = lax.axis_size("seq"), lax.axis_size("ch")
    rows, width = x_in.shape
    inner = w_out.shape[2]
    f32, b16 = jnp.float32, jnp.bfloat16
    shape = jax.ShapeDtypeStruct
    vmem = pl.BlockSpec(memory_space=pltpu.VMEM)
    hbm = pl.BlockSpec(memory_space=pl.ANY)
    wide = min(512, inner)
    return pl.pallas_call(
        functools.partial(front_kernel, (count, twins)),
        in_specs=[vmem] * 8 + [hbm] * 2,
        out_specs=[vmem] * 7,
        out_shape=[
            shape((rows, inner), b16), shape((rows, inner), f32), shape((2, 2, count, rows // 2, width // count), b16),
            shape((rows + 8, inner), f32), shape((rows // 16, 16, inner), f32), shape((rows // 16, 16, inner), b16),
            shape((rows, 256), f32),
        ],
        scratch_shapes=[
            pltpu.VMEM((rows, width), b16), pltpu.VMEM((rows, width), b16), pltpu.SemaphoreType.DMA((2, 2)),
            pltpu.SemaphoreType.DMA((2, count - 1)), pltpu.SemaphoreType.DMA((2, count - 1)),
            pltpu.SemaphoreType.DMA((2,)), pltpu.SemaphoreType.DMA((2,)),
            pltpu.VMEM((rows, inner), b16), pltpu.VMEM((16, inner), b16), pltpu.VMEM((256, inner), b16),
            pltpu.VMEM((rows, 256), b16), pltpu.VMEM((twins - 1, rows, 256), b16),
            pltpu.SemaphoreType.DMA((twins - 1,)), pltpu.SemaphoreType.DMA((twins - 1,)),
            pltpu.VMEM((rows, 128), jnp.float32),
            pltpu.VMEM((2 * rows, 2 * width), jnp.bfloat16),
            pltpu.SemaphoreType.DMA((1,)),
            pltpu.SemaphoreType.DMA((1,)),
            pltpu.VMEM((2, 2, width, 2, 128), jnp.bfloat16),
            pltpu.VMEM((2, width, wide), jnp.bfloat16),
            pltpu.SemaphoreType.DMA((2, 2)),
            pltpu.SemaphoreType.DMA((2,)),
            pltpu.SemaphoreType.DMA((twins - 1,)),
            pltpu.SemaphoreType.DMA((twins - 1,)),
            pltpu.SemaphoreType.DMA((1,)),
        ],
        compiler_params=pltpu.CompilerParams(collective_id=1, has_side_effects=True, vmem_limit_bytes=56 << 20),
        name="front",
    )(x_in, gain, modes, cot, starts, taps, cbias, x_proj_t, w_in, w_out)


def tile_lanes(v, lanes):
    return jnp.concatenate([v] * (lanes // 128), axis=1)

def ring_places(count):
    ring = cycle_of(count)
    where = {s: i for i, s in enumerate(ring)}
    me = lax.axis_index("seq")
    onward = table_of(me, [ring[(where[s] + 1) % count] for s in range(count)])
    backward = table_of(me, [ring[(where[s] - 1) % count] for s in range(count)])
    place = table_of(me, [where[s] for s in range(count)])
    return ring, place, onward, backward


def add_products(accs, kind, k, cols_ref, blocks, modes_ref, ring, place, count):
    parts = []
    for way in (0, 1):
        step = k if way else count - k
        source = table_of(lax.rem(place + step, count), ring)
        parts.append((jnp.transpose(cols_ref[kind, way, k]), modes_ref[pl.ds(2 * source + way, 1), :]))
    right = jnp.concatenate(blocks, axis=0)
    for m, acc in enumerate(accs):
        left = jnp.concatenate(
            [part * jnp.where(row == m, 1.0, 0.0).astype(jnp.bfloat16) for part, row in parts], axis=1
        )
        found = jnp.dot(left, right, preferred_element_type=jnp.float32)
        acc[...] += found.reshape(acc.shape)


def core_kernel(
    sizes, w_in_ref, w_out_ref, cols_hbm, ext_hbm, pre_hbm, x_in_hbm, conv_ref, part_ref, z_ref, dgated_ref, starts_ref,
    taps_ref, x_t_ref, dt_proj_ref, dt_bias_ref, a_log_ref, skip_ref, modes_ref, gain_ref,
    dwo_ref, dwz_ref, dwx_ref, mix_ref, small_ref, slice_ref, dots_ref, dgain_ref, scale_ref,
    cols_ref, ext_ref, pre_ref, x_in_ref, late_sem, x_proj_ref, same_ref, mode_ref, free_sem, g_ref, step_ref, dtd_ref, u_ref, sig_ref, low_t_ref, b_ref, c_ref, rate_ref, ends_ref,
    ends_sent, ends_got, steps_sent, steps_got, gap_ref, h0_ref, gz_ref,
    racc_ref, rows_ref, sum_ref, half_ref, half_got, four_ref, four_b16, four_got, in_buf, out_buf, mix_sent, mix_got,
    norm_sent, norm_got, dots_sent, dots_got, gain_sent, gain_got,
    ring_ref, hist_ref, lam_ref, w_ref, pend_ref, gstep_ref, gscan_ref, grad_ref, sent_ref, got_ref,
    gpre_ref, edge_ref,
    in_sem, out_sem, mix_send, mix_recv, half_send, half_recv, four_send, four_recv, last_send, last_recv, all_send, all_recv,
    ends_send, ends_recv, steps_send, steps_recv, norm_send, norm_recv, dots_send, dots_recv,
    gain_send, gain_recv, dwo_sem,
    ring_send, ring_recv, gx_send, gx_recv, ch_send, ch_recv, edge_send, edge_recv,
):
    count, twins = sizes
    chunks, _, chans = pre_ref.shape
    rows = chunks * 16
    gx_ref = gz_ref.at[2]
    slab = cols_ref.shape[4]
    n = a_log_ref.shape[0]
    half = rows // 2
    ring, place, onward, backward = ring_places(count)
    me = lax.axis_index("seq")
    mine = lax.axis_index("ch")
    before = lax.rem(me + count - 1, count)
    nt = (((1,), (1,)), ((), ()))
    f32, b16 = jnp.float32, jnp.bfloat16
    lb = min(512, chans)

    modes, width = w_out_ref.shape[:2]
    part = width // twins
    eighths = chans // 128
    across = half_ref.shape[1]
    tall = half_ref.shape[0]
    depth = half_ref.shape[2]
    z_at = me // across
    x_at = lax.rem(me, across)

    def chunk_of(step):
        return pl.ds(pl.multiple_of(lax.rem(mine + 1 + step // modes, twins) * part, part), part)

    def in_copy(step, b):
        slot = step % 2
        return pltpu.make_async_copy(w_in_ref.at[step % modes, chunk_of(step), b], in_buf.at[slot, b], in_sem.at[slot, b])

    def in_copies(step, wait):
        for b in range(eighths):
            if wait:
                in_copy(step, b).wait()
            else:
                in_copy(step, b).start()

    def out_copy(step):
        slot = step % 2
        return pltpu.make_async_copy(w_out_ref.at[step % modes, chunk_of(step)], out_buf.at[slot], out_sem.at[slot])

    barrier = pltpu.get_barrier_semaphore()
    for k in range(1, count):
        pl.semaphore_signal(barrier, inc=1, device_id={"seq": lax.rem(me + k, count)}, device_id_type=MESH)
    for k in range(1, twins):
        peer = {"ch": lax.rem(mine + k, twins)}
        pl.semaphore_signal(barrier, inc=1, device_id=peer, device_id_type=MESH)
    in_copies(0, 0)
    out_copy(0).start()
    late_operands = ((cols_hbm, cols_ref), (ext_hbm, ext_ref), (pre_hbm, pre_ref), (x_in_hbm, x_in_ref))
    late_fetches = [
        pltpu.make_async_copy(source, target, late_sem.at[i]) for i, (source, target) in enumerate(late_operands)
    ]
    for copy in late_fetches:
        copy.start()
    pl.semaphore_wait(barrier, count - 1 + twins - 1)

    passed = documents(starts_ref, count * rows)

    def maps_copies(send, recv):
        return [
            pltpu.make_async_remote_copy(
                src_ref=sent_ref, dst_ref=got_ref.at[k - 1], send_sem=send.at[k - 1],
                recv_sem=recv.at[k - 1], device_id={"ch": lax.rem(mine + k, twins)}, device_id_type=MESH,
            )
            for k in range(1, twins)
        ]


    def gate_body(i, carry):
        z = z_ref[i].astype(f32)
        g_ref[i] = dgated_ref[i] * (z / (1.0 + jnp.exp(-z)))
        return carry

    lax.fori_loop(0, chunks, gate_body, 0, unroll=2)
    rate_ref[...] = -math.log2(math.e) * jnp.exp(a_log_ref[...])
    own = (
        lax.broadcasted_iota(jnp.int32, (16, 16 * n), 1) // n == lax.broadcasted_iota(jnp.int32, (16, 16 * n), 0)
    )
    ones = own.astype(b16)
    token_row = lax.broadcasted_iota(jnp.int32, (16 * n, 16), 0) // n
    repeat = (token_row == lax.broadcasted_iota(jnp.int32, (16 * n, 16), 1)).astype(b16)
    pick_row = lax.broadcasted_iota(jnp.int32, (16 * n, 128), 0)
    pick_col = lax.broadcasted_iota(jnp.int32, (16 * n, 128), 1)
    is_b = pick_row % n == pick_col
    is_c = pick_row % n + n == pick_col
    pick_b = is_b.astype(b16)
    pick_c = is_c.astype(b16)
    flat = jnp.ones((256, 128), b16)
    total = part_ref[...]
    low_t_ref[...] = jnp.transpose(total[:, 0:128]).astype(b16)
    raw = jnp.dot(total[:, 0:128].astype(b16), dt_proj_ref[...], preferred_element_type=f32)
    step_ref[...] = raw.reshape(chunks, 16, chans)

    def step_body(i, carry):
        raw = step_ref[i] + dt_bias_ref[...]
        step = jnp.maximum(raw, 0.0) + jnp.log1p(jnp.exp(-jnp.abs(raw)))
        step_ref[i] = step
        sig_ref[i] = 1.0 / (1.0 + jnp.exp(-raw))
        at = lax.broadcasted_iota(jnp.int32, (16, 128), 0) + (me * rows + i * 16)
        big = jnp.where(passed(at) == passed(at - 1), 0.0, 1e30)
        dtd_ref[i] = step + jnp.concatenate([big] * (chans // 128), axis=1)
        u_ref[i] = step * conv_ref[i].astype(f32)
        maps = part_ref[pl.ds(pl.multiple_of(i * 16, 16), 16), 128:256]
        high = maps.astype(b16)
        low = (maps - high.astype(f32)).astype(b16)
        high = jnp.dot(repeat, high, preferred_element_type=f32)
        low = jnp.dot(repeat, low, preferred_element_type=f32)
        for target, chosen in ((b_ref, is_b), (c_ref, is_c)):
            terms = [jnp.where(chosen, term, 0.0).astype(b16) for term in (high, low)]
            found = jnp.dot(jnp.concatenate(terms, axis=1), flat, preferred_element_type=f32)
            target[pl.ds(i * 16, 16)] = found.reshape(16, n, 128)
        return carry

    lax.fori_loop(0, chunks, step_body, 0, unroll=2)

    def maps_block(chunk, pick):
        maps = part_ref[pl.ds(pl.multiple_of(chunk * 16, 16), 16), 128:256].astype(b16)
        found = lax.dot_general(maps, pick, nt, preferred_element_type=f32)
        return jnp.where(own, found, 0.0).astype(b16)

    ends_ref[0:n] = jnp.zeros((n, chans), f32)
    ends_ref[n : 2 * n] = jnp.ones((n, chans), f32)
    ends_ref[2 * n : 3 * n] = jnp.zeros((n, chans), f32)

    def end_body(chunk, carry):
        for block in range(chans // lb):
            cut = slice(block * lb, (block + 1) * lb)
            rate = rate_ref[:, cut]
            h = ends_ref[0:n, cut]
            for t in range(16):
                decay = jnp.exp2(dtd_ref[chunk, t : t + 1, cut] * rate)
                h = decay * h + u_ref[chunk, t : t + 1, cut] * tile_lanes(b_ref[chunk * 16 + t], lb)
            ends_ref[0:n, cut] = h
        return carry

    def head_body(chunk, carry):
        for block in range(chans // lb):
            cut = slice(block * lb, (block + 1) * lb)
            rate = rate_ref[:, cut]
            reach = ends_ref[n : 2 * n, cut]
            head = ends_ref[2 * n : 3 * n, cut]
            for t in range(16):
                reach = reach * jnp.exp2(dtd_ref[chunk, t : t + 1, cut] * rate)
                head = head + reach * (g_ref[chunk, t : t + 1, cut] * tile_lanes(c_ref[chunk * 16 + t], lb))
            ends_ref[n : 2 * n, cut] = reach
            ends_ref[2 * n : 3 * n, cut] = head
        return carry

    def state_copy(side, k):
        return pltpu.make_async_remote_copy(
            src_ref=ends_sent.at[side], dst_ref=ends_got.at[k - 1], send_sem=ends_send.at[k - 1],
            recv_sem=ends_recv.at[k - 1], device_id={"seq": lax.rem(me + k, count)}, device_id_type=MESH,
        )

    steps_copies = [
        pltpu.make_async_remote_copy(
            src_ref=steps_sent, dst_ref=steps_got.at[k - 1], send_sem=steps_send.at[k - 1],
            recv_sem=steps_recv.at[k - 1], device_id={"seq": lax.rem(me + k, count)}, device_id_type=MESH,
        )
        for k in range(1, count)
    ]
    steps_sent[...] = jnp.sum(jnp.sum(dtd_ref[...], axis=0), axis=0, keepdims=True)
    for copy in steps_copies:
        copy.start()
    lax.fori_loop(0, chunks, end_body, 0, unroll=2)
    ends_sent[0] = ends_ref[0:n].astype(b16)
    for k in range(1, count):

        @pl.when(me + k < count)
        def _():
            state_copy(0, k).start()

    lax.fori_loop(0, chunks, head_body, 0, unroll=2)
    ends_sent[1] = ends_ref[2 * n : 3 * n].astype(b16)
    for k in range(1, count):

        @pl.when(me + k >= count)
        def _():
            state_copy(1, k).start()

    for copy in steps_copies:
        copy.wait_recv()
    for k in range(1, count):

        @pl.when(me >= k)
        def _():
            state_copy(0, k).wait_recv()

    h0_ref[...] = jnp.zeros_like(h0_ref)
    gap_ref[...] = jnp.zeros_like(gap_ref)
    for k in range(1, count):

        @pl.when(me >= k)
        def _():
            h0_ref[...] += ends_got[k - 1].astype(f32) * jnp.exp2(rate_ref[...] * gap_ref[...])

        gap_ref[...] += steps_got[k - 1]

    racc_ref[...] = h0_ref[...]

    def forward_body(chunk, carry):
        for block in range(chans // lb):
            cut = slice(block * lb, (block + 1) * lb)
            rate = rate_ref[:, cut]
            h = racc_ref[:, cut]
            for t in range(16):
                decay = jnp.exp2(dtd_ref[chunk, t : t + 1, cut] * rate)
                h = decay * h + u_ref[chunk, t : t + 1, cut] * tile_lanes(b_ref[chunk * 16 + t], lb)
                hist_ref[chunk, t * n : (t + 1) * n, cut] = h.astype(b16)
            racc_ref[:, cut] = h
        ssm = jnp.dot(maps_block(chunk, pick_c), hist_ref[chunk], preferred_element_type=f32)
        ssm = ssm + skip_ref[...] * conv_ref[chunk].astype(f32)
        z = z_ref[chunk].astype(f32)
        sig = 1.0 / (1.0 + jnp.exp(-z))
        rc = pl.ds(pl.multiple_of(chunk * 16, 16), 16)
        gz_ref[0, rc] = (ssm * (z * sig)).astype(b16)
        gz_ref[1, rc] = (dgated_ref[chunk] * ssm * (sig * (1.0 + z * (1.0 - sig)))).astype(b16)
        return carry

    lax.fori_loop(0, chunks, forward_body, 0, unroll=2)

    def ring_copy(kind, way, k):
        if k == 0:
            source = gz_ref.at[kind, pl.ds(way * half, half)]
        else:
            source = ring_ref.at[kind, way, k - 1]
        return pltpu.make_async_remote_copy(
            src_ref=source, dst_ref=ring_ref.at[kind, way, k], send_sem=ring_send.at[kind, way, k],
            recv_sem=ring_recv.at[kind, way, k], device_id={"seq": backward if way else onward}, device_id_type=MESH,
        )

    def relay(kind, k):
        for way in (0, 1):
            if kind == 2:
                gx_copy(way, k - 1).wait_recv()
                if k < count - 1:
                    gx_copy(way, k).start()
            else:
                ring_copy(kind, way, k - 1).wait_recv()
                if k < count - 1:
                    ring_copy(kind, way, k).start()

    def gx_slot(way, k):
        slot = way * (count - 1) + k
        return hist_ref.at[slot // 2, pl.ds(slot % 2 * half, half)]

    def gx_copy(way, k):
        return pltpu.make_async_remote_copy(
            src_ref=gx_slot(way, k - 1) if k else gx_ref.at[pl.ds(way * half, half)], dst_ref=gx_slot(way, k),
            send_sem=gx_send.at[way, k], recv_sem=gx_recv.at[way, k], device_id={"seq": backward if way else onward},
            device_id_type=MESH,
        )

    for kind in (0, 1):
        for way in (0, 1):
            ring_copy(kind, way, 0).start()
    for copy in late_fetches:
        copy.wait()
    for k in range(1, count):

        @pl.when(me < k)
        def _():
            state_copy(1, k).wait_recv()

    pend_ref[...] = jnp.zeros_like(pend_ref)
    gap_ref[...] = jnp.zeros_like(gap_ref)
    for k in range(1, count):
        slot = count - 1 - k

        @pl.when(me + k < count)
        def _():
            pend_ref[...] += ends_got[slot].astype(f32) * jnp.exp2(rate_ref[...] * gap_ref[...])

        gap_ref[...] += steps_got[slot]

    turns = [(kind, k) for k in range(1, count) for kind in (0, 1)]
    early = turns[:2]
    late = turns[2:]

    racc_ref[...] = jnp.zeros_like(racc_ref)

    def span_body(i, carry):
        at = spans - 1 - i
        for sub in reversed(range(span // 16)):
            chunk = at * (span // 16) + sub
            for block in range(chans // lb):
                cut = slice(block * lb, (block + 1) * lb)
                rate = rate_ref[:, cut]
                pend = pend_ref[:, cut]
                racc = racc_ref[:, cut]
                for t in reversed(range(16)):
                    decay = jnp.exp2(dtd_ref[chunk, t : t + 1, cut] * rate)
                    lam = g_ref[chunk, t : t + 1, cut] * tile_lanes(c_ref[chunk * 16 + t], lb) + pend
                    pend = decay * lam
                    if t:
                        prior = hist_ref[chunk, (t - 1) * n : t * n, cut].astype(jnp.float32)
                    else:
                        prior = hist_ref[jnp.maximum(chunk - 1, 0), 15 * n : 16 * n, cut].astype(jnp.float32)
                        prior = jnp.where(chunk == 0, h0_ref[:, cut], prior)
                    w = pend * prior
                    racc = racc + w * step_ref[chunk, t : t + 1, cut]
                    lam_ref[t * n : (t + 1) * n, cut] = lam.astype(jnp.bfloat16)
                    w_ref[t * n : (t + 1) * n, cut] = (w * rate).astype(jnp.bfloat16)
                pend_ref[:, cut] = pend
                racc_ref[:, cut] = racc
            step = step_ref[chunk]
            conv = conv_ref[chunk].astype(jnp.float32)
            adj = jnp.dot(maps_block(chunk, pick_b), lam_ref[...], preferred_element_type=jnp.float32)
            wsum = jnp.dot(ones, w_ref[...], preferred_element_type=jnp.float32)
            gstep_ref[chunk] = wsum * math.log(2.0) + adj * conv
            gscan_ref[chunk] = adj * step
            gb = lax.dot_general(u_ref[chunk].astype(jnp.bfloat16), lam_ref[...], nt, preferred_element_type=jnp.float32)
            gc = lax.dot_general(
                g_ref[chunk].astype(jnp.bfloat16), hist_ref[chunk], nt, preferred_element_type=jnp.float32
            )
            gb = jnp.where(own, gb, 0.0).astype(jnp.bfloat16)
            gc = jnp.where(own, gc, 0.0).astype(jnp.bfloat16)
            grad_ref[pl.ds(pl.multiple_of(chunk * 16, 16), 16), 128:256] = jnp.dot(
                gb, pick_b, preferred_element_type=jnp.float32
            ) + jnp.dot(gc, pick_c, preferred_element_type=jnp.float32)
        return carry

    span = 32
    spans = rows // span
    mode_columns(modes_ref, mode_ref)
    padded(x_t_ref, x_proj_ref)
    passed = documents(starts_ref, count * rows)
    spot = lax.broadcasted_iota(jnp.int32, (rows, 128), 0) + me * rows
    here = passed(spot)
    for i in range(7):
        same_ref[i] = jnp.where(passed(spot + (i - 3)) == here, 1.0, 0.0).astype(b16)
    lax.fori_loop(0, spans // 2, span_body, 0)
    relay(*early[0])
    lax.fori_loop(spans // 2, spans, span_body, 0)
    for peer in (onward, backward):
        pl.semaphore_signal(free_sem, inc=1, device_id={"seq": peer}, device_id_type=MESH)
    relay(*early[1])

    rows_ref[...] = jnp.zeros_like(rows_ref)

    def raw_body(i, carry):
        full = gstep_ref[i] * sig_ref[i]
        rows_ref[5:6] += jnp.sum(full, axis=0, keepdims=True)
        rows_ref[6:7] += jnp.sum(g_ref[i] * conv_ref[i].astype(jnp.float32), axis=0, keepdims=True)
        gx_ref[pl.ds(pl.multiple_of(i * 16, 16), 16), :] = full.astype(jnp.bfloat16)
        return carry

    lax.fori_loop(0, chunks, raw_body, 0)
    grad_ref[:, 0:128] = lax.dot_general(gx_ref[...], dt_proj_ref[...], nt, preferred_element_type=jnp.float32)
    sent_ref[...] = grad_ref[...].astype(jnp.bfloat16)
    ch_copies = maps_copies(ch_send, ch_recv)
    for copy in ch_copies:
        copy.start()
    relay(*late[0])
    sum_ref[160:288] = jnp.dot(low_t_ref[...], gx_ref[...], preferred_element_type=jnp.float32)
    for copy in ch_copies:
        copy.wait_recv()
    total = grad_ref[...]
    for k in range(twins - 1):
        total = total + got_ref[k].astype(jnp.float32)
    grad_ref[...] = total
    relay(*late[1])

    skip = skip_ref[...]
    def pre_body(i, carry):
        rc = pl.ds(pl.multiple_of(i * 16, 16), 16)
        g_conv = jnp.dot(grad_ref[rc, :].astype(jnp.bfloat16), x_proj_ref[...], preferred_element_type=jnp.float32)
        g_conv = g_conv + skip * g_ref[i] + gscan_ref[i]
        pre = pre_ref[i]
        sig = 1.0 / (1.0 + jnp.exp(-pre))
        gpre = g_conv * sig * (1.0 + pre * (1.0 - sig))
        gpre_ref[rc, :] = gpre
        return carry

    pre_body(0, 0)
    edge_ref[...] = gpre_ref[0:8, :]
    edge_copy = pltpu.make_async_remote_copy(
        src_ref=edge_ref, dst_ref=gpre_ref.at[pl.ds(rows, 8)], send_sem=edge_send.at[0], recv_sem=edge_recv.at[0],
        device_id={"seq": before}, device_id_type=MESH,
    )
    edge_copy.start()
    lax.fori_loop(1, chunks, pre_body, 0)
    flipped = jnp.transpose(grad_ref[...]).astype(jnp.bfloat16)
    sum_ref[0:160] = jnp.dot(flipped[0:160], conv_ref[...].reshape(rows, chans), preferred_element_type=jnp.float32)
    relay(*late[2])
    edge_copy.wait_recv()

    def taps_body(block, carry):
        cut = pl.ds(pl.multiple_of(block * 128, 128), 128)
        gpre = gpre_ref[0:rows, cut]
        rows_ref[4:5, cut] = jnp.sum(gpre, axis=0, keepdims=True)
        total = jnp.zeros((rows, 128), jnp.float32)
        for k in range(4):
            lag = 3 - k
            total = total + gpre_ref[lag : lag + rows, cut] * taps_ref[k : k + 1, cut] * same_ref[3 + lag].astype(jnp.float32)
            rows_ref[k : k + 1, cut] = jnp.sum(
                gpre * ext_ref[5 + k : 5 + k + rows, cut] * same_ref[k].astype(jnp.float32), axis=0, keepdims=True
            )
        gx_ref[:, cut] = total.astype(jnp.bfloat16)
        return carry

    lax.fori_loop(0, chans // 128, taps_body, 0)
    pl.semaphore_wait(free_sem, 2)
    for way in (0, 1):
        gx_copy(way, 0).start()
    sum_ref[288:304] = racc_ref[...] * rate_ref[...] * math.log(2.0)
    sum_ref[304:312] = rows_ref[...]
    if tall * across * depth > 312:
        sum_ref[312:] = jnp.zeros((tall * across * depth - 312, chans), jnp.float32)
    for z in range(tall):
        for x in range(across):
            first = (z * across + x) * depth
            half_ref[z, x] = sum_ref[first : first + depth].astype(jnp.bfloat16)

    def to(device):
        return dict(device_id={"seq": device}, device_id_type=MESH)

    half_copies = [
        pltpu.make_async_remote_copy(
            src_ref=half_ref.at[:, lax.rem(x_at + k, across)], dst_ref=half_got.at[k - 1], send_sem=half_send.at[k - 1],
            recv_sem=half_recv.at[k - 1], **to(z_at * across + lax.rem(x_at + k, across)),
        )
        for k in range(1, across)
    ]
    four_copies = [
        pltpu.make_async_remote_copy(
            src_ref=four_b16.at[lax.rem(z_at + k, tall)], dst_ref=four_got.at[k - 1], send_sem=four_send.at[k - 1],
            recv_sem=four_recv.at[k - 1], **to(lax.rem(z_at + k, tall) * across + x_at),
        )
        for k in range(1, tall)
    ]
    last_copies = [
        pltpu.make_async_remote_copy(
            src_ref=small_ref.at[z_at, x_at], dst_ref=small_ref.at[z_at, x_at], send_sem=last_send.at[k - 1],
            recv_sem=last_recv.at[k - 1], **to(lax.rem(z_at + k, tall) * across + x_at),
        )
        for k in range(1, tall)
    ]
    all_copies = [
        pltpu.make_async_remote_copy(
            src_ref=small_ref.at[:, x_at], dst_ref=small_ref.at[:, x_at], send_sem=all_send.at[k - 1],
            recv_sem=all_recv.at[k - 1], **to(z_at * across + lax.rem(x_at + k, across)),
        )
        for k in range(1, across)
    ]

    def small_phase(phase):
        if phase == 0:
            for copy in half_copies:
                copy.start()
        elif phase == 1:
            for copy in half_copies:
                copy.wait_recv()
            for z in range(tall):
                first = pl.multiple_of((z * across + x_at) * depth, depth)
                total = sum_ref[pl.ds(first, depth)]
                for k in range(across - 1):
                    total = total + half_got[k, z].astype(jnp.float32)
                four_ref[z] = total
                four_b16[z] = total.astype(jnp.bfloat16)
            for copy in four_copies:
                copy.start()
        elif phase == 2:
            for copy in four_copies:
                copy.wait_recv()
            total = four_ref[z_at]
            for k in range(tall - 1):
                total = total + four_got[k].astype(jnp.float32)
            small_ref[z_at, x_at] = total.astype(jnp.bfloat16)
            for copy in last_copies:
                copy.start()
        elif phase == 3:
            for copy in last_copies:
                copy.wait_recv()
            for copy in all_copies:
                copy.start()
        else:
            for copy in all_copies:
                copy.wait_recv()
            for copy in half_copies + four_copies + last_copies + all_copies:
                copy.wait_send()

    small_phase(0)
    dwo_accs = [ref.at[0 : slab // 16] for ref in (dtd_ref, u_ref, sig_ref)]
    dwz_accs = [ref.at[0 : slab // 16] for ref in (step_ref, g_ref, gscan_ref)]
    dwx_accs = [dwx_ref.at[m] for m in range(modes)]
    for acc in dwo_accs + dwz_accs + dwx_accs:
        acc[...] = jnp.zeros_like(acc)

    def products(kind, k):
        if k == 0:
            source = gx_ref if kind == 2 else gz_ref.at[kind]
            blocks = [source[way * half : (way + 1) * half] for way in (0, 1)]
        else:
            blocks = [gx_slot(way, k - 1)[...] if kind == 2 else ring_ref[kind, way, k - 1] for way in (0, 1)]
        accs = (dwo_accs, dwz_accs, dwx_accs)[kind]
        add_products(accs, 0 if kind else 1, k, cols_ref, blocks, modes_ref, ring, place, count)
        if kind < 2 and k == count - 1:
            for copy in out_copies[kind]:
                copy.start()

    out_copies = [
        [pltpu.make_async_copy(acc, target.at[m], dwo_sem.at[kind, m]) for m, acc in enumerate(accs)]
        for kind, (accs, target) in enumerate(((dwo_accs, dwo_ref), (dwz_accs, dwz_ref)))
    ]

    def mix_copy(j):
        return pltpu.make_async_remote_copy(
            src_ref=mix_sent.at[j], dst_ref=mix_got.at[j], send_sem=mix_send.at[j], recv_sem=mix_recv.at[j],
            device_id={"ch": lax.rem(mine + 1 + j, twins)}, device_id_type=MESH,
        )

    steps = twins * modes

    def norm_copy(j):
        return pltpu.make_async_remote_copy(
            src_ref=norm_sent.at[j], dst_ref=norm_got.at[j], send_sem=norm_send.at[j], recv_sem=norm_recv.at[j],
            device_id={"ch": lax.rem(mine + 1 + j, twins)}, device_id_type=MESH,
        )

    def normed_unit(j, m):
        step = j * modes + m
        if step + 1 < steps:
            in_copies(step + 1, 0)
        in_copies(step, 1)
        spread_products(in_buf.at[step % 2], gz_ref, mode_ref, slice_ref, m, part)

    def normed_end(j):
        for q in range(part // 128):
            lanes = slice(q * 128, (q + 1) * 128)
            cut = pl.ds(pl.multiple_of(lax.rem(mine + 1 + j, twins) * part + q * 128, 128), 128)
            dots_ref[...] += slice_ref[:, lanes] * x_in_ref[:, cut].astype(f32) * gain_ref[:, cut]
        if j < twins - 1:
            norm_sent[j] = slice_ref[...].astype(b16)
            norm_copy(j).start()

    def mix_unit(j):
        for m in range(modes):
            step = j * modes + m
            if step + 1 < steps:
                out_copy(step + 1).start()
            out_copy(step).wait()
            mask = jnp.concatenate([mode_ref[...]] * (part // 128), axis=1) == float(m)
            found = lax.dot_general(gz_ref[0], out_buf[step % 2], nt, preferred_element_type=jnp.float32)
            mix_ref[...] = jnp.where(mask, found, mix_ref[...]) if m else found
        if j < twins - 1:
            mix_sent[j] = mix_ref[...].astype(jnp.bfloat16)
            mix_copy(j).start()

    dots_copies = [
        pltpu.make_async_remote_copy(
            src_ref=dots_sent, dst_ref=dots_got.at[k - 1], send_sem=dots_send.at[k - 1], recv_sem=dots_recv.at[k - 1],
            device_id={"ch": lax.rem(mine + k, twins)}, device_id_type=MESH,
        )
        for k in range(1, twins)
    ]
    gain_copies = [
        pltpu.make_async_remote_copy(
            src_ref=gain_sent, dst_ref=gain_got.at[k - 1], send_sem=gain_send.at[k - 1], recv_sem=gain_recv.at[k - 1],
            device_id={"seq": lax.rem(me + k, count)}, device_id_type=MESH,
        )
        for k in range(1, count)
    ]

    def scale_body(i, carry):
        rc = pl.ds(pl.multiple_of(i * 16, 16), 16)
        scale_ref[rc] = jnp.broadcast_to(row_scale(x_in_ref[rc].astype(f32)), (16, 128))
        return carry

    def dots_unit():
        lax.fori_loop(0, chunks, scale_body, 0)
        dots_sent[...] = dots_ref[...].astype(b16)
        for copy in dots_copies:
            copy.start()

    def slice_unit():
        for j in range(twins - 1):
            norm_copy(j).wait_recv()
            slice_ref[...] += norm_got[j].astype(f32)
        for q in range(part // 128):
            lanes = slice(q * 128, (q + 1) * 128)
            cut = pl.ds(pl.multiple_of(mine * part + q * 128, 128), 128)
            terms = slice_ref[:, lanes] * x_in_ref[:, cut].astype(f32) * scale_ref[...]
            gain_sent[:, lanes] = jnp.broadcast_to(jnp.sum(terms, axis=0, keepdims=True), (8, 128))
        for copy in gain_copies:
            copy.start()

    def gain_unit():
        total = gain_sent[...]
        for k, copy in enumerate(gain_copies):
            copy.wait_recv()
            total = total + gain_got[k]
        dgain_ref[...] = total
        for k, copy in enumerate(dots_copies):
            copy.wait_recv()
            dots_ref[...] += dots_got[k].astype(f32)
        mean = jnp.sum(dots_ref[...], axis=1, keepdims=True) / width
        dots_ref[...] = jnp.broadcast_to(mean, (rows, 128))
        for j in range(twins - 1):
            mix_copy(j).wait_recv()
            mix_ref[...] += mix_got[j].astype(f32)

    edge_copy.wait_send()
    dots_ref[...] = jnp.zeros_like(dots_ref)
    work = []
    for j in range(twins):
        for m in range(modes):
            work.append(functools.partial(normed_unit, j, m))
        work.append(functools.partial(normed_end, j))
        if j < 4:
            work.append(functools.partial(small_phase, j + 1))
    work.append(dots_unit)
    for j in range(twins):
        work.append(functools.partial(mix_unit, j))
    work += [slice_unit, gain_unit]
    ready = [(0, 0), (1, 0), (2, 0)] + early + late[:3]
    rest, last = late[3:], [(2, k) for k in range(1, count)]
    turns = []
    while rest or last:
        turns += rest[:2] + last[:1]
        rest, last = rest[2:], last[1:]
    for i, turn in enumerate(turns):
        left = len(turns) - i
        for _ in range(min(len(work), max(1, -(-len(work) // left)))):
            work.pop(0)()
        relay(*turn)
        ready.append(turn)
        for _ in range(2 if len(ready) > left else 1):
            if len(ready) > 1:
                products(*ready.pop(0))
    for unit in work:
        unit()
    for turn in ready:
        products(*turn)
    for copy in out_copies[0] + out_copies[1]:
        copy.wait()
    for j in range(twins - 1):
        mix_copy(j).wait_send()
        norm_copy(j).wait_send()
    for copy in dots_copies + gain_copies:
        copy.wait_send()
    for way in (0, 1):
        for k in range(count - 1):
            gx_copy(way, k).wait_send()

    for kind in (0, 1):
        for way in (0, 1):
            for k in range(count - 1):
                ring_copy(kind, way, k).wait_send()
    for copy in ch_copies + steps_copies:
        copy.wait_send()
    for k in range(1, count):
        state_copy(0, k).wait_send()


def spread_products(buf, trio_ref, mode_ref, target, m, part):
    nt = (((1,), (1,)), ((), ()))
    chosen = mode_ref[...] == float(m)
    row = lax.broadcasted_iota(jnp.int32, (256, 128), 0)
    column = lax.broadcasted_iota(jnp.int32, (256, 128), 1)
    picks = [(row == 2 * column + j).astype(jnp.bfloat16) for j in (1, 0)]
    rows = trio_ref.shape[1]
    stacked = trio_ref[1:3].reshape(2 * rows, trio_ref.shape[2])
    for q in range(2 * part // 256):
        weights = jnp.concatenate(
            [buf.at[b].reshape(2 * part, 128)[q * 256 : (q + 1) * 256] for b in range(buf.shape[0])], axis=1
        )
        found = lax.dot_general(stacked, weights, nt, preferred_element_type=jnp.float32).astype(jnp.bfloat16)
        total = jnp.dot(found[:rows], picks[0], preferred_element_type=jnp.float32)
        total = total + jnp.dot(found[rows:], picks[1], preferred_element_type=jnp.float32)
        cut = pl.ds(q * 128, 128)
        target[:, cut] = jnp.where(chosen, total, target[:, cut]) if m else total


def core(
    w_in, w_out, cols, ext, pre, conv, maps, z, dgated, starts, taps, x_proj_t, dt_proj, dt_bias, a_log, skip, modes,
    x_in, gain,
):
    count, twins = lax.axis_size("seq"), lax.axis_size("ch")
    rows, chans = z.shape
    n = a_log.shape[0]
    chunks = rows // 16
    width = w_out.shape[1]
    slab = width // count
    part = width // twins
    tall, across = 4, count // 4
    depth = -(-320 // (8 * count)) * 8
    vmem = pl.BlockSpec(memory_space=pltpu.VMEM)
    hbm = pl.BlockSpec(memory_space=pl.ANY)
    cube = lambda a: a.reshape((chunks, a.shape[0] // chunks) + a.shape[1:])
    f32, b16 = jnp.float32, jnp.bfloat16
    shape = jax.ShapeDtypeStruct
    dma = pltpu.SemaphoreType.DMA
    keep = pltpu.VMEM
    operands = [w_in, w_out, cols, ext, pre, x_in, conv, maps, cube(z), cube(dgated), starts, taps, x_proj_t, dt_proj, dt_bias,
                a_log, skip, modes, gain]
    block = (chunks, 16, chans)
    pair = lambda size: [dma((size,)), dma((size,))]
    return pl.pallas_call(
        functools.partial(core_kernel, (count, twins)),
        in_specs=[hbm] * 6 + [vmem] * (len(operands) - 6),
        out_specs=[hbm] * 2 + [vmem] * 7,
        out_shape=[
            shape((3, slab // 16, 16, chans), f32), shape((3, slab // 16, 16, chans), f32), shape((3, slab, chans), f32),
            shape((rows, part), f32), shape((tall, across, depth, chans), b16), shape((rows, part), f32),
            shape((rows, 128), f32), shape((8, part), f32), shape((rows, 128), f32),
        ],
        scratch_shapes=[
            keep(cols.shape, b16), keep(ext.shape, f32), keep(pre.shape, f32), keep(x_in.shape, b16), dma((4,)),
            keep((256, chans), b16), keep((7, rows, 128), b16), keep((rows, 128), f32), pltpu.SemaphoreType.REGULAR, keep(block, f32), keep(block, f32),
            keep(block, f32), keep(block, f32), keep(block, f32), keep((128, rows), b16), keep((rows, n, 128), f32),
            keep((rows, n, 128), f32), keep((n, chans), f32), keep((3 * n, chans), f32),
            keep((2, n, chans), b16), keep((count - 1, n, chans), b16), keep((1, chans), f32),
            keep((count - 1, 1, chans), f32), keep((1, chans), f32), keep((n, chans), f32), keep((3, rows, chans), b16),
            keep((n, chans), f32), keep((8, chans), f32), keep((tall * across * depth, chans), f32),
            keep((tall, across, depth, chans), b16), keep((across - 1, tall, depth, chans), b16),
            keep((tall, depth, chans), f32), keep((tall, depth, chans), b16), keep((tall - 1, depth, chans), b16),
            keep((2, chans // 128, part, 2, 128), b16), keep((2, part, chans), b16), keep((twins - 1, rows, part), b16),
            keep((twins - 1, rows, part), b16),
            keep((twins - 1, rows, part), b16), keep((twins - 1, rows, part), b16), keep((rows, 128), b16),
            keep((twins - 1, rows, 128), b16), keep((8, part), f32), keep((count - 1, 8, part), f32),
            keep((2, 2, count - 1, rows // 2, chans), b16),
            keep((chunks, 16 * n, chans), b16), keep((16 * n, chans), b16),
            keep((16 * n, chans), b16), keep((n, chans), f32), keep(block, f32), keep(block, f32), keep((rows, 256), f32), keep((rows, 256), b16), keep((twins - 1, rows, 256), b16),
            keep((rows + 8, chans), f32), keep((8, chans), f32),
            dma((2, chans // 128)), dma((2,)), *pair(twins - 1), *pair(across - 1), *pair(tall - 1), *pair(tall - 1),
            *pair(across - 1), *pair(count - 1), *pair(count - 1), *pair(twins - 1), *pair(twins - 1),
            *pair(count - 1), dma((2, 3)),
            dma((2, 2, count - 1)), dma((2, 2, count - 1)), dma((2, count - 1)), dma((2, count - 1)), *pair(twins - 1), dma((1,)), dma((1,)),
        ],
        compiler_params=pltpu.CompilerParams(collective_id=2, has_side_effects=True, vmem_limit_bytes=63 << 20),
        name="core",
    )(*operands)


def lane_blocks(w_in):
    kinds, width, _, chans = w_in.shape
    return w_in.reshape(kinds, width, 2, chans // 128, 128).transpose(0, 1, 3, 2, 4)


def finish_kernel(
    x_part_ref, z_part_ref, out_part_ref, *refs,
):
    sources, refs = refs[:9], refs[9:]
    (
        dw_in_ref, dw_out_ref, block_ref, dx_ref, gain_out_ref, taps_ref, cbias_ref, x_proj_ref, dt_proj_ref, dt_bias_ref,
        a_log_ref, skip_ref,
    ) = refs[:12]
    buffers, (x_buf, z_buf, out_buf, sems, out_sem, in_sem, big_sem) = refs[12:21], refs[21:]
    small_ref, slice_ref, mix_ref, mean_ref, scale_ref, cot_ref, x_ref, gain_ref, dgain_ref = buffers
    kinds, _, chans = x_part_ref.shape
    part = slice_ref.shape[1]
    mine = lax.axis_index("ch")
    own_part = pl.ds(pl.multiple_of(mine * part, part), part)
    fetches = [
        pltpu.make_async_copy(source.at[:, own_part] if i in (6, 7) else source, buffer, in_sem.at[i])
        for i, (source, buffer) in enumerate(zip(sources, buffers))
    ]
    large = [
        [
            pltpu.make_async_copy(source.at[m], target.at[m], big_sem.at[i, m])
            for i, (source, target) in enumerate(((x_part_ref, x_buf), (z_part_ref, z_buf), (out_part_ref, out_buf)))
        ]
        for m in range(kinds)
    ]
    for copy in fetches + sum(large, []):
        copy.start()
    for copy in fetches:
        copy.wait()
    scale = scale_ref[...]
    bent = scale * scale * scale * mean_ref[...]
    for q in range(part // 128):
        lanes = slice(q * 128, (q + 1) * 128)
        x = x_ref[:, lanes].astype(jnp.float32)
        block_ref[:, lanes] = (x + mix_ref[:, lanes]).astype(jnp.bfloat16)
        weighted = slice_ref[:, lanes] * gain_ref[:, lanes]
        dx_ref[:, lanes] = cot_ref[:, lanes].astype(jnp.float32) + scale * weighted - x * bent
    gain_out_ref[...] = dgain_ref[0:1]
    x_proj_ref[...] = small_ref[0:160].astype(jnp.float32)
    dt_proj_ref[...] = small_ref[160:288].astype(jnp.float32)
    a_log_ref[...] = small_ref[288:304].astype(jnp.float32)
    rest = small_ref[304:320].astype(jnp.float32)
    taps_ref[...] = rest[0:4]
    cbias_ref[...] = rest[4:5]
    dt_bias_ref[...] = rest[5:6]
    skip_ref[...] = rest[6:7]
    copies = []
    for m in range(kinds):
        for copy in large[m]:
            copy.wait()
        first = len(copies)
        copies.append(pltpu.make_async_copy(out_buf.at[m], dw_out_ref.at[m], out_sem.at[m]))
        for b in range(chans // 128):
            for j, source in enumerate((x_buf, z_buf)):
                slot = (m * (chans // 128) + b) * 2 + j
                copies.append(
                    pltpu.make_async_copy(source.at[m, :, pl.ds(b * 128, 128)], dw_in_ref.at[m, :, b, j], sems.at[slot])
                )
        for copy in copies[first:]:
            copy.start()
    for copy in copies:
        copy.wait()


def finish(x_part, z_part, out_part, small, total, mix, mean, scale, cot, x_in, gain, dgain):
    kinds, slab, chans = x_part.shape
    rows, part = total.shape
    vmem = pl.BlockSpec(memory_space=pltpu.VMEM)
    hbm = pl.BlockSpec(memory_space=pl.ANY)
    f32 = jnp.float32
    shape = jax.ShapeDtypeStruct
    outs = pl.pallas_call(
        finish_kernel,
        in_specs=[hbm] * 12,
        out_specs=[hbm] * 2 + [vmem] * 10,
        out_shape=[
            shape((kinds, slab, chans // 128, 2, 128), f32), shape((kinds, slab, chans), f32),
            shape((rows, part), jnp.bfloat16), shape((rows, part), f32), shape((1, part), f32), shape((4, chans), f32),
            shape((1, chans), f32), shape((160, chans), f32), shape((128, chans), f32), shape((1, chans), f32),
            shape((16, chans), f32), shape((1, chans), f32),
        ],
        scratch_shapes=[
            pltpu.VMEM(small.shape, small.dtype), pltpu.VMEM((rows, part), f32), pltpu.VMEM((rows, part), f32),
            pltpu.VMEM((rows, 128), f32), pltpu.VMEM((rows, 128), f32), pltpu.VMEM((rows, part), cot.dtype),
            pltpu.VMEM((rows, part), x_in.dtype), pltpu.VMEM((1, part), f32), pltpu.VMEM(dgain.shape, f32),
            pltpu.VMEM(x_part.shape, f32), pltpu.VMEM(x_part.shape, f32), pltpu.VMEM(x_part.shape, f32),
            pltpu.SemaphoreType.DMA((kinds * chans // 64,)), pltpu.SemaphoreType.DMA((kinds,)), pltpu.SemaphoreType.DMA((9,)),
            pltpu.SemaphoreType.DMA((3, kinds)),
        ],
        compiler_params=pltpu.CompilerParams(vmem_limit_bytes=60 << 20),
        name="finish",
    )(x_part, z_part, out_part, small, total, mix, mean, scale, cot, x_in, gain, dgain)
    dw_in = outs[0].transpose(0, 1, 3, 2, 4).reshape(kinds, slab, 2, chans)
    return (outs[2], outs[3], outs[4][0], dw_in, outs[5], outs[6][0], outs[7].T, outs[8], outs[9][0], outs[10], outs[11][0], outs[1])


def shards(
    x_in,
    norm_gain,
    w_in,
    conv_weight,
    conv_bias,
    x_proj,
    dt_proj,
    dt_bias,
    a_log,
    d_skip,
    w_out,
    modes,
    doc_lengths,
    cotangent,
):
    seq_count = lax.axis_size("seq")
    tok_rows = x_in.shape[0]
    inner_local = conv_bias.shape[0]
    docs = doc_lengths.shape[0]
    order = jnp.arange(docs, dtype=jnp.int32)
    starts = jnp.sum(jnp.where(order[:, None] > order[None, :], doc_lengths[None, :], 0), axis=1)
    starts = jnp.broadcast_to(starts[:, None], (docs, 128))
    mode_rows = modes.reshape(2 * seq_count, tok_rows // 2)
    blocks = lane_blocks(w_in)
    gain = norm_gain[None]
    x_proj_t = x_proj.T
    z_branch, d_gated, columns, extended, conv_pre, conv_out, maps = front(
        x_in, gain, mode_rows, cotangent, starts, conv_weight, conv_bias[None], x_proj_t, blocks, w_out
    )
    d_w_out, d_w_z, d_w_x, mixer, smalls, d_slice, mean, d_gain, scale = core(
        blocks, w_out, columns, extended, conv_pre, conv_out, maps, z_branch, d_gated, starts, conv_weight, x_proj_t,
        dt_proj, dt_bias[None], a_log, d_skip[None], mode_rows, x_in, gain,
    )
    return finish(
        d_w_x, d_w_z.reshape(d_w_x.shape), d_w_out.reshape(d_w_x.shape), smalls.reshape(-1, inner_local), d_slice, mixer,
        mean, scale, cotangent, x_in, gain, d_gain,
    )


def solution(mesh):
    return jax.shard_map(
        shards,
        mesh=mesh,
        in_specs=(
            P("seq", None),
            P(),
            P(None, None, None, "ch"),
            P(None, "ch"),
            P("ch"),
            P("ch", None),
            P(None, "ch"),
            P("ch"),
            P(None, "ch"),
            P("ch"),
            P(None, None, "ch"),
            P(),
            P(),
            P("seq", "ch"),
        ),
        out_specs=(
            P("seq", "ch"),
            P("seq", "ch"),
            P("ch"),
            P(None, "seq", None, "ch"),
            P(None, "ch"),
            P("ch"),
            P("ch", None),
            P(None, "ch"),
            P("ch"),
            P(None, "ch"),
            P("ch"),
            P(None, "seq", "ch"),
        ),
        check_vma=False,
    )
```

```python
import functools
import math

import jax
import jax.numpy as jnp
from jax import lax
from jax.experimental import pallas as pl
from jax.experimental.pallas import tpu as pltpu
from jax.sharding import PartitionSpec as P

EPSILON = 1e-05


MESH = pl.DeviceIdType.MESH


def cycle_of(count):
    across = count // 4
    walk = [(0, x) for x in range(across)]
    for turn, x in enumerate(reversed(range(across))):
        column = [(z, x) for z in range(1, 4)]
        walk += column[::-1] if turn % 2 else column
    return [z * across + x for z, x in walk]


def table_of(index, values):
    picked = jnp.int32(values[0])
    for i in range(1, len(values)):
        picked = jnp.where(index == i, jnp.int32(values[i]), picked)
    return picked


def mode_columns(modes_ref, target_ref):
    half = target_ref.shape[0] // 2
    for way in (0, 1):
        row = modes_ref[pl.ds(2 * lax.axis_index("seq") + way, 1), :].astype(jnp.float32)
        target_ref[way * half : (way + 1) * half] = jnp.transpose(jnp.broadcast_to(row, (128, half)))


def row_scale(x):
    return lax.rsqrt(jnp.mean(x * x, axis=1, keepdims=True) + EPSILON)


def documents(starts_ref, tokens):
    def passed(at):
        total = jnp.zeros(at.shape, jnp.float32)
        for i in range(starts_ref.shape[0]):
            total = total + jnp.where(at >= starts_ref[i : i + 1], 1.0, 0.0)
        return jnp.where(at >= tokens, -1.0, total)

    return passed


def padded(x_proj_ref, target_ref):
    tall = x_proj_ref.shape[0]
    target_ref[0:tall] = x_proj_ref[...]
    target_ref[tall:] = jnp.zeros((target_ref.shape[0] - tall, target_ref.shape[1]), target_ref.dtype)


def front_kernel(
    sizes, x_in_ref, gain_ref, modes_ref, cot_ref, starts_ref, taps_ref, cbias_ref, x_proj_ref, w_in_ref, w_out_ref,
    z_ref, gated_ref, cols_ref, ext_ref, pre_ref, conv_ref, part_ref,
    cotg_ref, normed_ref, cols_sem, seq_send, seq_recv, twin_send, twin_recv, x_ref, halo_ref, padded_ref, sent_ref, got_ref, low_send, low_recv, mode_ref, x2_ref, halo_send, halo_recv, in_buf, out_buf, in_sem, out_sem, cot_send, cot_recv, own_sem,
):
    count, twins = sizes
    rows, width = x_in_ref.shape
    modes = w_out_ref.shape[0]
    part = cot_ref.shape[1]
    inner = x_ref.shape[1]
    me = lax.axis_index("seq")
    mine = lax.axis_index("ch")
    barrier = pltpu.get_barrier_semaphore()
    for k in range(1, count):
        pl.semaphore_signal(barrier, inc=1, device_id={"seq": lax.rem(me + k, count)}, device_id_type=MESH)
    for k in range(1, twins):
        peer = {"ch": lax.rem(mine + k, twins)}
        pl.semaphore_signal(barrier, inc=1, device_id=peer, device_id_type=MESH)

    pairs = inner // 256
    steps = pairs * modes

    def in_copy(step, b):
        slot = lax.rem(step, 2)
        return pltpu.make_async_copy(
            w_in_ref.at[lax.rem(step, modes), :, step // modes * 2 + b], in_buf.at[slot, b], in_sem.at[slot, b]
        )

    wide = out_buf.shape[2]
    out_steps = inner // wide * modes

    def out_copy(step):
        slot = lax.rem(step, 2)
        columns = pl.ds(pl.multiple_of(step // modes * wide, wide), wide)
        return pltpu.make_async_copy(
            w_out_ref.at[lax.rem(step, modes), :, columns], out_buf.at[slot], out_sem.at[slot]
        )

    for b in (0, 1):
        in_copy(0, b).start()
    out_copy(0).start()
    mode_columns(modes_ref, mode_ref)

    def norm_body(i, carry):
        rc = pl.ds(pl.multiple_of(i * 16, 16), 16)
        x = x_in_ref[rc, :].astype(jnp.float32)
        normed_ref[rc, :] = (x * row_scale(x) * gain_ref[...]).astype(jnp.bfloat16)
        return carry

    lax.fori_loop(0, rows // 16, norm_body, 0, unroll=4)
    pl.semaphore_wait(barrier, count - 1 + twins - 1)
    slab = cols_ref.shape[4]
    half = rows // 2
    ring = cycle_of(count)
    where = {s: i for i, s in enumerate(ring)}
    place = table_of(me, [where[s] for s in range(count)])
    side = lax.rem(mine, 2)
    twin = mine + 1 - 2 * side
    side_rows = pl.ds(pl.multiple_of(side * half, half), half)

    def column_source(kind, owner, those):
        return (normed_ref, cotg_ref)[kind].at[those, pl.ds(pl.multiple_of(owner * slab, slab), slab)]

    own_columns = [
        pltpu.make_async_copy(
            column_source(kind, me, pl.ds(way * half, half)), cols_ref.at[kind, way, 0], cols_sem.at[kind, way]
        )
        for kind in (0, 1)
        for way in (0, 1)
    ]
    seq_copies = []
    for kind in (0, 1):
        for k in range(1, count):
            peer = table_of(lax.rem(place + jnp.where(side == 0, k, count - k), count), ring)
            seq_copies.append(
                pltpu.make_async_remote_copy(
                    src_ref=column_source(kind, peer, side_rows), dst_ref=cols_ref.at[kind, side, k],
                    send_sem=seq_send.at[kind, k - 1], recv_sem=seq_recv.at[kind, k - 1], device_id={"seq": peer},
                    device_id_type=MESH,
                )
            )
    twin_copies = [
        pltpu.make_async_remote_copy(
            src_ref=cols_ref.at[kind, side, pl.ds(1, count - 1)], dst_ref=cols_ref.at[kind, side, pl.ds(1, count - 1)],
            send_sem=twin_send.at[kind], recv_sem=twin_recv.at[kind], device_id={"ch": twin}, device_id_type=MESH,
        )
        for kind in (0, 1)
    ]


    own_part = pl.ds(pl.multiple_of(mine * part, part), part)
    cot_copies = [
        pltpu.make_async_remote_copy(
            src_ref=cot_ref, dst_ref=cotg_ref.at[:, own_part], send_sem=cot_send.at[k - 1], recv_sem=cot_recv.at[k - 1],
            device_id={"ch": lax.rem(mine + k, twins)}, device_id_type=MESH,
        )
        for k in range(1, twins)
    ]
    for copy in cot_copies:
        copy.start()
    own_copy = pltpu.make_async_copy(cot_ref, cotg_ref.at[:, own_part], own_sem.at[0])
    own_copy.start()
    for copy in seq_copies[: count - 1] + own_columns[:2]:
        copy.start()

    def in_step(step, carry):
        slot = lax.rem(step, 2)
        mode = lax.rem(step, modes)

        @pl.when(step + 1 < steps)
        def _():
            for b in (0, 1):
                in_copy(step + 1, b).start()

        for b in (0, 1):
            in_copy(step, b).wait()
        weights = jnp.concatenate([in_buf.at[slot, b].reshape(2 * width, 128)[...] for b in (0, 1)], axis=1)
        mask = jnp.concatenate([mode_ref[...]] * 2, axis=1) == mode.astype(jnp.float32)
        columns = pl.ds(pl.multiple_of(step // modes * 256, 256), 256)
        both = jnp.dot(x2_ref[...], weights, preferred_element_type=jnp.float32)
        for j, target in enumerate((x_ref, z_ref)):
            found = jnp.where(mask, both[j * rows : (j + 1) * rows], target[:, columns].astype(jnp.float32))
            target[:, columns] = found.astype(jnp.bfloat16)
        return carry

    x_ref[...] = jnp.zeros_like(x_ref)
    z_ref[...] = jnp.zeros_like(z_ref)
    row = lax.broadcasted_iota(jnp.int32, (256, 512), 0)
    column = lax.broadcasted_iota(jnp.int32, (256, 512), 1)
    for j in (0, 1):
        spread = (column == 2 * row + j).astype(jnp.bfloat16)
        for block in range(width // 256):
            x2_ref[j * rows : (j + 1) * rows, block * 512 : (block + 1) * 512] = jnp.dot(
                normed_ref[:, block * 256 : (block + 1) * 256], spread, preferred_element_type=jnp.float32
            ).astype(jnp.bfloat16)
    lax.fori_loop(0, steps // 2, in_step, 0)
    own_copy.wait()
    for copy in cot_copies:
        copy.wait_recv()
    for copy in seq_copies[count - 1 :] + own_columns[2:]:
        copy.start()
    lax.fori_loop(steps // 2, steps, in_step, 0)
    halo_copy = pltpu.make_async_remote_copy(
        src_ref=x_ref.at[pl.ds(rows - 16, 16)], dst_ref=halo_ref, send_sem=halo_send.at[0], recv_sem=halo_recv.at[0],
        device_id={"seq": lax.rem(me + 1, count)}, device_id_type=MESH,
    )
    halo_copy.start()
    for copy in seq_copies[: count - 1]:
        copy.wait_recv()
    twin_copies[0].start()

    def out_step(step, carry):
        slot = lax.rem(step, 2)
        mode = lax.rem(step, modes)

        @pl.when(step + 1 < out_steps)
        def _():
            out_copy(step + 1).start()

        out_copy(step).wait()
        mask = jnp.concatenate([mode_ref[...]] * (wide // 128), axis=1) == mode.astype(jnp.float32)
        columns = pl.ds(pl.multiple_of(step // modes * wide, wide), wide)
        found = jnp.dot(cotg_ref[...], out_buf[slot], preferred_element_type=jnp.float32)
        gated_ref[:, columns] = jnp.where(mask, found, gated_ref[:, columns])
        return carry

    gated_ref[...] = jnp.zeros_like(gated_ref)
    lax.fori_loop(0, out_steps // 2, out_step, 0)

    chunks, _, inner = pre_ref.shape
    padded(x_proj_ref, padded_ref)
    passed = documents(starts_ref, count * rows)
    spot = lax.broadcasted_iota(jnp.int32, (rows, 128), 0) + me * rows
    here = passed(spot)
    same = [jnp.where(passed(spot - lag) == here, 1.0, 0.0) for lag in (3, 2, 1, 0)]
    halo_copy.wait_recv()
    ext_ref[0:8] = halo_ref[8:16].astype(jnp.float32)
    ext_ref[8:] = x_ref[...].astype(jnp.float32)

    def conv_body(block, carry):
        cut = pl.ds(pl.multiple_of(block * 128, 128), 128)
        pre = jnp.zeros((rows, 128), jnp.float32) + cbias_ref[:, cut]
        for k in range(4):
            pre = pre + taps_ref[k : k + 1, cut] * ext_ref[5 + k : 5 + k + rows, cut] * same[k]
        pre_ref[:, :, cut] = pre.reshape(chunks, 16, 128)
        conv_ref[:, :, cut] = (pre / (1.0 + jnp.exp(-pre))).astype(jnp.bfloat16).reshape(chunks, 16, 128)
        return carry

    lax.fori_loop(0, inner // 128, conv_body, 0, unroll=2)
    part_ref[...] = lax.dot_general(
        conv_ref[...].reshape(rows, inner), padded_ref[...], (((1,), (1,)), ((), ())), preferred_element_type=jnp.float32
    )
    sent_ref[...] = part_ref[...].astype(jnp.bfloat16)
    low_copies = [
        pltpu.make_async_remote_copy(
            src_ref=sent_ref, dst_ref=got_ref.at[k - 1], send_sem=low_send.at[k - 1], recv_sem=low_recv.at[k - 1],
            device_id={"ch": lax.rem(mine + k, twins)}, device_id_type=MESH,
        )
        for k in range(1, twins)
    ]
    for copy in low_copies:
        copy.start()
    for copy in seq_copies[count - 1 :]:
        copy.wait_recv()
    twin_copies[1].start()
    lax.fori_loop(out_steps // 2, out_steps, out_step, 0)
    for k, copy in enumerate(low_copies):
        copy.wait_recv()
        part_ref[...] += got_ref[k].astype(jnp.float32)
    for copy in own_columns:
        copy.wait()
    for copy in twin_copies:
        copy.wait_recv()
    for copy in cot_copies + low_copies + seq_copies + twin_copies + [halo_copy]:
        copy.wait_send()


def front(x_in, gain, modes, cot, starts, taps, cbias, x_proj_t, w_in, w_out):
    count, twins = lax.axis_size("seq"), lax.axis_size("ch")
    rows, width = x_in.shape
    inner = w_out.shape[2]
    f32, b16 = jnp.float32, jnp.bfloat16
    shape = jax.ShapeDtypeStruct
    vmem = pl.BlockSpec(memory_space=pltpu.VMEM)
    hbm = pl.BlockSpec(memory_space=pl.ANY)
    wide = min(512, inner)
    return pl.pallas_call(
        functools.partial(front_kernel, (count, twins)),
        in_specs=[vmem] * 8 + [hbm] * 2,
        out_specs=[vmem] * 7,
        out_shape=[
            shape((rows, inner), b16), shape((rows, inner), f32), shape((2, 2, count, rows // 2, width // count), b16),
            shape((rows + 8, inner), f32), shape((rows // 16, 16, inner), f32), shape((rows // 16, 16, inner), b16),
            shape((rows, 256), f32),
        ],
        scratch_shapes=[
            pltpu.VMEM((rows, width), b16), pltpu.VMEM((rows, width), b16), pltpu.SemaphoreType.DMA((2, 2)),
            pltpu.SemaphoreType.DMA((2, count - 1)), pltpu.SemaphoreType.DMA((2, count - 1)),
            pltpu.SemaphoreType.DMA((2,)), pltpu.SemaphoreType.DMA((2,)),
            pltpu.VMEM((rows, inner), b16), pltpu.VMEM((16, inner), b16), pltpu.VMEM((256, inner), b16),
            pltpu.VMEM((rows, 256), b16), pltpu.VMEM((twins - 1, rows, 256), b16),
            pltpu.SemaphoreType.DMA((twins - 1,)), pltpu.SemaphoreType.DMA((twins - 1,)),
            pltpu.VMEM((rows, 128), jnp.float32),
            pltpu.VMEM((2 * rows, 2 * width), jnp.bfloat16),
            pltpu.SemaphoreType.DMA((1,)),
            pltpu.SemaphoreType.DMA((1,)),
            pltpu.VMEM((2, 2, width, 2, 128), jnp.bfloat16),
            pltpu.VMEM((2, width, wide), jnp.bfloat16),
            pltpu.SemaphoreType.DMA((2, 2)),
            pltpu.SemaphoreType.DMA((2,)),
            pltpu.SemaphoreType.DMA((twins - 1,)),
            pltpu.SemaphoreType.DMA((twins - 1,)),
            pltpu.SemaphoreType.DMA((1,)),
        ],
        compiler_params=pltpu.CompilerParams(collective_id=1, has_side_effects=True, vmem_limit_bytes=56 << 20),
        name="front",
    )(x_in, gain, modes, cot, starts, taps, cbias, x_proj_t, w_in, w_out)


def tile_lanes(v, lanes):
    return jnp.concatenate([v] * (lanes // 128), axis=1)

def ring_places(count):
    ring = cycle_of(count)
    where = {s: i for i, s in enumerate(ring)}
    me = lax.axis_index("seq")
    onward = table_of(me, [ring[(where[s] + 1) % count] for s in range(count)])
    backward = table_of(me, [ring[(where[s] - 1) % count] for s in range(count)])
    place = table_of(me, [where[s] for s in range(count)])
    return ring, place, onward, backward


def add_products(accs, kind, k, cols_ref, blocks, modes_ref, ring, place, count):
    parts = []
    for way in (0, 1):
        step = k if way else count - k
        source = table_of(lax.rem(place + step, count), ring)
        parts.append((jnp.transpose(cols_ref[kind, way, k]), modes_ref[pl.ds(2 * source + way, 1), :]))
    right = jnp.concatenate(blocks, axis=0)
    for m, acc in enumerate(accs):
        left = jnp.concatenate(
            [part * jnp.where(row == m, 1.0, 0.0).astype(jnp.bfloat16) for part, row in parts], axis=1
        )
        found = jnp.dot(left, right, preferred_element_type=jnp.float32)
        acc[...] += found.reshape(acc.shape)


def core_kernel(
    sizes, w_in_ref, w_out_ref, cols_hbm, ext_hbm, pre_hbm, x_in_hbm, conv_ref, part_ref, z_ref, dgated_ref, starts_ref,
    taps_ref, x_t_ref, dt_proj_ref, dt_bias_ref, a_log_ref, skip_ref, modes_ref, gain_ref,
    dwo_ref, dwz_ref, dwx_ref, mix_ref, small_ref, slice_ref, dots_ref, dgain_ref, scale_ref,
    cols_ref, ext_ref, pre_ref, x_in_ref, late_sem, x_proj_ref, same_ref, mode_ref, free_sem, g_ref, step_ref, dtd_ref, u_ref, sig_ref, low_t_ref, b_ref, c_ref, rate_ref, ends_ref,
    ends_sent, ends_got, steps_sent, steps_got, gap_ref, h0_ref, gz_ref,
    racc_ref, rows_ref, sum_ref, half_ref, half_got, four_ref, four_b16, four_got, in_buf, out_buf, mix_sent, mix_got,
    norm_sent, norm_got, dots_sent, dots_got, gain_sent, gain_got,
    ring_ref, hist_ref, lam_ref, w_ref, pend_ref, gstep_ref, gscan_ref, grad_ref, sent_ref, got_ref,
    gpre_ref, edge_ref,
    in_sem, out_sem, mix_send, mix_recv, half_send, half_recv, four_send, four_recv, last_send, last_recv, all_send, all_recv,
    ends_send, ends_recv, steps_send, steps_recv, norm_send, norm_recv, dots_send, dots_recv,
    gain_send, gain_recv, dwo_sem,
    ring_send, ring_recv, gx_send, gx_recv, ch_send, ch_recv, edge_send, edge_recv,
):
    count, twins = sizes
    chunks, _, chans = pre_ref.shape
    rows = chunks * 16
    gx_ref = gz_ref.at[2]
    slab = cols_ref.shape[4]
    n = a_log_ref.shape[0]
    half = rows // 2
    ring, place, onward, backward = ring_places(count)
    me = lax.axis_index("seq")
    mine = lax.axis_index("ch")
    before = lax.rem(me + count - 1, count)
    nt = (((1,), (1,)), ((), ()))
    f32, b16 = jnp.float32, jnp.bfloat16
    lb = min(512, chans)

    modes, width = w_out_ref.shape[:2]
    part = width // twins
    eighths = chans // 128
    across = half_ref.shape[1]
    tall = half_ref.shape[0]
    depth = half_ref.shape[2]
    z_at = me // across
    x_at = lax.rem(me, across)

    def chunk_of(step):
        return pl.ds(pl.multiple_of(lax.rem(mine + 1 + step // modes, twins) * part, part), part)

    def in_copy(step, b):
        slot = step % 2
        return pltpu.make_async_copy(w_in_ref.at[step % modes, chunk_of(step), b], in_buf.at[slot, b], in_sem.at[slot, b])

    def in_copies(step, wait):
        for b in range(eighths):
            if wait:
                in_copy(step, b).wait()
            else:
                in_copy(step, b).start()

    def out_copy(step):
        slot = step % 2
        return pltpu.make_async_copy(w_out_ref.at[step % modes, chunk_of(step)], out_buf.at[slot], out_sem.at[slot])

    barrier = pltpu.get_barrier_semaphore()
    for k in range(1, count):
        pl.semaphore_signal(barrier, inc=1, device_id={"seq": lax.rem(me + k, count)}, device_id_type=MESH)
    for k in range(1, twins):
        peer = {"ch": lax.rem(mine + k, twins)}
        pl.semaphore_signal(barrier, inc=1, device_id=peer, device_id_type=MESH)
    in_copies(0, 0)
    out_copy(0).start()
    late_operands = ((cols_hbm, cols_ref), (ext_hbm, ext_ref), (pre_hbm, pre_ref), (x_in_hbm, x_in_ref))
    late_fetches = [
        pltpu.make_async_copy(source, target, late_sem.at[i]) for i, (source, target) in enumerate(late_operands)
    ]
    for copy in late_fetches:
        copy.start()
    pl.semaphore_wait(barrier, count - 1 + twins - 1)

    passed = documents(starts_ref, count * rows)

    def maps_copies(send, recv):
        return [
            pltpu.make_async_remote_copy(
                src_ref=sent_ref, dst_ref=got_ref.at[k - 1], send_sem=send.at[k - 1],
                recv_sem=recv.at[k - 1], device_id={"ch": lax.rem(mine + k, twins)}, device_id_type=MESH,
            )
            for k in range(1, twins)
        ]


    def gate_body(i, carry):
        z = z_ref[i].astype(f32)
        g_ref[i] = dgated_ref[i] * (z / (1.0 + jnp.exp(-z)))
        return carry

    lax.fori_loop(0, chunks, gate_body, 0, unroll=2)
    rate_ref[...] = -math.log2(math.e) * jnp.exp(a_log_ref[...])
    own = (
        lax.broadcasted_iota(jnp.int32, (16, 16 * n), 1) // n == lax.broadcasted_iota(jnp.int32, (16, 16 * n), 0)
    )
    ones = own.astype(b16)
    token_row = lax.broadcasted_iota(jnp.int32, (16 * n, 16), 0) // n
    repeat = (token_row == lax.broadcasted_iota(jnp.int32, (16 * n, 16), 1)).astype(b16)
    pick_row = lax.broadcasted_iota(jnp.int32, (16 * n, 128), 0)
    pick_col = lax.broadcasted_iota(jnp.int32, (16 * n, 128), 1)
    is_b = pick_row % n == pick_col
    is_c = pick_row % n + n == pick_col
    pick_b = is_b.astype(b16)
    pick_c = is_c.astype(b16)
    flat = jnp.ones((256, 128), b16)
    total = part_ref[...]
    low_t_ref[...] = jnp.transpose(total[:, 0:128]).astype(b16)
    raw = jnp.dot(total[:, 0:128].astype(b16), dt_proj_ref[...], preferred_element_type=f32)
    step_ref[...] = raw.reshape(chunks, 16, chans)

    def step_body(i, carry):
        raw = step_ref[i] + dt_bias_ref[...]
        step = jnp.maximum(raw, 0.0) + jnp.log1p(jnp.exp(-jnp.abs(raw)))
        step_ref[i] = step
        sig_ref[i] = 1.0 / (1.0 + jnp.exp(-raw))
        at = lax.broadcasted_iota(jnp.int32, (16, 128), 0) + (me * rows + i * 16)
        big = jnp.where(passed(at) == passed(at - 1), 0.0, 1e30)
        dtd_ref[i] = step + jnp.concatenate([big] * (chans // 128), axis=1)
        u_ref[i] = step * conv_ref[i].astype(f32)
        maps = part_ref[pl.ds(pl.multiple_of(i * 16, 16), 16), 128:256]
        high = maps.astype(b16)
        low = (maps - high.astype(f32)).astype(b16)
        high = jnp.dot(repeat, high, preferred_element_type=f32)
        low = jnp.dot(repeat, low, preferred_element_type=f32)
        for target, chosen in ((b_ref, is_b), (c_ref, is_c)):
            terms = [jnp.where(chosen, term, 0.0).astype(b16) for term in (high, low)]
            found = jnp.dot(jnp.concatenate(terms, axis=1), flat, preferred_element_type=f32)
            target[pl.ds(i * 16, 16)] = found.reshape(16, n, 128)
        return carry

    lax.fori_loop(0, chunks, step_body, 0, unroll=2)

    def maps_block(chunk, pick):
        maps = part_ref[pl.ds(pl.multiple_of(chunk * 16, 16), 16), 128:256].astype(b16)
        found = lax.dot_general(maps, pick, nt, preferred_element_type=f32)
        return jnp.where(own, found, 0.0).astype(b16)

    ends_ref[0:n] = jnp.zeros((n, chans), f32)
    ends_ref[n : 2 * n] = jnp.ones((n, chans), f32)
    ends_ref[2 * n : 3 * n] = jnp.zeros((n, chans), f32)

    def end_body(chunk, carry):
        for block in range(chans // lb):
            cut = slice(block * lb, (block + 1) * lb)
            rate = rate_ref[:, cut]
            h = ends_ref[0:n, cut]
            for t in range(16):
                decay = jnp.exp2(dtd_ref[chunk, t : t + 1, cut] * rate)
                h = decay * h + u_ref[chunk, t : t + 1, cut] * tile_lanes(b_ref[chunk * 16 + t], lb)
            ends_ref[0:n, cut] = h
        return carry

    def head_body(chunk, carry):
        for block in range(chans // lb):
            cut = slice(block * lb, (block + 1) * lb)
            rate = rate_ref[:, cut]
            reach = ends_ref[n : 2 * n, cut]
            head = ends_ref[2 * n : 3 * n, cut]
            for t in range(16):
                reach = reach * jnp.exp2(dtd_ref[chunk, t : t + 1, cut] * rate)
                head = head + reach * (g_ref[chunk, t : t + 1, cut] * tile_lanes(c_ref[chunk * 16 + t], lb))
            ends_ref[n : 2 * n, cut] = reach
            ends_ref[2 * n : 3 * n, cut] = head
        return carry

    def state_copy(side, k):
        return pltpu.make_async_remote_copy(
            src_ref=ends_sent.at[side], dst_ref=ends_got.at[k - 1], send_sem=ends_send.at[k - 1],
            recv_sem=ends_recv.at[k - 1], device_id={"seq": lax.rem(me + k, count)}, device_id_type=MESH,
        )

    steps_copies = [
        pltpu.make_async_remote_copy(
            src_ref=steps_sent, dst_ref=steps_got.at[k - 1], send_sem=steps_send.at[k - 1],
            recv_sem=steps_recv.at[k - 1], device_id={"seq": lax.rem(me + k, count)}, device_id_type=MESH,
        )
        for k in range(1, count)
    ]
    steps_sent[...] = jnp.sum(jnp.sum(dtd_ref[...], axis=0), axis=0, keepdims=True)
    for copy in steps_copies:
        copy.start()
    lax.fori_loop(0, chunks, end_body, 0, unroll=2)
    ends_sent[0] = ends_ref[0:n].astype(b16)
    for k in range(1, count):

        @pl.when(me + k < count)
        def _():
            state_copy(0, k).start()

    lax.fori_loop(0, chunks, head_body, 0, unroll=2)
    ends_sent[1] = ends_ref[2 * n : 3 * n].astype(b16)
    for k in range(1, count):

        @pl.when(me + k >= count)
        def _():
            state_copy(1, k).start()

    for copy in steps_copies:
        copy.wait_recv()
    for k in range(1, count):

        @pl.when(me >= k)
        def _():
            state_copy(0, k).wait_recv()

    h0_ref[...] = jnp.zeros_like(h0_ref)
    gap_ref[...] = jnp.zeros_like(gap_ref)
    for k in range(1, count):

        @pl.when(me >= k)
        def _():
            h0_ref[...] += ends_got[k - 1].astype(f32) * jnp.exp2(rate_ref[...] * gap_ref[...])

        gap_ref[...] += steps_got[k - 1]

    racc_ref[...] = h0_ref[...]

    def forward_body(chunk, carry):
        for block in range(chans // lb):
            cut = slice(block * lb, (block + 1) * lb)
            rate = rate_ref[:, cut]
            h = racc_ref[:, cut]
            for t in range(16):
                decay = jnp.exp2(dtd_ref[chunk, t : t + 1, cut] * rate)
                h = decay * h + u_ref[chunk, t : t + 1, cut] * tile_lanes(b_ref[chunk * 16 + t], lb)
                hist_ref[chunk, t * n : (t + 1) * n, cut] = h.astype(b16)
            racc_ref[:, cut] = h
        ssm = jnp.dot(maps_block(chunk, pick_c), hist_ref[chunk], preferred_element_type=f32)
        ssm = ssm + skip_ref[...] * conv_ref[chunk].astype(f32)
        z = z_ref[chunk].astype(f32)
        sig = 1.0 / (1.0 + jnp.exp(-z))
        rc = pl.ds(pl.multiple_of(chunk * 16, 16), 16)
        gz_ref[0, rc] = (ssm * (z * sig)).astype(b16)
        gz_ref[1, rc] = (dgated_ref[chunk] * ssm * (sig * (1.0 + z * (1.0 - sig)))).astype(b16)
        return carry

    lax.fori_loop(0, chunks, forward_body, 0, unroll=2)

    def ring_copy(kind, way, k):
        if k == 0:
            source = gz_ref.at[kind, pl.ds(way * half, half)]
        else:
            source = ring_ref.at[kind, way, k - 1]
        return pltpu.make_async_remote_copy(
            src_ref=source, dst_ref=ring_ref.at[kind, way, k], send_sem=ring_send.at[kind, way, k],
            recv_sem=ring_recv.at[kind, way, k], device_id={"seq": backward if way else onward}, device_id_type=MESH,
        )

    def relay(kind, k):
        for way in (0, 1):
            if kind == 2:
                gx_copy(way, k - 1).wait_recv()
                if k < count - 1:
                    gx_copy(way, k).start()
            else:
                ring_copy(kind, way, k - 1).wait_recv()
                if k < count - 1:
                    ring_copy(kind, way, k).start()

    def gx_slot(way, k):
        slot = way * (count - 1) + k
        return hist_ref.at[slot // 2, pl.ds(slot % 2 * half, half)]

    def gx_copy(way, k):
        return pltpu.make_async_remote_copy(
            src_ref=gx_slot(way, k - 1) if k else gx_ref.at[pl.ds(way * half, half)], dst_ref=gx_slot(way, k),
            send_sem=gx_send.at[way, k], recv_sem=gx_recv.at[way, k], device_id={"seq": backward if way else onward},
            device_id_type=MESH,
        )

    for kind in (0, 1):
        for way in (0, 1):
            ring_copy(kind, way, 0).start()
    for copy in late_fetches:
        copy.wait()
    for k in range(1, count):

        @pl.when(me < k)
        def _():
            state_copy(1, k).wait_recv()

    pend_ref[...] = jnp.zeros_like(pend_ref)
    gap_ref[...] = jnp.zeros_like(gap_ref)
    for k in range(1, count):
        slot = count - 1 - k

        @pl.when(me + k < count)
        def _():
            pend_ref[...] += ends_got[slot].astype(f32) * jnp.exp2(rate_ref[...] * gap_ref[...])

        gap_ref[...] += steps_got[slot]

    turns = [(kind, k) for k in range(1, count) for kind in (0, 1)]
    early = turns[:2]
    late = turns[2:]

    racc_ref[...] = jnp.zeros_like(racc_ref)

    def span_body(i, carry):
        at = spans - 1 - i
        for sub in reversed(range(span // 16)):
            chunk = at * (span // 16) + sub
            for block in range(chans // lb):
                cut = slice(block * lb, (block + 1) * lb)
                rate = rate_ref[:, cut]
                pend = pend_ref[:, cut]
                racc = racc_ref[:, cut]
                for t in reversed(range(16)):
                    decay = jnp.exp2(dtd_ref[chunk, t : t + 1, cut] * rate)
                    lam = g_ref[chunk, t : t + 1, cut] * tile_lanes(c_ref[chunk * 16 + t], lb) + pend
                    pend = decay * lam
                    if t:
                        prior = hist_ref[chunk, (t - 1) * n : t * n, cut].astype(jnp.float32)
                    else:
                        prior = hist_ref[jnp.maximum(chunk - 1, 0), 15 * n : 16 * n, cut].astype(jnp.float32)
                        prior = jnp.where(chunk == 0, h0_ref[:, cut], prior)
                    w = pend * prior
                    racc = racc + w * step_ref[chunk, t : t + 1, cut]
                    lam_ref[t * n : (t + 1) * n, cut] = lam.astype(jnp.bfloat16)
                    w_ref[t * n : (t + 1) * n, cut] = (w * rate).astype(jnp.bfloat16)
                pend_ref[:, cut] = pend
                racc_ref[:, cut] = racc
            step = step_ref[chunk]
            conv = conv_ref[chunk].astype(jnp.float32)
            adj = jnp.dot(maps_block(chunk, pick_b), lam_ref[...], preferred_element_type=jnp.float32)
            wsum = jnp.dot(ones, w_ref[...], preferred_element_type=jnp.float32)
            gstep_ref[chunk] = wsum * math.log(2.0) + adj * conv
            gscan_ref[chunk] = adj * step
            gb = lax.dot_general(u_ref[chunk].astype(jnp.bfloat16), lam_ref[...], nt, preferred_element_type=jnp.float32)
            gc = lax.dot_general(
                g_ref[chunk].astype(jnp.bfloat16), hist_ref[chunk], nt, preferred_element_type=jnp.float32
            )
            gb = jnp.where(own, gb, 0.0).astype(jnp.bfloat16)
            gc = jnp.where(own, gc, 0.0).astype(jnp.bfloat16)
            grad_ref[pl.ds(pl.multiple_of(chunk * 16, 16), 16), 128:256] = jnp.dot(
                gb, pick_b, preferred_element_type=jnp.float32
            ) + jnp.dot(gc, pick_c, preferred_element_type=jnp.float32)
        return carry

    span = 32
    spans = rows // span
    mode_columns(modes_ref, mode_ref)
    padded(x_t_ref, x_proj_ref)
    passed = documents(starts_ref, count * rows)
    spot = lax.broadcasted_iota(jnp.int32, (rows, 128), 0) + me * rows
    here = passed(spot)
    for i in range(7):
        same_ref[i] = jnp.where(passed(spot + (i - 3)) == here, 1.0, 0.0).astype(b16)
    lax.fori_loop(0, spans // 2, span_body, 0)
    relay(*early[0])
    lax.fori_loop(spans // 2, spans, span_body, 0)
    for peer in (onward, backward):
        pl.semaphore_signal(free_sem, inc=1, device_id={"seq": peer}, device_id_type=MESH)
    relay(*early[1])

    rows_ref[...] = jnp.zeros_like(rows_ref)

    def raw_body(i, carry):
        full = gstep_ref[i] * sig_ref[i]
        rows_ref[5:6] += jnp.sum(full, axis=0, keepdims=True)
        rows_ref[6:7] += jnp.sum(g_ref[i] * conv_ref[i].astype(jnp.float32), axis=0, keepdims=True)
        gx_ref[pl.ds(pl.multiple_of(i * 16, 16), 16), :] = full.astype(jnp.bfloat16)
        return carry

    lax.fori_loop(0, chunks, raw_body, 0)
    grad_ref[:, 0:128] = lax.dot_general(gx_ref[...], dt_proj_ref[...], nt, preferred_element_type=jnp.float32)
    sent_ref[...] = grad_ref[...].astype(jnp.bfloat16)
    ch_copies = maps_copies(ch_send, ch_recv)
    for copy in ch_copies:
        copy.start()
    relay(*late[0])
    sum_ref[160:288] = jnp.dot(low_t_ref[...], gx_ref[...], preferred_element_type=jnp.float32)
    for copy in ch_copies:
        copy.wait_recv()
    total = grad_ref[...]
    for k in range(twins - 1):
        total = total + got_ref[k].astype(jnp.float32)
    grad_ref[...] = total
    relay(*late[1])

    skip = skip_ref[...]
    def pre_body(i, carry):
        rc = pl.ds(pl.multiple_of(i * 16, 16), 16)
        g_conv = jnp.dot(grad_ref[rc, :].astype(jnp.bfloat16), x_proj_ref[...], preferred_element_type=jnp.float32)
        g_conv = g_conv + skip * g_ref[i] + gscan_ref[i]
        pre = pre_ref[i]
        sig = 1.0 / (1.0 + jnp.exp(-pre))
        gpre = g_conv * sig * (1.0 + pre * (1.0 - sig))
        gpre_ref[rc, :] = gpre
        return carry

    pre_body(0, 0)
    edge_ref[...] = gpre_ref[0:8, :]
    edge_copy = pltpu.make_async_remote_copy(
        src_ref=edge_ref, dst_ref=gpre_ref.at[pl.ds(rows, 8)], send_sem=edge_send.at[0], recv_sem=edge_recv.at[0],
        device_id={"seq": before}, device_id_type=MESH,
    )
    edge_copy.start()
    lax.fori_loop(1, chunks, pre_body, 0)
    flipped = jnp.transpose(grad_ref[...]).astype(jnp.bfloat16)
    sum_ref[0:160] = jnp.dot(flipped[0:160], conv_ref[...].reshape(rows, chans), preferred_element_type=jnp.float32)
    relay(*late[2])
    edge_copy.wait_recv()

    def taps_body(block, carry):
        cut = pl.ds(pl.multiple_of(block * 128, 128), 128)
        gpre = gpre_ref[0:rows, cut]
        rows_ref[4:5, cut] = jnp.sum(gpre, axis=0, keepdims=True)
        total = jnp.zeros((rows, 128), jnp.float32)
        for k in range(4):
            lag = 3 - k
            total = total + gpre_ref[lag : lag + rows, cut] * taps_ref[k : k + 1, cut] * same_ref[3 + lag].astype(jnp.float32)
            rows_ref[k : k + 1, cut] = jnp.sum(
                gpre * ext_ref[5 + k : 5 + k + rows, cut] * same_ref[k].astype(jnp.float32), axis=0, keepdims=True
            )
        gx_ref[:, cut] = total.astype(jnp.bfloat16)
        return carry

    lax.fori_loop(0, chans // 128, taps_body, 0)
    pl.semaphore_wait(free_sem, 2)
    for way in (0, 1):
        gx_copy(way, 0).start()
    sum_ref[288:304] = racc_ref[...] * rate_ref[...] * math.log(2.0)
    sum_ref[304:312] = rows_ref[...]
    if tall * across * depth > 312:
        sum_ref[312:] = jnp.zeros((tall * across * depth - 312, chans), jnp.float32)
    for z in range(tall):
        for x in range(across):
            first = (z * across + x) * depth
            half_ref[z, x] = sum_ref[first : first + depth].astype(jnp.bfloat16)

    def to(device):
        return dict(device_id={"seq": device}, device_id_type=MESH)

    half_copies = [
        pltpu.make_async_remote_copy(
            src_ref=half_ref.at[:, lax.rem(x_at + k, across)], dst_ref=half_got.at[k - 1], send_sem=half_send.at[k - 1],
            recv_sem=half_recv.at[k - 1], **to(z_at * across + lax.rem(x_at + k, across)),
        )
        for k in range(1, across)
    ]
    four_copies = [
        pltpu.make_async_remote_copy(
            src_ref=four_b16.at[lax.rem(z_at + k, tall)], dst_ref=four_got.at[k - 1], send_sem=four_send.at[k - 1],
            recv_sem=four_recv.at[k - 1], **to(lax.rem(z_at + k, tall) * across + x_at),
        )
        for k in range(1, tall)
    ]
    last_copies = [
        pltpu.make_async_remote_copy(
            src_ref=small_ref.at[z_at, x_at], dst_ref=small_ref.at[z_at, x_at], send_sem=last_send.at[k - 1],
            recv_sem=last_recv.at[k - 1], **to(lax.rem(z_at + k, tall) * across + x_at),
        )
        for k in range(1, tall)
    ]
    all_copies = [
        pltpu.make_async_remote_copy(
            src_ref=small_ref.at[:, x_at], dst_ref=small_ref.at[:, x_at], send_sem=all_send.at[k - 1],
            recv_sem=all_recv.at[k - 1], **to(z_at * across + lax.rem(x_at + k, across)),
        )
        for k in range(1, across)
    ]

    def small_phase(phase):
        if phase == 0:
            for copy in half_copies:
                copy.start()
        elif phase == 1:
            for copy in half_copies:
                copy.wait_recv()
            for z in range(tall):
                first = pl.multiple_of((z * across + x_at) * depth, depth)
                total = sum_ref[pl.ds(first, depth)]
                for k in range(across - 1):
                    total = total + half_got[k, z].astype(jnp.float32)
                four_ref[z] = total
                four_b16[z] = total.astype(jnp.bfloat16)
            for copy in four_copies:
                copy.start()
        elif phase == 2:
            for copy in four_copies:
                copy.wait_recv()
            total = four_ref[z_at]
            for k in range(tall - 1):
                total = total + four_got[k].astype(jnp.float32)
            small_ref[z_at, x_at] = total.astype(jnp.bfloat16)
            for copy in last_copies:
                copy.start()
        elif phase == 3:
            for copy in last_copies:
                copy.wait_recv()
            for copy in all_copies:
                copy.start()
        else:
            for copy in all_copies:
                copy.wait_recv()
            for copy in half_copies + four_copies + last_copies + all_copies:
                copy.wait_send()

    small_phase(0)
    dwo_accs = [ref.at[0 : slab // 16] for ref in (dtd_ref, u_ref, sig_ref)]
    dwz_accs = [ref.at[0 : slab // 16] for ref in (step_ref, g_ref, gscan_ref)]
    dwx_accs = [dwx_ref.at[m] for m in range(modes)]
    for acc in dwo_accs + dwz_accs + dwx_accs:
        acc[...] = jnp.zeros_like(acc)

    def products(kind, k):
        if k == 0:
            source = gx_ref if kind == 2 else gz_ref.at[kind]
            blocks = [source[way * half : (way + 1) * half] for way in (0, 1)]
        else:
            blocks = [gx_slot(way, k - 1)[...] if kind == 2 else ring_ref[kind, way, k - 1] for way in (0, 1)]
        accs = (dwo_accs, dwz_accs, dwx_accs)[kind]
        add_products(accs, 0 if kind else 1, k, cols_ref, blocks, modes_ref, ring, place, count)
        if kind < 2 and k == count - 1:
            for copy in out_copies[kind]:
                copy.start()

    out_copies = [
        [pltpu.make_async_copy(acc, target.at[m], dwo_sem.at[kind, m]) for m, acc in enumerate(accs)]
        for kind, (accs, target) in enumerate(((dwo_accs, dwo_ref), (dwz_accs, dwz_ref)))
    ]

    def mix_copy(j):
        return pltpu.make_async_remote_copy(
            src_ref=mix_sent.at[j], dst_ref=mix_got.at[j], send_sem=mix_send.at[j], recv_sem=mix_recv.at[j],
            device_id={"ch": lax.rem(mine + 1 + j, twins)}, device_id_type=MESH,
        )

    steps = twins * modes

    def norm_copy(j):
        return pltpu.make_async_remote_copy(
            src_ref=norm_sent.at[j], dst_ref=norm_got.at[j], send_sem=norm_send.at[j], recv_sem=norm_recv.at[j],
            device_id={"ch": lax.rem(mine + 1 + j, twins)}, device_id_type=MESH,
        )

    def normed_unit(j, m):
        step = j * modes + m
        if step + 1 < steps:
            in_copies(step + 1, 0)
        in_copies(step, 1)
        spread_products(in_buf.at[step % 2], gz_ref, mode_ref, slice_ref, m, part)

    def normed_end(j):
        for q in range(part // 128):
            lanes = slice(q * 128, (q + 1) * 128)
            cut = pl.ds(pl.multiple_of(lax.rem(mine + 1 + j, twins) * part + q * 128, 128), 128)
            dots_ref[...] += slice_ref[:, lanes] * x_in_ref[:, cut].astype(f32) * gain_ref[:, cut]
        if j < twins - 1:
            norm_sent[j] = slice_ref[...].astype(b16)
            norm_copy(j).start()

    def mix_unit(j):
        for m in range(modes):
            step = j * modes + m
            if step + 1 < steps:
                out_copy(step + 1).start()
            out_copy(step).wait()
            mask = jnp.concatenate([mode_ref[...]] * (part // 128), axis=1) == float(m)
            found = lax.dot_general(gz_ref[0], out_buf[step % 2], nt, preferred_element_type=jnp.float32)
            mix_ref[...] = jnp.where(mask, found, mix_ref[...]) if m else found
        if j < twins - 1:
            mix_sent[j] = mix_ref[...].astype(jnp.bfloat16)
            mix_copy(j).start()

    dots_copies = [
        pltpu.make_async_remote_copy(
            src_ref=dots_sent, dst_ref=dots_got.at[k - 1], send_sem=dots_send.at[k - 1], recv_sem=dots_recv.at[k - 1],
            device_id={"ch": lax.rem(mine + k, twins)}, device_id_type=MESH,
        )
        for k in range(1, twins)
    ]
    gain_copies = [
        pltpu.make_async_remote_copy(
            src_ref=gain_sent, dst_ref=gain_got.at[k - 1], send_sem=gain_send.at[k - 1], recv_sem=gain_recv.at[k - 1],
            device_id={"seq": lax.rem(me + k, count)}, device_id_type=MESH,
        )
        for k in range(1, count)
    ]

    def scale_body(i, carry):
        rc = pl.ds(pl.multiple_of(i * 16, 16), 16)
        scale_ref[rc] = jnp.broadcast_to(row_scale(x_in_ref[rc].astype(f32)), (16, 128))
        return carry

    def dots_unit():
        lax.fori_loop(0, chunks, scale_body, 0)
        dots_sent[...] = dots_ref[...].astype(b16)
        for copy in dots_copies:
            copy.start()

    def slice_unit():
        for j in range(twins - 1):
            norm_copy(j).wait_recv()
            slice_ref[...] += norm_got[j].astype(f32)
        for q in range(part // 128):
            lanes = slice(q * 128, (q + 1) * 128)
            cut = pl.ds(pl.multiple_of(mine * part + q * 128, 128), 128)
            terms = slice_ref[:, lanes] * x_in_ref[:, cut].astype(f32) * scale_ref[...]
            gain_sent[:, lanes] = jnp.broadcast_to(jnp.sum(terms, axis=0, keepdims=True), (8, 128))
        for copy in gain_copies:
            copy.start()

    def gain_unit():
        total = gain_sent[...]
        for k, copy in enumerate(gain_copies):
            copy.wait_recv()
            total = total + gain_got[k]
        dgain_ref[...] = total
        for k, copy in enumerate(dots_copies):
            copy.wait_recv()
            dots_ref[...] += dots_got[k].astype(f32)
        mean = jnp.sum(dots_ref[...], axis=1, keepdims=True) / width
        dots_ref[...] = jnp.broadcast_to(mean, (rows, 128))
        for j in range(twins - 1):
            mix_copy(j).wait_recv()
            mix_ref[...] += mix_got[j].astype(f32)

    edge_copy.wait_send()
    dots_ref[...] = jnp.zeros_like(dots_ref)
    work = []
    for j in range(twins):
        for m in range(modes):
            work.append(functools.partial(normed_unit, j, m))
        work.append(functools.partial(normed_end, j))
        if j < 4:
            work.append(functools.partial(small_phase, j + 1))
    work.append(dots_unit)
    for j in range(twins):
        work.append(functools.partial(mix_unit, j))
    work += [slice_unit, gain_unit]
    ready = [(0, 0), (1, 0), (2, 0)] + early + late[:3]
    rest, last = late[3:], [(2, k) for k in range(1, count)]
    paced = [((i + 1) / len(turns), turn) for turns in (rest, last) for i, turn in enumerate(turns)]
    turns = [turn for _, turn in sorted(paced, key=lambda entry: entry[0])]
    for i, turn in enumerate(turns):
        left = len(turns) - i
        for _ in range(min(len(work), max(1, -(-len(work) // left)))):
            work.pop(0)()
        relay(*turn)
        ready.append(turn)
        for _ in range(2 if len(ready) > left else 1):
            if len(ready) > 1:
                products(*ready.pop(0))
    for unit in work:
        unit()
    for turn in ready:
        products(*turn)
    for copy in out_copies[0] + out_copies[1]:
        copy.wait()
    for j in range(twins - 1):
        mix_copy(j).wait_send()
        norm_copy(j).wait_send()
    for copy in dots_copies + gain_copies:
        copy.wait_send()
    for way in (0, 1):
        for k in range(count - 1):
            gx_copy(way, k).wait_send()

    for kind in (0, 1):
        for way in (0, 1):
            for k in range(count - 1):
                ring_copy(kind, way, k).wait_send()
    for copy in ch_copies + steps_copies:
        copy.wait_send()
    for k in range(1, count):
        state_copy(0, k).wait_send()


def spread_products(buf, trio_ref, mode_ref, target, m, part):
    nt = (((1,), (1,)), ((), ()))
    chosen = mode_ref[...] == float(m)
    row = lax.broadcasted_iota(jnp.int32, (256, 128), 0)
    column = lax.broadcasted_iota(jnp.int32, (256, 128), 1)
    picks = [(row == 2 * column + j).astype(jnp.bfloat16) for j in (1, 0)]
    rows = trio_ref.shape[1]
    stacked = trio_ref[1:3].reshape(2 * rows, trio_ref.shape[2])
    for q in range(2 * part // 256):
        weights = jnp.concatenate(
            [buf.at[b].reshape(2 * part, 128)[q * 256 : (q + 1) * 256] for b in range(buf.shape[0])], axis=1
        )
        found = lax.dot_general(stacked, weights, nt, preferred_element_type=jnp.float32).astype(jnp.bfloat16)
        total = jnp.dot(found[:rows], picks[0], preferred_element_type=jnp.float32)
        total = total + jnp.dot(found[rows:], picks[1], preferred_element_type=jnp.float32)
        cut = pl.ds(q * 128, 128)
        target[:, cut] = jnp.where(chosen, total, target[:, cut]) if m else total


def core(
    w_in, w_out, cols, ext, pre, conv, maps, z, dgated, starts, taps, x_proj_t, dt_proj, dt_bias, a_log, skip, modes,
    x_in, gain,
):
    count, twins = lax.axis_size("seq"), lax.axis_size("ch")
    rows, chans = z.shape
    n = a_log.shape[0]
    chunks = rows // 16
    width = w_out.shape[1]
    slab = width // count
    part = width // twins
    tall, across = 4, count // 4
    depth = -(-320 // (8 * count)) * 8
    vmem = pl.BlockSpec(memory_space=pltpu.VMEM)
    hbm = pl.BlockSpec(memory_space=pl.ANY)
    cube = lambda a: a.reshape((chunks, a.shape[0] // chunks) + a.shape[1:])
    f32, b16 = jnp.float32, jnp.bfloat16
    shape = jax.ShapeDtypeStruct
    dma = pltpu.SemaphoreType.DMA
    keep = pltpu.VMEM
    operands = [w_in, w_out, cols, ext, pre, x_in, conv, maps, cube(z), cube(dgated), starts, taps, x_proj_t, dt_proj, dt_bias,
                a_log, skip, modes, gain]
    block = (chunks, 16, chans)
    pair = lambda size: [dma((size,)), dma((size,))]
    return pl.pallas_call(
        functools.partial(core_kernel, (count, twins)),
        in_specs=[hbm] * 6 + [vmem] * (len(operands) - 6),
        out_specs=[hbm] * 2 + [vmem] * 7,
        out_shape=[
            shape((3, slab // 16, 16, chans), f32), shape((3, slab // 16, 16, chans), f32), shape((3, slab, chans), f32),
            shape((rows, part), f32), shape((tall, across, depth, chans), b16), shape((rows, part), f32),
            shape((rows, 128), f32), shape((8, part), f32), shape((rows, 128), f32),
        ],
        scratch_shapes=[
            keep(cols.shape, b16), keep(ext.shape, f32), keep(pre.shape, f32), keep(x_in.shape, b16), dma((4,)),
            keep((256, chans), b16), keep((7, rows, 128), b16), keep((rows, 128), f32), pltpu.SemaphoreType.REGULAR, keep(block, f32), keep(block, f32),
            keep(block, f32), keep(block, f32), keep(block, f32), keep((128, rows), b16), keep((rows, n, 128), f32),
            keep((rows, n, 128), f32), keep((n, chans), f32), keep((3 * n, chans), f32),
            keep((2, n, chans), b16), keep((count - 1, n, chans), b16), keep((1, chans), f32),
            keep((count - 1, 1, chans), f32), keep((1, chans), f32), keep((n, chans), f32), keep((3, rows, chans), b16),
            keep((n, chans), f32), keep((8, chans), f32), keep((tall * across * depth, chans), f32),
            keep((tall, across, depth, chans), b16), keep((across - 1, tall, depth, chans), b16),
            keep((tall, depth, chans), f32), keep((tall, depth, chans), b16), keep((tall - 1, depth, chans), b16),
            keep((2, chans // 128, part, 2, 128), b16), keep((2, part, chans), b16), keep((twins - 1, rows, part), b16),
            keep((twins - 1, rows, part), b16),
            keep((twins - 1, rows, part), b16), keep((twins - 1, rows, part), b16), keep((rows, 128), b16),
            keep((twins - 1, rows, 128), b16), keep((8, part), f32), keep((count - 1, 8, part), f32),
            keep((2, 2, count - 1, rows // 2, chans), b16),
            keep((chunks, 16 * n, chans), b16), keep((16 * n, chans), b16),
            keep((16 * n, chans), b16), keep((n, chans), f32), keep(block, f32), keep(block, f32), keep((rows, 256), f32), keep((rows, 256), b16), keep((twins - 1, rows, 256), b16),
            keep((rows + 8, chans), f32), keep((8, chans), f32),
            dma((2, chans // 128)), dma((2,)), *pair(twins - 1), *pair(across - 1), *pair(tall - 1), *pair(tall - 1),
            *pair(across - 1), *pair(count - 1), *pair(count - 1), *pair(twins - 1), *pair(twins - 1),
            *pair(count - 1), dma((2, 3)),
            dma((2, 2, count - 1)), dma((2, 2, count - 1)), dma((2, count - 1)), dma((2, count - 1)), *pair(twins - 1), dma((1,)), dma((1,)),
        ],
        compiler_params=pltpu.CompilerParams(collective_id=2, has_side_effects=True, vmem_limit_bytes=63 << 20),
        name="core",
    )(*operands)


def lane_blocks(w_in):
    kinds, width, _, chans = w_in.shape
    return w_in.reshape(kinds, width, 2, chans // 128, 128).transpose(0, 1, 3, 2, 4)


def finish_kernel(
    x_part_ref, z_part_ref, out_part_ref, *refs,
):
    sources, refs = refs[:9], refs[9:]
    (
        dw_in_ref, dw_out_ref, block_ref, dx_ref, gain_out_ref, taps_ref, cbias_ref, x_proj_ref, dt_proj_ref, dt_bias_ref,
        a_log_ref, skip_ref,
    ) = refs[:12]
    buffers, (x_buf, z_buf, out_buf, sems, out_sem, in_sem, big_sem) = refs[12:21], refs[21:]
    small_ref, slice_ref, mix_ref, mean_ref, scale_ref, cot_ref, x_ref, gain_ref, dgain_ref = buffers
    kinds, _, chans = x_part_ref.shape
    part = slice_ref.shape[1]
    mine = lax.axis_index("ch")
    own_part = pl.ds(pl.multiple_of(mine * part, part), part)
    fetches = [
        pltpu.make_async_copy(source.at[:, own_part] if i in (6, 7) else source, buffer, in_sem.at[i])
        for i, (source, buffer) in enumerate(zip(sources, buffers))
    ]
    large = [
        [
            pltpu.make_async_copy(source.at[m], target.at[m], big_sem.at[i, m])
            for i, (source, target) in enumerate(((x_part_ref, x_buf), (z_part_ref, z_buf), (out_part_ref, out_buf)))
        ]
        for m in range(kinds)
    ]
    for copy in fetches + sum(large, []):
        copy.start()
    for copy in fetches:
        copy.wait()
    scale = scale_ref[...]
    bent = scale * scale * scale * mean_ref[...]
    for q in range(part // 128):
        lanes = slice(q * 128, (q + 1) * 128)
        x = x_ref[:, lanes].astype(jnp.float32)
        block_ref[:, lanes] = (x + mix_ref[:, lanes]).astype(jnp.bfloat16)
        weighted = slice_ref[:, lanes] * gain_ref[:, lanes]
        dx_ref[:, lanes] = cot_ref[:, lanes].astype(jnp.float32) + scale * weighted - x * bent
    gain_out_ref[...] = dgain_ref[0:1]
    x_proj_ref[...] = small_ref[0:160].astype(jnp.float32)
    dt_proj_ref[...] = small_ref[160:288].astype(jnp.float32)
    a_log_ref[...] = small_ref[288:304].astype(jnp.float32)
    rest = small_ref[304:320].astype(jnp.float32)
    taps_ref[...] = rest[0:4]
    cbias_ref[...] = rest[4:5]
    dt_bias_ref[...] = rest[5:6]
    skip_ref[...] = rest[6:7]
    copies = []
    for m in range(kinds):
        for copy in large[m]:
            copy.wait()
        first = len(copies)
        copies.append(pltpu.make_async_copy(out_buf.at[m], dw_out_ref.at[m], out_sem.at[m]))
        for b in range(chans // 128):
            for j, source in enumerate((x_buf, z_buf)):
                slot = (m * (chans // 128) + b) * 2 + j
                copies.append(
                    pltpu.make_async_copy(source.at[m, :, pl.ds(b * 128, 128)], dw_in_ref.at[m, :, b, j], sems.at[slot])
                )
        for copy in copies[first:]:
            copy.start()
    for copy in copies:
        copy.wait()


def finish(x_part, z_part, out_part, small, total, mix, mean, scale, cot, x_in, gain, dgain):
    kinds, slab, chans = x_part.shape
    rows, part = total.shape
    vmem = pl.BlockSpec(memory_space=pltpu.VMEM)
    hbm = pl.BlockSpec(memory_space=pl.ANY)
    f32 = jnp.float32
    shape = jax.ShapeDtypeStruct
    outs = pl.pallas_call(
        finish_kernel,
        in_specs=[hbm] * 12,
        out_specs=[hbm] * 2 + [vmem] * 10,
        out_shape=[
            shape((kinds, slab, chans // 128, 2, 128), f32), shape((kinds, slab, chans), f32),
            shape((rows, part), jnp.bfloat16), shape((rows, part), f32), shape((1, part), f32), shape((4, chans), f32),
            shape((1, chans), f32), shape((160, chans), f32), shape((128, chans), f32), shape((1, chans), f32),
            shape((16, chans), f32), shape((1, chans), f32),
        ],
        scratch_shapes=[
            pltpu.VMEM(small.shape, small.dtype), pltpu.VMEM((rows, part), f32), pltpu.VMEM((rows, part), f32),
            pltpu.VMEM((rows, 128), f32), pltpu.VMEM((rows, 128), f32), pltpu.VMEM((rows, part), cot.dtype),
            pltpu.VMEM((rows, part), x_in.dtype), pltpu.VMEM((1, part), f32), pltpu.VMEM(dgain.shape, f32),
            pltpu.VMEM(x_part.shape, f32), pltpu.VMEM(x_part.shape, f32), pltpu.VMEM(x_part.shape, f32),
            pltpu.SemaphoreType.DMA((kinds * chans // 64,)), pltpu.SemaphoreType.DMA((kinds,)), pltpu.SemaphoreType.DMA((9,)),
            pltpu.SemaphoreType.DMA((3, kinds)),
        ],
        compiler_params=pltpu.CompilerParams(vmem_limit_bytes=60 << 20),
        name="finish",
    )(x_part, z_part, out_part, small, total, mix, mean, scale, cot, x_in, gain, dgain)
    dw_in = outs[0].transpose(0, 1, 3, 2, 4).reshape(kinds, slab, 2, chans)
    return (outs[2], outs[3], outs[4][0], dw_in, outs[5], outs[6][0], outs[7].T, outs[8], outs[9][0], outs[10], outs[11][0], outs[1])


def shards(
    x_in,
    norm_gain,
    w_in,
    conv_weight,
    conv_bias,
    x_proj,
    dt_proj,
    dt_bias,
    a_log,
    d_skip,
    w_out,
    modes,
    doc_lengths,
    cotangent,
):
    seq_count = lax.axis_size("seq")
    tok_rows = x_in.shape[0]
    inner_local = conv_bias.shape[0]
    docs = doc_lengths.shape[0]
    order = jnp.arange(docs, dtype=jnp.int32)
    starts = jnp.sum(jnp.where(order[:, None] > order[None, :], doc_lengths[None, :], 0), axis=1)
    starts = jnp.broadcast_to(starts[:, None], (docs, 128))
    mode_rows = modes.reshape(2 * seq_count, tok_rows // 2)
    blocks = lane_blocks(w_in)
    gain = norm_gain[None]
    x_proj_t = x_proj.T
    z_branch, d_gated, columns, extended, conv_pre, conv_out, maps = front(
        x_in, gain, mode_rows, cotangent, starts, conv_weight, conv_bias[None], x_proj_t, blocks, w_out
    )
    d_w_out, d_w_z, d_w_x, mixer, smalls, d_slice, mean, d_gain, scale = core(
        blocks, w_out, columns, extended, conv_pre, conv_out, maps, z_branch, d_gated, starts, conv_weight, x_proj_t,
        dt_proj, dt_bias[None], a_log, d_skip[None], mode_rows, x_in, gain,
    )
    return finish(
        d_w_x, d_w_z.reshape(d_w_x.shape), d_w_out.reshape(d_w_x.shape), smalls.reshape(-1, inner_local), d_slice, mixer,
        mean, scale, cotangent, x_in, gain, d_gain,
    )


def solution(mesh):
    return jax.shard_map(
        shards,
        mesh=mesh,
        in_specs=(
            P("seq", None),
            P(),
            P(None, None, None, "ch"),
            P(None, "ch"),
            P("ch"),
            P("ch", None),
            P(None, "ch"),
            P("ch"),
            P(None, "ch"),
            P("ch"),
            P(None, None, "ch"),
            P(),
            P(),
            P("seq", "ch"),
        ),
        out_specs=(
            P("seq", "ch"),
            P("seq", "ch"),
            P("ch"),
            P(None, "seq", None, "ch"),
            P(None, "ch"),
            P("ch"),
            P("ch", None),
            P(None, "ch"),
            P("ch"),
            P(None, "ch"),
            P("ch"),
            P(None, "seq", "ch"),
        ),
        check_vma=False,
    )
```
